32 devices in a mesh: dp: 8 (over z, y), ctx: 4 (over x, core).
Axes of the slice: x: 2, y: 2, z: 4, core: 2. Of those that a mesh axis runs over, the one named last changes fastest.
Arguments:
- layer_input: bfloat16 [4096, 2048], P(('dp', 'ctx')), may hold values from -6 to 6
- lengths: int32 [8], P('dp'), may hold values from 128 to 512, as said below
- cotangent: bfloat16 [4096, 2048], P(('dp', 'ctx')), may hold values from -6 to 6
- qkv_weight: bfloat16 [2048, 6144], P(('dp', 'ctx')), may hold values from -0.125 to 0.125
- qkv_bias: bfloat16 [6144], P(('dp', 'ctx')), may hold values from -1 to 1
- out_weight: bfloat16 [2048, 2048], P(('dp', 'ctx')), may hold values from -0.75 to 0.75
- out_bias: bfloat16 [2048], P(('dp', 'ctx')), may hold values from -1 to 1
- up_weight: bfloat16 [2048, 8192], P(('dp', 'ctx')), may hold values from -0.125 to 0.125
- up_bias: bfloat16 [8192], P(('dp', 'ctx')), may hold values from -1 to 1
- down_weight: bfloat16 [8192, 2048], P(('dp', 'ctx')), may hold values from -0.0625 to 0.0625
- down_bias: bfloat16 [2048], P(('dp', 'ctx')), may hold values from -1 to 1
- first_gain: bfloat16 [2048], P(('dp', 'ctx')), may hold values from 0.5 to 1.5
- first_bias: bfloat16 [2048], P(('dp', 'ctx')), may hold values from -1 to 1
- second_gain: bfloat16 [2048], P(('dp', 'ctx')), may hold values from 0.5 to 1.5
- second_bias: bfloat16 [2048], P(('dp', 'ctx')), may hold values from -1 to 1
Outputs:
- output: bfloat16 [4096, 2048], P(('dp', 'ctx'))
- input_grad: bfloat16 [4096, 2048], P(('dp', 'ctx'))
- qkv_weight_grad: float32 [2048, 6144], P(('dp', 'ctx'))
- qkv_bias_grad: float32 [6144], P(('dp', 'ctx'))
- out_weight_grad: float32 [2048, 2048], P(('dp', 'ctx'))
- out_bias_grad: float32 [2048], P(('dp', 'ctx'))
- up_weight_grad: float32 [2048, 8192], P(('dp', 'ctx'))
- up_bias_grad: float32 [8192], P(('dp', 'ctx'))
- down_weight_grad: float32 [8192, 2048], P(('dp', 'ctx'))
- down_bias_grad: float32 [2048], P(('dp', 'ctx'))
- first_gain_grad: float32 [2048], P(('dp', 'ctx'))
- first_bias_grad: float32 [2048], P(('dp', 'ctx'))
- second_gain_grad: float32 [2048], P(('dp', 'ctx'))
- second_bias_grad: float32 [2048], P(('dp', 'ctx'))
The draws below stay inside these ranges and needn't reach their ends.
Inputs may be any that keep to these rules, and one draw needn't show every extreme that they name: `lengths`: every slot's live positions come first; one slot has exactly 512 live positions and another exactly 128.
All inputs are finite; a program needn't handle non-finite values.
Results may differ from the reference program's by a relative error of at most 0.009.
Values may be sent and summed in bfloat16 or wider, within the bound.
A program may use at most 384 MiB of HBM per device.

```python
import math
import jax
import jax.numpy as jnp
from jax import lax

D = 2048
FF = 8192
HEADS = 8
HEAD_DIM = 256
ROT = 64
SLOT = 512
SLOTS = 8
TOKENS = 4096


def draw_lengths(key, part):
    first_key, second_key = jax.random.split(key)
    counts = jax.random.randint(first_key, (SLOTS,), SLOT // 4, SLOT + 1)
    chosen = jax.random.randint(second_key, (), 0, SLOTS)
    counts = counts.at[chosen].set(SLOT)
    counts = counts.at[(chosen + 1) % SLOTS].set(SLOT // 4)
    return counts.astype(jnp.int32)


def block_scale(rng, dims, cuts, smallest, high):
    gain, own = 1.0, jax.random.fold_in(rng, 6)
    for position, shards_of in cuts:
        draws = jnp.exp(jax.random.uniform(jax.random.fold_in(own, position), (shards_of,), jnp.float32, smallest / len(cuts), high / len(cuts)))
        gain = gain * jnp.repeat(draws, dims[position] // shards_of).reshape([-1 if axis == position else 1 for axis in range(len(dims))])
    return gain


def bell_draw(rng, dims, scale, limit, cuts=(), kind=jnp.bfloat16):
    gain = block_scale(rng, dims, cuts, -0.22, 0.18) if cuts else 1.0
    values = jax.random.normal(rng, dims, jnp.float32) * scale * gain
    return jnp.minimum(jnp.maximum(values, -limit), limit).astype(kind)


def setup_inputs(seed: int = 0) -> dict:
    key_of = jax.random.split(jax.random.key(seed), 16)
    return {
        "layer_input": bell_draw(key_of[0], (TOKENS, D), 1.0, 6.0, ((0, 32),)),
        "lengths": draw_lengths(jax.random.fold_in(key_of[15], 71), 0),
        "cotangent": bell_draw(key_of[2], (TOKENS, D), 1.0, 6.0, ((0, 32),)),
        "qkv_weight": bell_draw(key_of[3], (D, 3 * D), D ** -0.5, 0.125, ((0, 32),)),
        "qkv_bias": bell_draw(key_of[4], (3 * D,), 0.2, 1.0, ((0, 32),)),
        "out_weight": bell_draw(key_of[5], (D, D), (D // 32) ** -0.5, 0.75, ((0, 32),)),
        "out_bias": bell_draw(key_of[6], (D,), 0.2, 1.0, ((0, 32),)),
        "up_weight": bell_draw(key_of[7], (D, FF), D ** -0.5, 0.125, ((0, 32),)),
        "up_bias": bell_draw(key_of[8], (FF,), 0.2, 1.0, ((0, 32),)),
        "down_weight": bell_draw(key_of[9], (FF, D), FF ** -0.5, 0.0625, ((0, 32),)),
        "down_bias": bell_draw(key_of[10], (D,), 0.2, 1.0, ((0, 32),)),
        "first_gain": jnp.clip(1.0 + 0.1 * jax.random.normal(key_of[11], (D,), jnp.float32), 0.5, 1.5).astype(jnp.bfloat16),
        "first_bias": bell_draw(key_of[12], (D,), 0.2, 1.0, ((0, 32),)),
        "second_gain": jnp.clip(1.0 + 0.1 * jax.random.normal(key_of[13], (D,), jnp.float32), 0.5, 1.5).astype(jnp.bfloat16),
        "second_bias": bell_draw(key_of[14], (D,), 0.2, 1.0, ((0, 32),)),
    }


HIGHEST = lax.Precision.HIGHEST

@jax.custom_vjp
def low(v):
    return lax.optimization_barrier(v.astype(jnp.bfloat16)).astype(jnp.float32)

@jax.custom_vjp
def low_back(v):
    return v

def low_keep(v):
    return (low(v), None)

def low_pass(kept, grad):
    return (grad,)

def back_keep(v):
    return (v, None)

def back_low(kept, grad):
    return (low(grad),)
low.defvjp(low_keep, low_pass)
low_back.defvjp(back_keep, back_low)

def product(left, right):
    return jnp.dot(left, right, precision=HIGHEST, preferred_element_type=jnp.float32)

def normalize(values, gain_vec, shift_vec):
    center = lax.optimization_barrier(jnp.mean(values, axis=-1, keepdims=True))
    spread = lax.optimization_barrier(jnp.mean(jnp.square(values - center), axis=-1, keepdims=True))
    return (values - center) * lax.rsqrt(spread + 1e-05) * gain_vec + shift_vec

def tables(positions):
    half_rot = ROT // 2
    frequency = 10000.0 ** (-2.0 * jnp.arange(half_rot, dtype=jnp.float32) / ROT)
    angles = positions.astype(jnp.float32)[:, None] * frequency[None, :]
    return (jnp.cos(angles)[:, None, :], jnp.sin(angles)[:, None, :])

def rotate(vectors, cosine_tab, sine_tab):
    half_rot = ROT // 2
    low_half = vectors[..., :half_rot]
    high_half = vectors[..., half_rot:ROT]
    return jnp.concatenate([low_half * cosine_tab - high_half * sine_tab, high_half * cosine_tab + low_half * sine_tab, vectors[..., ROT:]], axis=-1)

def forward(params, slot_x, length):
    qkv_w, qkv_b, out_w, out_b, up_w, up_b, down_w, down_b, gain_one, shift_one, gain_two, shift_two = params
    positions = jnp.arange(SLOT, dtype=jnp.int32)
    valid_rows = positions < length
    normed_first = low(normalize(slot_x, gain_one, shift_one))
    joint_proj = low_back(product(normed_first, qkv_w) + qkv_b)
    cosine_tab, sine_tab = tables(positions)
    queries = low(rotate(joint_proj[:, :D].reshape(SLOT, HEADS, HEAD_DIM), cosine_tab, sine_tab))
    key_rows = low(rotate(joint_proj[:, D:2 * D].reshape(SLOT, HEADS, HEAD_DIM), cosine_tab, sine_tab))
    value_rows = low(joint_proj[:, 2 * D:].reshape(SLOT, HEADS, HEAD_DIM))
    score_scale = 1.0 / math.sqrt(HEAD_DIM)
    scores = low_back(jnp.einsum('qhd,khd->hqk', queries, key_rows, precision=HIGHEST) * score_scale)
    allowed = (positions[None, :] <= positions[:, None]) & valid_rows[None, :]
    scores = jnp.where(allowed[None], scores, -1e+30)
    attention = low(jax.nn.softmax(scores, axis=-1))
    mixed = jnp.einsum('hqk,khd->qhd', attention, value_rows, precision=HIGHEST).reshape(SLOT, D)
    head_out = low(low_back(mixed))
    attn_out = product(head_out, out_w) + out_b
    normed_second = low(normalize(slot_x, gain_two, shift_two))
    pre_act = low_back(product(normed_second, up_w) + up_b)
    hidden = low(jax.nn.gelu(pre_act, approximate=False))
    ffn_out = product(hidden, down_w) + down_b
    return jnp.where(valid_rows[:, None], slot_x + attn_out + ffn_out, 0.0)

def reference(layer_input, lengths, cotangent, qkv_weight, qkv_bias, out_weight, out_bias, up_weight, up_bias, down_weight, down_bias, first_gain, first_bias, second_gain, second_bias):
    weights = tuple((w.astype(jnp.float32) for w in (qkv_weight, qkv_bias, out_weight, out_bias, up_weight, up_bias, down_weight, down_bias, first_gain, first_bias, second_gain, second_bias)))
    slots_in = layer_input.astype(jnp.float32).reshape(SLOTS, SLOT, D)
    slots_cot = cotangent.astype(jnp.float32).reshape(SLOTS, SLOT, D)
    zero_grads = tuple((jnp.zeros_like(w) for w in weights))

    def advance(totals, inputs):
        slot_x, slot_cot, length = inputs
        result, pullback = jax.vjp(lambda params, values: forward(params, values, length), weights, slot_x)
        params_grad, values_grad = pullback(slot_cot)
        totals = jax.tree.map(jnp.add, totals, params_grad)
        return (totals, (result.astype(jnp.bfloat16), values_grad.astype(jnp.bfloat16)))
    totals, (outputs, in_grads) = lax.scan(advance, zero_grads, (slots_in, slots_cot, lengths))
    return (outputs.reshape(TOKENS, D), in_grads.reshape(TOKENS, D), totals[0], totals[1], totals[2], totals[3], totals[4], totals[5], totals[6], totals[7], totals[8], totals[9], totals[10], totals[11])
```

```python
import functools
import math

import jax
import jax.numpy as jnp
from jax import lax
from jax.experimental import pallas as pl
from jax.experimental.pallas import tpu as pltpu
from jax.sharding import PartitionSpec as P

HEADS = 8
HEAD_DIM = 256
ROT = 64
EPS = 1e-05
MESH = pl.DeviceIdType.MESH
BF = jnp.bfloat16
F32 = jnp.float32
VEC = 1024


class Plan:
    def __init__(self, dp, ctx, tok, d, ff):
        self.C = ctx
        self.X = ctx // 2
        self.A = HEADS // self.X
        self.S = dp // self.A
        self.n = dp * ctx
        self.tok = tok
        self.d = d
        self.ff = ff
        self.r = d // self.n
        self.R = ff // self.n
        self.ffl = self.S * self.R
        self.W = max(self.R, 128)
        self.P = self.W // self.R
        self.hc = 3 * HEAD_DIM
        self.m = HEAD_DIM // self.r // 2
        self.rows = self.A * self.C * tok


def remote(src, dst, send, recv, dev):
    return pltpu.make_async_remote_copy(
        src_ref=src, dst_ref=dst, send_sem=send, recv_sem=recv, device_id=dev, device_id_type=MESH
    )


def drain(ref, sem):
    pltpu.make_async_copy(ref, ref, sem).wait()


def unit_run(p, aa, cc, j):
    if p.P == 1:
        return p.R * ((aa * p.S + j) * p.C + cc)
    return p.R * ((aa * p.S + 2 * j + lax.rem(cc, 2)) * p.C + lax.div(cc, 2) * 2)


def unit_home(p, b, xh, core):
    if p.P == 1:
        return xh * 2 + core, b * p.R
    return xh * 2 + lax.rem(b, 2), (lax.div(b, 2) * 2 + core) * p.R


def place(p):
    dp = lax.axis_index("dp")
    c = lax.axis_index("ctx")
    a = lax.div(dp, p.S)
    b = lax.rem(dp, p.S)
    xh = lax.div(c, 2)
    core = lax.rem(c, 2)
    return dp, c, a, b, xh, core


def greet_all(p, me):
    barrier = pltpu.get_barrier_semaphore()

    def greet(k, carry):
        other = lax.rem(me + k, p.n)
        pl.semaphore_signal(
            barrier,
            inc=1,
            device_id=(lax.div(other, p.C), lax.rem(other, p.C)),
            device_id_type=MESH,
        )
        return carry

    lax.fori_loop(1, p.n, greet, 0)
    pl.semaphore_wait(barrier, p.n - 1)


def spread_kernel(
    p,
    x,
    g,
    qkv,
    outw,
    up,
    down,
    small,
    xa,
    ga,
    qw,
    dw,
    uw,
    sm,
    loc,
    s_sm,
    r_sm,
    s_up,
    r_up,
    s_upb,
    r_upb,
    s_q,
    r_q,
    s_qb,
    r_qb,
    s_qc,
    r_qc,
    s_o,
    r_o,
    s_oc,
    r_oc,
    s_d,
    r_d,
    s_r,
    r_r,
    s_l,
    r_l,
    s_x,
    r_x,
    s_s,
    r_s,
):
    A, S, C, r, R = p.A, p.S, p.C, p.r, p.R
    dp, c, a, b, xh, core = place(p)
    me = dp * C + c
    t = a * C + c
    head = a * p.X + xh
    sib = (dp, xh * 2 + 1 - core)
    xnb = (dp, (1 - xh) * 2 + core)
    right = (dp + S, c)
    left = (dp - S, c)
    greet_all(p, me)

    own_small = pltpu.make_async_copy(small, sm.at[me], loc.at[0])
    own_small.start()
    own_x = pltpu.make_async_copy(x, xa.at[a, c], loc.at[1])
    own_x.start()
    own_g = pltpu.make_async_copy(g, ga.at[a, c], loc.at[2])
    own_g.start()

    def up_piece(aa, cc, j):
        col = pl.multiple_of(unit_run(p, aa, cc, j), 128)
        return up.at[:, pl.ds(col, p.W)], uw.at[a, b, c, :, pl.ds(j * p.W, p.W)]

    def up_send(k, carry):
        tt = lax.rem(t + k, A * C)
        aa, cc = lax.div(tt, C), lax.rem(tt, C)
        for j in range(p.ffl // p.W):
            src, dst = up_piece(aa, cc, j)
            remote(src, dst, s_up, r_up, (aa * S + b, cc)).start()
        return carry

    lax.fori_loop(1, A * C, up_send, 0)
    for j in range(p.ffl // p.W):
        src, dst = up_piece(a, c, j)
        pltpu.make_async_copy(src, dst, r_up).start()

    def q_piece(hh, j):
        col = pl.multiple_of(j * p.d + hh * HEAD_DIM, HEAD_DIM)
        return (
            qkv.at[:, pl.ds(col, HEAD_DIM)],
            qw.at[a, b, xh, core, :, pl.ds(j * HEAD_DIM, HEAD_DIM)],
        )

    def q_send(k, carry):
        hh = lax.rem(head + k, HEADS)
        for j in range(3):
            src, dst = q_piece(hh, j)
            dev = (lax.div(hh, p.X) * S + b, lax.rem(hh, p.X) * 2 + core)
            remote(src, dst, s_q, r_q, dev).start()
        return carry

    lax.fori_loop(1, HEADS, q_send, 0)
    for j in range(3):
        src, dst = q_piece(head, j)
        pltpu.make_async_copy(src, dst, r_q).start()

    row_head = lax.div(me * r, HEAD_DIM)
    row_part = lax.div(lax.rem(me * r, HEAD_DIM), 2 * r)
    o_dst = dw.at[pl.ds(pl.multiple_of(p.ffl + (row_part * 2 + core) * r, r), r)]

    def o_dev(bb):
        return lax.div(row_head, p.X) * S + bb, lax.rem(row_head, p.X) * 2 + core

    for bb in range(S):
        od, oc = o_dev(bb)
        here = (od == dp) & (oc == c)

        @pl.when(jnp.logical_not(here))
        def _():
            remote(outw, o_dst, s_o.at[bb], r_o, (od, oc)).start()

        @pl.when(here)
        def _():
            pltpu.make_async_copy(outw, o_dst, r_o).start()

    d_ctx, d_row = unit_home(p, b, xh, core)
    d_dst = dw.at[pl.ds(pl.multiple_of(d_row, R), R)]
    for bb in range(S):
        here = (bb == b) & (d_ctx == c)

        @pl.when(jnp.logical_not(here))
        def _():
            remote(down, d_dst, s_d.at[bb], r_d, (a * S + bb, d_ctx)).start()

        @pl.when(here)
        def _():
            pltpu.make_async_copy(down, d_dst, r_d).start()

    streams = ((x, xa), (g, ga))

    for j, (own, full) in enumerate(streams):
        slot = full.at[a, c]

        @pl.when(a < A - 1)
        def _():
            remote(own, slot, s_r.at[j, 0], r_r.at[j, 0], right).start()

        @pl.when(a > 0)
        def _():
            remote(own, slot, s_l.at[j, 0], r_l.at[j, 0], left).start()

        remote(own, slot, s_x.at[j, a], r_x.at[j, a], xnb).start()
        remote(own, slot, s_s.at[j], r_s.at[j], sib).start()

    def small_send(k, carry):
        other = lax.rem(me + k, p.n)
        dev = (lax.div(other, C), lax.rem(other, C))
        remote(small, sm.at[me], s_sm, r_sm, dev).start()
        return carry

    lax.fori_loop(1, p.n, small_send, 0)

    drain(uw.at[:, b], r_up)

    def up_cross(k, carry):
        bb = lax.rem(b + k, S)
        remote(uw.at[:, b], uw.at[:, b], s_upb, r_upb, (a * S + bb, c)).start()
        return carry

    lax.fori_loop(1, S, up_cross, 0)
    drain(qw.at[:, b, :, core], r_q)

    def q_cross(k, carry):
        bb = lax.rem(b + k, S)
        part = qw.at[:, b, :, core]
        remote(part, part, s_qb, r_qb, (a * S + bb, c)).start()
        return carry

    lax.fori_loop(1, S, q_cross, 0)
    drain(dw.at[pl.ds(p.ffl, p.m * r)], r_o)
    for k in range(p.m):
        rows = dw.at[pl.ds(pl.multiple_of(p.ffl + (2 * k + core) * r, r), r)]
        remote(rows, rows, s_oc.at[k], r_oc.at[k], sib).start()

    for s in range(A - 1):
        for j, (own, full) in enumerate(streams):

            @pl.when(a - 1 - s >= 0)
            def _():
                blk = full.at[a - 1 - s, c]
                remote(blk, blk, s_r.at[j, s], r_r.at[j, s], left).wait_recv()
                if s + 1 < A - 1:

                    @pl.when(a < A - 1)
                    def _():
                        remote(blk, blk, s_r.at[j, s + 1], r_r.at[j, s + 1], right).start()

                remote(blk, blk, s_x.at[j, a - 1 - s], r_x.at[j, a - 1 - s], xnb).start()
                remote(blk, blk, s_s.at[j], r_s.at[j], sib).start()

            @pl.when(a + 1 + s <= A - 1)
            def _():
                blk = full.at[a + 1 + s, c]
                remote(blk, blk, s_l.at[j, s], r_l.at[j, s], right).wait_recv()
                if s + 1 < A - 1:

                    @pl.when(a > 0)
                    def _():
                        remote(blk, blk, s_l.at[j, s + 1], r_l.at[j, s + 1], left).start()

                remote(blk, blk, s_x.at[j, a + 1 + s], r_x.at[j, a + 1 + s], xnb).start()
                remote(blk, blk, s_s.at[j], r_s.at[j], sib).start()

        if s == 0:
            for _ in range(S - 1):
                drain(qw.at[:, b, :, core], r_qb)
            half = qw.at[:, :, :, core]
            remote(half, half, s_qc, r_qc, sib).start()

    xc = (1 - xh) * 2 + core
    for j, (own, full) in enumerate(streams):

        def cross(k):
            blk = full.at[k, xc]
            remote(blk, blk, s_x.at[j, k], r_x.at[j, k], xnb).wait_recv()
            remote(blk, blk, s_s.at[j], r_s.at[j], sib).start()

        cross(a)
        for s in range(A - 1):

            @pl.when(a - 1 - s >= 0)
            def _():
                cross(a - 1 - s)

            @pl.when(a + 1 + s <= A - 1)
            def _():
                cross(a + 1 + s)

    other_half = qw.at[:, :, :, 1 - core]
    drain(other_half, r_qc)
    for _ in range(S - 1):
        drain(uw.at[:, b], r_upb)
    drain(dw.at[pl.ds(0, p.ffl)], r_d)
    for k in range(p.m):
        drain(dw.at[pl.ds(0, r)], r_oc.at[k])
    drain(sm.at[pl.ds(0, p.n - 1)], r_sm)
    for j, (own, full) in enumerate(streams):
        drain(full.at[:, pl.ds(0, p.X)], r_s.at[j])

    own_small.wait()
    own_x.wait()
    own_g.wait()
    drain(sm.at[pl.ds(0, p.n - 1)], s_sm)
    for _ in range(A * C - 1):
        drain(uw.at[a, b, c], s_up)
    for _ in range(HEADS - 1):
        drain(qw.at[a, b, xh, core], s_q)
    for bb in range(S):
        od, oc = o_dev(bb)

        @pl.when(jnp.logical_not((od == dp) & (oc == c)))
        def _():
            drain(outw, s_o.at[bb])

        @pl.when(jnp.logical_not((bb == b) & (d_ctx == c)))
        def _():
            drain(down, s_d.at[bb])

    for k in range(p.m):
        drain(dw.at[pl.ds(0, r)], s_oc.at[k])
    for _ in range(S - 1):
        drain(uw.at[:, b], s_upb)
        drain(qw.at[:, b, :, core], s_qb)
    drain(other_half, s_qc)
    for j, (own, full) in enumerate(streams):
        for s in range(A - 1):

            @pl.when((a < A - 1) & (a - s >= 0))
            def _():
                drain(own, s_r.at[j, s])

            @pl.when((a > 0) & (a + s <= A - 1))
            def _():
                drain(own, s_l.at[j, s])

        for k in range(A):
            drain(own, s_x.at[j, k])
        drain(full.at[:, pl.ds(0, p.X)], s_s.at[j])


def spread(p, x, g, qkv, outw, up, down, small):
    dma = pltpu.SemaphoreType.DMA
    A, S, C, r = p.A, p.S, p.C, p.r
    return pl.pallas_call(
        functools.partial(spread_kernel, p),
        out_shape=(
            jax.ShapeDtypeStruct((A, C, p.tok, p.d), BF),
            jax.ShapeDtypeStruct((A, C, p.tok, p.d), BF),
            jax.ShapeDtypeStruct((A, S, p.X, 2, r, p.hc), BF),
            jax.ShapeDtypeStruct((p.ffl + HEAD_DIM, p.d), BF),
            jax.ShapeDtypeStruct((A, S, C, r, p.ffl), BF),
            jax.ShapeDtypeStruct((p.n, 8, VEC // 8), F32),
        ),
        in_specs=[pl.BlockSpec(memory_space=pltpu.VMEM)] * 7,
        out_specs=[pl.BlockSpec(memory_space=pl.ANY)] * 6,
        scratch_shapes=[
            dma((3,)),
            dma,
            dma,
            dma,
            dma,
            dma,
            dma,
            dma,
            dma,
            dma,
            dma,
            dma,
            dma,
            dma((S,)),
            dma,
            dma((p.m,)),
            dma((p.m,)),
            dma((S,)),
            dma,
            dma((2, A - 1)),
            dma((2, A - 1)),
            dma((2, A - 1)),
            dma((2, A - 1)),
            dma((2, A)),
            dma((2, A)),
            dma((2,)),
            dma((2,)),
        ],
        compiler_params=pltpu.CompilerParams(collective_id=0, has_side_effects=True),
        name="spread",
    )(x, g, qkv, outw, up, down, small)


def add_rows(dst, parts, rows):
    step = 16

    def body(k, carry):
        at = pl.ds(pl.multiple_of(k * step, step), step)
        total = parts[0][at, :].astype(F32)
        for part in parts[1:]:
            total = total + part[at, :].astype(F32)
        dst[at, :] = total.astype(dst.dtype)
        return carry

    lax.fori_loop(0, rows // step, body, 0)


def collect_kernel(
    p,
    op,
    ep,
    qg,
    og,
    ug,
    dg,
    vec,
    o_sum,
    e_sum,
    q_out,
    o_out,
    u_out,
    d_out,
    v_all,
    mine,
    from_sib,
    from_x,
    from_l,
    from_r,
    to_x,
    line,
    q_mine,
    q_sib,
    q_group,
    q_fin,
    o_mine,
    o_sib,
    o_parts,
    u_mine,
    u_parts,
    u_fin,
    d_mine,
    d_parts,
    loc,
    s_v,
    r_v,
    s_s,
    r_s,
    s_x,
    r_x,
    s_r,
    r_r,
    s_l,
    r_l,
    s_q,
    r_q,
    s_qb,
    r_qb,
    s_qa,
    r_qa,
    s_o,
    r_o,
    s_oa,
    r_oa,
    s_u,
    r_u,
    s_ua,
    r_ua,
    s_d,
    r_d,
):
    A, S, C, X, r, R = p.A, p.S, p.C, p.X, p.r, p.R
    dp, c, a, b, xh, core = place(p)
    me = dp * C + c
    t = a * C + c
    head = a * X + xh
    sib = (dp, xh * 2 + 1 - core)
    xnb = (dp, (1 - xh) * 2 + core)
    right = (dp + S, c)
    left = (dp - S, c)
    far = 1 - xh
    greet_all(p, me)

    parts = (op, ep)
    remote(qg.at[:, :, :, 1 - core], q_sib, s_q, r_q, sib).start()
    for j in range(2):
        for k in range(2):
            side = far if k == 0 else xh
            remote(
                parts[j].at[:, side, 1 - core],
                from_sib.at[j, :, side],
                s_s.at[j, k],
                r_s.at[j, k],
                sib,
            ).start()
            pltpu.make_async_copy(
                parts[j].at[:, side, core], mine.at[j, :, side], loc.at[2 * j + k]
            ).start()
    remote(og.at[:, 1 - core], o_sib, s_o, r_o, sib).start()
    own_q = pltpu.make_async_copy(qg.at[:, :, :, core], q_mine, loc.at[4])
    own_q.start()
    own_o = pltpu.make_async_copy(og.at[:, core], o_mine, loc.at[5])
    own_o.start()
    own_u = pltpu.make_async_copy(ug.at[:, b], u_mine, loc.at[6])
    own_u.start()
    own_v = pltpu.make_async_copy(vec, v_all.at[me], loc.at[7])
    own_v.start()

    def u_send(k, carry):
        bb = lax.rem(b + k, S)
        remote(ug.at[:, bb], u_parts.at[b], s_u, r_u, (a * S + bb, c)).start()
        return carry

    lax.fori_loop(1, S, u_send, 0)

    d_ctx, _ = unit_home(p, b, xh, core)
    for j in range(S):
        if p.P == 1:
            own_b, own_c = j, c
        else:
            own_b, own_c = 2 * (j // 2) + core, xh * 2 + j % 2
        src = dg.at[pl.ds(j * R, R)]
        here = (own_b == b) & (own_c == c)

        @pl.when(jnp.logical_not(here))
        def _():
            remote(src, d_parts.at[b], s_d.at[j], r_d, (a * S + own_b, own_c)).start()

        @pl.when(here)
        def _():
            pltpu.make_async_copy(src, d_parts.at[b], r_d).start()

    def v_send(k, carry):
        other = lax.rem(me + k, p.n)
        dev = (lax.div(other, C), lax.rem(other, C))
        remote(vec, v_all.at[me], s_v, r_v, dev).start()
        return carry

    lax.fori_loop(1, p.n, v_send, 0)

    def far_first(step):
        for s in range(A - 1, 0, -1):

            @pl.when(a + s <= A - 1)
            def _():
                step(a + s)

            @pl.when(a - s >= 0)
            def _():
                step(a - s)

        step(a)

    def halves(j):
        drain(mine.at[j, :, far], loc.at[2 * j])
        drain(from_sib.at[j, :, far], r_s.at[j, 0])

        def send_x(k):
            add_rows(to_x.at[j, k], (mine.at[j, k, far], from_sib.at[j, k, far]), p.tok)
            remote(to_x.at[j, k], from_x.at[j, k], s_x.at[j, k], r_x.at[j, k], xnb).start()

        far_first(send_x)

    halves(0)
    own_q.wait()
    drain(q_sib, r_q)
    for aa in range(A):
        for bb in range(S):
            for xx in range(X):
                add_rows(
                    q_mine.at[aa, bb, xx], (q_mine.at[aa, bb, xx], q_sib.at[aa, bb, xx]), r
                )

    def q_cross(k, carry):
        bb = lax.rem(b + k, S)
        remote(q_mine.at[:, bb], q_group.at[b], s_qb, r_qb, (a * S + bb, c)).start()
        return carry

    lax.fori_loop(1, S, q_cross, 0)
    own_o.wait()
    drain(o_sib, r_o)
    for k in range(p.m):
        add_rows(o_mine.at[k], (o_mine.at[k], o_sib.at[k]), r)
        owner = lax.div(head * HEAD_DIM, r) + 2 * k + core
        od, oc = lax.div(owner, C), lax.rem(owner, C)
        here = owner == me

        @pl.when(jnp.logical_not(here))
        def _():
            remote(o_mine.at[k], o_parts.at[b], s_oa.at[k], r_oa, (od, oc)).start()

        @pl.when(here)
        def _():
            pltpu.make_async_copy(o_mine.at[k], o_parts.at[b], r_oa).start()

    halves(1)

    own_u.wait()
    for _ in range(S - 1):
        drain(u_mine, r_u)
    for aa in range(A):
        for cc in range(C):
            if S == 2:
                add_rows(
                    u_fin.at[aa, cc], (u_mine.at[aa, cc], u_parts.at[1 - b, aa, cc]), r
                )
            else:
                for k in range(1, S):
                    add_rows(
                        u_mine.at[aa, cc],
                        (u_mine.at[aa, cc], u_parts.at[lax.rem(b + k, S), aa, cc]),
                        r,
                    )
                add_rows(u_fin.at[aa, cc], (u_mine.at[aa, cc],), r)

    def u_piece(tt, j):
        col = pl.multiple_of(unit_run(p, a, c, j), 128)
        aa, cc = lax.div(tt, C), lax.rem(tt, C)
        return u_fin.at[aa, cc, :, pl.ds(j * p.W, p.W)], u_out.at[:, pl.ds(col, p.W)]

    def u_back(k, carry):
        tt = lax.rem(t + k, A * C)
        for j in range(p.ffl // p.W):
            src, dst = u_piece(tt, j)
            remote(src, dst, s_ua, r_ua, (lax.div(tt, C) * S + b, lax.rem(tt, C))).start()
        return carry

    lax.fori_loop(1, A * C, u_back, 0)
    for j in range(p.ffl // p.W):
        src, dst = u_piece(t, j)
        pltpu.make_async_copy(src, dst, r_ua).start()

    for _ in range(S - 1):
        drain(q_group.at[0], r_qb)
    for aa in range(A):
        for xx in range(X):
            if S == 2:
                add_rows(
                    q_fin.at[aa, xx], (q_mine.at[aa, b, xx], q_group.at[1 - b, aa, xx]), r
                )
            else:
                for k in range(1, S):
                    add_rows(
                        q_mine.at[aa, b, xx],
                        (q_mine.at[aa, b, xx], q_group.at[lax.rem(b + k, S), aa, xx]),
                        r,
                    )
                add_rows(q_fin.at[aa, xx], (q_mine.at[aa, b, xx],), r)

    def q_piece(hh, j):
        col = pl.multiple_of(j * p.d + head * HEAD_DIM, HEAD_DIM)
        return (
            q_fin.at[lax.div(hh, X), lax.rem(hh, X), :, pl.ds(j * HEAD_DIM, HEAD_DIM)],
            q_out.at[:, pl.ds(col, HEAD_DIM)],
        )

    def q_back(k, carry):
        hh = lax.rem(head + k, HEADS)
        dev = (lax.div(hh, X) * S + b, lax.rem(hh, X) * 2 + core)
        for j in range(3):
            src, dst = q_piece(hh, j)
            remote(src, dst, s_qa, r_qa, dev).start()
        return carry

    lax.fori_loop(1, HEADS, q_back, 0)
    for j in range(3):
        src, dst = q_piece(head, j)
        pltpu.make_async_copy(src, dst, r_qa).start()

    def column(j, total):
        drain(mine.at[j, :, xh], loc.at[2 * j + 1])
        drain(from_sib.at[j, :, xh], r_s.at[j, 1])

        def hop(k, first, came, s_, r_, dev, whence):
            got = (mine.at[j, k, xh], from_sib.at[j, k, xh], from_x.at[j, k])

            @pl.when(first)
            def _():
                add_rows(line.at[j, k], got, p.tok)

            @pl.when(jnp.logical_not(first))
            def _():
                remote(came.at[j, k], came.at[j, k], s_.at[j, k], r_.at[j, k], whence).wait_recv()
                add_rows(line.at[j, k], got + (came.at[j, k],), p.tok)

            remote(line.at[j, k], came.at[j, k], s_.at[j, k], r_.at[j, k], dev).start()

        for s in range(A - 1, 0, -1):

            @pl.when(a + s <= A - 1)
            def _():
                k = a + s
                remote(to_x.at[j, k], from_x.at[j, k], s_x.at[j, k], r_x.at[j, k], xnb).wait_recv()
                hop(k, a == 0, from_l, s_r, r_r, right, left)

            @pl.when(a - s >= 0)
            def _():
                k = a - s
                remote(to_x.at[j, k], from_x.at[j, k], s_x.at[j, k], r_x.at[j, k], xnb).wait_recv()
                hop(k, a == A - 1, from_r, s_l, r_l, left, right)

        remote(to_x.at[j, a], from_x.at[j, a], s_x.at[j, a], r_x.at[j, a], xnb).wait_recv()
        add_rows(
            line.at[j, a], (mine.at[j, a, xh], from_sib.at[j, a, xh], from_x.at[j, a]), p.tok
        )

    column(0, o_sum)
    column(1, e_sum)
    for j, total in enumerate((o_sum, e_sum)):

        @pl.when(a == 0)
        def _():
            remote(from_r.at[j, a], from_r.at[j, a], s_l.at[j, a], r_l.at[j, a], right).wait_recv()
            add_rows(total, (line.at[j, a], from_r.at[j, a]), p.tok)

        @pl.when(a == A - 1)
        def _():
            remote(from_l.at[j, a], from_l.at[j, a], s_r.at[j, a], r_r.at[j, a], left).wait_recv()
            add_rows(total, (line.at[j, a], from_l.at[j, a]), p.tok)

        @pl.when((a > 0) & (a < A - 1))
        def _():
            remote(from_r.at[j, a], from_r.at[j, a], s_l.at[j, a], r_l.at[j, a], right).wait_recv()
            remote(from_l.at[j, a], from_l.at[j, a], s_r.at[j, a], r_r.at[j, a], left).wait_recv()
            add_rows(total, (line.at[j, a], from_l.at[j, a], from_r.at[j, a]), p.tok)

    drain(d_parts, r_d)
    add_rows(d_out, tuple(d_parts.at[k] for k in range(S)), R)
    drain(o_parts, r_oa)
    add_rows(o_out, tuple(o_parts.at[k] for k in range(S)), r)

    drain(u_out, r_ua)
    drain(q_out, r_qa)
    drain(v_all.at[pl.ds(0, p.n - 1)], r_v)

    own_v.wait()
    drain(v_all.at[pl.ds(0, p.n - 1)], s_v)
    drain(q_sib, s_q)
    drain(o_sib, s_o)
    for _ in range(S - 1):
        drain(u_mine, s_u)
        drain(q_group.at[0], s_qb)
    for _ in range(A * C - 1):
        drain(u_fin.at[0, 0], s_ua)
    for _ in range(HEADS - 1):
        drain(q_fin.at[0, 0], s_qa)
    for k in range(p.m):

        @pl.when(lax.div(head * HEAD_DIM, r) + 2 * k + core != me)
        def _():
            drain(o_mine.at[k], s_oa.at[k])

    for j in range(S):
        if p.P == 1:
            own_b, own_c = j, c
        else:
            own_b, own_c = 2 * (j // 2) + core, xh * 2 + j % 2

        @pl.when(jnp.logical_not((own_b == b) & (own_c == c)))
        def _():
            drain(d_parts.at[0], s_d.at[j])

    for j in range(2):
        for k in range(2):
            drain(from_sib.at[j, :, 0], s_s.at[j, k])
        for k in range(A):
            drain(to_x.at[j, k], s_x.at[j, k])

            @pl.when(k > a)
            def _():
                drain(line.at[j, k], s_r.at[j, k])

            @pl.when(k < a)
            def _():
                drain(line.at[j, k], s_l.at[j, k])


def collect(p, op, ep, qg, og, ug, dg, vec):
    dma = pltpu.SemaphoreType.DMA
    A, S, C, X, r, R = p.A, p.S, p.C, p.X, p.r, p.R
    vm = pltpu.VMEM
    return pl.pallas_call(
        functools.partial(collect_kernel, p),
        out_shape=(
            jax.ShapeDtypeStruct((p.tok, p.d), F32),
            jax.ShapeDtypeStruct((p.tok, p.d), F32),
            jax.ShapeDtypeStruct((r, 3 * p.d), BF),
            jax.ShapeDtypeStruct((r, p.d), F32),
            jax.ShapeDtypeStruct((r, p.ff), BF),
            jax.ShapeDtypeStruct((R, p.d), F32),
            jax.ShapeDtypeStruct((p.n, 16, 128), F32),
        ),
        in_specs=[pl.BlockSpec(memory_space=pl.ANY)] * 6 + [pl.BlockSpec(memory_space=pltpu.VMEM)],
        out_specs=[pl.BlockSpec(memory_space=pltpu.VMEM)] * 7,
        scratch_shapes=[
            vm((2, A, X, p.tok, p.d), BF),
            vm((2, A, X, p.tok, p.d), BF),
            vm((2, A, p.tok, p.d), BF),
            vm((2, A, p.tok, p.d), BF),
            vm((2, A, p.tok, p.d), BF),
            vm((2, A, p.tok, p.d), BF),
            vm((2, A, p.tok, p.d), BF),
            vm((A, S, X, r, p.hc), BF),
            vm((A, S, X, r, p.hc), BF),
            vm((S, A, X, r, p.hc), BF),
            vm((A, X, r, p.hc), BF),
            vm((p.m, r, p.d), BF),
            vm((p.m, r, p.d), BF),
            vm((S, r, p.d), BF),
            vm((A, C, r, p.ffl), BF),
            vm((S, A, C, r, p.ffl), BF),
            vm((A, C, r, p.ffl), BF),
            vm((1, 8, 128), BF),
            vm((S, R, p.d), BF),
            dma((8,)),
            dma,
            dma,
            dma((2, 2)),
            dma((2, 2)),
            dma((2, A)),
            dma((2, A)),
            dma((2, A)),
            dma((2, A)),
            dma((2, A)),
            dma((2, A)),
            dma,
            dma,
            dma,
            dma,
            dma,
            dma,
            dma,
            dma,
            dma((p.m,)),
            dma,
            dma,
            dma,
            dma,
            dma,
            dma((S,)),
            dma,
        ],
        compiler_params=pltpu.CompilerParams(
            collective_id=1, has_side_effects=True, vmem_limit_bytes=60 * 1024 * 1024
        ),
        name="collect",
    )(op, ep, qg, og, ug, dg, vec)


def norm_stats(values):
    center = jnp.mean(values, axis=-1, keepdims=True)
    spread = jnp.mean(jnp.square(values - center), axis=-1, keepdims=True)
    inv_std = lax.rsqrt(spread + EPS)
    return (values - center) * inv_std, inv_std


def tables(length):
    half = ROT // 2
    frequency = 10000.0 ** (-2.0 * jnp.arange(half, dtype=F32) / ROT)
    angles = jnp.arange(length, dtype=F32)[:, None] * frequency[None, :]
    return jnp.cos(angles), jnp.sin(angles)


def rotate(v, cos, sin):
    half = ROT // 2
    lo, hi = v[..., :half], v[..., half:ROT]
    return jnp.concatenate([lo * cos - hi * sin, hi * cos + lo * sin, v[..., ROT:]], axis=-1)


def dot(x, y):
    return jnp.dot(x, y, preferred_element_type=F32)


def dot_t(x, y):
    return lax.dot_general(x, y, (((1,), (1,)), ((), ())), preferred_element_type=F32)


def t_dot(x, y):
    return lax.dot_general(x, y, (((0,), (0,)), ((), ())), preferred_element_type=F32)


def attention(joint, d_heads, length, scale):
    cos, sin = tables(length)
    joint = joint.reshape(-1, length, 3 * HEAD_DIM)
    q = rotate(joint[..., :HEAD_DIM], cos, sin).astype(BF)
    k = rotate(joint[..., HEAD_DIM : 2 * HEAD_DIM], cos, sin).astype(BF)
    v = joint[..., 2 * HEAD_DIM :].astype(BF)
    pos = jnp.arange(length, dtype=jnp.int32)
    allowed = (pos[None, :] <= pos[:, None])[None]
    scores = jnp.einsum("sqd,skd->sqk", q, k, preferred_element_type=F32) * scale
    scores = jnp.where(allowed, scores, -1e30)
    expo = jnp.exp(scores - jnp.max(scores, axis=-1, keepdims=True))
    probs = expo / jnp.sum(expo, axis=-1, keepdims=True)
    low = probs.astype(BF)
    head_out = jnp.einsum("sqk,skd->sqd", low, v, preferred_element_type=F32).astype(BF)
    d_heads = d_heads.reshape(head_out.shape)
    dv = jnp.einsum("sqk,sqd->skd", low, d_heads, preferred_element_type=F32)
    dp = jnp.einsum("sqd,skd->sqk", d_heads, v, preferred_element_type=F32)
    delta = jnp.sum(probs * dp, axis=-1, keepdims=True)
    ds = (probs * (dp - delta)).astype(BF)
    dq = jnp.einsum("sqk,skd->sqd", ds, k, preferred_element_type=F32) * scale
    dk = jnp.einsum("sqk,sqd->skd", ds, q, preferred_element_type=F32) * scale
    d_joint = jnp.concatenate([rotate(dq, cos, -sin), rotate(dk, cos, -sin), dv], axis=-1)
    return head_out.reshape(-1, HEAD_DIM), d_joint.reshape(-1, 3 * HEAD_DIM).astype(BF)


def gelu_and_slope(v):
    phi = 0.5 * (1.0 + lax.erf(v * (1.0 / math.sqrt(2.0))))
    density = jnp.exp(-0.5 * v * v) * (1.0 / math.sqrt(2.0 * math.pi))
    return v * phi, phi + v * density


def local(
    dp_size,
    ctx_size,
    layer_input,
    lengths,
    cotangent,
    qkv_weight,
    qkv_bias,
    out_weight,
    out_bias,
    up_weight,
    up_bias,
    down_weight,
    down_bias,
    first_gain,
    first_bias,
    second_gain,
    second_bias,
):
    tok, d = layer_input.shape
    ff = up_weight.shape[1]
    p = Plan(dp_size, ctx_size, tok, d, ff)
    A, S, C, X, r, R = p.A, p.S, p.C, p.X, p.r, p.R
    dp, c, a, b, xh, core = place(p)
    me = dp * C + c
    t = a * C + c
    length = C * tok

    valid = (c * tok + jnp.arange(tok, dtype=jnp.int32) < lengths[0])[:, None]
    grad_out = jnp.where(valid, cotangent, jnp.zeros_like(cotangent))
    smalls = (
        qkv_bias,
        out_bias,
        up_bias,
        down_bias,
        first_gain,
        first_bias,
        second_gain,
        second_bias,
    )
    small = jnp.concatenate([v.astype(F32) for v in smalls])
    small = jnp.pad(small, (0, VEC - small.shape[0])).reshape(8, VEC // 8)
    x_all, g_all, qw, dw, uw, sm = spread(
        p, layer_input, grad_out, qkv_weight, out_weight, up_weight, down_weight, small
    )
    sm = sm.reshape(p.n, VEC)
    full, at = [], 0
    for v in smalls:
        full.append(sm[:, at : at + v.shape[0]].reshape(-1))
        at += v.shape[0]
    qkvb, outb, upb, downb, gain1, bias1, gain2, bias2 = full
    rows = p.rows
    mine = rows // 2
    head = a * X + xh
    x_all = x_all.reshape(rows, d)
    g_all = g_all.reshape(rows, d)
    qw = qw.reshape(d, p.hc)
    uw = uw.reshape(d, p.ffl)
    qb = lax.dynamic_index_in_dim(qkvb.reshape(3, HEADS, HEAD_DIM), head, 1, False).reshape(-1)
    if p.P == 1:
        ub = lax.dynamic_slice(upb.reshape(A, S, C, R), (a, 0, c, 0), (1, S, 1, R))
    else:
        ub = lax.dynamic_slice(
            upb.reshape(A, S // 2, 2, X, p.W), (a, 0, core, xh, 0), (1, S // 2, 1, 1, p.W)
        )
    ub = ub.reshape(-1)

    xs = lax.dynamic_slice(x_all, (core * mine, 0), (mine, d)).astype(F32)
    gs = lax.dynamic_slice(g_all, (core * mine, 0), (mine, d))
    xhat_s, _ = norm_stats(xs)
    n1 = (xhat_s * gain1 + bias1).astype(BF)
    joint = dot(n1, qw) + qb
    ow = dw[p.ffl :]
    d_heads = dot_t(gs, ow).astype(BF)
    head_out, d_joint = attention(joint, d_heads, length, 1.0 / math.sqrt(HEAD_DIM))
    out_grad = t_dot(head_out, gs).astype(BF)
    qkv_grad = t_dot(n1, d_joint).astype(BF)
    e1 = (dot_t(d_joint, qw) * gain1).astype(BF)
    qkv_bias_part = jnp.sum(d_joint.astype(F32), axis=0)

    xhat, _ = norm_stats(x_all.astype(F32))
    n2 = (xhat * gain2 + bias2).astype(BF)
    pre = dot(n2, uw) + ub
    act, slope = gelu_and_slope(pre)
    hidden = act.astype(BF)
    wide = jnp.zeros((rows, HEAD_DIM), BF)
    wide = lax.dynamic_update_slice(wide, head_out, (core * mine, 0))
    out_part = dot(jnp.concatenate([hidden, wide], axis=1), dw).astype(BF)
    down_grad = t_dot(hidden, g_all).astype(BF)
    d_pre = (dot_t(g_all, dw[: p.ffl]) * slope).astype(BF)
    up_grad = t_dot(n2, d_pre).astype(BF)
    up_bias_part = jnp.sum(d_pre.astype(F32), axis=0)
    e_part = dot_t(d_pre, uw) * gain2
    e_wide = jnp.zeros((rows, d), BF)
    e_wide = lax.dynamic_update_slice(e_wide, e1, (core * mine, 0))
    e_part = (e_part + e_wide.astype(F32)).astype(BF)

    g_cols = d // (A * C)
    g_part = lax.dynamic_slice(g_all, (0, t * g_cols), (rows, g_cols))
    g_part = jnp.sum(g_part.astype(F32), axis=0)
    vec = jnp.concatenate([qkv_bias_part, up_bias_part, g_part])
    vec = jnp.pad(vec, (0, 2048 - vec.shape[0])).reshape(16, 128)

    o_sum, e_sum, q_out, o_out, u_out, d_out, v_all = collect(
        p,
        out_part.reshape(A, X, 2, tok, d),
        e_part.reshape(A, X, 2, tok, d),
        qkv_grad.reshape(A, S, X, 2, r, p.hc),
        out_grad.reshape(p.m, 2, r, d),
        up_grad.reshape(A, S, C, r, p.ffl),
        down_grad,
        vec,
    )

    xf = layer_input.astype(F32)
    output = jnp.where(valid, xf + o_sum + (outb + downb), 0.0).astype(BF)
    xhat_o, inv = norm_stats(xf)
    dx = inv * (
        e_sum
        - jnp.mean(e_sum, axis=-1, keepdims=True)
        - xhat_o * jnp.mean(e_sum * xhat_o, axis=-1, keepdims=True)
    )
    input_grad = (grad_out.astype(F32) + dx).astype(BF)

    v_all = v_all.reshape(A, S, C, 2048)
    v_sum = jnp.sum(v_all, axis=1)
    q_bias = v_sum[..., : p.hc].reshape(A, X, 2, 3, HEAD_DIM).sum(axis=2)
    q_bias = q_bias.reshape(HEADS, 3, HEAD_DIM).transpose(1, 0, 2).reshape(-1)
    u_bias = v_sum[..., p.hc : p.hc + p.ffl]
    if p.P == 1:
        u_bias = u_bias.reshape(A, C, S, R).transpose(0, 2, 1, 3).reshape(-1)
    else:
        u_bias = u_bias.reshape(A, X, 2, S // 2, p.W).transpose(0, 3, 2, 1, 4).reshape(-1)
    g_bias = v_sum[..., p.hc + p.ffl : p.hc + p.ffl + g_cols].reshape(-1)

    def own(vector):
        size = vector.shape[0] // p.n
        return lax.dynamic_slice(vector, (me * size,), (size,))

    def norm_grads(weight, grad, bias_grad, gain, shift):
        weight = weight.astype(F32)
        shift_grad = jnp.sum(weight * bias_grad, axis=1)
        gain_grad = (jnp.sum(weight * grad, axis=1) - shift.astype(F32) * shift_grad) / gain.astype(
            F32
        )
        return gain_grad, shift_grad

    q_grad = q_out.astype(F32)
    u_grad = u_out.astype(F32)
    gain1_grad, bias1_grad = norm_grads(qkv_weight, q_grad, q_bias, first_gain, first_bias)
    gain2_grad, bias2_grad = norm_grads(up_weight, u_grad, u_bias, second_gain, second_bias)
    g_own = own(g_bias)
    return (
        output,
        input_grad,
        q_grad,
        own(q_bias),
        o_out,
        g_own,
        u_grad,
        own(u_bias),
        d_out,
        g_own,
        gain1_grad,
        bias1_grad,
        gain2_grad,
        bias2_grad,
    )


def solution(mesh):
    rows = P(("dp", "ctx"), None)
    vector = P(("dp", "ctx"))
    return jax.shard_map(
        functools.partial(local, mesh.shape["dp"], mesh.shape["ctx"]),
        mesh=mesh,
        in_specs=(
            rows,
            P("dp"),
            rows,
            rows,
            vector,
            rows,
            vector,
            rows,
            vector,
            rows,
            vector,
            vector,
            vector,
            vector,
            vector,
        ),
        out_specs=(
            rows,
            rows,
            rows,
            vector,
            rows,
            vector,
            rows,
            vector,
            rows,
            vector,
            vector,
            vector,
            vector,
            vector,
        ),
        check_vma=False,
    )
```

```python
import functools
import math

import jax
import jax.numpy as jnp
from jax import lax
from jax.experimental import pallas as pl
from jax.experimental.pallas import tpu as pltpu
from jax.sharding import PartitionSpec as P

HEADS = 8
HEAD_DIM = 256
ROT = 64
EPS = 1e-05
SCALE = 1.0 / math.sqrt(HEAD_DIM)
MESH = pl.DeviceIdType.MESH
BF = jnp.bfloat16
F32 = jnp.float32
TILE = 256
LANES = 128


class Plan:
    def __init__(self, dp, ctx, tok, d, ff):
        self.C = ctx
        self.X = ctx // 2
        self.A = HEADS // self.X
        self.S = dp // self.A
        self.n = dp * ctx
        self.tok = tok
        self.d = d
        self.ff = ff
        self.r = d // self.n
        self.R = ff // self.n
        self.ffl = self.S * self.R
        self.W = max(self.R, 128)
        self.P = self.W // self.R
        self.hc = 3 * HEAD_DIM
        self.m = HEAD_DIM // self.r // 2
        self.rows = self.A * self.C * tok


def remote(src, dst, send, recv, dev):
    return pltpu.make_async_remote_copy(
        src_ref=src, dst_ref=dst, send_sem=send, recv_sem=recv, device_id=dev, device_id_type=MESH
    )


def drain(ref, sem):
    pltpu.make_async_copy(ref, ref, sem).wait()


def unit_run(p, aa, cc, j):
    if p.P == 1:
        return p.R * ((aa * p.S + j) * p.C + cc)
    return p.R * ((aa * p.S + 2 * j + lax.rem(cc, 2)) * p.C + lax.div(cc, 2) * 2)


def unit_home(p, b, xh, core):
    if p.P == 1:
        return xh * 2 + core, b * p.R
    return xh * 2 + lax.rem(b, 2), (lax.div(b, 2) * 2 + core) * p.R


def place(p):
    dp = lax.axis_index("dp")
    c = lax.axis_index("ctx")
    a = lax.div(dp, p.S)
    b = lax.rem(dp, p.S)
    xh = lax.div(c, 2)
    core = lax.rem(c, 2)
    return dp, c, a, b, xh, core


def greet_all(p, me):
    barrier = pltpu.get_barrier_semaphore()

    def greet(k, carry):
        other = lax.rem(me + k, p.n)
        pl.semaphore_signal(
            barrier,
            inc=1,
            device_id=(lax.div(other, p.C), lax.rem(other, p.C)),
            device_id_type=MESH,
        )
        return carry

    lax.fori_loop(1, p.n, greet, 0)
    pl.semaphore_wait(barrier, p.n - 1)


def dot(x, y):
    return jnp.dot(x, y, preferred_element_type=F32)


def dot_t(x, y):
    return lax.dot_general(x, y, (((1,), (1,)), ((), ())), preferred_element_type=F32)


def t_dot(x, y):
    return lax.dot_general(x, y, (((0,), (0,)), ((), ())), preferred_element_type=F32)


def tiles(count, body, size=TILE):
    def run(i, carry):
        body(pl.multiple_of(i * size, size))
        return carry

    lax.fori_loop(0, count // size, run, 0)


def pick(values, i):
    out = values[0]
    for k in range(1, len(values)):
        out = jnp.where(i == k, values[k], out)
    return out


def far_order(p, a):
    order = []
    lo, hi = 0, p.A - 1
    for _ in range(p.A):
        up_far = hi - a >= a - lo
        order.append(jnp.where(up_far, hi, lo))
        lo = jnp.where(up_far, lo, lo + 1)
        hi = jnp.where(up_far, hi - 1, hi)
    return order


def add_rows(dst, parts, rows):
    step = 16

    def body(k, carry):
        at = pl.ds(pl.multiple_of(k * step, step), step)
        total = parts[0][at, :].astype(F32)
        for part in parts[1:]:
            total = total + part[at, :].astype(F32)
        dst[at, :] = total.astype(dst.dtype)
        return carry

    lax.fori_loop(0, rows // step, body, 0)


def angle_tables(cos_v, sin_v):
    rows = cos_v.shape[0]
    half = ROT // 2

    def body(at):
        shape = (64, LANES)
        lane = lax.broadcasted_iota(jnp.int32, shape, 1)
        pos = (lax.broadcasted_iota(jnp.int32, shape, 0) + at).astype(F32)
        exponent = lax.rem(lane, half).astype(F32) * (-2.0 * math.log(10000.0) / ROT)
        angle = pos * jnp.exp(exponent)
        turned = lane < ROT
        sign = jnp.where(lane < half, -1.0, 1.0)
        cos_v[pl.ds(at, 64), :] = jnp.where(turned, jnp.cos(angle), 1.0)
        sin_v[pl.ds(at, 64), :] = jnp.where(turned, jnp.sin(angle) * sign, 0.0)

    tiles(rows, body, 64)


def turn(v, cos, sin):
    first = v[:, :LANES]
    half = ROT // 2
    lane = lax.broadcasted_iota(jnp.int32, first.shape, 1)
    partner = jnp.where(
        lane < half, pltpu.roll(first, LANES - half, 1), pltpu.roll(first, half, 1)
    )
    return jnp.concatenate([first * cos + partner * sin, v[:, LANES:]], axis=1)


def probabilities(q, k, row0, scale):
    scores = dot_t(q, k) * scale
    row = lax.broadcasted_iota(jnp.int32, scores.shape, 0) + row0
    col = lax.broadcasted_iota(jnp.int32, scores.shape, 1)
    scores = jnp.where(col <= row, scores, -1e30)
    expo = jnp.exp(scores - jnp.max(scores, axis=1, keepdims=True))
    return expo / jnp.sum(expo, axis=1, keepdims=True)


def front_kernel(
    p,
    x,
    g,
    qkv,
    outw,
    up,
    down,
    lens,
    qkv_b,
    out_b,
    up_b,
    down_b,
    gain1,
    bias1,
    gain2,
    bias2,
    xa,
    ga,
    qw,
    dw,
    uw,
    sm,
    n1,
    n2,
    hid,
    slope,
    heads,
    joint,
    rows_out,
    small,
    pads,
    gm,
    sm_v,
    vecs,
    ub,
    qb,
    cos_v,
    sin_v,
    uw_v,
    qw_v,
    xs,
    n1_v,
    n2_v,
    hid_v,
    slope_v,
    heads_v,
    joint_v,
    loc,
    s_sm,
    r_sm,
    s_up,
    r_up,
    s_upb,
    r_upb,
    s_q,
    r_q,
    s_qb,
    r_qb,
    s_qc,
    r_qc,
    s_o,
    r_o,
    s_oc,
    r_oc,
    s_d,
    r_d,
    s_r,
    r_r,
    s_l,
    r_l,
    s_x,
    r_x,
    s_s,
    r_s,
):
    A, S, C, r, R = p.A, p.S, p.C, p.r, p.R
    dp, c, a, b, xh, core = place(p)
    me = dp * C + c
    t = a * C + c
    head = a * p.X + xh
    sib = (dp, xh * 2 + 1 - core)
    xnb = (dp, (1 - xh) * 2 + core)
    right = (dp + S, c)
    left = (dp - S, c)
    L = C * p.tok
    half = A // 2

    length = lens[0]

    def mask(at):
        row = lax.broadcasted_iota(jnp.int32, (32, p.d), 0) + (at + c * p.tok)
        rows = g[pl.ds(at, 32), :].astype(F32)
        gm[pl.ds(at, 32), :] = jnp.where(row < length, rows, 0.0).astype(BF)

    tiles(p.tok, mask, 32)

    pads[...] = jnp.zeros_like(pads)
    vectors = (qkv_b, up_b, gain1, bias1, gain2, bias2, out_b)
    for k, v in enumerate(vectors):
        value = v[...].astype(F32)
        if k == len(vectors) - 1:
            value = value + down_b[...].astype(F32)
        pads[k : k + 1, 0 : v.shape[1]] = value
    for k, v in enumerate(vectors):
        placed = pltpu.roll(pads[k : k + 1, :], lax.rem(v.shape[1] * me, LANES), 1)
        small[2 * k : 2 * k + 1, :] = placed[:, :LANES]
        small[2 * k + 1 : 2 * k + 2, :] = placed[:, LANES:]
    small[2 * len(vectors) :, :] = jnp.zeros((2, LANES), F32)
    greet_all(p, me)

    own_small = pltpu.make_async_copy(small, sm.at[me], loc.at[0])
    own_small.start()
    own_x = pltpu.make_async_copy(x, xa.at[a, pl.ds(pl.multiple_of(c * p.tok, p.tok), p.tok)], loc.at[1])
    own_x.start()
    own_g = pltpu.make_async_copy(gm, ga.at[a, pl.ds(pl.multiple_of(c * p.tok, p.tok), p.tok)], loc.at[2])
    own_g.start()

    def small_send(k, carry):
        other = lax.rem(me + k, p.n)
        dev = (lax.div(other, C), lax.rem(other, C))
        remote(small, sm.at[me], s_sm, r_sm, dev).start()
        return carry

    lax.fori_loop(1, p.n, small_send, 0)

    def up_piece(aa, cc, j):
        col = pl.multiple_of(unit_run(p, aa, cc, j), 128)
        return up.at[:, pl.ds(col, p.W)], uw.at[a, b, c, :, pl.ds(j * p.W, p.W)]

    def up_send(k, carry):
        tt = lax.rem(t + k, A * C)
        aa, cc = lax.div(tt, C), lax.rem(tt, C)
        for j in range(p.ffl // p.W):
            src, dst = up_piece(aa, cc, j)
            remote(src, dst, s_up, r_up, (aa * S + b, cc)).start()
        return carry

    lax.fori_loop(1, A * C, up_send, 0)
    for j in range(p.ffl // p.W):
        src, dst = up_piece(a, c, j)
        pltpu.make_async_copy(src, dst, r_up).start()

    def q_piece(hh, j):
        col = pl.multiple_of(j * p.d + hh * HEAD_DIM, HEAD_DIM)
        return (
            qkv.at[:, pl.ds(col, HEAD_DIM)],
            qw.at[a, b, xh, core, :, pl.ds(j * HEAD_DIM, HEAD_DIM)],
        )

    def q_send(k, carry):
        hh = lax.rem(head + k, HEADS)
        for j in range(3):
            src, dst = q_piece(hh, j)
            dev = (lax.div(hh, p.X) * S + b, lax.rem(hh, p.X) * 2 + core)
            remote(src, dst, s_q, r_q, dev).start()
        return carry

    lax.fori_loop(1, HEADS, q_send, 0)
    for j in range(3):
        src, dst = q_piece(head, j)
        pltpu.make_async_copy(src, dst, r_q).start()

    row_head = lax.div(me * r, HEAD_DIM)
    row_part = lax.div(lax.rem(me * r, HEAD_DIM), 2 * r)
    o_dst = dw.at[pl.ds(pl.multiple_of(p.ffl + (row_part * 2 + core) * r, r), r)]

    def o_dev(bb):
        return lax.div(row_head, p.X) * S + bb, lax.rem(row_head, p.X) * 2 + core

    for bb in range(S):
        od, oc = o_dev(bb)
        here = (od == dp) & (oc == c)

        @pl.when(jnp.logical_not(here))
        def _():
            remote(outw, o_dst, s_o.at[bb], r_o, (od, oc)).start()

        @pl.when(here)
        def _():
            pltpu.make_async_copy(outw, o_dst, r_o).start()

    d_ctx, d_row = unit_home(p, b, xh, core)
    d_dst = dw.at[pl.ds(pl.multiple_of(d_row, R), R)]
    for bb in range(S):
        here = (bb == b) & (d_ctx == c)

        @pl.when(jnp.logical_not(here))
        def _():
            remote(down, d_dst, s_d.at[bb], r_d, (a * S + bb, d_ctx)).start()

        @pl.when(here)
        def _():
            pltpu.make_async_copy(down, d_dst, r_d).start()

    streams = ((x, xa), (gm, ga))

    def blk(j, k, cc):
        return streams[j][1].at[k, pl.ds(pl.multiple_of(cc * p.tok, p.tok), p.tok)]

    def send_own(j):
        own, slot = streams[j][0], blk(j, a, c)

        @pl.when(a < A - 1)
        def _():
            remote(own, slot, s_r.at[j, 0], r_r.at[j, 0], right).start()

        @pl.when(a > 0)
        def _():
            remote(own, slot, s_l.at[j, 0], r_l.at[j, 0], left).start()

        remote(own, slot, s_x.at[j, a], r_x.at[j, a], xnb).start()
        remote(own, slot, s_s.at[j, a], r_s.at[j, a], sib).start()

    def z_step(j, s):
        @pl.when(a - 1 - s >= 0)
        def _():
            k = a - 1 - s
            part = blk(j, k, c)
            drain(part, r_r.at[j, s])

            @pl.when((s + 1 < A - 1) & (a < A - 1))
            def _():
                nxt = jnp.minimum(s + 1, A - 2)
                remote(part, part, s_r.at[j, nxt], r_r.at[j, nxt], right).start()

            remote(part, part, s_x.at[j, k], r_x.at[j, k], xnb).start()
            remote(part, part, s_s.at[j, k], r_s.at[j, k], sib).start()

        @pl.when(a + 1 + s <= A - 1)
        def _():
            k = a + 1 + s
            part = blk(j, k, c)
            drain(part, r_l.at[j, s])

            @pl.when((s + 1 < A - 1) & (a > 0))
            def _():
                nxt = jnp.minimum(s + 1, A - 2)
                remote(part, part, s_l.at[j, nxt], r_l.at[j, nxt], left).start()

            remote(part, part, s_x.at[j, k], r_x.at[j, k], xnb).start()
            remote(part, part, s_s.at[j, k], r_s.at[j, k], sib).start()

    xc = (1 - xh) * 2 + core

    def cross(j, k):
        part = blk(j, k, xc)
        drain(part, r_x.at[j, k])
        remote(part, part, s_s.at[j, k], r_s.at[j, k], sib).start()

    send_own(0)
    angle_tables(cos_v, sin_v)

    own_small.wait()
    drain(sm.at[pl.ds(0, p.n - 1)], r_sm)
    get_small = pltpu.make_async_copy(sm, sm_v, loc.at[0])
    get_small.start()
    get_small.wait()

    def chunk(which, jj):
        size = vectors[which].shape[1]
        if size % LANES == 0:
            count = 1
        elif LANES % size == 0:
            count = LANES // size
        else:
            count = (LANES - 1) // size + 2
        total = jnp.zeros((1, LANES), F32)
        for o in range(count):
            i = lax.div(LANES * jj, size) + o
            row = jj - lax.div(i * size, LANES)
            good = ((row >= 0) & (row <= 1) & (i < p.n)).astype(F32)
            at = 2 * which + jnp.clip(row, 0, 1)
            total = total + good * sm_v[jnp.minimum(i, p.n - 1), pl.ds(at, 1), :]
        return total

    def fill(jj, carry):
        for k in range(5):
            vecs[k : k + 1, pl.ds(pl.multiple_of(jj * LANES, LANES), LANES)] = chunk(2 + k, jj)
        return carry

    lax.fori_loop(0, p.d // LANES, fill, 0)
    for j in range(p.ffl // LANES):
        run, rest = j * LANES // p.W, (j * LANES % p.W) // LANES
        first = lax.div(unit_run(p, a, c, run), LANES) + rest
        ub[:, j * LANES : (j + 1) * LANES] = chunk(1, first)
    for j in range(3):
        for k in range(HEAD_DIM // LANES):
            first = (j * p.d + head * HEAD_DIM) // LANES + k
            at = j * HEAD_DIM + k * LANES
            qb[:, at : at + LANES] = chunk(0, first)

    drain(uw.at[:, b], r_up)

    def up_cross(k, carry):
        bb = lax.rem(b + k, S)
        remote(uw.at[:, b], uw.at[:, b], s_upb, r_upb, (a * S + bb, c)).start()
        return carry

    lax.fori_loop(1, S, up_cross, 0)
    drain(qw.at[:, b, :, core], r_q)

    def q_cross(k, carry):
        bb = lax.rem(b + k, S)
        part = qw.at[:, b, :, core]
        remote(part, part, s_qb, r_qb, (a * S + bb, c)).start()
        return carry

    lax.fori_loop(1, S, q_cross, 0)
    drain(dw.at[pl.ds(p.ffl, p.m * r)], r_o)
    for k in range(p.m):
        rows = dw.at[pl.ds(pl.multiple_of(p.ffl + (2 * k + core) * r, r), r)]
        remote(rows, rows, s_oc.at[k], r_oc.at[k], sib).start()

    near = far_order(p, a)[::-1]

    def slot_rows(k):
        return pl.ds(pl.multiple_of(k * L, L), L)

    def forward_slot(k):
        get = pltpu.make_async_copy(xa.at[k], xs, loc.at[3])
        get.start()
        get.wait()
        mine = lax.div(k, half) == core

        def norm(at):
            rows = xs[pl.ds(at, 16), :].astype(F32)
            center = jnp.mean(rows, axis=1, keepdims=True)
            rows = rows - center
            spread = jnp.mean(rows * rows, axis=1, keepdims=True)
            rows = rows * lax.rsqrt(spread + EPS)
            n2_v[pl.ds(at, 16), :] = (rows * vecs[2:3, :] + vecs[3:4, :]).astype(BF)

            @pl.when(mine)
            def _():
                own_at = pl.multiple_of(lax.rem(k, half) * L + at, 16)
                n1_v[pl.ds(own_at, 16), :] = (rows * vecs[0:1, :] + vecs[1:2, :]).astype(BF)

        tiles(L, norm, 16)
        put = pltpu.make_async_copy(n2_v, n2.at[slot_rows(k)], loc.at[4])
        put.start()

        def unit_tile(n):
            at = pl.ds(n, TILE)
            w = uw_v[:, :, :, :, at].reshape(p.d, TILE)
            v = dot(n2_v[...], w) + ub[:, at]
            phi = 0.5 * (1.0 + lax.erf(v * (1.0 / math.sqrt(2.0))))
            density = jnp.exp(-0.5 * v * v) * (1.0 / math.sqrt(2.0 * math.pi))
            hid_v[slot_rows(k), at] = (v * phi).astype(BF)
            slope_v[slot_rows(k), at] = (phi + v * density).astype(BF)

        tiles(p.ffl, unit_tile)
        put.wait()

    def x_round(i, carry):
        k = pick(near, i)

        @pl.when(i < A - 1)
        def _():
            z_step(0, i)

        cross(0, k)

        @pl.when(i == 0)
        def _():
            send_own(1)
            own_x.wait()
            for _ in range(S - 1):
                drain(uw.at[:, b], r_upb)
            get = pltpu.make_async_copy(uw, uw_v, loc.at[3])
            get.start()
            for _ in range(S - 1):
                drain(qw.at[:, b, :, core], r_qb)
            part = qw.at[:, :, :, core]
            remote(part, part, s_qc, r_qc, sib).start()
            get.wait()

        drain(xa.at[k, pl.ds(0, p.X * p.tok)], r_s.at[0, k])
        forward_slot(k)

        @pl.when(i > 0)
        def _():
            z_step(1, i - 1)

        return carry

    lax.fori_loop(0, A, x_round, 0)
    put_hid = pltpu.make_async_copy(hid_v, hid, loc.at[4])
    put_hid.start()
    put_slope = pltpu.make_async_copy(slope_v, slope, loc.at[5])
    put_slope.start()
    put_n1 = pltpu.make_async_copy(n1_v, n1, loc.at[6])
    put_n1.start()
    put_rows = pltpu.make_async_copy(vecs, rows_out, loc.at[7])
    put_rows.start()
    drain(qw.at[:, :, :, 1 - core], r_qc)
    get_qw = pltpu.make_async_copy(qw, qw_v, loc.at[3])
    get_qw.start()
    get_qw.wait()

    def attend(i):
        own = pl.ds(pl.multiple_of(i * L, L), L)
        cols = [pl.ds(j * HEAD_DIM, HEAD_DIM) for j in range(3)]
        for j in range(3):
            w = qw_v[:, :, :, :, :, cols[j]].reshape(p.d, HEAD_DIM)
            v = dot(n1_v[own, :], w) + qb[:, cols[j]]
            if j < 2:
                v = turn(v, cos_v[...], sin_v[...])
            joint_v[own, cols[j]] = v.astype(BF)
        rows = L // 2
        for h in range(2):
            at = pl.ds(pl.multiple_of(i * L + h * rows, rows), rows)
            keys = pl.ds(pl.multiple_of(i * L, L), (h + 1) * rows)
            probs = probabilities(joint_v[at, cols[0]], joint_v[keys, cols[1]], h * rows, SCALE)
            heads_v[at, :] = dot(probs.astype(BF), joint_v[keys, cols[2]]).astype(BF)

    def g_round(i, carry):
        cross(1, pick(near, i))

        @pl.when(i < half)
        def _():
            attend(i)

        return carry

    lax.fori_loop(0, A, g_round, 0)
    put_heads = pltpu.make_async_copy(heads_v, heads, loc.at[0])
    put_heads.start()
    put_joint = pltpu.make_async_copy(joint_v, joint, loc.at[1])
    put_joint.start()

    drain(dw.at[pl.ds(0, p.ffl)], r_d)
    for k in range(p.m):
        drain(dw.at[pl.ds(0, r)], r_oc.at[k])
    for k in range(A):
        drain(ga.at[k, pl.ds(0, p.X * p.tok)], r_s.at[1, k])

    own_g.wait()
    put_hid.wait()
    put_slope.wait()
    put_n1.wait()
    put_rows.wait()
    put_heads.wait()
    put_joint.wait()
    drain(sm.at[pl.ds(0, p.n - 1)], s_sm)
    for _ in range(A * C - 1):
        drain(uw.at[a, b, c], s_up)
    for _ in range(HEADS - 1):
        drain(qw.at[a, b, xh, core], s_q)
    for bb in range(S):
        od, oc = o_dev(bb)

        @pl.when(jnp.logical_not((od == dp) & (oc == c)))
        def _():
            drain(outw, s_o.at[bb])

        @pl.when(jnp.logical_not((bb == b) & (d_ctx == c)))
        def _():
            drain(down, s_d.at[bb])

    for k in range(p.m):
        drain(dw.at[pl.ds(0, r)], s_oc.at[k])
    for _ in range(S - 1):
        drain(uw.at[:, b], s_upb)
        drain(qw.at[:, b, :, core], s_qb)
    drain(qw.at[:, :, :, core], s_qc)
    for j in range(2):
        for s in range(A - 1):

            @pl.when((a < A - 1) & (a - s >= 0))
            def _():
                drain(x, s_r.at[j, s])

            @pl.when((a > 0) & (a + s <= A - 1))
            def _():
                drain(x, s_l.at[j, s])

        for k in range(A):
            drain(x, s_x.at[j, k])
            drain(xa.at[k, pl.ds(0, p.X * p.tok)], s_s.at[j, k])


def front(p, x, g, qkv, outw, up, down, lens, *vectors):
    dma = pltpu.SemaphoreType.DMA
    A, S, C, r = p.A, p.S, p.C, p.r
    L = C * p.tok
    vm = pltpu.VMEM
    hbm = pl.BlockSpec(memory_space=pl.ANY)
    vmem = pl.BlockSpec(memory_space=pltpu.VMEM)
    half = p.rows // 2
    qw_shape = (A, S, p.X, 2, r, p.hc)
    uw_shape = (A, S, C, r, p.ffl)
    return pl.pallas_call(
        functools.partial(front_kernel, p),
        out_shape=(
            jax.ShapeDtypeStruct((A, L, p.d), BF),
            jax.ShapeDtypeStruct((A, L, p.d), BF),
            jax.ShapeDtypeStruct(qw_shape, BF),
            jax.ShapeDtypeStruct((p.ffl + HEAD_DIM, p.d), BF),
            jax.ShapeDtypeStruct(uw_shape, BF),
            jax.ShapeDtypeStruct((p.n, 16, LANES), F32),
            jax.ShapeDtypeStruct((half, p.d), BF),
            jax.ShapeDtypeStruct((p.rows, p.d), BF),
            jax.ShapeDtypeStruct((p.rows, p.ffl), BF),
            jax.ShapeDtypeStruct((p.rows, p.ffl), BF),
            jax.ShapeDtypeStruct((half, HEAD_DIM), BF),
            jax.ShapeDtypeStruct((half, p.hc), BF),
            jax.ShapeDtypeStruct((8, p.d), F32),
        ),
        in_specs=[vmem] * 6 + [pl.BlockSpec(memory_space=pltpu.SMEM)] + [vmem] * 8,
        out_specs=[hbm] * 13,
        scratch_shapes=[
            vm((16, LANES), F32),
            vm((8, 2 * LANES), F32),
            vm((p.tok, p.d), BF),
            vm((p.n, 16, LANES), F32),
            vm((8, p.d), F32),
            vm((1, p.ffl), F32),
            vm((1, p.hc), F32),
            vm((L, LANES), F32),
            vm((L, LANES), F32),
            vm(uw_shape, BF),
            vm(qw_shape, BF),
            vm((L, p.d), BF),
            vm((half, p.d), BF),
            vm((L, p.d), BF),
            vm((p.rows, p.ffl), BF),
            vm((p.rows, p.ffl), BF),
            vm((half, HEAD_DIM), BF),
            vm((half, p.hc), BF),
            dma((8,)),
            dma,
            dma,
            dma,
            dma,
            dma,
            dma,
            dma,
            dma,
            dma,
            dma,
            dma,
            dma,
            dma((S,)),
            dma,
            dma((p.m,)),
            dma((p.m,)),
            dma((S,)),
            dma,
            dma((2, A - 1)),
            dma((2, A - 1)),
            dma((2, A - 1)),
            dma((2, A - 1)),
            dma((2, A)),
            dma((2, A)),
            dma((2, A)),
            dma((2, A)),
        ],
        compiler_params=pltpu.CompilerParams(
            collective_id=0, has_side_effects=True, vmem_limit_bytes=60 * 1024 * 1024
        ),
        name="front",
    )(x, g, qkv, outw, up, down, lens, *vectors)


def back_kernel(
    p,
    hid,
    heads,
    slope,
    g,
    joint,
    n1,
    n2,
    dw,
    uw,
    qw,
    gains,
    o_sum,
    e_sum,
    q_out,
    u_out,
    d_parts,
    o_parts,
    v_all,
    hid_v,
    heads_v,
    dpre,
    ge,
    joint_v,
    dw_v,
    uw_v,
    qw_v,
    n_v,
    t_v,
    dh_v,
    cos_v,
    sin_v,
    op,
    from_sib,
    from_x,
    came,
    dgrad,
    q_g,
    q_sib,
    q_group,
    o_g,
    o_sib,
    u_parts,
    vec,
    loc,
    n_sem,
    s_v,
    r_v,
    s_s,
    r_s,
    s_x,
    r_x,
    s_c,
    r_c,
    s_q,
    r_q,
    s_qb,
    r_qb,
    s_qa,
    r_qa,
    s_o,
    r_o,
    s_oa,
    r_oa,
    s_u,
    r_u,
    s_ua,
    r_ua,
    s_d,
    r_d,
    free,
):
    A, S, C, X, r, R = p.A, p.S, p.C, p.X, p.r, p.R
    dp, c, a, b, xh, core = place(p)
    me = dp * C + c
    t = a * C + c
    head = a * X + xh
    sib = (dp, xh * 2 + 1 - core)
    xnb = (dp, (1 - xh) * 2 + core)
    far = 1 - xh
    L = C * p.tok
    D, ffl = p.d, p.ffl
    half = A // 2
    ugrad = hid_v

    loads = [
        pltpu.make_async_copy(src, dst, loc.at[k])
        for k, (src, dst) in enumerate(
            (
                (hid, hid_v.at[pl.ds(0, p.rows)]),
                (dw, dw_v),
                (heads, heads_v),
                (g, ge),
                (joint, joint_v),
                (slope, dpre),
                (uw, uw_v),
                (qw, qw_v),
            )
        )
    ]
    for load in loads:
        load.start()
    vec[...] = jnp.zeros_like(vec)
    angle_tables(cos_v, sin_v)
    greet_all(p, me)

    order = far_order(p, a)
    parts = (op, ge)

    def rows_of(side, cc):
        return pl.ds(pl.multiple_of((side * 2 + cc) * p.tok, p.tok), p.tok)

    def send_sib(j, k):
        for side in range(X):
            src = parts[j].at[k, rows_of(side, 1 - core)]
            remote(src, from_sib.at[k, side], s_s.at[j, k], r_s.at[j, k], sib).start()

    def chip_sum(j, k):
        drain(from_sib.at[k], r_s.at[j, k])
        mine = parts[j].at[k, rows_of(far, core)]
        add_rows(mine, (mine, from_sib.at[k, far]), p.tok)
        remote(mine, from_x.at[j, k], s_x.at[j, k], r_x.at[j, k], xnb).start()
        mine = parts[j].at[k, rows_of(xh, core)]
        add_rows(mine, (mine, from_sib.at[k, xh]), p.tok)

    def hop(j, k):
        drain(from_x.at[j, k], r_x.at[j, k])
        mine = parts[j].at[k, rows_of(xh, core)]
        first = jnp.where(k > a, a == 0, a == A - 1)

        @pl.when(first)
        def _():
            add_rows(mine, (mine, from_x.at[j, k]), p.tok)

        @pl.when(jnp.logical_not(first))
        def _():
            drain(came.at[j, k], r_c.at[j, k])
            add_rows(mine, (mine, from_x.at[j, k], came.at[j, k]), p.tok)

        to = jnp.where((k < a) & (k == a - 1), A, k)
        dev = (dp + jnp.where(k > a, S, -S), c)
        remote(mine, came.at[j, to], s_c.at[j, k], r_c.at[j, to], dev).start()

    def last(j, total):
        drain(from_x.at[j, a], r_x.at[j, a])
        mine = parts[j].at[a, rows_of(xh, core)]

        @pl.when(a == 0)
        def _():
            drain(came.at[j, A], r_c.at[j, A])
            add_rows(total, (mine, from_x.at[j, a], came.at[j, A]), p.tok)

        @pl.when(a == A - 1)
        def _():
            drain(came.at[j, a], r_c.at[j, a])
            add_rows(total, (mine, from_x.at[j, a], came.at[j, a]), p.tok)

        @pl.when((a > 0) & (a < A - 1))
        def _():
            drain(came.at[j, a], r_c.at[j, a])
            drain(came.at[j, A], r_c.at[j, A])
            add_rows(
                total, (mine, from_x.at[j, a], came.at[j, a], came.at[j, A]), p.tok
            )

    def slot_rows(k):
        return pl.ds(pl.multiple_of(k * L, L), L)

    def mine_rows(k):
        return pl.ds(pl.multiple_of(lax.rem(k, half) * L, L), L)

    for k in range(3):
        loads[k].wait()

    def out_slot(i):
        k = order[i]
        own = lax.div(k, half) == core

        @pl.when(own)
        def _():
            def tile(n):
                acc = dot(hid_v[slot_rows(k), :], dw_v[0:ffl, pl.ds(n, TILE)])
                acc += dot(heads_v[mine_rows(k), :], dw_v[ffl:, pl.ds(n, TILE)])
                op[k, :, pl.ds(n, TILE)] = acc.astype(BF)

            tiles(D, tile)

        @pl.when(jnp.logical_not(own))
        def _():
            def tile(n):
                acc = dot(hid_v[slot_rows(k), :], dw_v[0:ffl, pl.ds(n, TILE)])
                op[k, :, pl.ds(n, TILE)] = acc.astype(BF)

            tiles(D, tile)

        send_sib(0, k)

    for i in range(A):
        out_slot(i)
        if i > 0:
            chip_sum(0, order[i - 1])

    chip_sum(0, order[A - 1])
    pl.semaphore_signal(free, inc=1, device_id=sib, device_id_type=MESH)

    loads[3].wait()
    loads[4].wait()
    cols = [pl.ds(j * HEAD_DIM, HEAD_DIM) for j in range(3)]
    rows2 = L // 2

    def attend_back(i, carry):
        own = pl.ds(pl.multiple_of(i * L, L), L)
        dh_v[own, :] = dot_t(ge[core * half + i], dw_v[ffl:, :]).astype(BF)
        dq, dk, dv = [], [], []
        for h in range(2):
            at = pl.ds(pl.multiple_of(i * L + h * rows2, rows2), rows2)
            keys = pl.ds(pl.multiple_of(i * L, L), (h + 1) * rows2)
            q, k, v = joint_v[at, cols[0]], joint_v[keys, cols[1]], joint_v[keys, cols[2]]
            dh = dh_v[at, :]
            probs = probabilities(q, k, h * rows2, SCALE)
            d_probs = dot_t(dh, v)
            delta = jnp.sum(probs * d_probs, axis=1, keepdims=True)
            d_scores = (probs * (d_probs - delta)).astype(BF)
            dq.append(dot(d_scores, k) * SCALE)
            dk.append(t_dot(d_scores, q) * SCALE)
            dv.append(t_dot(probs.astype(BF), dh))
        dq = jnp.concatenate(dq, axis=0)
        dk = jnp.concatenate([dk[0] + dk[1][:rows2], dk[1][rows2:]], axis=0)
        dv = jnp.concatenate([dv[0] + dv[1][:rows2], dv[1][rows2:]], axis=0)
        cos, sin = cos_v[...], sin_v[...]
        for j, d_part in enumerate((turn(dq, cos, -sin), turn(dk, cos, -sin), dv)):
            low = d_part.astype(BF)
            joint_v[own, cols[j]] = low
            sums = jnp.sum(low.astype(F32), axis=0, keepdims=True)
            for k in range(HEAD_DIM // LANES):
                at = j * (HEAD_DIM // LANES) + k
                vec[at : at + 1, :] += sums[:, k * LANES : (k + 1) * LANES]
        return carry

    lax.fori_loop(0, half, attend_back, 0)
    hop(0, order[0])

    def n_load(src, i, slot):
        count = src.shape[0]
        return pltpu.make_async_copy(
            src.at[:, pl.ds(pl.multiple_of(i * TILE, TILE), TILE)],
            n_v.at[slot, pl.ds(0, count)],
            n_sem.at[slot],
        )

    def stream(src, use):
        n_load(src, 0, 0).start()

        def step(i, carry):
            slot = lax.rem(i, 2)
            n_load(src, i, slot).wait()

            @pl.when(i + 1 < D // TILE)
            def _():
                n_load(src, i + 1, 1 - slot).start()

            use(i, slot)
            return carry

        lax.fori_loop(0, D // TILE, step, 0)

    pairs = TILE // (2 * r)

    def q_tile(i, slot):
        for j in range(3):
            acc = t_dot(n_v[slot, 0 : p.rows // 2, :], joint_v[:, cols[j]]).astype(BF)
            for k in range(pairs):
                for kk in range(2):
                    at = (2 * k + kk) * r
                    q_g[i * pairs + k, kk, :, cols[j]] = acc[at : at + r]

    stream(n1, q_tile)
    remote(q_g.at[:, 1 - core], q_sib, s_q, r_q, sib).start()

    for k in range(half):
        t_v[:, k * L : (k + 1) * L] = heads_v[k * L : (k + 1) * L, :].astype(F32).T.astype(BF)

    def o_tile(n):
        acc = dot(t_v[:, 0:L], ge[core * half, :, pl.ds(n, TILE)])
        for k in range(1, half):
            acc += dot(t_v[:, k * L : (k + 1) * L], ge[core * half + k, :, pl.ds(n, TILE)])
        acc = acc.astype(BF)
        for k in range(p.m):
            for kk in range(2):
                at = (2 * k + kk) * r
                o_g[k, kk, :, pl.ds(n, TILE)] = acc[at : at + r]

    tiles(D, o_tile)
    remote(o_g.at[:, 1 - core], o_sib, s_o, r_o, sib).start()

    loads[5].wait()
    up_row = p.hc // LANES

    def dpre_slot(k, carry):
        def tile(n):
            dh = dot_t(ge[k], dw_v[pl.ds(n, TILE), :])
            value = (dh * dpre[slot_rows(k), pl.ds(n, TILE)].astype(F32)).astype(BF)
            dpre[slot_rows(k), pl.ds(n, TILE)] = value

        tiles(ffl, tile)
        return carry

    lax.fori_loop(0, A, dpre_slot, 0)

    def sum_rows(i, carry):
        at = pl.ds(pl.multiple_of(i * 64, 64), 64)
        return carry + jnp.sum(dpre[at, :].astype(F32), axis=0, keepdims=True)

    up_bias = lax.fori_loop(0, p.rows // 64, sum_rows, jnp.zeros((1, ffl), F32))
    for i in range(ffl // LANES):
        vec[up_row + i : up_row + i + 1, :] = up_bias[:, i * LANES : (i + 1) * LANES]
    g_row = up_row + ffl // LANES
    share = D // (A * C)

    def sum_g(i, carry):
        at = pl.ds(pl.multiple_of(lax.rem(i * 64, L), 64), 64)
        part = ge[lax.div(i * 64, L), at, pl.ds(pl.multiple_of(t * share, share), share)]
        return carry + jnp.sum(part.astype(F32), axis=0, keepdims=True)

    vec[g_row : g_row + 1, :] = lax.fori_loop(
        0, p.rows // 64, sum_g, jnp.zeros((1, share), F32)
    )

    def down_units(f, carry):
        at = pl.ds(pl.multiple_of(f * TILE, TILE), TILE)
        for k in range(A):
            t_v[:, k * L : (k + 1) * L] = hid_v[k * L : (k + 1) * L, at].astype(F32).T.astype(BF)

        def tile(n):
            acc = dot(t_v[:, 0:L], ge[0, :, pl.ds(n, TILE)])
            for k in range(1, A):
                acc += dot(t_v[:, k * L : (k + 1) * L], ge[k, :, pl.ds(n, TILE)])
            dgrad[at, pl.ds(n, TILE)] = acc.astype(BF)

        tiles(D, tile)
        return carry

    lax.fori_loop(0, ffl // TILE, down_units, 0)
    d_ctx, _ = unit_home(p, b, xh, core)
    for j in range(S):
        if p.P == 1:
            own_b, own_c = j, c
        else:
            own_b, own_c = 2 * (j // 2) + core, xh * 2 + j % 2
        src = dgrad.at[pl.ds(j * R, R)]
        here = (own_b == b) & (own_c == c)

        @pl.when(jnp.logical_not(here))
        def _():
            remote(src, d_parts.at[b], s_d.at[j], r_d, (a * S + own_b, own_c)).start()

        @pl.when(here)
        def _():
            pltpu.make_async_copy(src, d_parts.at[b], r_d).start()

    hop(0, order[1])

    drain(q_sib, r_q)

    def q_add(i, carry):
        mine = q_g.at[i, core]
        add_rows(mine, (mine, q_sib.at[i]), r)
        return carry

    lax.fori_loop(0, A * S * X, q_add, 0)

    def q_rows(aa, bb):
        return q_g.at[pl.ds((aa * S + bb) * X, X), core]

    def q_cross(k, carry):
        bb = lax.rem(b + k, S)
        for aa in range(A):
            remote(q_rows(aa, bb), q_group.at[k - 1, aa], s_qb, r_qb, (a * S + bb, c)).start()
        return carry

    lax.fori_loop(1, S, q_cross, 0)
    drain(o_sib, r_o)
    for k in range(p.m):
        mine = o_g.at[k, core]
        add_rows(mine, (mine, o_sib.at[k]), r)
        owner = lax.div(head * HEAD_DIM, r) + 2 * k + core
        od, oc = lax.div(owner, C), lax.rem(owner, C)
        here = owner == me

        @pl.when(jnp.logical_not(here))
        def _():
            remote(mine, o_parts.at[b], s_oa.at[k], r_oa, (od, oc)).start()

        @pl.when(here)
        def _():
            pltpu.make_async_copy(mine, o_parts.at[b], r_oa).start()

    loads[6].wait()
    loads[7].wait()
    pl.semaphore_wait(free, 1)

    def e_slot(i):
        k = order[i]
        own = lax.div(k, half) == core

        @pl.when(own)
        def _():
            def tile(n):
                acc = dot_t(dpre[slot_rows(k), :], uw_v[pl.ds(n, TILE), :])
                acc1 = dot_t(joint_v[mine_rows(k), :], qw_v[pl.ds(n, TILE), :])
                acc = acc * gains[2:3, pl.ds(n, TILE)] + acc1 * gains[0:1, pl.ds(n, TILE)]
                ge[k, :, pl.ds(n, TILE)] = acc.astype(BF)

            tiles(D, tile)

        @pl.when(jnp.logical_not(own))
        def _():
            def tile(n):
                acc = dot_t(dpre[slot_rows(k), :], uw_v[pl.ds(n, TILE), :])
                acc = acc * gains[2:3, pl.ds(n, TILE)]
                ge[k, :, pl.ds(n, TILE)] = acc.astype(BF)

            tiles(D, tile)

        send_sib(1, k)

    for i in range(A):
        e_slot(i)
        if i > 0:
            chip_sum(1, order[i - 1])
        if i == 2:
            hop(0, order[2])
    chip_sum(1, order[A - 1])

    own_v = pltpu.make_async_copy(vec, v_all.at[me], loc.at[8])
    own_v.start()

    def v_send(k, carry):
        other = lax.rem(me + k, p.n)
        dev = (lax.div(other, C), lax.rem(other, C))
        remote(vec, v_all.at[me], s_v, r_v, dev).start()
        return carry

    lax.fori_loop(1, p.n, v_send, 0)

    for k in range(1, S):
        drain(q_group.at[k - 1], r_qb)
    for k in range(1, S):

        def q_fin(i, carry):
            aa, xx = lax.div(i, X), lax.rem(i, X)
            mine = q_g.at[(aa * S + b) * X + xx, core]
            add_rows(mine, (mine, q_group.at[k - 1, aa, xx]), r)
            return carry

        lax.fori_loop(0, A * X, q_fin, 0)

    def q_piece(hh, j):
        col = pl.multiple_of(j * D + head * HEAD_DIM, HEAD_DIM)
        at = (lax.div(hh, X) * S + b) * X + lax.rem(hh, X)
        return q_g.at[at, core, :, cols[j]], q_out.at[:, pl.ds(col, HEAD_DIM)]

    def q_back(k, carry):
        hh = lax.rem(head + k, HEADS)
        dev = (lax.div(hh, X) * S + b, lax.rem(hh, X) * 2 + core)
        for j in range(3):
            src, dst = q_piece(hh, j)
            remote(src, dst, s_qa, r_qa, dev).start()
        return carry

    lax.fori_loop(1, HEADS, q_back, 0)
    for j in range(3):
        src, dst = q_piece(head, j)
        pltpu.make_async_copy(src, dst, r_qa).start()

    def up_tile(i, slot):
        at = pl.ds(pl.multiple_of(i * TILE, TILE), TILE)
        ugrad[at, :] = t_dot(n_v[slot], dpre[...]).astype(BF)

    stream(n2, up_tile)
    blk = C * r

    def u_rows(aa, bb):
        return ugrad.at[pl.ds(pl.multiple_of((aa * S + bb) * blk, blk), blk)]

    def u_send(k, carry):
        bb = lax.rem(b + k, S)
        for aa in range(A):
            remote(u_rows(aa, bb), u_parts.at[k - 1, aa], s_u, r_u, (a * S + bb, c)).start()
        return carry

    lax.fori_loop(1, S, u_send, 0)

    hop(1, order[0])
    last(0, o_sum)

    for k in range(1, S):
        drain(u_parts.at[k - 1], r_u)
    for k in range(1, S):
        for aa in range(A):
            add_rows(u_rows(aa, b), (u_rows(aa, b), u_parts.at[k - 1, aa]), blk)

    def u_piece(tt, j):
        col = pl.multiple_of(unit_run(p, a, c, j), 128)
        aa, cc = lax.div(tt, C), lax.rem(tt, C)
        at = pl.multiple_of((aa * S + b) * blk + cc * r, r)
        return ugrad.at[pl.ds(at, r), pl.ds(j * p.W, p.W)], u_out.at[:, pl.ds(col, p.W)]

    def u_back(k, carry):
        tt = lax.rem(t + k, A * C)
        for j in range(ffl // p.W):
            src, dst = u_piece(tt, j)
            remote(src, dst, s_ua, r_ua, (lax.div(tt, C) * S + b, lax.rem(tt, C))).start()
        return carry

    lax.fori_loop(1, A * C, u_back, 0)
    for j in range(ffl // p.W):
        src, dst = u_piece(t, j)
        pltpu.make_async_copy(src, dst, r_ua).start()

    for i in range(1, A - 1):
        hop(1, order[i])
    last(1, e_sum)

    drain(u_out, r_ua)
    drain(q_out, r_qa)
    drain(v_all.at[pl.ds(0, p.n - 1)], r_v)
    drain(d_parts, r_d)
    drain(o_parts, r_oa)

    own_v.wait()
    drain(v_all.at[pl.ds(0, p.n - 1)], s_v)
    drain(q_sib, s_q)
    drain(o_sib, s_o)
    for k in range(1, S):
        drain(u_parts.at[0], s_u)
        drain(q_group.at[0], s_qb)
    for _ in range(A * C - 1):
        drain(ugrad.at[pl.ds(0, r)], s_ua)
    for _ in range(HEADS - 1):
        drain(q_g.at[0, 0], s_qa)
    for k in range(p.m):

        @pl.when(lax.div(head * HEAD_DIM, r) + 2 * k + core != me)
        def _():
            drain(o_g.at[k, 0], s_oa.at[k])

    for j in range(S):
        if p.P == 1:
            own_b, own_c = j, c
        else:
            own_b, own_c = 2 * (j // 2) + core, xh * 2 + j % 2

        @pl.when(jnp.logical_not((own_b == b) & (own_c == c)))
        def _():
            drain(d_parts.at[0], s_d.at[j])

    for j in range(2):
        for k in range(A):
            drain(from_sib.at[0], s_s.at[j, k])
            drain(from_x.at[0, 0], s_x.at[j, k])

            @pl.when(k != a)
            def _():
                drain(from_x.at[0, 0], s_c.at[j, k])


def back(p, *args):
    dma = pltpu.SemaphoreType.DMA
    A, S, C, X, r, R = p.A, p.S, p.C, p.X, p.r, p.R
    L = C * p.tok
    vm = pltpu.VMEM
    hbm = pl.BlockSpec(memory_space=pl.ANY)
    vmem = pl.BlockSpec(memory_space=pltpu.VMEM)
    groups = max(S - 1, 1)
    return pl.pallas_call(
        functools.partial(back_kernel, p),
        out_shape=(
            jax.ShapeDtypeStruct((p.tok, p.d), F32),
            jax.ShapeDtypeStruct((p.tok, p.d), F32),
            jax.ShapeDtypeStruct((r, 3 * p.d), BF),
            jax.ShapeDtypeStruct((r, p.ff), BF),
            jax.ShapeDtypeStruct((S, R, p.d), BF),
            jax.ShapeDtypeStruct((S, r, p.d), BF),
            jax.ShapeDtypeStruct((p.n, 16, 128), F32),
        ),
        in_specs=[hbm] * 10 + [vmem],
        out_specs=[vmem] * 2 + [hbm] * 5,
        scratch_shapes=[
            vm((max(p.rows, p.d), p.ffl), BF),
            vm((p.rows // 2, HEAD_DIM), BF),
            vm((p.rows, p.ffl), BF),
            vm((A, L, p.d), BF),
            vm((p.rows // 2, p.hc), BF),
            vm((p.ffl + HEAD_DIM, p.d), BF),
            vm((p.d, p.ffl), BF),
            vm((p.d, p.hc), BF),
            vm((2, p.rows, TILE), BF),
            vm((TILE, p.rows), BF),
            vm((p.rows // 2, HEAD_DIM), BF),
            vm((L, LANES), F32),
            vm((L, LANES), F32),
            vm((A, L, p.d), BF),
            vm((A, X, p.tok, p.d), BF),
            vm((2, A, p.tok, p.d), BF),
            vm((2, A + 1, p.tok, p.d), BF),
            vm((p.ffl, p.d), BF),
            vm((A * S * X, 2, r, p.hc), BF),
            vm((A * S * X, r, p.hc), BF),
            vm((groups, A, X, r, p.hc), BF),
            vm((p.m, 2, r, p.d), BF),
            vm((p.m, r, p.d), BF),
            vm((groups, A, C * r, p.ffl), BF),
            vm((16, 128), F32),
            dma((9,)),
            dma((2,)),
            dma,
            dma,
            dma((2, A)),
            dma((2, A)),
            dma((2, A)),
            dma((2, A)),
            dma((2, A)),
            dma((2, A + 1)),
            dma,
            dma,
            dma,
            dma,
            dma,
            dma,
            dma,
            dma,
            dma((p.m,)),
            dma,
            dma,
            dma,
            dma,
            dma,
            dma((S,)),
            dma,
            pltpu.SemaphoreType.REGULAR,
        ],
        compiler_params=pltpu.CompilerParams(
            collective_id=1, has_side_effects=True, vmem_limit_bytes=67043328
        ),
        name="back",
    )(*args)


def norm_stats(values):
    center = jnp.mean(values, axis=-1, keepdims=True)
    spread = jnp.mean(jnp.square(values - center), axis=-1, keepdims=True)
    inv_std = lax.rsqrt(spread + EPS)
    return (values - center) * inv_std, inv_std


def local(
    dp_size,
    ctx_size,
    layer_input,
    lengths,
    cotangent,
    qkv_weight,
    qkv_bias,
    out_weight,
    out_bias,
    up_weight,
    up_bias,
    down_weight,
    down_bias,
    first_gain,
    first_bias,
    second_gain,
    second_bias,
):
    tok, d = layer_input.shape
    ff = up_weight.shape[1]
    p = Plan(dp_size, ctx_size, tok, d, ff)
    A, S, C, X, r, R = p.A, p.S, p.C, p.X, p.r, p.R
    dp, c, a, b, xh, core = place(p)
    me = dp * C + c
    t = a * C + c
    valid = (c * tok + jnp.arange(tok, dtype=jnp.int32) < lengths[0])[:, None]
    grad_out = jnp.where(valid, cotangent, jnp.zeros_like(cotangent))
    vectors = (
        qkv_bias,
        out_bias,
        up_bias,
        down_bias,
        first_gain,
        first_bias,
        second_gain,
        second_bias,
    )
    (_, g_all, qw, dw, uw, _, n1, n2, hid, slope, heads, joint, full) = front(
        p,
        layer_input,
        cotangent,
        qkv_weight,
        out_weight,
        up_weight,
        down_weight,
        lengths,
        *(v.reshape(1, -1) for v in vectors),
    )
    o_sum, e_sum, q_out, u_out, d_parts, o_parts, v_all = back(
        p,
        hid,
        heads,
        slope,
        g_all,
        joint,
        n1,
        n2,
        dw,
        uw.reshape(d, p.ffl),
        qw.reshape(d, p.hc),
        full,
    )
    g_cols = d // (A * C)
    o_out = jnp.sum(o_parts.astype(F32), axis=0)
    d_out = jnp.sum(d_parts.astype(F32), axis=0)

    xf = layer_input.astype(F32)
    output = jnp.where(valid, xf + o_sum + full[4:5], 0.0).astype(BF)
    xhat_o, inv = norm_stats(xf)
    dx = inv * (
        e_sum
        - jnp.mean(e_sum, axis=-1, keepdims=True)
        - xhat_o * jnp.mean(e_sum * xhat_o, axis=-1, keepdims=True)
    )
    input_grad = (grad_out.astype(F32) + dx).astype(BF)

    v_all = v_all.reshape(A, S, C, 2048)
    v_sum = jnp.sum(v_all, axis=1)
    q_bias = v_sum[..., : p.hc].reshape(A, X, 2, 3, HEAD_DIM).sum(axis=2)
    q_bias = q_bias.reshape(HEADS, 3, HEAD_DIM).transpose(1, 0, 2).reshape(-1)
    u_bias = v_sum[..., p.hc : p.hc + p.ffl]
    if p.P == 1:
        u_bias = u_bias.reshape(A, C, S, R).transpose(0, 2, 1, 3).reshape(-1)
    else:
        u_bias = u_bias.reshape(A, X, 2, S // 2, p.W).transpose(0, 3, 2, 1, 4).reshape(-1)
    g_bias = v_sum[..., p.hc + p.ffl : p.hc + p.ffl + g_cols].reshape(-1)

    def own(vector):
        size = vector.shape[0] // p.n
        return lax.dynamic_slice(vector, (me * size,), (size,))

    def norm_grads(weight, grad, bias_grad, gain, shift):
        weight = weight.astype(F32)
        shift_grad = jnp.sum(weight * bias_grad, axis=1)
        gain_grad = (jnp.sum(weight * grad, axis=1) - shift.astype(F32) * shift_grad) / gain.astype(
            F32
        )
        return gain_grad, shift_grad

    q_grad = q_out.astype(F32)
    u_grad = u_out.astype(F32)
    gain1_grad, bias1_grad = norm_grads(qkv_weight, q_grad, q_bias, first_gain, first_bias)
    gain2_grad, bias2_grad = norm_grads(up_weight, u_grad, u_bias, second_gain, second_bias)
    g_own = own(g_bias)
    return (
        output,
        input_grad,
        q_grad,
        own(q_bias),
        o_out,
        g_own,
        u_grad,
        own(u_bias),
        d_out,
        g_own,
        gain1_grad,
        bias1_grad,
        gain2_grad,
        bias2_grad,
    )


def solution(mesh):
    rows = P(("dp", "ctx"), None)
    vector = P(("dp", "ctx"))
    return jax.shard_map(
        functools.partial(local, mesh.shape["dp"], mesh.shape["ctx"]),
        mesh=mesh,
        in_specs=(
            rows,
            P("dp"),
            rows,
            rows,
            vector,
            rows,
            vector,
            rows,
            vector,
            rows,
            vector,
            vector,
            vector,
            vector,
            vector,
        ),
        out_specs=(
            rows,
            rows,
            rows,
            vector,
            rows,
            vector,
            rows,
            vector,
            rows,
            vector,
            vector,
            vector,
            vector,
            vector,
        ),
        check_vma=False,
    )
```

```python
import functools
import math

import jax
import jax.numpy as jnp
from jax import lax
from jax.experimental import pallas as pl
from jax.experimental.pallas import tpu as pltpu
from jax.sharding import PartitionSpec as P

HEADS = 8
HEAD_DIM = 256
ROT = 64
EPS = 1e-05
SCALE = 1.0 / math.sqrt(HEAD_DIM)
MESH = pl.DeviceIdType.MESH
BF = jnp.bfloat16
F32 = jnp.float32
TILE = 256
LANES = 128


class Plan:
    def __init__(self, dp, ctx, tok, d, ff):
        self.C = ctx
        self.X = ctx // 2
        self.A = HEADS // self.X
        self.S = dp // self.A
        self.n = dp * ctx
        self.tok = tok
        self.d = d
        self.ff = ff
        self.r = d // self.n
        self.R = ff // self.n
        self.ffl = self.S * self.R
        self.W = max(self.R, 128)
        self.P = self.W // self.R
        self.hc = 3 * HEAD_DIM
        self.m = HEAD_DIM // self.r // 2
        self.rows = self.A * self.C * tok


def remote(src, dst, send, recv, dev):
    return pltpu.make_async_remote_copy(
        src_ref=src, dst_ref=dst, send_sem=send, recv_sem=recv, device_id=dev, device_id_type=MESH
    )


def drain(ref, sem):
    pltpu.make_async_copy(ref, ref, sem).wait()


def unit_run(p, aa, cc, j):
    if p.P == 1:
        return p.R * ((aa * p.S + j) * p.C + cc)
    return p.R * ((aa * p.S + 2 * j + lax.rem(cc, 2)) * p.C + lax.div(cc, 2) * 2)


def unit_home(p, b, xh, core):
    if p.P == 1:
        return xh * 2 + core, b * p.R
    return xh * 2 + lax.rem(b, 2), (lax.div(b, 2) * 2 + core) * p.R


def place(p):
    dp = lax.axis_index("dp")
    c = lax.axis_index("ctx")
    a = lax.div(dp, p.S)
    b = lax.rem(dp, p.S)
    xh = lax.div(c, 2)
    core = lax.rem(c, 2)
    return dp, c, a, b, xh, core


def greet_all(p, me):
    barrier = pltpu.get_barrier_semaphore()

    def greet(k, carry):
        other = lax.rem(me + k, p.n)
        pl.semaphore_signal(
            barrier,
            inc=1,
            device_id=(lax.div(other, p.C), lax.rem(other, p.C)),
            device_id_type=MESH,
        )
        return carry

    lax.fori_loop(1, p.n, greet, 0)
    pl.semaphore_wait(barrier, p.n - 1)


def dot(x, y):
    return jnp.dot(x, y, preferred_element_type=F32)


def dot_t(x, y):
    return lax.dot_general(x, y, (((1,), (1,)), ((), ())), preferred_element_type=F32)


def t_dot(x, y):
    return lax.dot_general(x, y, (((0,), (0,)), ((), ())), preferred_element_type=F32)


def tiles(count, body, size=TILE):
    def run(i, carry):
        body(pl.multiple_of(i * size, size))
        return carry

    lax.fori_loop(0, count // size, run, 0)


def pick(values, i):
    out = values[0]
    for k in range(1, len(values)):
        out = jnp.where(i == k, values[k], out)
    return out


def far_order(p, a):
    order = []
    lo, hi = 0, p.A - 1
    for _ in range(p.A):
        up_far = hi - a >= a - lo
        order.append(jnp.where(up_far, hi, lo))
        lo = jnp.where(up_far, lo, lo + 1)
        hi = jnp.where(up_far, hi - 1, hi)
    return order


def add_rows(dst, parts, rows):
    step = 16

    def body(k, carry):
        at = pl.ds(pl.multiple_of(k * step, step), step)
        total = parts[0][at, :].astype(F32)
        for part in parts[1:]:
            total = total + part[at, :].astype(F32)
        dst[at, :] = total.astype(dst.dtype)
        return carry

    lax.fori_loop(0, rows // step, body, 0)


def angle_tables(cos_v, sin_v):
    rows = cos_v.shape[0]
    half = ROT // 2

    def body(at):
        shape = (64, LANES)
        lane = lax.broadcasted_iota(jnp.int32, shape, 1)
        pos = (lax.broadcasted_iota(jnp.int32, shape, 0) + at).astype(F32)
        exponent = lax.rem(lane, half).astype(F32) * (-2.0 * math.log(10000.0) / ROT)
        angle = pos * jnp.exp(exponent)
        turned = lane < ROT
        sign = jnp.where(lane < half, -1.0, 1.0)
        cos_v[pl.ds(at, 64), :] = jnp.where(turned, jnp.cos(angle), 1.0)
        sin_v[pl.ds(at, 64), :] = jnp.where(turned, jnp.sin(angle) * sign, 0.0)

    tiles(rows, body, 64)


def turn(v, cos, sin):
    first = v[:, :LANES]
    half = ROT // 2
    lane = lax.broadcasted_iota(jnp.int32, first.shape, 1)
    partner = jnp.where(
        lane < half, pltpu.roll(first, LANES - half, 1), pltpu.roll(first, half, 1)
    )
    return jnp.concatenate([first * cos + partner * sin, v[:, LANES:]], axis=1)


def probabilities(q, k, row0, scale):
    scores = dot_t(q, k) * scale
    row = lax.broadcasted_iota(jnp.int32, scores.shape, 0) + row0
    col = lax.broadcasted_iota(jnp.int32, scores.shape, 1)
    scores = jnp.where(col <= row, scores, -1e30)
    expo = jnp.exp(scores - jnp.max(scores, axis=1, keepdims=True))
    return expo / jnp.sum(expo, axis=1, keepdims=True)


def front_kernel(
    p,
    x,
    g,
    qkv,
    outw,
    up,
    down,
    lens,
    qkv_b,
    out_b,
    up_b,
    down_b,
    gain1,
    bias1,
    gain2,
    bias2,
    xa,
    ga,
    qw,
    dw,
    uw,
    sm,
    n1,
    n2,
    hid,
    slope,
    heads,
    joint,
    rows_out,
    small,
    pads,
    gm,
    sm_v,
    vecs,
    ub,
    qb,
    cos_v,
    sin_v,
    uw_v,
    qw_v,
    xs,
    n1_v,
    n2_v,
    hid_v,
    slope_v,
    heads_v,
    joint_v,
    ux,
    qx,
    loc,
    puts,
    s_ux,
    r_ux,
    s_qx,
    r_qx,
    s_sm,
    r_sm,
    s_up,
    r_up,
    s_upb,
    r_upb,
    s_q,
    r_q,
    s_qb,
    r_qb,
    s_qc,
    r_qc,
    s_o,
    r_o,
    s_ob,
    s_oc,
    r_oc,
    s_d,
    r_d,
    s_r,
    r_r,
    s_l,
    r_l,
    s_x,
    r_x,
    s_s,
    r_s,
):
    A, S, C, r, R = p.A, p.S, p.C, p.r, p.R
    dp, c, a, b, xh, core = place(p)
    me = dp * C + c
    t = a * C + c
    head = a * p.X + xh
    sib = (dp, xh * 2 + 1 - core)
    xnb = (dp, (1 - xh) * 2 + core)
    right = (dp + S, c)
    left = (dp - S, c)
    L = C * p.tok
    half = A // 2

    length = lens[0]

    def mask(at):
        row = lax.broadcasted_iota(jnp.int32, (32, p.d), 0) + (at + c * p.tok)
        rows = g[pl.ds(at, 32), :].astype(F32)
        gm[pl.ds(at, 32), :] = jnp.where(row < length, rows, 0.0).astype(BF)

    tiles(p.tok, mask, 32)

    pads[...] = jnp.zeros_like(pads)
    vectors = (qkv_b, up_b, gain1, bias1, gain2, bias2, out_b)
    for k, v in enumerate(vectors):
        value = v[...].astype(F32)
        if k == len(vectors) - 1:
            value = value + down_b[...].astype(F32)
        pads[k : k + 1, 0 : v.shape[1]] = value
    for k, v in enumerate(vectors):
        placed = pltpu.roll(pads[k : k + 1, :], lax.rem(v.shape[1] * me, LANES), 1)
        small[2 * k : 2 * k + 1, :] = placed[:, :LANES]
        small[2 * k + 1 : 2 * k + 2, :] = placed[:, LANES:]
    small[2 * len(vectors) :, :] = jnp.zeros((2, LANES), F32)
    greet_all(p, me)

    own_small = pltpu.make_async_copy(small, sm.at[me], loc.at[0])
    own_small.start()
    own_x = pltpu.make_async_copy(x, xa.at[a, pl.ds(pl.multiple_of(c * p.tok, p.tok), p.tok)], loc.at[1])
    own_x.start()
    own_g = pltpu.make_async_copy(gm, ga.at[a, pl.ds(pl.multiple_of(c * p.tok, p.tok), p.tok)], loc.at[2])
    own_g.start()

    row_head = lax.div(me * r, HEAD_DIM)
    row_part = lax.div(lax.rem(me * r, HEAD_DIM), 2 * r)
    o_dp, o_ctx = lax.div(row_head, p.X) * S + b, lax.rem(row_head, p.X) * 2 + core
    o_here = (o_dp == dp) & (o_ctx == c)

    def o_rows(k, cc):
        return dw.at[pl.ds(pl.multiple_of(p.ffl + (2 * k + cc) * r, r), r)]

    def o_first(k):
        owner = lax.div(head * HEAD_DIM, r) + 2 * k + core
        return lax.rem(lax.div(owner, C), S) == b

    streams = ((x, xa), (gm, ga))

    def blk(j, k, cc):
        return streams[j][1].at[k, pl.ds(pl.multiple_of(cc * p.tok, p.tok), p.tok)]

    def send_z(j):
        own, slot = streams[j][0], blk(j, a, c)

        @pl.when(a < A - 1)
        def _():
            remote(own, slot, s_r.at[j, 0], r_r.at[j, 0], right).start()

        @pl.when(a > 0)
        def _():
            remote(own, slot, s_l.at[j, 0], r_l.at[j, 0], left).start()

    def send_x(j):
        own, slot = streams[j][0], blk(j, a, c)
        remote(own, slot, s_x.at[j, a], r_x.at[j, a], xnb).start()
        remote(own, slot, s_s.at[j, a], r_s.at[j, a], sib).start()

    def z_step(j, s):
        @pl.when(a - 1 - s >= 0)
        def _():
            k = a - 1 - s
            part = blk(j, k, c)
            drain(part, r_r.at[j, s])

            @pl.when((s + 1 < A - 1) & (a < A - 1))
            def _():
                nxt = jnp.minimum(s + 1, A - 2)
                remote(part, part, s_r.at[j, nxt], r_r.at[j, nxt], right).start()

            remote(part, part, s_x.at[j, k], r_x.at[j, k], xnb).start()
            remote(part, part, s_s.at[j, k], r_s.at[j, k], sib).start()

        @pl.when(a + 1 + s <= A - 1)
        def _():
            k = a + 1 + s
            part = blk(j, k, c)
            drain(part, r_l.at[j, s])

            @pl.when((s + 1 < A - 1) & (a > 0))
            def _():
                nxt = jnp.minimum(s + 1, A - 2)
                remote(part, part, s_l.at[j, nxt], r_l.at[j, nxt], left).start()

            remote(part, part, s_x.at[j, k], r_x.at[j, k], xnb).start()
            remote(part, part, s_s.at[j, k], r_s.at[j, k], sib).start()

    xc = (1 - xh) * 2 + core

    def cross(j, k):
        part = blk(j, k, xc)
        drain(part, r_x.at[j, k])
        remote(part, part, s_s.at[j, k], r_s.at[j, k], sib).start()

    runs = p.ffl // p.W

    def up_cols(aa, cc, j):
        return up.at[:, pl.ds(pl.multiple_of(unit_run(p, aa, cc, j), LANES), p.W)]

    def up_over(i, carry):
        aa, kk = lax.div(i, 2), lax.rem(i, 2)
        for j in range(runs):
            dst = ux.at[aa, kk, :, pl.ds(j * p.W, p.W)]
            remote(up_cols(aa, (1 - xh) * 2 + kk, j), dst, s_ux, r_ux, xnb).start()
        return carry

    def up_along(i, carry):
        aa, kk = lax.rem(a + 1 + lax.div(i, 2), A), lax.rem(i, 2)
        cc = xh * 2 + kk
        here = (aa == a) & (kk == core)
        for j in range(runs):
            dst = uw.at[a, b, c, :, pl.ds(j * p.W, p.W)]

            @pl.when(jnp.logical_not(here))
            def _():
                remote(up_cols(aa, cc, j), dst, s_up, r_up, (aa * S + b, cc)).start()

            @pl.when(here)
            def _():
                pltpu.make_async_copy(up_cols(aa, cc, j), dst, r_up).start()

        return carry

    def up_onward(i, carry):
        aa, kk = lax.rem(a + 1 + lax.div(i, 2), A), lax.rem(i, 2)
        here = (aa == a) & (kk == core)
        src, dst = ux.at[aa, kk], uw.at[a, b, (1 - xh) * 2 + core]

        @pl.when(jnp.logical_not(here))
        def _():
            remote(src, dst, s_up, r_up, (aa * S + b, xh * 2 + kk)).start()

        @pl.when(here)
        def _():
            pltpu.make_async_copy(src, dst, r_up).start()

        return carry

    def q_cols(aa, xx, j):
        col = pl.multiple_of(j * p.d + (aa * p.X + xx) * HEAD_DIM, HEAD_DIM)
        return qkv.at[:, pl.ds(col, HEAD_DIM)]

    def q_over(aa, carry):
        for j in range(3):
            dst = qx.at[aa, :, pl.ds(j * HEAD_DIM, HEAD_DIM)]
            remote(q_cols(aa, 1 - xh, j), dst, s_qx, r_qx, xnb).start()
        return carry

    def q_along(i, carry):
        aa = lax.rem(a + 1 + i, A)
        for j in range(3):
            dst = qw.at[a, b, xh, core, :, pl.ds(j * HEAD_DIM, HEAD_DIM)]

            @pl.when(aa != a)
            def _():
                remote(q_cols(aa, xh, j), dst, s_q, r_q, (aa * S + b, c)).start()

            @pl.when(aa == a)
            def _():
                pltpu.make_async_copy(q_cols(aa, xh, j), dst, r_q).start()

        return carry

    def q_onward(i, carry):
        aa = lax.rem(a + 1 + i, A)
        src, dst = qx.at[aa], qw.at[a, b, 1 - xh, core]

        @pl.when(aa != a)
        def _():
            remote(src, dst, s_q, r_q, (aa * S + b, c)).start()

        @pl.when(aa == a)
        def _():
            pltpu.make_async_copy(src, dst, r_q).start()

        return carry

    def up_cross(k, carry):
        bb = lax.rem(b + k, S)
        remote(uw.at[:, b], uw.at[:, b], s_upb, r_upb, (a * S + bb, c)).start()
        return carry

    def q_cross(k, carry):
        bb = lax.rem(b + k, S)
        part = qw.at[:, b, :, core]
        remote(part, part, s_qb, r_qb, (a * S + bb, c)).start()
        return carry

    def slot_rows(k):
        return pl.ds(pl.multiple_of(k * L, L), L)

    near = far_order(p, a)[::-1]

    def norm_slot(i):
        k = near[i]
        drain(xa.at[k, pl.ds(0, p.X * p.tok)], r_s.at[0, k])
        get = pltpu.make_async_copy(xa.at[k], xs, loc.at[3])
        get.start()
        get.wait()
        mine = lax.div(k, half) == core
        step = 32

        def unit_rows(at):
            rows = xs[pl.ds(at, step), :].astype(F32)
            rows = rows - jnp.mean(rows, axis=1, keepdims=True)
            spread = jnp.mean(rows * rows, axis=1, keepdims=True)
            rows = rows * lax.rsqrt(spread + EPS)
            to = pl.multiple_of(k * L + at, step)
            n2_v[pl.ds(to, step), :] = (rows * vecs[2:3, :] + vecs[3:4, :]).astype(BF)
            return rows

        @pl.when(mine)
        def _():
            def both(at):
                rows = unit_rows(at)
                to = pl.multiple_of(lax.rem(k, half) * L + at, step)
                n1_v[pl.ds(to, step), :] = (rows * vecs[0:1, :] + vecs[1:2, :]).astype(BF)

            tiles(L, both, step)

        @pl.when(jnp.logical_not(mine))
        def _():
            def one(at):
                unit_rows(at)

            tiles(L, one, step)

        pltpu.make_async_copy(n2_v.at[slot_rows(k)], n2.at[slot_rows(k)], puts.at[i]).start()

    def units(i):
        k = near[i]

        def unit_tile(n):
            at = pl.ds(n, TILE)
            w = uw_v[:, :, :, :, at].reshape(p.d, TILE)
            v = dot(n2_v[slot_rows(k), :], w) + ub[:, at]
            phi = 0.5 * (1.0 + lax.erf(v * (1.0 / math.sqrt(2.0))))
            density = jnp.exp(-0.5 * v * v) * (1.0 / math.sqrt(2.0 * math.pi))
            hid_v[slot_rows(k), at] = (v * phi).astype(BF)
            slope_v[slot_rows(k), at] = (phi + v * density).astype(BF)

        tiles(p.ffl, unit_tile)

    d_ctx, d_row = unit_home(p, b, xh, core)
    d_dst = dw.at[pl.ds(pl.multiple_of(d_row, R), R)]
    def small_all():
        def small_send(k, carry):
            other = lax.rem(me + k, p.n)
            dev = (lax.div(other, C), lax.rem(other, C))
            remote(small, sm.at[me], s_sm, r_sm, dev).start()
            return carry

        lax.fori_loop(1, p.n, small_send, 0)

    def down_all():
        for bb in range(S):
            here = (bb == b) & (d_ctx == c)

            @pl.when(jnp.logical_not(here))
            def _():
                remote(down, d_dst, s_d.at[bb], r_d, (a * S + bb, d_ctx)).start()

            @pl.when(here)
            def _():
                pltpu.make_async_copy(down, d_dst, r_d).start()

    def out_send():
        @pl.when(jnp.logical_not(o_here))
        def _():
            remote(outw, o_rows(row_part, core), s_o, r_o.at[row_part], (o_dp, o_ctx)).start()

        @pl.when(o_here)
        def _():
            pltpu.make_async_copy(outw, o_rows(row_part, core), r_o.at[row_part]).start()

    def chunk(which, jj):
        size = vectors[which].shape[1]
        if size % LANES == 0:
            count = 1
        elif LANES % size == 0:
            count = LANES // size
        else:
            count = (LANES - 1) // size + 2
        total = jnp.zeros((1, LANES), F32)
        for o in range(count):
            i = lax.div(LANES * jj, size) + o
            row = jj - lax.div(i * size, LANES)
            good = ((row >= 0) & (row <= 1) & (i < p.n)).astype(F32)
            at = 2 * which + jnp.clip(row, 0, 1)
            total = total + good * sm_v[jnp.minimum(i, p.n - 1), pl.ds(at, 1), :]
        return total

    def vectors_whole():
        own_small.wait()
        drain(sm.at[pl.ds(0, p.n - 1)], r_sm)
        get_small = pltpu.make_async_copy(sm, sm_v, loc.at[0])
        get_small.start()
        get_small.wait()

        def fill(jj, carry):
            for k in range(5):
                vecs[k : k + 1, pl.ds(pl.multiple_of(jj * LANES, LANES), LANES)] = chunk(2 + k, jj)
            return carry

        lax.fori_loop(0, p.d // LANES, fill, 0)
        for j in range(p.ffl // LANES):
            run, rest = j * LANES // p.W, (j * LANES % p.W) // LANES
            first = lax.div(unit_run(p, a, c, run), LANES) + rest
            ub[:, j * LANES : (j + 1) * LANES] = chunk(1, first)
        for j in range(3):
            for k in range(HEAD_DIM // LANES):
                first = (j * p.d + head * HEAD_DIM) // LANES + k
                at = j * HEAD_DIM + k * LANES
                qb[:, at : at + LANES] = chunk(0, first)

    def out_onward():
        for k in range(p.m):
            drain(o_rows(k, core), r_o.at[k])

            @pl.when(o_first(k))
            def _():
                def o_cross(kk, carry):
                    bb = lax.rem(b + kk, S)
                    rows = o_rows(k, core)
                    remote(rows, rows, s_ob.at[k], r_o.at[k], (a * S + bb, c)).start()
                    return carry

                lax.fori_loop(1, S, o_cross, 0)

            remote(o_rows(k, core), o_rows(k, core), s_oc.at[k], r_oc.at[k], sib).start()

    def load_uw():
        for _ in range(S - 1):
            drain(uw.at[:, b], r_upb)
        get = pltpu.make_async_copy(uw, uw_v, loc.at[3])
        get.start()
        get.wait()

    def send_half_qw():
        for _ in range(S - 1):
            drain(qw.at[:, b, :, core], r_qb)
        part = qw.at[:, :, :, core]
        remote(part, part, s_qc, r_qc, sib).start()

    def load_qw():
        drain(qw.at[:, :, :, 1 - core], r_qc)
        get = pltpu.make_async_copy(qw, qw_v, loc.at[3])
        get.start()
        get.wait()

    def attend(i):
        own = pl.ds(pl.multiple_of(i * L, L), L)
        cols = [pl.ds(j * HEAD_DIM, HEAD_DIM) for j in range(3)]
        for j in range(3):
            w = qw_v[:, :, :, :, :, cols[j]].reshape(p.d, HEAD_DIM)
            v = dot(n1_v[own, :], w) + qb[:, cols[j]]
            if j < 2:
                v = turn(v, cos_v[...], sin_v[...])
            joint_v[own, cols[j]] = v.astype(BF)
        rows = L // 2
        for h in range(2):
            at = pl.ds(pl.multiple_of(i * L + h * rows, rows), rows)
            keys = pl.ds(pl.multiple_of(i * L, L), (h + 1) * rows)
            probs = probabilities(joint_v[at, cols[0]], joint_v[keys, cols[1]], h * rows, SCALE)
            heads_v[at, :] = dot(probs.astype(BF), joint_v[keys, cols[2]]).astype(BF)

    send_z(0)
    send_x(0)
    small_all()
    lax.fori_loop(0, 2 * A, up_over, 0)
    angle_tables(cos_v, sin_v)
    z_step(0, 0)
    cross(0, near[0])
    lax.fori_loop(0, 2 * A, up_along, 0)
    z_step(0, 1)
    drain(ux, r_ux)
    lax.fori_loop(0, 2 * A, up_onward, 0)
    down_all()
    cross(0, near[1])
    vectors_whole()
    own_x.wait()
    norm_slot(0)
    lax.fori_loop(0, A, q_over, 0)
    send_x(1)
    out_send()
    norm_slot(1)
    lax.fori_loop(0, A, q_along, 0)
    cross(0, near[2])
    send_z(1)
    norm_slot(2)
    drain(uw.at[:, b], r_up)
    lax.fori_loop(1, S, up_cross, 0)
    drain(qx, r_qx)
    lax.fori_loop(0, A, q_onward, 0)
    z_step(0, 2)
    cross(1, near[0])
    z_step(1, 0)
    out_onward()
    load_uw()
    drain(qw.at[:, b, :, core], r_q)
    lax.fori_loop(1, S, q_cross, 0)
    cross(1, near[1])
    z_step(1, 1)
    units(0)
    cross(0, near[3])
    units(1)
    send_half_qw()
    norm_slot(3)
    put_n1 = pltpu.make_async_copy(n1_v, n1, loc.at[6])
    put_n1.start()
    put_rows = pltpu.make_async_copy(vecs, rows_out, loc.at[7])
    put_rows.start()
    z_step(1, 2)
    units(2)
    load_qw()
    attend(0)
    units(3)
    put_hid = pltpu.make_async_copy(hid_v, hid, loc.at[4])
    put_hid.start()
    put_slope = pltpu.make_async_copy(slope_v, slope, loc.at[5])
    put_slope.start()
    cross(1, near[2])
    attend(1)
    cross(1, near[3])

    put_heads = pltpu.make_async_copy(heads_v, heads, loc.at[0])
    put_heads.start()
    put_joint = pltpu.make_async_copy(joint_v, joint, loc.at[1])
    put_joint.start()

    drain(dw.at[pl.ds(0, p.ffl)], r_d)
    for k in range(p.m):
        drain(dw.at[pl.ds(0, r)], r_oc.at[k])
    for k in range(A):
        drain(ga.at[k, pl.ds(0, p.X * p.tok)], r_s.at[1, k])

    own_g.wait()
    put_hid.wait()
    put_slope.wait()
    put_n1.wait()
    put_rows.wait()
    put_heads.wait()
    put_joint.wait()
    for i in range(A):
        drain(n2_v.at[pl.ds(0, L)], puts.at[i])
    drain(sm.at[pl.ds(0, p.n - 1)], s_sm)
    drain(ux, s_ux)
    drain(qx, s_qx)
    for _ in range(4 * A - 2):
        drain(uw.at[a, b, c], s_up)
    for _ in range(2 * A - 2):
        drain(qw.at[a, b, xh, core], s_q)
    for bb in range(S):

        @pl.when(jnp.logical_not((bb == b) & (d_ctx == c)))
        def _():
            drain(down, s_d.at[bb])

    @pl.when(jnp.logical_not(o_here))
    def _():
        drain(outw, s_o)

    for k in range(p.m):

        @pl.when(o_first(k))
        def _():
            for _ in range(S - 1):
                drain(outw, s_ob.at[k])

    for k in range(p.m):
        drain(dw.at[pl.ds(0, r)], s_oc.at[k])
    for _ in range(S - 1):
        drain(uw.at[:, b], s_upb)
        drain(qw.at[:, b, :, core], s_qb)
    drain(qw.at[:, :, :, core], s_qc)
    for j in range(2):
        for s in range(A - 1):

            @pl.when((a < A - 1) & (a - s >= 0))
            def _():
                drain(x, s_r.at[j, s])

            @pl.when((a > 0) & (a + s <= A - 1))
            def _():
                drain(x, s_l.at[j, s])

        for k in range(A):
            drain(x, s_x.at[j, k])
            drain(xa.at[k, pl.ds(0, p.X * p.tok)], s_s.at[j, k])


def front(p, x, g, qkv, outw, up, down, lens, *vectors):
    dma = pltpu.SemaphoreType.DMA
    A, S, C, r = p.A, p.S, p.C, p.r
    L = C * p.tok
    vm = pltpu.VMEM
    hbm = pl.BlockSpec(memory_space=pl.ANY)
    vmem = pl.BlockSpec(memory_space=pltpu.VMEM)
    half = p.rows // 2
    qw_shape = (A, S, p.X, 2, r, p.hc)
    uw_shape = (A, S, C, r, p.ffl)
    return pl.pallas_call(
        functools.partial(front_kernel, p),
        out_shape=(
            jax.ShapeDtypeStruct((A, L, p.d), BF),
            jax.ShapeDtypeStruct((A, L, p.d), BF),
            jax.ShapeDtypeStruct(qw_shape, BF),
            jax.ShapeDtypeStruct((p.ffl + HEAD_DIM, p.d), BF),
            jax.ShapeDtypeStruct(uw_shape, BF),
            jax.ShapeDtypeStruct((p.n, 16, LANES), F32),
            jax.ShapeDtypeStruct((half, p.d), BF),
            jax.ShapeDtypeStruct((p.rows, p.d), BF),
            jax.ShapeDtypeStruct((p.rows, p.ffl), BF),
            jax.ShapeDtypeStruct((p.rows, p.ffl), BF),
            jax.ShapeDtypeStruct((half, HEAD_DIM), BF),
            jax.ShapeDtypeStruct((half, p.hc), BF),
            jax.ShapeDtypeStruct((8, p.d), F32),
        ),
        in_specs=[vmem] * 6 + [pl.BlockSpec(memory_space=pltpu.SMEM)] + [vmem] * 8,
        out_specs=[hbm] * 13,
        scratch_shapes=[
            vm((16, LANES), F32),
            vm((8, 2 * LANES), F32),
            vm((p.tok, p.d), BF),
            vm((p.n, 16, LANES), F32),
            vm((8, p.d), F32),
            vm((1, p.ffl), F32),
            vm((1, p.hc), F32),
            vm((L, LANES), F32),
            vm((L, LANES), F32),
            vm(uw_shape, BF),
            vm(qw_shape, BF),
            vm((L, p.d), BF),
            vm((half, p.d), BF),
            vm((p.rows, p.d), BF),
            vm((p.rows, p.ffl), BF),
            vm((p.rows, p.ffl), BF),
            vm((half, HEAD_DIM), BF),
            vm((half, p.hc), BF),
            vm((A, 2, r, p.ffl), BF),
            vm((A, r, p.hc), BF),
            dma((8,)),
            dma((A,)),
            dma,
            dma,
            dma,
            dma,
            dma,
            dma,
            dma,
            dma,
            dma,
            dma,
            dma,
            dma,
            dma,
            dma,
            dma,
            dma,
            dma,
            dma((p.m,)),
            dma((p.m,)),
            dma((p.m,)),
            dma((p.m,)),
            dma((S,)),
            dma,
            dma((2, A - 1)),
            dma((2, A - 1)),
            dma((2, A - 1)),
            dma((2, A - 1)),
            dma((2, A)),
            dma((2, A)),
            dma((2, A)),
            dma((2, A)),
        ],
        compiler_params=pltpu.CompilerParams(
            collective_id=0, has_side_effects=True, vmem_limit_bytes=60 * 1024 * 1024
        ),
        name="front",
    )(x, g, qkv, outw, up, down, lens, *vectors)


def back_kernel(
    p,
    hid,
    heads,
    slope,
    g,
    joint,
    n1,
    n2,
    dw,
    uw,
    qw,
    gains,
    o_sum,
    e_sum,
    q_out,
    u_out,
    d_parts,
    o_parts,
    v_all,
    hid_v,
    heads_v,
    dpre,
    ge,
    joint_v,
    dw_v,
    uw_v,
    qw_v,
    n_v,
    t_v,
    dh_v,
    cos_v,
    sin_v,
    op,
    from_sib,
    from_x,
    came,
    dgrad,
    q_g,
    q_sib,
    q_group,
    o_g,
    o_sib,
    u_parts,
    vec,
    loc,
    n_sem,
    s_v,
    r_v,
    s_s,
    r_s,
    s_x,
    r_x,
    s_c,
    r_c,
    s_q,
    r_q,
    s_qb,
    r_qb,
    s_qa,
    r_qa,
    s_o,
    r_o,
    s_oa,
    r_oa,
    s_u,
    r_u,
    s_ua,
    r_ua,
    s_d,
    r_d,
    free,
):
    A, S, C, X, r, R = p.A, p.S, p.C, p.X, p.r, p.R
    dp, c, a, b, xh, core = place(p)
    me = dp * C + c
    t = a * C + c
    head = a * X + xh
    sib = (dp, xh * 2 + 1 - core)
    xnb = (dp, (1 - xh) * 2 + core)
    far = 1 - xh
    L = C * p.tok
    D, ffl = p.d, p.ffl
    half = A // 2
    ugrad = hid_v

    loads = [
        pltpu.make_async_copy(src, dst, loc.at[k])
        for k, (src, dst) in enumerate(
            (
                (hid, hid_v.at[pl.ds(0, p.rows)]),
                (dw, dw_v),
                (heads, heads_v),
                (g, ge),
                (joint, joint_v),
                (slope, dpre),
                (uw, uw_v),
                (qw, qw_v),
            )
        )
    ]
    for load in loads:
        load.start()
    vec[...] = jnp.zeros_like(vec)
    angle_tables(cos_v, sin_v)
    greet_all(p, me)

    order = far_order(p, a)
    parts = (op, ge)

    def rows_of(side, cc):
        return pl.ds(pl.multiple_of((side * 2 + cc) * p.tok, p.tok), p.tok)

    def send_sib(j, k):
        for side in range(X):
            src = parts[j].at[k, rows_of(side, 1 - core)]
            remote(src, from_sib.at[k, side], s_s.at[j, k], r_s.at[j, k], sib).start()

    def chip_sum(j, k):
        drain(from_sib.at[k], r_s.at[j, k])
        mine = parts[j].at[k, rows_of(far, core)]
        add_rows(mine, (mine, from_sib.at[k, far]), p.tok)
        remote(mine, from_x.at[j, k], s_x.at[j, k], r_x.at[j, k], xnb).start()
        mine = parts[j].at[k, rows_of(xh, core)]
        add_rows(mine, (mine, from_sib.at[k, xh]), p.tok)

    def hop(j, k):
        drain(from_x.at[j, k], r_x.at[j, k])
        mine = parts[j].at[k, rows_of(xh, core)]
        first = jnp.where(k > a, a == 0, a == A - 1)

        @pl.when(first)
        def _():
            add_rows(mine, (mine, from_x.at[j, k]), p.tok)

        @pl.when(jnp.logical_not(first))
        def _():
            drain(came.at[j, k], r_c.at[j, k])
            add_rows(mine, (mine, from_x.at[j, k], came.at[j, k]), p.tok)

        to = jnp.where((k < a) & (k == a - 1), A, k)
        dev = (dp + jnp.where(k > a, S, -S), c)
        remote(mine, came.at[j, to], s_c.at[j, k], r_c.at[j, to], dev).start()

    def last(j, total):
        drain(from_x.at[j, a], r_x.at[j, a])
        mine = parts[j].at[a, rows_of(xh, core)]

        @pl.when(a == 0)
        def _():
            drain(came.at[j, A], r_c.at[j, A])
            add_rows(total, (mine, from_x.at[j, a], came.at[j, A]), p.tok)

        @pl.when(a == A - 1)
        def _():
            drain(came.at[j, a], r_c.at[j, a])
            add_rows(total, (mine, from_x.at[j, a], came.at[j, a]), p.tok)

        @pl.when((a > 0) & (a < A - 1))
        def _():
            drain(came.at[j, a], r_c.at[j, a])
            drain(came.at[j, A], r_c.at[j, A])
            add_rows(
                total, (mine, from_x.at[j, a], came.at[j, a], came.at[j, A]), p.tok
            )

    def slot_rows(k):
        return pl.ds(pl.multiple_of(k * L, L), L)

    def mine_rows(k):
        return pl.ds(pl.multiple_of(lax.rem(k, half) * L, L), L)

    for k in range(3):
        loads[k].wait()

    def out_slot(i):
        k = order[i]
        own = lax.div(k, half) == core

        @pl.when(own)
        def _():
            def tile(n):
                acc = dot(hid_v[slot_rows(k), :], dw_v[0:ffl, pl.ds(n, TILE)])
                acc += dot(heads_v[mine_rows(k), :], dw_v[ffl:, pl.ds(n, TILE)])
                op[k, :, pl.ds(n, TILE)] = acc.astype(BF)

            tiles(D, tile)

        @pl.when(jnp.logical_not(own))
        def _():
            def tile(n):
                acc = dot(hid_v[slot_rows(k), :], dw_v[0:ffl, pl.ds(n, TILE)])
                op[k, :, pl.ds(n, TILE)] = acc.astype(BF)

            tiles(D, tile)

        send_sib(0, k)

    for i in range(A):
        out_slot(i)
        if i > 0:
            chip_sum(0, order[i - 1])

    chip_sum(0, order[A - 1])
    pl.semaphore_signal(free, inc=1, device_id=sib, device_id_type=MESH)

    loads[3].wait()
    loads[5].wait()
    up_row = p.hc // LANES

    def dpre_slot(k, carry):
        def tile(n):
            dh = dot_t(ge[k], dw_v[pl.ds(n, TILE), :])
            value = (dh * dpre[slot_rows(k), pl.ds(n, TILE)].astype(F32)).astype(BF)
            dpre[slot_rows(k), pl.ds(n, TILE)] = value

        tiles(ffl, tile)
        return carry

    lax.fori_loop(0, A, dpre_slot, 0)

    def sum_rows(i, carry):
        at = pl.ds(pl.multiple_of(i * 64, 64), 64)
        return carry + jnp.sum(dpre[at, :].astype(F32), axis=0, keepdims=True)

    up_bias = lax.fori_loop(0, p.rows // 64, sum_rows, jnp.zeros((1, ffl), F32))
    for i in range(ffl // LANES):
        vec[up_row + i : up_row + i + 1, :] = up_bias[:, i * LANES : (i + 1) * LANES]
    g_row = up_row + ffl // LANES
    share = D // (A * C)

    def sum_g(i, carry):
        at = pl.ds(pl.multiple_of(lax.rem(i * 64, L), 64), 64)
        part = ge[lax.div(i * 64, L), at, pl.ds(pl.multiple_of(t * share, share), share)]
        return carry + jnp.sum(part.astype(F32), axis=0, keepdims=True)

    vec[g_row : g_row + 1, :] = lax.fori_loop(
        0, p.rows // 64, sum_g, jnp.zeros((1, share), F32)
    )

    def down_units(f, carry):
        at = pl.ds(pl.multiple_of(f * TILE, TILE), TILE)
        for k in range(A):
            t_v[:, k * L : (k + 1) * L] = hid_v[k * L : (k + 1) * L, at].astype(F32).T.astype(BF)

        def tile(n):
            acc = dot(t_v[:, 0:L], ge[0, :, pl.ds(n, TILE)])
            for k in range(1, A):
                acc += dot(t_v[:, k * L : (k + 1) * L], ge[k, :, pl.ds(n, TILE)])
            dgrad[at, pl.ds(n, TILE)] = acc.astype(BF)

        tiles(D, tile)
        return carry

    lax.fori_loop(0, ffl // TILE, down_units, 0)
    d_ctx, _ = unit_home(p, b, xh, core)
    for j in range(S):
        if p.P == 1:
            own_b, own_c = j, c
        else:
            own_b, own_c = 2 * (j // 2) + core, xh * 2 + j % 2
        src = dgrad.at[pl.ds(j * R, R)]
        here = (own_b == b) & (own_c == c)

        @pl.when(jnp.logical_not(here))
        def _():
            remote(src, d_parts.at[b], s_d.at[j], r_d, (a * S + own_b, own_c)).start()

        @pl.when(here)
        def _():
            pltpu.make_async_copy(src, d_parts.at[b], r_d).start()

    def n_load(src, i, slot):
        count = src.shape[0]
        return pltpu.make_async_copy(
            src.at[:, pl.ds(pl.multiple_of(i * TILE, TILE), TILE)],
            n_v.at[slot, pl.ds(0, count)],
            n_sem.at[slot],
        )

    def stream(src, use):
        n_load(src, 0, 0).start()

        def step(i, carry):
            slot = lax.rem(i, 2)
            n_load(src, i, slot).wait()

            @pl.when(i + 1 < D // TILE)
            def _():
                n_load(src, i + 1, 1 - slot).start()

            use(i, slot)
            return carry

        lax.fori_loop(0, D // TILE, step, 0)

    def up_tile(i, slot):
        at = pl.ds(pl.multiple_of(i * TILE, TILE), TILE)
        ugrad[at, :] = t_dot(n_v[slot], dpre[...]).astype(BF)

    stream(n2, up_tile)
    blk = C * r

    def u_rows(aa, bb):
        return ugrad.at[pl.ds(pl.multiple_of((aa * S + bb) * blk, blk), blk)]

    def u_send(k, carry):
        bb = lax.rem(b + k, S)
        for aa in range(A):
            remote(u_rows(aa, bb), u_parts.at[k - 1, aa], s_u, r_u, (a * S + bb, c)).start()
        return carry

    lax.fori_loop(1, S, u_send, 0)

    hop(0, order[0])

    loads[4].wait()
    cols = [pl.ds(j * HEAD_DIM, HEAD_DIM) for j in range(3)]
    rows2 = L // 2

    def attend_back(i, carry):
        own = pl.ds(pl.multiple_of(i * L, L), L)
        dh_v[own, :] = dot_t(ge[core * half + i], dw_v[ffl:, :]).astype(BF)
        dq, dk, dv = [], [], []
        for h in range(2):
            at = pl.ds(pl.multiple_of(i * L + h * rows2, rows2), rows2)
            keys = pl.ds(pl.multiple_of(i * L, L), (h + 1) * rows2)
            q, k, v = joint_v[at, cols[0]], joint_v[keys, cols[1]], joint_v[keys, cols[2]]
            dh = dh_v[at, :]
            probs = probabilities(q, k, h * rows2, SCALE)
            d_probs = dot_t(dh, v)
            delta = jnp.sum(probs * d_probs, axis=1, keepdims=True)
            d_scores = (probs * (d_probs - delta)).astype(BF)
            dq.append(dot(d_scores, k) * SCALE)
            dk.append(t_dot(d_scores, q) * SCALE)
            dv.append(t_dot(probs.astype(BF), dh))
        dq = jnp.concatenate(dq, axis=0)
        dk = jnp.concatenate([dk[0] + dk[1][:rows2], dk[1][rows2:]], axis=0)
        dv = jnp.concatenate([dv[0] + dv[1][:rows2], dv[1][rows2:]], axis=0)
        cos, sin = cos_v[...], sin_v[...]
        for j, d_part in enumerate((turn(dq, cos, -sin), turn(dk, cos, -sin), dv)):
            low = d_part.astype(BF)
            joint_v[own, cols[j]] = low
            sums = jnp.sum(low.astype(F32), axis=0, keepdims=True)
            for k in range(HEAD_DIM // LANES):
                at = j * (HEAD_DIM // LANES) + k
                vec[at : at + 1, :] += sums[:, k * LANES : (k + 1) * LANES]
        return carry

    lax.fori_loop(0, half, attend_back, 0)
    for k in range(half):
        t_v[:, k * L : (k + 1) * L] = heads_v[k * L : (k + 1) * L, :].astype(F32).T.astype(BF)

    def o_tile(n):
        acc = dot(t_v[:, 0:L], ge[core * half, :, pl.ds(n, TILE)])
        for k in range(1, half):
            acc += dot(t_v[:, k * L : (k + 1) * L], ge[core * half + k, :, pl.ds(n, TILE)])
        acc = acc.astype(BF)
        for k in range(p.m):
            for kk in range(2):
                at = (2 * k + kk) * r
                o_g[k, kk, :, pl.ds(n, TILE)] = acc[at : at + r]

    tiles(D, o_tile)
    remote(o_g.at[:, 1 - core], o_sib, s_o, r_o, sib).start()

    hop(0, order[1])

    loads[6].wait()
    loads[7].wait()
    pl.semaphore_wait(free, 1)

    def e_slot(i):
        k = order[i]
        own = lax.div(k, half) == core

        @pl.when(own)
        def _():
            def tile(n):
                acc = dot_t(dpre[slot_rows(k), :], uw_v[pl.ds(n, TILE), :])
                acc1 = dot_t(joint_v[mine_rows(k), :], qw_v[pl.ds(n, TILE), :])
                acc = acc * gains[2:3, pl.ds(n, TILE)] + acc1 * gains[0:1, pl.ds(n, TILE)]
                ge[k, :, pl.ds(n, TILE)] = acc.astype(BF)

            tiles(D, tile)

        @pl.when(jnp.logical_not(own))
        def _():
            def tile(n):
                acc = dot_t(dpre[slot_rows(k), :], uw_v[pl.ds(n, TILE), :])
                acc = acc * gains[2:3, pl.ds(n, TILE)]
                ge[k, :, pl.ds(n, TILE)] = acc.astype(BF)

            tiles(D, tile)

        send_sib(1, k)

    for i in range(A):
        e_slot(i)
        if i > 0:
            chip_sum(1, order[i - 1])
        if i == 2:
            hop(0, order[2])
    chip_sum(1, order[A - 1])

    pairs = TILE // (2 * r)

    def q_tile(i, slot):
        for j in range(3):
            acc = t_dot(n_v[slot, 0 : p.rows // 2, :], joint_v[:, cols[j]]).astype(BF)
            for k in range(pairs):
                for kk in range(2):
                    at = (2 * k + kk) * r
                    q_g[i * pairs + k, kk, :, cols[j]] = acc[at : at + r]

    stream(n1, q_tile)
    remote(q_g.at[:, 1 - core], q_sib, s_q, r_q, sib).start()

    for k in range(1, S):
        drain(u_parts.at[k - 1], r_u)
    for k in range(1, S):
        for aa in range(A):
            add_rows(u_rows(aa, b), (u_rows(aa, b), u_parts.at[k - 1, aa]), blk)

    def u_piece(tt, j):
        col = pl.multiple_of(unit_run(p, a, c, j), 128)
        aa, cc = lax.div(tt, C), lax.rem(tt, C)
        at = pl.multiple_of((aa * S + b) * blk + cc * r, r)
        return ugrad.at[pl.ds(at, r), pl.ds(j * p.W, p.W)], u_out.at[:, pl.ds(col, p.W)]

    def u_back(k, carry):
        tt = lax.rem(t + k, A * C)
        for j in range(ffl // p.W):
            src, dst = u_piece(tt, j)
            remote(src, dst, s_ua, r_ua, (lax.div(tt, C) * S + b, lax.rem(tt, C))).start()
        return carry

    lax.fori_loop(1, A * C, u_back, 0)
    for j in range(ffl // p.W):
        src, dst = u_piece(t, j)
        pltpu.make_async_copy(src, dst, r_ua).start()

    drain(q_sib, r_q)

    def q_add(i, carry):
        mine = q_g.at[i, core]
        add_rows(mine, (mine, q_sib.at[i]), r)
        return carry

    lax.fori_loop(0, A * S * X, q_add, 0)

    def q_rows(aa, bb):
        return q_g.at[pl.ds((aa * S + bb) * X, X), core]

    def q_cross(k, carry):
        bb = lax.rem(b + k, S)
        for aa in range(A):
            remote(q_rows(aa, bb), q_group.at[k - 1, aa], s_qb, r_qb, (a * S + bb, c)).start()
        return carry

    lax.fori_loop(1, S, q_cross, 0)
    drain(o_sib, r_o)
    for k in range(p.m):
        mine = o_g.at[k, core]
        add_rows(mine, (mine, o_sib.at[k]), r)
        owner = lax.div(head * HEAD_DIM, r) + 2 * k + core
        od, oc = lax.div(owner, C), lax.rem(owner, C)
        here = owner == me

        @pl.when(jnp.logical_not(here))
        def _():
            remote(mine, o_parts.at[b], s_oa.at[k], r_oa, (od, oc)).start()

        @pl.when(here)
        def _():
            pltpu.make_async_copy(mine, o_parts.at[b], r_oa).start()

    last(0, o_sum)

    own_v = pltpu.make_async_copy(vec, v_all.at[me], loc.at[8])
    own_v.start()

    def v_send(k, carry):
        other = lax.rem(me + k, p.n)
        dev = (lax.div(other, C), lax.rem(other, C))
        remote(vec, v_all.at[me], s_v, r_v, dev).start()
        return carry

    lax.fori_loop(1, p.n, v_send, 0)

    hop(1, order[0])
    hop(1, order[1])

    for k in range(1, S):
        drain(q_group.at[k - 1], r_qb)
    for k in range(1, S):

        def q_fin(i, carry):
            aa, xx = lax.div(i, X), lax.rem(i, X)
            mine = q_g.at[(aa * S + b) * X + xx, core]
            add_rows(mine, (mine, q_group.at[k - 1, aa, xx]), r)
            return carry

        lax.fori_loop(0, A * X, q_fin, 0)

    def q_piece(hh, j):
        col = pl.multiple_of(j * D + head * HEAD_DIM, HEAD_DIM)
        at = (lax.div(hh, X) * S + b) * X + lax.rem(hh, X)
        return q_g.at[at, core, :, cols[j]], q_out.at[:, pl.ds(col, HEAD_DIM)]

    def q_back(k, carry):
        hh = lax.rem(head + k, HEADS)
        dev = (lax.div(hh, X) * S + b, lax.rem(hh, X) * 2 + core)
        for j in range(3):
            src, dst = q_piece(hh, j)
            remote(src, dst, s_qa, r_qa, dev).start()
        return carry

    lax.fori_loop(1, HEADS, q_back, 0)
    for j in range(3):
        src, dst = q_piece(head, j)
        pltpu.make_async_copy(src, dst, r_qa).start()

    for i in range(2, A - 1):
        hop(1, order[i])
    last(1, e_sum)

    drain(u_out, r_ua)
    drain(q_out, r_qa)
    drain(v_all.at[pl.ds(0, p.n - 1)], r_v)
    drain(d_parts, r_d)
    drain(o_parts, r_oa)

    own_v.wait()
    drain(v_all.at[pl.ds(0, p.n - 1)], s_v)
    drain(q_sib, s_q)
    drain(o_sib, s_o)
    for k in range(1, S):
        drain(u_parts.at[0], s_u)
        drain(q_group.at[0], s_qb)
    for _ in range(A * C - 1):
        drain(ugrad.at[pl.ds(0, r)], s_ua)
    for _ in range(HEADS - 1):
        drain(q_g.at[0, 0], s_qa)
    for k in range(p.m):

        @pl.when(lax.div(head * HEAD_DIM, r) + 2 * k + core != me)
        def _():
            drain(o_g.at[k, 0], s_oa.at[k])

    for j in range(S):
        if p.P == 1:
            own_b, own_c = j, c
        else:
            own_b, own_c = 2 * (j // 2) + core, xh * 2 + j % 2

        @pl.when(jnp.logical_not((own_b == b) & (own_c == c)))
        def _():
            drain(d_parts.at[0], s_d.at[j])

    for j in range(2):
        for k in range(A):
            drain(from_sib.at[0], s_s.at[j, k])
            drain(from_x.at[0, 0], s_x.at[j, k])

            @pl.when(k != a)
            def _():
                drain(from_x.at[0, 0], s_c.at[j, k])


def back(p, *args):
    dma = pltpu.SemaphoreType.DMA
    A, S, C, X, r, R = p.A, p.S, p.C, p.X, p.r, p.R
    L = C * p.tok
    vm = pltpu.VMEM
    hbm = pl.BlockSpec(memory_space=pl.ANY)
    vmem = pl.BlockSpec(memory_space=pltpu.VMEM)
    groups = max(S - 1, 1)
    return pl.pallas_call(
        functools.partial(back_kernel, p),
        out_shape=(
            jax.ShapeDtypeStruct((p.tok, p.d), F32),
            jax.ShapeDtypeStruct((p.tok, p.d), F32),
            jax.ShapeDtypeStruct((r, 3 * p.d), BF),
            jax.ShapeDtypeStruct((r, p.ff), BF),
            jax.ShapeDtypeStruct((S, R, p.d), BF),
            jax.ShapeDtypeStruct((S, r, p.d), BF),
            jax.ShapeDtypeStruct((p.n, 16, 128), F32),
        ),
        in_specs=[hbm] * 10 + [vmem],
        out_specs=[vmem] * 2 + [hbm] * 5,
        scratch_shapes=[
            vm((max(p.rows, p.d), p.ffl), BF),
            vm((p.rows // 2, HEAD_DIM), BF),
            vm((p.rows, p.ffl), BF),
            vm((A, L, p.d), BF),
            vm((p.rows // 2, p.hc), BF),
            vm((p.ffl + HEAD_DIM, p.d), BF),
            vm((p.d, p.ffl), BF),
            vm((p.d, p.hc), BF),
            vm((2, p.rows, TILE), BF),
            vm((TILE, p.rows), BF),
            vm((p.rows // 2, HEAD_DIM), BF),
            vm((L, LANES), F32),
            vm((L, LANES), F32),
            vm((A, L, p.d), BF),
            vm((A, X, p.tok, p.d), BF),
            vm((2, A, p.tok, p.d), BF),
            vm((2, A + 1, p.tok, p.d), BF),
            vm((p.ffl, p.d), BF),
            vm((A * S * X, 2, r, p.hc), BF),
            vm((A * S * X, r, p.hc), BF),
            vm((groups, A, X, r, p.hc), BF),
            vm((p.m, 2, r, p.d), BF),
            vm((p.m, r, p.d), BF),
            vm((groups, A, C * r, p.ffl), BF),
            vm((16, 128), F32),
            dma((9,)),
            dma((2,)),
            dma,
            dma,
            dma((2, A)),
            dma((2, A)),
            dma((2, A)),
            dma((2, A)),
            dma((2, A)),
            dma((2, A + 1)),
            dma,
            dma,
            dma,
            dma,
            dma,
            dma,
            dma,
            dma,
            dma((p.m,)),
            dma,
            dma,
            dma,
            dma,
            dma,
            dma((S,)),
            dma,
            pltpu.SemaphoreType.REGULAR,
        ],
        compiler_params=pltpu.CompilerParams(
            collective_id=1, has_side_effects=True, vmem_limit_bytes=67043328
        ),
        name="back",
    )(*args)


def norm_stats(values):
    center = jnp.mean(values, axis=-1, keepdims=True)
    spread = jnp.mean(jnp.square(values - center), axis=-1, keepdims=True)
    inv_std = lax.rsqrt(spread + EPS)
    return (values - center) * inv_std, inv_std


def local(
    dp_size,
    ctx_size,
    layer_input,
    lengths,
    cotangent,
    qkv_weight,
    qkv_bias,
    out_weight,
    out_bias,
    up_weight,
    up_bias,
    down_weight,
    down_bias,
    first_gain,
    first_bias,
    second_gain,
    second_bias,
):
    tok, d = layer_input.shape
    ff = up_weight.shape[1]
    p = Plan(dp_size, ctx_size, tok, d, ff)
    A, S, C, X, r, R = p.A, p.S, p.C, p.X, p.r, p.R
    dp, c, a, b, xh, core = place(p)
    me = dp * C + c
    t = a * C + c
    valid = (c * tok + jnp.arange(tok, dtype=jnp.int32) < lengths[0])[:, None]
    grad_out = jnp.where(valid, cotangent, jnp.zeros_like(cotangent))
    vectors = (
        qkv_bias,
        out_bias,
        up_bias,
        down_bias,
        first_gain,
        first_bias,
        second_gain,
        second_bias,
    )
    (_, g_all, qw, dw, uw, _, n1, n2, hid, slope, heads, joint, full) = front(
        p,
        layer_input,
        cotangent,
        qkv_weight,
        out_weight,
        up_weight,
        down_weight,
        lengths,
        *(v.reshape(1, -1) for v in vectors),
    )
    o_sum, e_sum, q_out, u_out, d_parts, o_parts, v_all = back(
        p,
        hid,
        heads,
        slope,
        g_all,
        joint,
        n1,
        n2,
        dw,
        uw.reshape(d, p.ffl),
        qw.reshape(d, p.hc),
        full,
    )
    g_cols = d // (A * C)
    o_out = jnp.sum(o_parts.astype(F32), axis=0)
    d_out = jnp.sum(d_parts.astype(F32), axis=0)

    xf = layer_input.astype(F32)
    output = jnp.where(valid, xf + o_sum + full[4:5], 0.0).astype(BF)
    xhat_o, inv = norm_stats(xf)
    dx = inv * (
        e_sum
        - jnp.mean(e_sum, axis=-1, keepdims=True)
        - xhat_o * jnp.mean(e_sum * xhat_o, axis=-1, keepdims=True)
    )
    input_grad = (grad_out.astype(F32) + dx).astype(BF)

    v_all = v_all.reshape(A, S, C, 2048)
    v_sum = jnp.sum(v_all, axis=1)
    q_bias = v_sum[..., : p.hc].reshape(A, X, 2, 3, HEAD_DIM).sum(axis=2)
    q_bias = q_bias.reshape(HEADS, 3, HEAD_DIM).transpose(1, 0, 2).reshape(-1)
    u_bias = v_sum[..., p.hc : p.hc + p.ffl]
    if p.P == 1:
        u_bias = u_bias.reshape(A, C, S, R).transpose(0, 2, 1, 3).reshape(-1)
    else:
        u_bias = u_bias.reshape(A, X, 2, S // 2, p.W).transpose(0, 3, 2, 1, 4).reshape(-1)
    g_bias = v_sum[..., p.hc + p.ffl : p.hc + p.ffl + g_cols].reshape(-1)

    def own(vector):
        size = vector.shape[0] // p.n
        return lax.dynamic_slice(vector, (me * size,), (size,))

    def norm_grads(weight, grad, bias_grad, gain, shift):
        weight = weight.astype(F32)
        shift_grad = jnp.sum(weight * bias_grad, axis=1)
        gain_grad = (jnp.sum(weight * grad, axis=1) - shift.astype(F32) * shift_grad) / gain.astype(
            F32
        )
        return gain_grad, shift_grad

    q_grad = q_out.astype(F32)
    u_grad = u_out.astype(F32)
    gain1_grad, bias1_grad = norm_grads(qkv_weight, q_grad, q_bias, first_gain, first_bias)
    gain2_grad, bias2_grad = norm_grads(up_weight, u_grad, u_bias, second_gain, second_bias)
    g_own = own(g_bias)
    return (
        output,
        input_grad,
        q_grad,
        own(q_bias),
        o_out,
        g_own,
        u_grad,
        own(u_bias),
        d_out,
        g_own,
        gain1_grad,
        bias1_grad,
        gain2_grad,
        bias2_grad,
    )


def solution(mesh):
    rows = P(("dp", "ctx"), None)
    vector = P(("dp", "ctx"))
    return jax.shard_map(
        functools.partial(local, mesh.shape["dp"], mesh.shape["ctx"]),
        mesh=mesh,
        in_specs=(
            rows,
            P("dp"),
            rows,
            rows,
            vector,
            rows,
            vector,
            rows,
            vector,
            rows,
            vector,
            vector,
            vector,
            vector,
            vector,
        ),
        out_specs=(
            rows,
            rows,
            rows,
            vector,
            rows,
            vector,
            rows,
            vector,
            rows,
            vector,
            vector,
            vector,
            vector,
            vector,
        ),
        check_vma=False,
    )
```

```python
import functools
import math

import jax
import jax.numpy as jnp
from jax import lax
from jax.experimental import pallas as pl
from jax.experimental.pallas import tpu as pltpu
from jax.sharding import PartitionSpec as P

HEADS = 8
HEAD_DIM = 256
ROT = 64
EPS = 1e-05
SCALE = 1.0 / math.sqrt(HEAD_DIM)
MESH = pl.DeviceIdType.MESH
BF = jnp.bfloat16
F32 = jnp.float32
TILE = 256
LANES = 128


class Plan:
    def __init__(self, dp, ctx, tok, d, ff):
        self.C = ctx
        self.X = ctx // 2
        self.A = HEADS // self.X
        self.S = dp // self.A
        self.n = dp * ctx
        self.tok = tok
        self.d = d
        self.ff = ff
        self.r = d // self.n
        self.R = ff // self.n
        self.ffl = self.S * self.R
        self.W = max(self.R, 128)
        self.P = self.W // self.R
        self.hc = 3 * HEAD_DIM
        self.m = HEAD_DIM // self.r // 2
        self.rows = self.A * self.C * tok


def remote(src, dst, send, recv, dev):
    return pltpu.make_async_remote_copy(
        src_ref=src, dst_ref=dst, send_sem=send, recv_sem=recv, device_id=dev, device_id_type=MESH
    )


def drain(ref, sem):
    pltpu.make_async_copy(ref, ref, sem).wait()


def unit_run(p, aa, cc, j):
    if p.P == 1:
        return p.R * ((aa * p.S + j) * p.C + cc)
    return p.R * ((aa * p.S + 2 * j + lax.rem(cc, 2)) * p.C + lax.div(cc, 2) * 2)


def unit_home(p, b, xh, core):
    if p.P == 1:
        return xh * 2 + core, b * p.R
    return xh * 2 + lax.rem(b, 2), (lax.div(b, 2) * 2 + core) * p.R


def place(p):
    dp = lax.axis_index("dp")
    c = lax.axis_index("ctx")
    a = lax.div(dp, p.S)
    b = lax.rem(dp, p.S)
    xh = lax.div(c, 2)
    core = lax.rem(c, 2)
    return dp, c, a, b, xh, core


def greet_all(p, me):
    barrier = pltpu.get_barrier_semaphore()

    def greet(k, carry):
        other = lax.rem(me + k, p.n)
        pl.semaphore_signal(
            barrier,
            inc=1,
            device_id=(lax.div(other, p.C), lax.rem(other, p.C)),
            device_id_type=MESH,
        )
        return carry

    lax.fori_loop(1, p.n, greet, 0)
    pl.semaphore_wait(barrier, p.n - 1)


def dot(x, y):
    return jnp.dot(x, y, preferred_element_type=F32)


def dot_t(x, y):
    return lax.dot_general(x, y, (((1,), (1,)), ((), ())), preferred_element_type=F32)


def t_dot(x, y):
    return lax.dot_general(x, y, (((0,), (0,)), ((), ())), preferred_element_type=F32)


def tiles(count, body, size=TILE):
    def run(i, carry):
        body(pl.multiple_of(i * size, size))
        return carry

    lax.fori_loop(0, count // size, run, 0)


def pick(values, i):
    out = values[0]
    for k in range(1, len(values)):
        out = jnp.where(i == k, values[k], out)
    return out


def far_order(p, a):
    order = []
    lo, hi = 0, p.A - 1
    for _ in range(p.A):
        up_far = hi - a >= a - lo
        order.append(jnp.where(up_far, hi, lo))
        lo = jnp.where(up_far, lo, lo + 1)
        hi = jnp.where(up_far, hi - 1, hi)
    return order


def add_rows(dst, parts, rows):
    step = 16

    def body(k, carry):
        at = pl.ds(pl.multiple_of(k * step, step), step)
        total = parts[0][at, :].astype(F32)
        for part in parts[1:]:
            total = total + part[at, :].astype(F32)
        dst[at, :] = total.astype(dst.dtype)
        return carry

    lax.fori_loop(0, rows // step, body, 0)


def angle_tables(cos_v, sin_v):
    rows = cos_v.shape[0]
    half = ROT // 2

    def body(at):
        shape = (64, LANES)
        lane = lax.broadcasted_iota(jnp.int32, shape, 1)
        pos = (lax.broadcasted_iota(jnp.int32, shape, 0) + at).astype(F32)
        exponent = lax.rem(lane, half).astype(F32) * (-2.0 * math.log(10000.0) / ROT)
        angle = pos * jnp.exp(exponent)
        turned = lane < ROT
        sign = jnp.where(lane < half, -1.0, 1.0)
        cos_v[pl.ds(at, 64), :] = jnp.where(turned, jnp.cos(angle), 1.0)
        sin_v[pl.ds(at, 64), :] = jnp.where(turned, jnp.sin(angle) * sign, 0.0)

    tiles(rows, body, 64)


def turn(v, cos, sin):
    first = v[:, :LANES]
    half = ROT // 2
    lane = lax.broadcasted_iota(jnp.int32, first.shape, 1)
    partner = jnp.where(
        lane < half, pltpu.roll(first, LANES - half, 1), pltpu.roll(first, half, 1)
    )
    return jnp.concatenate([first * cos + partner * sin, v[:, LANES:]], axis=1)


def probabilities(q, k, row0, scale):
    scores = dot_t(q, k) * scale
    row = lax.broadcasted_iota(jnp.int32, scores.shape, 0) + row0
    col = lax.broadcasted_iota(jnp.int32, scores.shape, 1)
    scores = jnp.where(col <= row, scores, -1e30)
    expo = jnp.exp(scores - jnp.max(scores, axis=1, keepdims=True))
    return expo / jnp.sum(expo, axis=1, keepdims=True)


def front_kernel(
    p,
    x,
    g,
    qkv,
    outw,
    up,
    down,
    lens,
    qkv_b,
    out_b,
    up_b,
    down_b,
    gain1,
    bias1,
    gain2,
    bias2,
    xa,
    ga,
    qw,
    dw,
    uw,
    sm,
    n1,
    n2,
    hid,
    slope,
    heads,
    joint,
    rows_out,
    small,
    pads,
    gm,
    sm_v,
    vecs,
    ub,
    qb,
    cos_v,
    sin_v,
    uw_v,
    qw_v,
    xs,
    n1_v,
    n2_v,
    hid_v,
    slope_v,
    heads_v,
    joint_v,
    ux,
    qx,
    loc,
    puts,
    s_ux,
    r_ux,
    s_qx,
    r_qx,
    s_sm,
    r_sm,
    s_up,
    r_up,
    s_upb,
    r_upb,
    s_q,
    r_q,
    s_qb,
    r_qb,
    s_qc,
    r_qc,
    s_o,
    r_o,
    s_ob,
    s_oc,
    r_oc,
    s_d,
    r_d,
    s_r,
    r_r,
    s_l,
    r_l,
    s_x,
    r_x,
    s_s,
    r_s,
):
    A, S, C, r, R = p.A, p.S, p.C, p.r, p.R
    dp, c, a, b, xh, core = place(p)
    me = dp * C + c
    t = a * C + c
    head = a * p.X + xh
    sib = (dp, xh * 2 + 1 - core)
    xnb = (dp, (1 - xh) * 2 + core)
    right = (dp + S, c)
    left = (dp - S, c)
    L = C * p.tok
    half = A // 2

    length = lens[0]

    def mask(at):
        row = lax.broadcasted_iota(jnp.int32, (32, p.d), 0) + (at + c * p.tok)
        rows = g[pl.ds(at, 32), :].astype(F32)
        gm[pl.ds(at, 32), :] = jnp.where(row < length, rows, 0.0).astype(BF)

    tiles(p.tok, mask, 32)

    pads[...] = jnp.zeros_like(pads)
    vectors = (qkv_b, up_b, gain1, bias1, gain2, bias2, out_b)
    for k, v in enumerate(vectors):
        value = v[...].astype(F32)
        if k == len(vectors) - 1:
            value = value + down_b[...].astype(F32)
        pads[k : k + 1, 0 : v.shape[1]] = value
    for k, v in enumerate(vectors):
        placed = pltpu.roll(pads[k : k + 1, :], lax.rem(v.shape[1] * me, LANES), 1)
        small[2 * k : 2 * k + 1, :] = placed[:, :LANES]
        small[2 * k + 1 : 2 * k + 2, :] = placed[:, LANES:]
    small[2 * len(vectors) :, :] = jnp.zeros((2, LANES), F32)
    greet_all(p, me)

    own_small = pltpu.make_async_copy(small, sm.at[me], loc.at[0])
    own_small.start()
    own_x = pltpu.make_async_copy(x, xa.at[a, pl.ds(pl.multiple_of(c * p.tok, p.tok), p.tok)], loc.at[1])
    own_x.start()
    own_g = pltpu.make_async_copy(gm, ga.at[a, pl.ds(pl.multiple_of(c * p.tok, p.tok), p.tok)], loc.at[2])
    own_g.start()

    row_head = lax.div(me * r, HEAD_DIM)
    row_part = lax.div(lax.rem(me * r, HEAD_DIM), 2 * r)
    o_dp, o_ctx = lax.div(row_head, p.X) * S + b, lax.rem(row_head, p.X) * 2 + core
    o_here = (o_dp == dp) & (o_ctx == c)

    def o_rows(k, cc):
        return dw.at[pl.ds(pl.multiple_of(p.ffl + (2 * k + cc) * r, r), r)]

    def o_first(k):
        owner = lax.div(head * HEAD_DIM, r) + 2 * k + core
        return lax.rem(lax.div(owner, C), S) == b

    streams = ((x, xa), (gm, ga))

    def blk(j, k, cc):
        return streams[j][1].at[k, pl.ds(pl.multiple_of(cc * p.tok, p.tok), p.tok)]

    def send_z(j):
        own, slot = streams[j][0], blk(j, a, c)

        @pl.when(a < A - 1)
        def _():
            remote(own, slot, s_r.at[j, 0], r_r.at[j, 0], right).start()

        @pl.when(a > 0)
        def _():
            remote(own, slot, s_l.at[j, 0], r_l.at[j, 0], left).start()

    def send_x(j):
        own, slot = streams[j][0], blk(j, a, c)
        remote(own, slot, s_x.at[j, a], r_x.at[j, a], xnb).start()
        remote(own, slot, s_s.at[j, a], r_s.at[j, a], sib).start()

    def z_step(j, s):
        @pl.when(a - 1 - s >= 0)
        def _():
            k = a - 1 - s
            part = blk(j, k, c)
            drain(part, r_r.at[j, s])

            @pl.when((s + 1 < A - 1) & (a < A - 1))
            def _():
                nxt = jnp.minimum(s + 1, A - 2)
                remote(part, part, s_r.at[j, nxt], r_r.at[j, nxt], right).start()

            remote(part, part, s_x.at[j, k], r_x.at[j, k], xnb).start()
            remote(part, part, s_s.at[j, k], r_s.at[j, k], sib).start()

        @pl.when(a + 1 + s <= A - 1)
        def _():
            k = a + 1 + s
            part = blk(j, k, c)
            drain(part, r_l.at[j, s])

            @pl.when((s + 1 < A - 1) & (a > 0))
            def _():
                nxt = jnp.minimum(s + 1, A - 2)
                remote(part, part, s_l.at[j, nxt], r_l.at[j, nxt], left).start()

            remote(part, part, s_x.at[j, k], r_x.at[j, k], xnb).start()
            remote(part, part, s_s.at[j, k], r_s.at[j, k], sib).start()

    xc = (1 - xh) * 2 + core

    def cross(j, k):
        part = blk(j, k, xc)
        drain(part, r_x.at[j, k])
        remote(part, part, s_s.at[j, k], r_s.at[j, k], sib).start()

    runs = p.ffl // p.W

    def up_cols(aa, cc, j):
        return up.at[:, pl.ds(pl.multiple_of(unit_run(p, aa, cc, j), LANES), p.W)]

    def up_over(i, carry):
        aa, kk = lax.div(i, 2), lax.rem(i, 2)
        for j in range(runs):
            dst = ux.at[aa, kk, :, pl.ds(j * p.W, p.W)]
            remote(up_cols(aa, (1 - xh) * 2 + kk, j), dst, s_ux, r_ux, xnb).start()
        return carry

    def up_along(i, carry):
        aa, kk = lax.rem(a + 1 + lax.div(i, 2), A), lax.rem(i, 2)
        cc = xh * 2 + kk
        here = (aa == a) & (kk == core)
        for j in range(runs):
            dst = uw.at[a, b, c, :, pl.ds(j * p.W, p.W)]

            @pl.when(jnp.logical_not(here))
            def _():
                remote(up_cols(aa, cc, j), dst, s_up, r_up, (aa * S + b, cc)).start()

            @pl.when(here)
            def _():
                pltpu.make_async_copy(up_cols(aa, cc, j), dst, r_up).start()

        return carry

    def up_onward(i, carry):
        aa, kk = lax.rem(a + 1 + lax.div(i, 2), A), lax.rem(i, 2)
        here = (aa == a) & (kk == core)
        src, dst = ux.at[aa, kk], uw.at[a, b, (1 - xh) * 2 + core]

        @pl.when(jnp.logical_not(here))
        def _():
            remote(src, dst, s_up, r_up, (aa * S + b, xh * 2 + kk)).start()

        @pl.when(here)
        def _():
            pltpu.make_async_copy(src, dst, r_up).start()

        return carry

    def q_cols(aa, xx, j):
        col = pl.multiple_of(j * p.d + (aa * p.X + xx) * HEAD_DIM, HEAD_DIM)
        return qkv.at[:, pl.ds(col, HEAD_DIM)]

    def q_over(aa, carry):
        for j in range(3):
            dst = qx.at[aa, :, pl.ds(j * HEAD_DIM, HEAD_DIM)]
            remote(q_cols(aa, 1 - xh, j), dst, s_qx, r_qx, xnb).start()
        return carry

    def q_along(i, carry):
        aa = lax.rem(a + 1 + i, A)
        for j in range(3):
            dst = qw.at[a, b, xh, core, :, pl.ds(j * HEAD_DIM, HEAD_DIM)]

            @pl.when(aa != a)
            def _():
                remote(q_cols(aa, xh, j), dst, s_q, r_q, (aa * S + b, c)).start()

            @pl.when(aa == a)
            def _():
                pltpu.make_async_copy(q_cols(aa, xh, j), dst, r_q).start()

        return carry

    def q_onward(i, carry):
        aa = lax.rem(a + 1 + i, A)
        src, dst = qx.at[aa], qw.at[a, b, 1 - xh, core]

        @pl.when(aa != a)
        def _():
            remote(src, dst, s_q, r_q, (aa * S + b, c)).start()

        @pl.when(aa == a)
        def _():
            pltpu.make_async_copy(src, dst, r_q).start()

        return carry

    def up_cross(k, carry):
        bb = lax.rem(b + k, S)
        remote(uw.at[:, b], uw.at[:, b], s_upb, r_upb, (a * S + bb, c)).start()
        return carry

    def q_cross(k, carry):
        bb = lax.rem(b + k, S)
        part = qw.at[:, b, :, core]
        remote(part, part, s_qb, r_qb, (a * S + bb, c)).start()
        return carry

    def slot_rows(k):
        return pl.ds(pl.multiple_of(k * L, L), L)

    near = far_order(p, a)[::-1]

    def norm_slot(i):
        k = near[i]
        drain(xa.at[k, pl.ds(0, p.X * p.tok)], r_s.at[0, k])
        get = pltpu.make_async_copy(xa.at[k], xs, loc.at[3])
        get.start()
        get.wait()
        mine = lax.div(k, half) == core
        step = 32

        def unit_rows(at):
            rows = xs[pl.ds(at, step), :].astype(F32)
            rows = rows - jnp.mean(rows, axis=1, keepdims=True)
            spread = jnp.mean(rows * rows, axis=1, keepdims=True)
            rows = rows * lax.rsqrt(spread + EPS)
            to = pl.multiple_of(k * L + at, step)
            n2_v[pl.ds(to, step), :] = (rows * vecs[2:3, :] + vecs[3:4, :]).astype(BF)
            return rows

        @pl.when(mine)
        def _():
            def both(at):
                rows = unit_rows(at)
                to = pl.multiple_of(lax.rem(k, half) * L + at, step)
                n1_v[pl.ds(to, step), :] = (rows * vecs[0:1, :] + vecs[1:2, :]).astype(BF)

            tiles(L, both, step)

        @pl.when(jnp.logical_not(mine))
        def _():
            def one(at):
                unit_rows(at)

            tiles(L, one, step)

        pltpu.make_async_copy(n2_v.at[slot_rows(k)], n2.at[slot_rows(k)], puts.at[i]).start()

    def units(i):
        k = near[i]

        def unit_tile(n):
            at = pl.ds(n, TILE)
            w = uw_v[:, :, :, :, at].reshape(p.d, TILE)
            v = dot(n2_v[slot_rows(k), :], w) + ub[:, at]
            phi = 0.5 * (1.0 + lax.erf(v * (1.0 / math.sqrt(2.0))))
            density = jnp.exp(-0.5 * v * v) * (1.0 / math.sqrt(2.0 * math.pi))
            hid_v[slot_rows(k), at] = (v * phi).astype(BF)
            slope_v[slot_rows(k), at] = (phi + v * density).astype(BF)

        tiles(p.ffl, unit_tile)

    d_ctx, d_row = unit_home(p, b, xh, core)
    d_dst = dw.at[pl.ds(pl.multiple_of(d_row, R), R)]
    def small_all():
        def small_send(k, carry):
            other = lax.rem(me + k, p.n)
            dev = (lax.div(other, C), lax.rem(other, C))
            remote(small, sm.at[me], s_sm, r_sm, dev).start()
            return carry

        lax.fori_loop(1, p.n, small_send, 0)

    def down_all():
        for bb in range(S):
            here = (bb == b) & (d_ctx == c)

            @pl.when(jnp.logical_not(here))
            def _():
                remote(down, d_dst, s_d.at[bb], r_d, (a * S + bb, d_ctx)).start()

            @pl.when(here)
            def _():
                pltpu.make_async_copy(down, d_dst, r_d).start()

    def out_send():
        @pl.when(jnp.logical_not(o_here))
        def _():
            remote(outw, o_rows(row_part, core), s_o, r_o.at[row_part], (o_dp, o_ctx)).start()

        @pl.when(o_here)
        def _():
            pltpu.make_async_copy(outw, o_rows(row_part, core), r_o.at[row_part]).start()

    def chunk(which, jj):
        size = vectors[which].shape[1]
        if size % LANES == 0:
            count = 1
        elif LANES % size == 0:
            count = LANES // size
        else:
            count = (LANES - 1) // size + 2
        total = jnp.zeros((1, LANES), F32)
        for o in range(count):
            i = lax.div(LANES * jj, size) + o
            row = jj - lax.div(i * size, LANES)
            good = ((row >= 0) & (row <= 1) & (i < p.n)).astype(F32)
            at = 2 * which + jnp.clip(row, 0, 1)
            total = total + good * sm_v[jnp.minimum(i, p.n - 1), pl.ds(at, 1), :]
        return total

    def vectors_whole():
        own_small.wait()
        drain(sm.at[pl.ds(0, p.n - 1)], r_sm)
        get_small = pltpu.make_async_copy(sm, sm_v, loc.at[0])
        get_small.start()
        get_small.wait()

        def fill(jj, carry):
            for k in range(5):
                vecs[k : k + 1, pl.ds(pl.multiple_of(jj * LANES, LANES), LANES)] = chunk(2 + k, jj)
            return carry

        lax.fori_loop(0, p.d // LANES, fill, 0)
        for j in range(p.ffl // LANES):
            run, rest = j * LANES // p.W, (j * LANES % p.W) // LANES
            first = lax.div(unit_run(p, a, c, run), LANES) + rest
            ub[:, j * LANES : (j + 1) * LANES] = chunk(1, first)
        for j in range(3):
            for k in range(HEAD_DIM // LANES):
                first = (j * p.d + head * HEAD_DIM) // LANES + k
                at = j * HEAD_DIM + k * LANES
                qb[:, at : at + LANES] = chunk(0, first)

    def out_onward():
        for k in range(p.m):
            drain(o_rows(k, core), r_o.at[k])

            @pl.when(o_first(k))
            def _():
                def o_cross(kk, carry):
                    bb = lax.rem(b + kk, S)
                    rows = o_rows(k, core)
                    remote(rows, rows, s_ob.at[k], r_o.at[k], (a * S + bb, c)).start()
                    return carry

                lax.fori_loop(1, S, o_cross, 0)

            remote(o_rows(k, core), o_rows(k, core), s_oc.at[k], r_oc.at[k], sib).start()

    def load_uw():
        for _ in range(S - 1):
            drain(uw.at[:, b], r_upb)
        get = pltpu.make_async_copy(uw, uw_v, loc.at[3])
        get.start()
        get.wait()

    def send_half_qw():
        for _ in range(S - 1):
            drain(qw.at[:, b, :, core], r_qb)
        part = qw.at[:, :, :, core]
        remote(part, part, s_qc, r_qc, sib).start()

    def load_qw():
        drain(qw.at[:, :, :, 1 - core], r_qc)
        get = pltpu.make_async_copy(qw, qw_v, loc.at[3])
        get.start()
        get.wait()

    def attend(i):
        own = pl.ds(pl.multiple_of(i * L, L), L)
        cols = [pl.ds(j * HEAD_DIM, HEAD_DIM) for j in range(3)]
        for j in range(3):
            w = qw_v[:, :, :, :, :, cols[j]].reshape(p.d, HEAD_DIM)
            v = dot(n1_v[own, :], w) + qb[:, cols[j]]
            if j < 2:
                v = turn(v, cos_v[...], sin_v[...])
            joint_v[own, cols[j]] = v.astype(BF)
        rows = L // 2
        for h in range(2):
            at = pl.ds(pl.multiple_of(i * L + h * rows, rows), rows)
            keys = pl.ds(pl.multiple_of(i * L, L), (h + 1) * rows)
            probs = probabilities(joint_v[at, cols[0]], joint_v[keys, cols[1]], h * rows, SCALE)
            heads_v[at, :] = dot(probs.astype(BF), joint_v[keys, cols[2]]).astype(BF)

    send_z(0)
    send_x(0)
    small_all()
    lax.fori_loop(0, 2 * A, up_over, 0)
    angle_tables(cos_v, sin_v)
    z_step(0, 0)
    cross(0, near[0])
    lax.fori_loop(0, 2 * A, up_along, 0)
    z_step(0, 1)
    drain(ux, r_ux)
    lax.fori_loop(0, 2 * A, up_onward, 0)
    down_all()
    cross(0, near[1])
    vectors_whole()
    own_x.wait()
    norm_slot(0)
    lax.fori_loop(0, A, q_over, 0)
    send_x(1)
    out_send()
    norm_slot(1)
    lax.fori_loop(0, A, q_along, 0)
    cross(0, near[2])
    send_z(1)
    norm_slot(2)
    drain(uw.at[:, b], r_up)
    lax.fori_loop(1, S, up_cross, 0)
    drain(qx, r_qx)
    lax.fori_loop(0, A, q_onward, 0)
    z_step(0, 2)
    cross(1, near[0])
    z_step(1, 0)
    out_onward()
    load_uw()
    drain(qw.at[:, b, :, core], r_q)
    lax.fori_loop(1, S, q_cross, 0)
    cross(1, near[1])
    z_step(1, 1)
    units(0)
    cross(0, near[3])
    units(1)
    send_half_qw()
    norm_slot(3)
    put_n1 = pltpu.make_async_copy(n1_v, n1, loc.at[6])
    put_n1.start()
    put_rows = pltpu.make_async_copy(vecs, rows_out, loc.at[7])
    put_rows.start()
    z_step(1, 2)
    units(2)
    load_qw()
    attend(0)
    units(3)
    put_hid = pltpu.make_async_copy(hid_v, hid, loc.at[4])
    put_hid.start()
    put_slope = pltpu.make_async_copy(slope_v, slope, loc.at[5])
    put_slope.start()
    cross(1, near[2])
    attend(1)
    cross(1, near[3])

    put_heads = pltpu.make_async_copy(heads_v, heads, loc.at[0])
    put_heads.start()
    put_joint = pltpu.make_async_copy(joint_v, joint, loc.at[1])
    put_joint.start()

    drain(dw.at[pl.ds(0, p.ffl)], r_d)
    for k in range(p.m):
        drain(dw.at[pl.ds(0, r)], r_oc.at[k])
    for k in range(A):
        drain(ga.at[k, pl.ds(0, p.X * p.tok)], r_s.at[1, k])

    own_g.wait()
    put_hid.wait()
    put_slope.wait()
    put_n1.wait()
    put_rows.wait()
    put_heads.wait()
    put_joint.wait()
    for i in range(A):
        drain(n2_v.at[pl.ds(0, L)], puts.at[i])
    drain(sm.at[pl.ds(0, p.n - 1)], s_sm)
    drain(ux, s_ux)
    drain(qx, s_qx)
    for _ in range(4 * A - 2):
        drain(uw.at[a, b, c], s_up)
    for _ in range(2 * A - 2):
        drain(qw.at[a, b, xh, core], s_q)
    for bb in range(S):

        @pl.when(jnp.logical_not((bb == b) & (d_ctx == c)))
        def _():
            drain(down, s_d.at[bb])

    @pl.when(jnp.logical_not(o_here))
    def _():
        drain(outw, s_o)

    for k in range(p.m):

        @pl.when(o_first(k))
        def _():
            for _ in range(S - 1):
                drain(outw, s_ob.at[k])

    for k in range(p.m):
        drain(dw.at[pl.ds(0, r)], s_oc.at[k])
    for _ in range(S - 1):
        drain(uw.at[:, b], s_upb)
        drain(qw.at[:, b, :, core], s_qb)
    drain(qw.at[:, :, :, core], s_qc)
    for j in range(2):
        for s in range(A - 1):

            @pl.when((a < A - 1) & (a - s >= 0))
            def _():
                drain(x, s_r.at[j, s])

            @pl.when((a > 0) & (a + s <= A - 1))
            def _():
                drain(x, s_l.at[j, s])

        for k in range(A):
            drain(x, s_x.at[j, k])
            drain(xa.at[k, pl.ds(0, p.X * p.tok)], s_s.at[j, k])


def front(p, x, g, qkv, outw, up, down, lens, *vectors):
    dma = pltpu.SemaphoreType.DMA
    A, S, C, r = p.A, p.S, p.C, p.r
    L = C * p.tok
    vm = pltpu.VMEM
    hbm = pl.BlockSpec(memory_space=pl.ANY)
    vmem = pl.BlockSpec(memory_space=pltpu.VMEM)
    half = p.rows // 2
    qw_shape = (A, S, p.X, 2, r, p.hc)
    uw_shape = (A, S, C, r, p.ffl)
    return pl.pallas_call(
        functools.partial(front_kernel, p),
        out_shape=(
            jax.ShapeDtypeStruct((A, L, p.d), BF),
            jax.ShapeDtypeStruct((A, L, p.d), BF),
            jax.ShapeDtypeStruct(qw_shape, BF),
            jax.ShapeDtypeStruct((p.ffl + HEAD_DIM, p.d), BF),
            jax.ShapeDtypeStruct(uw_shape, BF),
            jax.ShapeDtypeStruct((p.n, 16, LANES), F32),
            jax.ShapeDtypeStruct((half, p.d), BF),
            jax.ShapeDtypeStruct((p.rows, p.d), BF),
            jax.ShapeDtypeStruct((p.rows, p.ffl), BF),
            jax.ShapeDtypeStruct((p.rows, p.ffl), BF),
            jax.ShapeDtypeStruct((half, HEAD_DIM), BF),
            jax.ShapeDtypeStruct((half, p.hc), BF),
            jax.ShapeDtypeStruct((8, p.d), F32),
        ),
        in_specs=[vmem] * 6 + [pl.BlockSpec(memory_space=pltpu.SMEM)] + [vmem] * 8,
        out_specs=[hbm] * 13,
        scratch_shapes=[
            vm((16, LANES), F32),
            vm((8, 2 * LANES), F32),
            vm((p.tok, p.d), BF),
            vm((p.n, 16, LANES), F32),
            vm((8, p.d), F32),
            vm((1, p.ffl), F32),
            vm((1, p.hc), F32),
            vm((L, LANES), F32),
            vm((L, LANES), F32),
            vm(uw_shape, BF),
            vm(qw_shape, BF),
            vm((L, p.d), BF),
            vm((half, p.d), BF),
            vm((p.rows, p.d), BF),
            vm((p.rows, p.ffl), BF),
            vm((p.rows, p.ffl), BF),
            vm((half, HEAD_DIM), BF),
            vm((half, p.hc), BF),
            vm((A, 2, r, p.ffl), BF),
            vm((A, r, p.hc), BF),
            dma((8,)),
            dma((A,)),
            dma,
            dma,
            dma,
            dma,
            dma,
            dma,
            dma,
            dma,
            dma,
            dma,
            dma,
            dma,
            dma,
            dma,
            dma,
            dma,
            dma,
            dma((p.m,)),
            dma((p.m,)),
            dma((p.m,)),
            dma((p.m,)),
            dma((S,)),
            dma,
            dma((2, A - 1)),
            dma((2, A - 1)),
            dma((2, A - 1)),
            dma((2, A - 1)),
            dma((2, A)),
            dma((2, A)),
            dma((2, A)),
            dma((2, A)),
        ],
        compiler_params=pltpu.CompilerParams(
            collective_id=0, has_side_effects=True, vmem_limit_bytes=60 * 1024 * 1024
        ),
        name="front",
    )(x, g, qkv, outw, up, down, lens, *vectors)


def back_kernel(
    p,
    hid,
    heads,
    slope,
    g,
    joint,
    n1,
    n2,
    dw,
    uw,
    qw,
    gains,
    o_sum,
    e_sum,
    q_out,
    u_out,
    d_parts,
    o_parts,
    v_all,
    u_z,
    q_z,
    hid_v,
    heads_v,
    dpre,
    g_v,
    joint_v,
    dw_v,
    uw_v,
    qw_v,
    n_v,
    hid_t,
    heads_t,
    dh_v,
    cos_v,
    sin_v,
    own,
    to_sib,
    from_sib,
    from_x,
    came,
    dgrad,
    q_g,
    q_sib,
    q_group,
    o_g,
    o_sib,
    u_parts,
    g_sum,
    vec,
    loc,
    n_sem,
    g_sem,
    s_v,
    r_v,
    s_s,
    r_s,
    s_x,
    r_x,
    s_c,
    r_c,
    s_q,
    r_q,
    s_qb,
    r_qb,
    s_qz,
    r_qz,
    s_qa,
    r_qa,
    s_o,
    r_o,
    s_oa,
    r_oa,
    s_u,
    r_u,
    s_uz,
    r_uz,
    s_ua,
    r_ua,
    s_d,
    r_d,
    free,
):
    A, S, C, X, r, R = p.A, p.S, p.C, p.X, p.r, p.R
    dp, c, a, b, xh, core = place(p)
    me = dp * C + c
    t = a * C + c
    head = a * X + xh
    sib = (dp, xh * 2 + 1 - core)
    xnb = (dp, (1 - xh) * 2 + core)
    far = 1 - xh
    L = C * p.tok
    D, ffl = p.d, p.ffl
    half = A // 2
    ugrad = hid_v
    blk = C * r

    loads = [
        pltpu.make_async_copy(src, dst, loc.at[k])
        for k, (src, dst) in enumerate(
            (
                (hid, hid_v.at[pl.ds(0, p.rows)]),
                (dw, dw_v),
                (heads, heads_v),
                (joint, joint_v),
                (slope, dpre),
                (uw, uw_v),
                (qw, qw_v),
            )
        )
    ]
    for load in loads:
        load.start()
    vec[...] = jnp.zeros_like(vec)
    angle_tables(cos_v, sin_v)
    greet_all(p, me)

    low = a < half
    order = [
        jnp.where(low, A - 1, 0),
        jnp.where(low, A - 2, 1),
        jnp.where(low, 1 - a, A + 1 - a),
        a,
    ]
    inner = (a == 1) | (a == A - 2)

    def slot_rows(k):
        return pl.ds(pl.multiple_of(k * L, L), L)

    def blocks(src, base):
        rows = []
        for cc in (core, 1 - core):
            for side in range(X):
                at = pl.multiple_of(base + (side * 2 + cc) * p.tok, p.tok)
                rows.append(src[pl.ds(at, p.tok), :])
        return jnp.concatenate(rows, axis=0)

    def keep(j, k, n, acc):
        acc = acc.astype(BF)
        for side in range(X):
            own[j, k, side, :, pl.ds(n, TILE)] = acc[side * p.tok : (side + 1) * p.tok]
            to_sib[k, side, :, pl.ds(n, TILE)] = acc[
                (X + side) * p.tok : (X + side + 1) * p.tok
            ]

    def partial(j, i):
        k = order[i]
        mine = lax.div(k, half) == core
        base = pl.multiple_of(lax.rem(k, half) * L, L)
        if j == 0 and i == 0:
            for n in range(3):
                loads[n].wait()
        if j == 1:
            if i == 0:
                loads[5].wait()
                loads[6].wait()
                pl.semaphore_wait(free, 1)
            drain(from_sib.at[k], s_s.at[0, k])
        units = blocks(dpre if j else hid_v, k * L)

        @pl.when(mine)
        def _():
            heads_rows = blocks(joint_v if j else heads_v, base)

            def tile(n):
                at = pl.ds(n, TILE)
                if j == 0:
                    acc = dot(units, dw_v[0:ffl, at]) + dot(heads_rows, dw_v[ffl:, at])
                else:
                    acc = dot_t(units, uw_v[at, :]) * gains[2:3, at]
                    acc += dot_t(heads_rows, qw_v[at, :]) * gains[0:1, at]
                keep(j, k, n, acc)

            tiles(D, tile)

        @pl.when(jnp.logical_not(mine))
        def _():
            def tile(n):
                at = pl.ds(n, TILE)
                if j == 0:
                    acc = dot(units, dw_v[0:ffl, at])
                else:
                    acc = dot_t(units, uw_v[at, :]) * gains[2:3, at]
                keep(j, k, n, acc)

            tiles(D, tile)

        remote(to_sib.at[k], from_sib.at[k], s_s.at[j, k], r_s.at[j, k], sib).start()

    def chip_sum(j, k):
        drain(from_sib.at[k], r_s.at[j, k])
        mine = own.at[j, k, far]
        add_rows(mine, (mine, from_sib.at[k, far]), p.tok)
        remote(mine, from_x.at[j, k], s_x.at[j, k], r_x.at[j, k], xnb).start()
        mine = own.at[j, k, xh]
        add_rows(mine, (mine, from_sib.at[k, xh]), p.tok)

    def hop(j, i, joins):
        k = order[i]
        across = i < 2
        if joins:
            run = inner
        else:
            run = jnp.logical_not(inner) if across else a >= 0

        @pl.when(run)
        def _():
            drain(from_x.at[j, k], r_x.at[j, k])
            mine = own.at[j, k, xh]
            if joins:
                drain(came.at[j, 0], r_c.at[j, lax.rem(k, 2)])
                add_rows(mine, (mine, from_x.at[j, k], came.at[j, lax.rem(k, 2)]), p.tok)
                to, at = k, 2
            else:
                add_rows(mine, (mine, from_x.at[j, k]), p.tok)
                if across:
                    to, at = jnp.where(a == 0, 1, A - 2), lax.rem(k, 2)
                else:
                    to, at = k, 3
            dev = (to * S + b, c)
            remote(mine, came.at[j, at], s_c.at[j, k], r_c.at[j, at], dev).start()

    def last(j, total):
        drain(from_x.at[j, a], r_x.at[j, a])
        drain(came.at[j, 2], r_c.at[j, 2])
        drain(came.at[j, 3], r_c.at[j, 3])
        mine = own.at[j, a, xh]
        add_rows(total, (mine, from_x.at[j, a], came.at[j, 2], came.at[j, 3]), p.tok)

    def unit_grads():
        loads[4].wait()
        for k in range(A):
            rows = slice(k * L, (k + 1) * L)
            for f in range(ffl // TILE):
                at = slice(f * TILE, (f + 1) * TILE)
                hid_t[at, rows] = hid_v[rows, at].astype(F32).T.astype(BF)
        for k in range(half):
            rows = slice(k * L, (k + 1) * L)
            heads_t[:, rows] = heads_v[rows, :].astype(F32).T.astype(BF)

        def g_load(i, slot):
            at = pl.ds(pl.multiple_of(i * TILE, TILE), TILE)
            return pltpu.make_async_copy(g.at[at], g_v.at[slot], g_sem.at[slot])

        g_load(0, 0).start()

        def step(i, carry):
            slot = lax.rem(i, 2)
            g_load(i, slot).wait()

            @pl.when(i + 1 < p.rows // TILE)
            def _():
                g_load(i + 1, 1 - slot).start()

            rows = pl.ds(pl.multiple_of(i * TILE, TILE), TILE)
            for f in range(ffl // TILE):
                at = pl.ds(f * TILE, TILE)
                d_unit = dot_t(g_v[slot], dw_v[f * TILE : (f + 1) * TILE, :])
                dpre[rows, at] = (d_unit * dpre[rows, at].astype(F32)).astype(BF)
            first = core * half * L

            @pl.when((i * TILE >= first) & (i * TILE < first + half * L))
            def _():
                at = pl.ds(pl.multiple_of(i * TILE - first, TILE), TILE)
                dh_v[at, :] = dot_t(g_v[slot], dw_v[ffl:, :]).astype(BF)

            return carry

        lax.fori_loop(0, p.rows // TILE, step, 0)
        loads[3].wait()

    cols = [pl.ds(j * HEAD_DIM, HEAD_DIM) for j in range(3)]
    rows2 = L // 2

    def attend_back(i, carry):
        rows = pl.ds(pl.multiple_of(i * L, L), L)
        dq, dk, dv = [], [], []
        for h in range(2):
            at = pl.ds(pl.multiple_of(i * L + h * rows2, rows2), rows2)
            keys = pl.ds(pl.multiple_of(i * L, L), (h + 1) * rows2)
            q, k, v = joint_v[at, cols[0]], joint_v[keys, cols[1]], joint_v[keys, cols[2]]
            dh = dh_v[at, :]
            probs = probabilities(q, k, h * rows2, SCALE)
            d_probs = dot_t(dh, v)
            delta = jnp.sum(probs * d_probs, axis=1, keepdims=True)
            d_scores = (probs * (d_probs - delta)).astype(BF)
            dq.append(dot(d_scores, k) * SCALE)
            dk.append(t_dot(d_scores, q) * SCALE)
            dv.append(t_dot(probs.astype(BF), dh))
        dq = jnp.concatenate(dq, axis=0)
        dk = jnp.concatenate([dk[0] + dk[1][:rows2], dk[1][rows2:]], axis=0)
        dv = jnp.concatenate([dv[0] + dv[1][:rows2], dv[1][rows2:]], axis=0)
        cos, sin = cos_v[...], sin_v[...]
        for j, d_part in enumerate((turn(dq, cos, -sin), turn(dk, cos, -sin), dv)):
            low = d_part.astype(BF)
            joint_v[rows, cols[j]] = low
            sums = jnp.sum(low.astype(F32), axis=0, keepdims=True)
            for k in range(HEAD_DIM // LANES):
                at = j * (HEAD_DIM // LANES) + k
                vec[at : at + 1, :] += sums[:, k * LANES : (k + 1) * LANES]
        return carry

    def n_load(src, i, slot):
        count = src.shape[0]
        return pltpu.make_async_copy(
            src.at[:, pl.ds(pl.multiple_of(i * TILE, TILE), TILE)],
            n_v.at[slot, pl.ds(0, count)],
            n_sem.at[slot],
        )

    def stream(src, use, low, high):
        n_load(src, low, low % 2).start()

        def step(i, carry):
            slot = lax.rem(i, 2)
            n_load(src, i, slot).wait()

            @pl.when(i + 1 < high)
            def _():
                n_load(src, i + 1, 1 - slot).start()

            use(i, slot)
            return carry

        lax.fori_loop(low, high, step, 0)

    pairs = TILE // (2 * r)

    def q_tile(i, slot):
        for j in range(3):
            acc = t_dot(n_v[slot, 0 : p.rows // 2, :], joint_v[:, cols[j]]).astype(BF)
            for k in range(pairs):
                for kk in range(2):
                    at = (2 * k + kk) * r
                    q_g[i * pairs + k, kk, :, cols[j]] = acc[at : at + r]

    def up_tile(i, slot):
        at = pl.ds(pl.multiple_of(i * TILE, TILE), TILE)
        ugrad[at, :] = t_dot(n_v[slot], dpre[...]).astype(BF)

    def down_tile(i, slot):
        at = pl.ds(pl.multiple_of(i * TILE, TILE), TILE)
        g_sum[:, at] = jnp.sum(n_v[slot].astype(F32), axis=0, keepdims=True)
        for f in range(ffl // TILE):
            rows = slice(f * TILE, (f + 1) * TILE)
            dgrad[rows, at] = dot(hid_t[rows, :], n_v[slot]).astype(BF)
        first = pl.multiple_of(core * half * L, L)
        acc = dot(heads_t[...], n_v[slot, pl.ds(first, half * L), :]).astype(BF)
        for k in range(p.m):
            for kk in range(2):
                to = (2 * k + kk) * r
                o_g[k, kk, :, at] = acc[to : to + r]

    def down_owner(j):
        if p.P == 1:
            return j, c
        return 2 * (j // 2) + core, xh * 2 + j % 2

    def down_send():
        for j in range(S):
            own_b, own_c = down_owner(j)
            src = dgrad.at[pl.ds(j * R, R)]
            here = (own_b == b) & (own_c == c)

            @pl.when(jnp.logical_not(here))
            def _():
                remote(src, d_parts.at[b], s_d.at[j], r_d, (a * S + own_b, own_c)).start()

            @pl.when(here)
            def _():
                pltpu.make_async_copy(src, d_parts.at[b], r_d).start()

        remote(o_g.at[:, 1 - core], o_sib, s_o, r_o, sib).start()

    def u_rows(aa, bb):
        return ugrad.at[pl.ds(pl.multiple_of((aa * S + bb) * blk, blk), blk)]

    def up_send():
        def one(k, carry):
            bb = lax.rem(b + k, S)
            for aa in range(A):
                remote(u_rows(aa, bb), u_parts.at[k - 1, aa], s_u, r_u, (a * S + bb, c)).start()
            return carry

        lax.fori_loop(1, S, one, 0)

    def up_along():
        for k in range(1, S):
            drain(u_parts.at[k - 1], r_u)
        for k in range(1, S):

            def add(aa, carry):
                add_rows(u_rows(aa, b), (u_rows(aa, b), u_parts.at[k - 1, aa]), blk)
                return carry

            lax.fori_loop(0, A, add, 0)
        for k in range(1, A):
            aa = lax.rem(a + k, A)
            remote(u_rows(aa, b), u_z.at[k - 1], s_uz, r_uz, (aa * S + b, c)).start()

    def up_home():
        drain(u_z, r_uz)
        for k in range(A):
            source = lax.rem(a - k + A, A)
            for step in range(C):
                cc = lax.rem(c + 1 + step, C)
                row = pl.multiple_of(cc * r, r)
                for j in range(ffl // p.W):
                    at = pl.ds(j * p.W, p.W)
                    if k == 0:
                        src = ugrad.at[
                            pl.ds(pl.multiple_of((a * S + b) * blk + cc * r, r), r), at
                        ]
                    else:
                        src = u_z.at[k - 1, pl.ds(row, r), at]
                    col = pl.multiple_of(unit_run(p, source, c, j), LANES)
                    dst = u_out.at[:, pl.ds(col, p.W)]
                    if step < C - 1:
                        remote(src, dst, s_ua, r_ua, (dp, cc)).start()
                    else:
                        pltpu.make_async_copy(src, dst, r_ua).start()

    def q_rows(aa, bb):
        return q_g.at[pl.ds((aa * S + bb) * X, X), core]

    def q_cross():
        drain(q_sib, r_q)

        def add(i, carry):
            mine = q_g.at[i, core]
            add_rows(mine, (mine, q_sib.at[i]), r)
            return carry

        lax.fori_loop(0, A * S * X, add, 0)

        def one(k, carry):
            bb = lax.rem(b + k, S)
            for aa in range(A):
                remote(q_rows(aa, bb), q_group.at[k - 1, aa], s_qb, r_qb, (a * S + bb, c)).start()
            return carry

        lax.fori_loop(1, S, one, 0)

    def q_along():
        for k in range(1, S):
            drain(q_group.at[k - 1], r_qb)
        for k in range(1, S):

            def add(i, carry):
                aa, xx = lax.div(i, X), lax.rem(i, X)
                mine = q_g.at[(aa * S + b) * X + xx, core]
                add_rows(mine, (mine, q_group.at[k - 1, aa, xx]), r)
                return carry

            lax.fori_loop(0, A * X, add, 0)
        for k in range(1, A):
            aa = lax.rem(a + k, A)
            remote(q_rows(aa, b), q_z.at[k - 1], s_qz, r_qz, (aa * S + b, c)).start()

    def q_home():
        drain(q_z, r_qz)
        for k in range(A):
            source = lax.rem(a - k + A, A)
            for xx in (far, xh):
                for j in range(3):
                    if k == 0:
                        src = q_g.at[(a * S + b) * X + xx, core, :, cols[j]]
                    else:
                        src = q_z.at[k - 1, xx, :, cols[j]]
                    col = pl.multiple_of(j * D + (source * X + xh) * HEAD_DIM, HEAD_DIM)
                    dst = q_out.at[:, pl.ds(col, HEAD_DIM)]
                    if xx is far:
                        remote(src, dst, s_qa, r_qa, xnb).start()
                    else:
                        pltpu.make_async_copy(src, dst, r_qa).start()

    def out_owner(k):
        return lax.div(head * HEAD_DIM, r) + 2 * k + core

    def out_home():
        drain(o_sib, r_o)
        for k in range(p.m):
            mine = o_g.at[k, core]
            add_rows(mine, (mine, o_sib.at[k]), r)
            od, oc = lax.div(out_owner(k), C), lax.rem(out_owner(k), C)

            @pl.when(out_owner(k) != me)
            def _():
                remote(mine, o_parts.at[b], s_oa.at[k], r_oa, (od, oc)).start()

            @pl.when(out_owner(k) == me)
            def _():
                pltpu.make_async_copy(mine, o_parts.at[b], r_oa).start()

    own_v = pltpu.make_async_copy(vec, v_all.at[me], loc.at[7])

    def sums_send():
        up_row = p.hc // LANES

        def sum_rows(i, carry):
            at = pl.ds(pl.multiple_of(i * 64, 64), 64)
            return carry + jnp.sum(dpre[at, :].astype(F32), axis=0, keepdims=True)

        sums = lax.fori_loop(0, p.rows // 64, sum_rows, jnp.zeros((1, ffl), F32))
        for i in range(ffl // LANES):
            vec[up_row + i : up_row + i + 1, :] = sums[:, i * LANES : (i + 1) * LANES]
        share = D // (A * C)
        g_row = up_row + ffl // LANES
        vec[g_row : g_row + 1, :] = g_sum[:, pl.ds(pl.multiple_of(t * share, share), share)]
        own_v.start()

        def one(k, carry):
            other = lax.rem(me + k, p.n)
            dev = (lax.div(other, C), lax.rem(other, C))
            remote(vec, v_all.at[me], s_v, r_v, dev).start()
            return carry

        lax.fori_loop(1, p.n, one, 0)

    def give_back():
        pl.semaphore_signal(free, inc=1, device_id=sib, device_id_type=MESH)

    partial(0, 0)
    partial(0, 1)
    chip_sum(0, order[0])
    partial(0, 2)
    chip_sum(0, order[1])
    partial(0, 3)
    chip_sum(0, order[2])
    chip_sum(0, order[3])
    give_back()
    unit_grads()
    hop(0, 0, False)
    stream(n2, up_tile, 0, 4)
    hop(0, 1, False)
    stream(n2, up_tile, 4, 8)
    up_send()
    lax.fori_loop(0, half, attend_back, 0)
    partial(1, 0)
    partial(1, 1)
    chip_sum(1, order[0])
    hop(0, 0, True)
    hop(0, 2, False)
    partial(1, 2)
    chip_sum(1, order[1])
    partial(1, 3)
    chip_sum(1, order[2])
    hop(0, 1, True)
    chip_sum(1, order[3])
    up_along()
    stream(n1, q_tile, 0, 4)
    hop(1, 0, False)
    stream(n1, q_tile, 4, 8)
    remote(q_g.at[:, 1 - core], q_sib, s_q, r_q, sib).start()
    q_cross()
    stream(g, down_tile, 0, 4)
    hop(1, 1, False)
    last(0, o_sum)
    stream(g, down_tile, 4, 8)
    down_send()
    hop(1, 2, False)
    hop(1, 0, True)
    q_along()
    out_home()
    sums_send()
    hop(1, 1, True)
    up_home()
    q_home()
    last(1, e_sum)

    drain(u_out, r_ua)
    drain(q_out, r_qa)
    drain(v_all.at[pl.ds(0, p.n - 1)], r_v)
    drain(d_parts, r_d)
    drain(o_parts, r_oa)

    own_v.wait()
    drain(v_all.at[pl.ds(0, p.n - 1)], s_v)
    drain(q_sib, s_q)
    drain(o_sib, s_o)
    for k in range(1, S):
        drain(u_parts.at[0], s_u)
        drain(q_group.at[0], s_qb)
    drain(u_z, s_uz)
    drain(q_z, s_qz)
    for _ in range(A):
        drain(ugrad.at[pl.ds(0, (C - 1) * r)], s_ua)
        drain(q_g.at[0, 0], s_qa)
    for k in range(p.m):

        @pl.when(out_owner(k) != me)
        def _():
            drain(o_g.at[k, 0], s_oa.at[k])

    for j in range(S):
        own_b, own_c = down_owner(j)

        @pl.when(jnp.logical_not((own_b == b) & (own_c == c)))
        def _():
            drain(d_parts.at[0], s_d.at[j])

    for k in range(A):
        drain(from_sib.at[0], s_s.at[1, k])
    for j in range(2):
        for k in range(A):
            drain(from_x.at[0, 0], s_x.at[j, k])

            @pl.when(k != a)
            def _():
                drain(from_x.at[0, 0], s_c.at[j, k])


def back(p, *args):
    dma = pltpu.SemaphoreType.DMA
    A, S, C, X, r, R = p.A, p.S, p.C, p.X, p.r, p.R
    L = C * p.tok
    vm = pltpu.VMEM
    hbm = pl.BlockSpec(memory_space=pl.ANY)
    vmem = pl.BlockSpec(memory_space=pltpu.VMEM)
    groups = max(S - 1, 1)
    return pl.pallas_call(
        functools.partial(back_kernel, p),
        out_shape=(
            jax.ShapeDtypeStruct((p.tok, p.d), F32),
            jax.ShapeDtypeStruct((p.tok, p.d), F32),
            jax.ShapeDtypeStruct((r, 3 * p.d), BF),
            jax.ShapeDtypeStruct((r, p.ff), BF),
            jax.ShapeDtypeStruct((S, R, p.d), BF),
            jax.ShapeDtypeStruct((S, r, p.d), BF),
            jax.ShapeDtypeStruct((p.n, 16, LANES), F32),
            jax.ShapeDtypeStruct((A - 1, C * r, p.ffl), BF),
            jax.ShapeDtypeStruct((A - 1, X, r, p.hc), BF),
        ),
        in_specs=[hbm] * 10 + [vmem],
        out_specs=[vmem] * 2 + [hbm] * 7,
        scratch_shapes=[
            vm((max(p.rows, p.d), p.ffl), BF),
            vm((p.rows // 2, HEAD_DIM), BF),
            vm((p.rows, p.ffl), BF),
            vm((2, TILE, p.d), BF),
            vm((p.rows // 2, p.hc), BF),
            vm((p.ffl + HEAD_DIM, p.d), BF),
            vm((p.d, p.ffl), BF),
            vm((p.d, p.hc), BF),
            vm((2, p.rows, TILE), BF),
            vm((p.ffl, p.rows), BF),
            vm((HEAD_DIM, p.rows // 2), BF),
            vm((p.rows // 2, HEAD_DIM), BF),
            vm((L, LANES), F32),
            vm((L, LANES), F32),
            vm((2, A, X, p.tok, p.d), BF),
            vm((A, X, p.tok, p.d), BF),
            vm((A, X, p.tok, p.d), BF),
            vm((2, A, p.tok, p.d), BF),
            vm((2, 4, p.tok, p.d), BF),
            vm((p.ffl, p.d), BF),
            vm((A * S * X, 2, r, p.hc), BF),
            vm((A * S * X, r, p.hc), BF),
            vm((groups, A, X, r, p.hc), BF),
            vm((p.m, 2, r, p.d), BF),
            vm((p.m, r, p.d), BF),
            vm((groups, A, C * r, p.ffl), BF),
            vm((1, p.d), F32),
            vm((16, LANES), F32),
            dma((8,)),
            dma((2,)),
            dma((2,)),
            dma,
            dma,
            dma((2, A)),
            dma((2, A)),
            dma((2, A)),
            dma((2, A)),
            dma((2, A)),
            dma((2, 4)),
            dma,
            dma,
            dma,
            dma,
            dma,
            dma,
            dma,
            dma,
            dma,
            dma,
            dma((p.m,)),
            dma,
            dma,
            dma,
            dma,
            dma,
            dma,
            dma,
            dma((S,)),
            dma,
            pltpu.SemaphoreType.REGULAR,
        ],
        compiler_params=pltpu.CompilerParams(
            collective_id=1, has_side_effects=True, vmem_limit_bytes=67043328
        ),
        name="back",
    )(*args)


def norm_stats(values):
    center = jnp.mean(values, axis=-1, keepdims=True)
    spread = jnp.mean(jnp.square(values - center), axis=-1, keepdims=True)
    inv_std = lax.rsqrt(spread + EPS)
    return (values - center) * inv_std, inv_std


def local(
    dp_size,
    ctx_size,
    layer_input,
    lengths,
    cotangent,
    qkv_weight,
    qkv_bias,
    out_weight,
    out_bias,
    up_weight,
    up_bias,
    down_weight,
    down_bias,
    first_gain,
    first_bias,
    second_gain,
    second_bias,
):
    tok, d = layer_input.shape
    ff = up_weight.shape[1]
    p = Plan(dp_size, ctx_size, tok, d, ff)
    A, S, C, X, r, R = p.A, p.S, p.C, p.X, p.r, p.R
    dp, c, a, b, xh, core = place(p)
    me = dp * C + c
    t = a * C + c
    valid = (c * tok + jnp.arange(tok, dtype=jnp.int32) < lengths[0])[:, None]
    grad_out = jnp.where(valid, cotangent, jnp.zeros_like(cotangent))
    vectors = (
        qkv_bias,
        out_bias,
        up_bias,
        down_bias,
        first_gain,
        first_bias,
        second_gain,
        second_bias,
    )
    (_, g_all, qw, dw, uw, _, n1, n2, hid, slope, heads, joint, full) = front(
        p,
        layer_input,
        cotangent,
        qkv_weight,
        out_weight,
        up_weight,
        down_weight,
        lengths,
        *(v.reshape(1, -1) for v in vectors),
    )
    o_sum, e_sum, q_out, u_out, d_parts, o_parts, v_all, _, _ = back(
        p,
        hid,
        heads,
        slope,
        g_all.reshape(p.rows, d),
        joint,
        n1,
        n2,
        dw,
        uw.reshape(d, p.ffl),
        qw.reshape(d, p.hc),
        full,
    )
    g_cols = d // (A * C)
    o_out = jnp.sum(o_parts.astype(F32), axis=0)
    d_out = jnp.sum(d_parts.astype(F32), axis=0)

    xf = layer_input.astype(F32)
    output = jnp.where(valid, xf + o_sum + full[4:5], 0.0).astype(BF)
    xhat_o, inv = norm_stats(xf)
    dx = inv * (
        e_sum
        - jnp.mean(e_sum, axis=-1, keepdims=True)
        - xhat_o * jnp.mean(e_sum * xhat_o, axis=-1, keepdims=True)
    )
    input_grad = (grad_out.astype(F32) + dx).astype(BF)

    v_all = v_all.reshape(A, S, C, 2048)
    v_sum = jnp.sum(v_all, axis=1)
    q_bias = v_sum[..., : p.hc].reshape(A, X, 2, 3, HEAD_DIM).sum(axis=2)
    q_bias = q_bias.reshape(HEADS, 3, HEAD_DIM).transpose(1, 0, 2).reshape(-1)
    u_bias = v_sum[..., p.hc : p.hc + p.ffl]
    if p.P == 1:
        u_bias = u_bias.reshape(A, C, S, R).transpose(0, 2, 1, 3).reshape(-1)
    else:
        u_bias = u_bias.reshape(A, X, 2, S // 2, p.W).transpose(0, 3, 2, 1, 4).reshape(-1)
    g_bias = v_sum[..., p.hc + p.ffl : p.hc + p.ffl + g_cols].reshape(-1)

    def own(vector):
        size = vector.shape[0] // p.n
        return lax.dynamic_slice(vector, (me * size,), (size,))

    def norm_grads(weight, grad, bias_grad, gain, shift):
        weight = weight.astype(F32)
        shift_grad = jnp.sum(weight * bias_grad, axis=1)
        gain_grad = (jnp.sum(weight * grad, axis=1) - shift.astype(F32) * shift_grad) / gain.astype(
            F32
        )
        return gain_grad, shift_grad

    q_grad = q_out.astype(F32)
    u_grad = u_out.astype(F32)
    gain1_grad, bias1_grad = norm_grads(qkv_weight, q_grad, q_bias, first_gain, first_bias)
    gain2_grad, bias2_grad = norm_grads(up_weight, u_grad, u_bias, second_gain, second_bias)
    g_own = own(g_bias)
    return (
        output,
        input_grad,
        q_grad,
        own(q_bias),
        o_out,
        g_own,
        u_grad,
        own(u_bias),
        d_out,
        g_own,
        gain1_grad,
        bias1_grad,
        gain2_grad,
        bias2_grad,
    )


def solution(mesh):
    rows = P(("dp", "ctx"), None)
    vector = P(("dp", "ctx"))
    return jax.shard_map(
        functools.partial(local, mesh.shape["dp"], mesh.shape["ctx"]),
        mesh=mesh,
        in_specs=(
            rows,
            P("dp"),
            rows,
            rows,
            vector,
            rows,
            vector,
            rows,
            vector,
            rows,
            vector,
            vector,
            vector,
            vector,
            vector,
        ),
        out_specs=(
            rows,
            rows,
            rows,
            vector,
            rows,
            vector,
            rows,
            vector,
            rows,
            vector,
            vector,
            vector,
            vector,
            vector,
        ),
        check_vma=False,
    )
```

```python
import functools
import math

import jax
import jax.numpy as jnp
from jax import lax
from jax.experimental import pallas as pl
from jax.experimental.pallas import tpu as pltpu
from jax.sharding import PartitionSpec as P

HEADS = 8
HEAD_DIM = 256
ROT = 64
EPS = 1e-05
SCALE = 1.0 / math.sqrt(HEAD_DIM)
MESH = pl.DeviceIdType.MESH
BF = jnp.bfloat16
F32 = jnp.float32
TILE = 256
LANES = 128


class Plan:
    def __init__(self, dp, ctx, tok, d, ff):
        self.C = ctx
        self.X = ctx // 2
        self.A = HEADS // self.X
        self.S = dp // self.A
        self.n = dp * ctx
        self.tok = tok
        self.d = d
        self.ff = ff
        self.r = d // self.n
        self.R = ff // self.n
        self.ffl = self.S * self.R
        self.W = max(self.R, 128)
        self.P = self.W // self.R
        self.hc = 3 * HEAD_DIM
        self.m = HEAD_DIM // self.r // 2
        self.rows = self.A * self.C * tok


def remote(src, dst, send, recv, dev):
    return pltpu.make_async_remote_copy(
        src_ref=src, dst_ref=dst, send_sem=send, recv_sem=recv, device_id=dev, device_id_type=MESH
    )


def drain(ref, sem):
    pltpu.make_async_copy(ref, ref, sem).wait()


def unit_run(p, aa, cc, j):
    if p.P == 1:
        return p.R * ((aa * p.S + j) * p.C + cc)
    return p.R * ((aa * p.S + 2 * j + lax.rem(cc, 2)) * p.C + lax.div(cc, 2) * 2)


def unit_home(p, b, xh, core):
    if p.P == 1:
        return xh * 2 + core, b * p.R
    return xh * 2 + lax.rem(b, 2), (lax.div(b, 2) * 2 + core) * p.R


def place(p):
    dp = lax.axis_index("dp")
    c = lax.axis_index("ctx")
    a = lax.div(dp, p.S)
    b = lax.rem(dp, p.S)
    xh = lax.div(c, 2)
    core = lax.rem(c, 2)
    return dp, c, a, b, xh, core


def greet_all(p, me):
    barrier = pltpu.get_barrier_semaphore()

    def greet(k, carry):
        other = lax.rem(me + k, p.n)
        pl.semaphore_signal(
            barrier,
            inc=1,
            device_id=(lax.div(other, p.C), lax.rem(other, p.C)),
            device_id_type=MESH,
        )
        return carry

    lax.fori_loop(1, p.n, greet, 0)
    pl.semaphore_wait(barrier, p.n - 1)


def dot(x, y):
    return jnp.dot(x, y, preferred_element_type=F32)


def dot_t(x, y):
    return lax.dot_general(x, y, (((1,), (1,)), ((), ())), preferred_element_type=F32)


def t_dot(x, y):
    return lax.dot_general(x, y, (((0,), (0,)), ((), ())), preferred_element_type=F32)


def tiles(count, body, size=TILE):
    def run(i, carry):
        body(pl.multiple_of(i * size, size))
        return carry

    lax.fori_loop(0, count // size, run, 0)


def pick(values, i):
    out = values[0]
    for k in range(1, len(values)):
        out = jnp.where(i == k, values[k], out)
    return out


def far_order(p, a):
    order = []
    lo, hi = 0, p.A - 1
    for _ in range(p.A):
        up_far = hi - a >= a - lo
        order.append(jnp.where(up_far, hi, lo))
        lo = jnp.where(up_far, lo, lo + 1)
        hi = jnp.where(up_far, hi - 1, hi)
    return order


def add_rows(dst, parts, rows):
    step = 16

    def body(k, carry):
        at = pl.ds(pl.multiple_of(k * step, step), step)
        total = parts[0][at, :].astype(F32)
        for part in parts[1:]:
            total = total + part[at, :].astype(F32)
        dst[at, :] = total.astype(dst.dtype)
        return carry

    lax.fori_loop(0, rows // step, body, 0)


def angle_tables(cos_v, sin_v):
    rows = cos_v.shape[0]
    half = ROT // 2

    def body(at):
        shape = (64, LANES)
        lane = lax.broadcasted_iota(jnp.int32, shape, 1)
        pos = (lax.broadcasted_iota(jnp.int32, shape, 0) + at).astype(F32)
        exponent = lax.rem(lane, half).astype(F32) * (-2.0 * math.log(10000.0) / ROT)
        angle = pos * jnp.exp(exponent)
        turned = lane < ROT
        sign = jnp.where(lane < half, -1.0, 1.0)
        cos_v[pl.ds(at, 64), :] = jnp.where(turned, jnp.cos(angle), 1.0)
        sin_v[pl.ds(at, 64), :] = jnp.where(turned, jnp.sin(angle) * sign, 0.0)

    tiles(rows, body, 64)


def turn(v, cos, sin):
    first = v[:, :LANES]
    half = ROT // 2
    lane = lax.broadcasted_iota(jnp.int32, first.shape, 1)
    partner = jnp.where(
        lane < half, pltpu.roll(first, LANES - half, 1), pltpu.roll(first, half, 1)
    )
    return jnp.concatenate([first * cos + partner * sin, v[:, LANES:]], axis=1)


def probabilities(q, k, row0, scale):
    scores = dot_t(q, k) * scale
    row = lax.broadcasted_iota(jnp.int32, scores.shape, 0) + row0
    col = lax.broadcasted_iota(jnp.int32, scores.shape, 1)
    scores = jnp.where(col <= row, scores, -1e30)
    expo = jnp.exp(scores - jnp.max(scores, axis=1, keepdims=True))
    return expo / jnp.sum(expo, axis=1, keepdims=True)


def front_kernel(
    p,
    x,
    g,
    qkv,
    outw,
    up,
    down,
    lens,
    qkv_b,
    out_b,
    up_b,
    down_b,
    gain1,
    bias1,
    gain2,
    bias2,
    xa,
    ga,
    qw,
    dw,
    uw,
    sm,
    n1,
    n2,
    hid,
    slope,
    heads,
    joint,
    rows_out,
    small,
    pads,
    gm,
    sm_v,
    vecs,
    ub,
    qb,
    cos_v,
    sin_v,
    uw_v,
    qw_v,
    xs,
    n1_v,
    n2_v,
    hid_v,
    slope_v,
    heads_v,
    joint_v,
    ux,
    qx,
    loc,
    puts,
    s_ux,
    r_ux,
    s_qx,
    r_qx,
    s_sm,
    r_sm,
    s_up,
    r_up,
    s_upb,
    r_upb,
    s_q,
    r_q,
    s_qb,
    r_qb,
    s_qc,
    r_qc,
    s_o,
    r_o,
    s_ob,
    s_oc,
    r_oc,
    s_d,
    r_d,
    s_r,
    r_r,
    s_l,
    r_l,
    s_x,
    r_x,
    s_s,
    r_s,
):
    A, S, C, r, R = p.A, p.S, p.C, p.r, p.R
    dp, c, a, b, xh, core = place(p)
    me = dp * C + c
    t = a * C + c
    head = a * p.X + xh
    sib = (dp, xh * 2 + 1 - core)
    xnb = (dp, (1 - xh) * 2 + core)
    right = (dp + S, c)
    left = (dp - S, c)
    L = C * p.tok
    half = A // 2

    length = lens[0]

    def mask(at):
        row = lax.broadcasted_iota(jnp.int32, (32, p.d), 0) + (at + c * p.tok)
        rows = g[pl.ds(at, 32), :].astype(F32)
        gm[pl.ds(at, 32), :] = jnp.where(row < length, rows, 0.0).astype(BF)

    tiles(p.tok, mask, 32)

    pads[...] = jnp.zeros_like(pads)
    vectors = (qkv_b, up_b, gain1, bias1, gain2, bias2, out_b)
    for k, v in enumerate(vectors):
        value = v[...].astype(F32)
        if k == len(vectors) - 1:
            value = value + down_b[...].astype(F32)
        pads[k : k + 1, 0 : v.shape[1]] = value
    for k, v in enumerate(vectors):
        placed = pltpu.roll(pads[k : k + 1, :], lax.rem(v.shape[1] * me, LANES), 1)
        small[2 * k : 2 * k + 1, :] = placed[:, :LANES]
        small[2 * k + 1 : 2 * k + 2, :] = placed[:, LANES:]
    small[2 * len(vectors) :, :] = jnp.zeros((2, LANES), F32)
    greet_all(p, me)

    own_small = pltpu.make_async_copy(small, sm.at[me], loc.at[0])
    own_small.start()
    own_x = pltpu.make_async_copy(x, xa.at[a, pl.ds(pl.multiple_of(c * p.tok, p.tok), p.tok)], loc.at[1])
    own_x.start()
    own_g = pltpu.make_async_copy(gm, ga.at[a, pl.ds(pl.multiple_of(c * p.tok, p.tok), p.tok)], loc.at[2])
    own_g.start()

    row_head = lax.div(me * r, HEAD_DIM)
    row_part = lax.div(lax.rem(me * r, HEAD_DIM), 2 * r)
    o_dp, o_ctx = lax.div(row_head, p.X) * S + b, lax.rem(row_head, p.X) * 2 + core
    o_here = (o_dp == dp) & (o_ctx == c)

    def o_rows(k, cc):
        return dw.at[pl.ds(pl.multiple_of(p.ffl + (2 * k + cc) * r, r), r)]

    def o_first(k):
        owner = lax.div(head * HEAD_DIM, r) + 2 * k + core
        return lax.rem(lax.div(owner, C), S) == b

    streams = ((x, xa), (gm, ga))

    def blk(j, k, cc):
        return streams[j][1].at[k, pl.ds(pl.multiple_of(cc * p.tok, p.tok), p.tok)]

    def send_z(j):
        own, slot = streams[j][0], blk(j, a, c)

        @pl.when(a < A - 1)
        def _():
            remote(own, slot, s_r.at[j, 0], r_r.at[j, 0], right).start()

        @pl.when(a > 0)
        def _():
            remote(own, slot, s_l.at[j, 0], r_l.at[j, 0], left).start()

    def send_x(j):
        own, slot = streams[j][0], blk(j, a, c)
        remote(own, slot, s_x.at[j, a], r_x.at[j, a], xnb).start()
        remote(own, slot, s_s.at[j, a], r_s.at[j, a], sib).start()

    last_slot = jnp.where(a < A // 2, A - 1, 0)

    def send_on(j, k, part):
        if j == 0:
            remote(part, part, s_x.at[j, k], r_x.at[j, k], xnb).start()
        else:

            @pl.when(k != last_slot)
            def _():
                remote(part, part, s_x.at[j, k], r_x.at[j, k], xnb).start()

        remote(part, part, s_s.at[j, k], r_s.at[j, k], sib).start()

    def z_step(j, s):
        @pl.when(a - 1 - s >= 0)
        def _():
            k = a - 1 - s
            part = blk(j, k, c)
            drain(part, r_r.at[j, s])

            @pl.when((s + 1 < A - 1) & (a < A - 1))
            def _():
                nxt = jnp.minimum(s + 1, A - 2)
                remote(part, part, s_r.at[j, nxt], r_r.at[j, nxt], right).start()

            send_on(j, k, part)

        @pl.when(a + 1 + s <= A - 1)
        def _():
            k = a + 1 + s
            part = blk(j, k, c)
            drain(part, r_l.at[j, s])

            @pl.when((s + 1 < A - 1) & (a > 0))
            def _():
                nxt = jnp.minimum(s + 1, A - 2)
                remote(part, part, s_l.at[j, nxt], r_l.at[j, nxt], left).start()

            send_on(j, k, part)

    xc = (1 - xh) * 2 + core

    def cross(j, k):
        part = blk(j, k, xc)
        drain(part, r_x.at[j, k])
        remote(part, part, s_s.at[j, k], r_s.at[j, k], sib).start()

    runs = p.ffl // p.W

    def up_cols(aa, cc, j):
        return up.at[:, pl.ds(pl.multiple_of(unit_run(p, aa, cc, j), LANES), p.W)]

    def up_over(i, carry):
        aa, kk = lax.div(i, 2), lax.rem(i, 2)
        for j in range(runs):
            dst = ux.at[aa, kk, :, pl.ds(j * p.W, p.W)]
            remote(up_cols(aa, (1 - xh) * 2 + kk, j), dst, s_ux, r_ux, xnb).start()
        return carry

    def up_along(i, carry):
        aa, kk = lax.rem(a + 1 + lax.div(i, 2), A), lax.rem(i, 2)
        cc = xh * 2 + kk
        here = (aa == a) & (kk == core)
        for j in range(runs):
            dst = uw.at[a, b, c, :, pl.ds(j * p.W, p.W)]

            @pl.when(jnp.logical_not(here))
            def _():
                remote(up_cols(aa, cc, j), dst, s_up, r_up, (aa * S + b, cc)).start()

            @pl.when(here)
            def _():
                pltpu.make_async_copy(up_cols(aa, cc, j), dst, r_up).start()

        return carry

    def up_onward(i, carry):
        aa, kk = lax.rem(a + 1 + lax.div(i, 2), A), lax.rem(i, 2)
        here = (aa == a) & (kk == core)
        src, dst = ux.at[aa, kk], uw.at[a, b, (1 - xh) * 2 + core]

        @pl.when(jnp.logical_not(here))
        def _():
            remote(src, dst, s_up, r_up, (aa * S + b, xh * 2 + kk)).start()

        @pl.when(here)
        def _():
            pltpu.make_async_copy(src, dst, r_up).start()

        return carry

    def q_cols(aa, xx, j):
        col = pl.multiple_of(j * p.d + (aa * p.X + xx) * HEAD_DIM, HEAD_DIM)
        return qkv.at[:, pl.ds(col, HEAD_DIM)]

    def q_over(aa, carry):
        for j in range(3):
            dst = qx.at[aa, :, pl.ds(j * HEAD_DIM, HEAD_DIM)]
            remote(q_cols(aa, 1 - xh, j), dst, s_qx, r_qx, xnb).start()
        return carry

    def q_along(i, carry):
        aa = lax.rem(a + 1 + i, A)
        for j in range(3):
            dst = qw.at[a, b, xh, core, :, pl.ds(j * HEAD_DIM, HEAD_DIM)]

            @pl.when(aa != a)
            def _():
                remote(q_cols(aa, xh, j), dst, s_q, r_q, (aa * S + b, c)).start()

            @pl.when(aa == a)
            def _():
                pltpu.make_async_copy(q_cols(aa, xh, j), dst, r_q).start()

        return carry

    def q_onward(i, carry):
        aa = lax.rem(a + 1 + i, A)
        src, dst = qx.at[aa], qw.at[a, b, 1 - xh, core]

        @pl.when(aa != a)
        def _():
            remote(src, dst, s_q, r_q, (aa * S + b, c)).start()

        @pl.when(aa == a)
        def _():
            pltpu.make_async_copy(src, dst, r_q).start()

        return carry

    def up_cross(k, carry):
        bb = lax.rem(b + k, S)
        remote(uw.at[:, b], uw.at[:, b], s_upb, r_upb, (a * S + bb, c)).start()
        return carry

    def q_cross(k, carry):
        bb = lax.rem(b + k, S)
        part = qw.at[:, b, :, core]
        remote(part, part, s_qb, r_qb, (a * S + bb, c)).start()
        return carry

    def slot_rows(k):
        return pl.ds(pl.multiple_of(k * L, L), L)

    near = far_order(p, a)[::-1]

    def norm_slot(i):
        k = near[i]
        drain(xa.at[k, pl.ds(0, p.X * p.tok)], r_s.at[0, k])
        get = pltpu.make_async_copy(xa.at[k], xs, loc.at[3])
        get.start()
        get.wait()
        mine = lax.div(k, half) == core
        step = 32

        def unit_rows(at):
            rows = xs[pl.ds(at, step), :].astype(F32)
            rows = rows - jnp.mean(rows, axis=1, keepdims=True)
            spread = jnp.mean(rows * rows, axis=1, keepdims=True)
            rows = rows * lax.rsqrt(spread + EPS)
            to = pl.multiple_of(k * L + at, step)
            n2_v[pl.ds(to, step), :] = (rows * vecs[2:3, :] + vecs[3:4, :]).astype(BF)
            return rows

        @pl.when(mine)
        def _():
            def both(at):
                rows = unit_rows(at)
                to = pl.multiple_of(lax.rem(k, half) * L + at, step)
                n1_v[pl.ds(to, step), :] = (rows * vecs[0:1, :] + vecs[1:2, :]).astype(BF)

            tiles(L, both, step)

        @pl.when(jnp.logical_not(mine))
        def _():
            def one(at):
                unit_rows(at)

            tiles(L, one, step)

        pltpu.make_async_copy(n2_v.at[slot_rows(k)], n2.at[slot_rows(k)], puts.at[i]).start()

    def units(i):
        k = near[i]

        def unit_tile(n):
            at = pl.ds(n, TILE)
            w = uw_v[:, :, :, :, at].reshape(p.d, TILE)
            v = dot(n2_v[slot_rows(k), :], w) + ub[:, at]
            phi = 0.5 * (1.0 + lax.erf(v * (1.0 / math.sqrt(2.0))))
            density = jnp.exp(-0.5 * v * v) * (1.0 / math.sqrt(2.0 * math.pi))
            hid_v[slot_rows(k), at] = (v * phi).astype(BF)
            slope_v[slot_rows(k), at] = (phi + v * density).astype(BF)

        tiles(p.ffl, unit_tile)

    d_ctx, d_row = unit_home(p, b, xh, core)
    d_dst = dw.at[pl.ds(pl.multiple_of(d_row, R), R)]
    def small_all():
        def small_send(k, carry):
            other = lax.rem(me + k, p.n)
            dev = (lax.div(other, C), lax.rem(other, C))
            remote(small, sm.at[me], s_sm, r_sm, dev).start()
            return carry

        lax.fori_loop(1, p.n, small_send, 0)

    def down_all():
        for bb in range(S):
            here = (bb == b) & (d_ctx == c)

            @pl.when(jnp.logical_not(here))
            def _():
                remote(down, d_dst, s_d.at[bb], r_d, (a * S + bb, d_ctx)).start()

            @pl.when(here)
            def _():
                pltpu.make_async_copy(down, d_dst, r_d).start()

    def out_send():
        @pl.when(jnp.logical_not(o_here))
        def _():
            remote(outw, o_rows(row_part, core), s_o, r_o.at[row_part], (o_dp, o_ctx)).start()

        @pl.when(o_here)
        def _():
            pltpu.make_async_copy(outw, o_rows(row_part, core), r_o.at[row_part]).start()

    def chunk(which, jj):
        size = vectors[which].shape[1]
        if size % LANES == 0:
            count = 1
        elif LANES % size == 0:
            count = LANES // size
        else:
            count = (LANES - 1) // size + 2
        total = jnp.zeros((1, LANES), F32)
        for o in range(count):
            i = lax.div(LANES * jj, size) + o
            row = jj - lax.div(i * size, LANES)
            good = ((row >= 0) & (row <= 1) & (i < p.n)).astype(F32)
            at = 2 * which + jnp.clip(row, 0, 1)
            total = total + good * sm_v[jnp.minimum(i, p.n - 1), pl.ds(at, 1), :]
        return total

    def vectors_whole():
        own_small.wait()
        drain(sm.at[pl.ds(0, p.n - 1)], r_sm)
        get_small = pltpu.make_async_copy(sm, sm_v, loc.at[0])
        get_small.start()
        get_small.wait()

        def fill(jj, carry):
            for k in range(5):
                vecs[k : k + 1, pl.ds(pl.multiple_of(jj * LANES, LANES), LANES)] = chunk(2 + k, jj)
            return carry

        lax.fori_loop(0, p.d // LANES, fill, 0)
        for j in range(p.ffl // LANES):
            run, rest = j * LANES // p.W, (j * LANES % p.W) // LANES
            first = lax.div(unit_run(p, a, c, run), LANES) + rest
            ub[:, j * LANES : (j + 1) * LANES] = chunk(1, first)
        for j in range(3):
            for k in range(HEAD_DIM // LANES):
                first = (j * p.d + head * HEAD_DIM) // LANES + k
                at = j * HEAD_DIM + k * LANES
                qb[:, at : at + LANES] = chunk(0, first)

    def out_onward(k):
        remote(o_rows(k, core), o_rows(k, core), s_oc.at[k], r_oc.at[k], sib).start()

    def out_first():
        for k in range(p.m):

            @pl.when(o_first(k))
            def _():
                drain(o_rows(k, core), r_o.at[k])

                def o_cross(kk, carry):
                    bb = lax.rem(b + kk, S)
                    rows = o_rows(k, core)
                    remote(rows, rows, s_ob.at[k], r_o.at[k], (a * S + bb, c)).start()
                    return carry

                lax.fori_loop(1, S, o_cross, 0)
                out_onward(k)

    def out_rest():
        for k in range(p.m):

            @pl.when(jnp.logical_not(o_first(k)))
            def _():
                drain(o_rows(k, core), r_o.at[k])
                out_onward(k)

    def load_uw():
        for _ in range(S - 1):
            drain(uw.at[:, b], r_upb)
        get = pltpu.make_async_copy(uw, uw_v, loc.at[3])
        get.start()
        get.wait()

    def send_half_qw():
        for _ in range(S - 1):
            drain(qw.at[:, b, :, core], r_qb)
        part = qw.at[:, :, :, core]
        remote(part, part, s_qc, r_qc, sib).start()

    def load_qw():
        drain(qw.at[:, :, :, 1 - core], r_qc)
        get = pltpu.make_async_copy(qw, qw_v, loc.at[3])
        get.start()
        get.wait()

    def attend(i):
        own = pl.ds(pl.multiple_of(i * L, L), L)
        cols = [pl.ds(j * HEAD_DIM, HEAD_DIM) for j in range(3)]
        for j in range(3):
            w = qw_v[:, :, :, :, :, cols[j]].reshape(p.d, HEAD_DIM)
            v = dot(n1_v[own, :], w) + qb[:, cols[j]]
            if j < 2:
                v = turn(v, cos_v[...], sin_v[...])
            joint_v[own, cols[j]] = v.astype(BF)
        rows = L // 2
        for h in range(2):
            at = pl.ds(pl.multiple_of(i * L + h * rows, rows), rows)
            keys = pl.ds(pl.multiple_of(i * L, L), (h + 1) * rows)
            probs = probabilities(joint_v[at, cols[0]], joint_v[keys, cols[1]], h * rows, SCALE)
            heads_v[at, :] = dot(probs.astype(BF), joint_v[keys, cols[2]]).astype(BF)

    send_z(0)
    send_x(0)
    angle_tables(cos_v, sin_v)
    small_all()
    lax.fori_loop(0, 2 * A, up_over, 0)
    z_step(0, 0)
    cross(0, near[0])
    lax.fori_loop(0, 2 * A, up_along, 0)
    down_all()
    z_step(0, 1)
    drain(ux, r_ux)
    lax.fori_loop(0, 2 * A, up_onward, 0)
    lax.fori_loop(0, A, q_over, 0)
    cross(0, near[1])
    vectors_whole()
    own_x.wait()
    norm_slot(0)
    lax.fori_loop(0, A, q_along, 0)
    send_x(1)
    norm_slot(1)
    drain(qx, r_qx)
    lax.fori_loop(0, A, q_onward, 0)
    out_send()
    cross(0, near[2])
    send_z(1)
    drain(uw.at[:, b], r_up)
    lax.fori_loop(1, S, up_cross, 0)
    drain(qw.at[:, b, :, core], r_q)
    lax.fori_loop(1, S, q_cross, 0)
    norm_slot(2)
    z_step(0, 2)
    cross(1, near[0])
    z_step(1, 0)
    out_first()
    cross(0, near[3])
    norm_slot(3)
    put_n1 = pltpu.make_async_copy(n1_v, n1, loc.at[6])
    put_n1.start()
    put_rows = pltpu.make_async_copy(vecs, rows_out, loc.at[7])
    put_rows.start()
    load_uw()
    send_half_qw()
    units(0)
    z_step(1, 1)
    cross(1, near[1])
    units(1)
    load_qw()
    attend(0)
    units(2)
    z_step(1, 2)
    attend(1)
    cross(1, near[2])
    units(3)
    put_hid = pltpu.make_async_copy(hid_v, hid, loc.at[4])
    put_hid.start()
    put_slope = pltpu.make_async_copy(slope_v, slope, loc.at[5])
    put_slope.start()
    out_rest()

    put_heads = pltpu.make_async_copy(heads_v, heads, loc.at[0])
    put_heads.start()
    put_joint = pltpu.make_async_copy(joint_v, joint, loc.at[1])
    put_joint.start()

    drain(dw.at[pl.ds(0, p.ffl)], r_d)
    for k in range(p.m):
        drain(dw.at[pl.ds(0, r)], r_oc.at[k])
    for k in range(A):

        @pl.when(k != last_slot)
        def _():
            drain(ga.at[k, pl.ds(0, p.X * p.tok)], r_s.at[1, k])

        @pl.when(k == last_slot)
        def _():
            drain(ga.at[k, pl.ds(0, p.tok)], r_s.at[1, k])


    own_g.wait()
    put_hid.wait()
    put_slope.wait()
    put_n1.wait()
    put_rows.wait()
    put_heads.wait()
    put_joint.wait()
    for i in range(A):
        drain(n2_v.at[pl.ds(0, L)], puts.at[i])
    drain(sm.at[pl.ds(0, p.n - 1)], s_sm)
    drain(ux, s_ux)
    drain(qx, s_qx)
    for _ in range(4 * A - 2):
        drain(uw.at[a, b, c], s_up)
    for _ in range(2 * A - 2):
        drain(qw.at[a, b, xh, core], s_q)
    for bb in range(S):

        @pl.when(jnp.logical_not((bb == b) & (d_ctx == c)))
        def _():
            drain(down, s_d.at[bb])

    @pl.when(jnp.logical_not(o_here))
    def _():
        drain(outw, s_o)

    for k in range(p.m):

        @pl.when(o_first(k))
        def _():
            for _ in range(S - 1):
                drain(outw, s_ob.at[k])

    for k in range(p.m):
        drain(dw.at[pl.ds(0, r)], s_oc.at[k])
    for _ in range(S - 1):
        drain(uw.at[:, b], s_upb)
        drain(qw.at[:, b, :, core], s_qb)
    drain(qw.at[:, :, :, core], s_qc)
    for j in range(2):
        for s in range(A - 1):

            @pl.when((a < A - 1) & (a - s >= 0))
            def _():
                drain(x, s_r.at[j, s])

            @pl.when((a > 0) & (a + s <= A - 1))
            def _():
                drain(x, s_l.at[j, s])

        for k in range(A):
            if j == 0:
                drain(x, s_x.at[j, k])
                drain(xa.at[k, pl.ds(0, p.X * p.tok)], s_s.at[j, k])
                continue

            @pl.when(k != last_slot)
            def _():
                drain(x, s_x.at[j, k])
                drain(xa.at[k, pl.ds(0, p.X * p.tok)], s_s.at[j, k])

            @pl.when(k == last_slot)
            def _():
                drain(x, s_s.at[j, k])


def front(p, x, g, qkv, outw, up, down, lens, *vectors):
    dma = pltpu.SemaphoreType.DMA
    A, S, C, r = p.A, p.S, p.C, p.r
    L = C * p.tok
    vm = pltpu.VMEM
    hbm = pl.BlockSpec(memory_space=pl.ANY)
    vmem = pl.BlockSpec(memory_space=pltpu.VMEM)
    half = p.rows // 2
    qw_shape = (A, S, p.X, 2, r, p.hc)
    uw_shape = (A, S, C, r, p.ffl)
    return pl.pallas_call(
        functools.partial(front_kernel, p),
        out_shape=(
            jax.ShapeDtypeStruct((A, L, p.d), BF),
            jax.ShapeDtypeStruct((A, L, p.d), BF),
            jax.ShapeDtypeStruct(qw_shape, BF),
            jax.ShapeDtypeStruct((p.ffl + HEAD_DIM, p.d), BF),
            jax.ShapeDtypeStruct(uw_shape, BF),
            jax.ShapeDtypeStruct((p.n, 16, LANES), F32),
            jax.ShapeDtypeStruct((half, p.d), BF),
            jax.ShapeDtypeStruct((p.rows, p.d), BF),
            jax.ShapeDtypeStruct((p.rows, p.ffl), BF),
            jax.ShapeDtypeStruct((p.rows, p.ffl), BF),
            jax.ShapeDtypeStruct((half, HEAD_DIM), BF),
            jax.ShapeDtypeStruct((half, p.hc), BF),
            jax.ShapeDtypeStruct((8, p.d), F32),
        ),
        in_specs=[vmem] * 6 + [pl.BlockSpec(memory_space=pltpu.SMEM)] + [vmem] * 8,
        out_specs=[hbm] * 13,
        scratch_shapes=[
            vm((16, LANES), F32),
            vm((8, 2 * LANES), F32),
            vm((p.tok, p.d), BF),
            vm((p.n, 16, LANES), F32),
            vm((8, p.d), F32),
            vm((1, p.ffl), F32),
            vm((1, p.hc), F32),
            vm((L, LANES), F32),
            vm((L, LANES), F32),
            vm(uw_shape, BF),
            vm(qw_shape, BF),
            vm((L, p.d), BF),
            vm((half, p.d), BF),
            vm((p.rows, p.d), BF),
            vm((p.rows, p.ffl), BF),
            vm((p.rows, p.ffl), BF),
            vm((half, HEAD_DIM), BF),
            vm((half, p.hc), BF),
            vm((A, 2, r, p.ffl), BF),
            vm((A, r, p.hc), BF),
            dma((8,)),
            dma((A,)),
            dma,
            dma,
            dma,
            dma,
            dma,
            dma,
            dma,
            dma,
            dma,
            dma,
            dma,
            dma,
            dma,
            dma,
            dma,
            dma,
            dma,
            dma((p.m,)),
            dma((p.m,)),
            dma((p.m,)),
            dma((p.m,)),
            dma((S,)),
            dma,
            dma((2, A - 1)),
            dma((2, A - 1)),
            dma((2, A - 1)),
            dma((2, A - 1)),
            dma((2, A)),
            dma((2, A)),
            dma((2, A)),
            dma((2, A)),
        ],
        compiler_params=pltpu.CompilerParams(
            collective_id=0, has_side_effects=True, vmem_limit_bytes=60 * 1024 * 1024
        ),
        name="front",
    )(x, g, qkv, outw, up, down, lens, *vectors)


def back_kernel(
    p,
    hid,
    heads,
    slope,
    g_in,
    joint,
    n1,
    n2,
    dw,
    uw,
    qw,
    gains,
    o_sum,
    e_sum,
    q_out,
    u_out,
    d_parts,
    o_parts,
    v_all,
    u_z,
    q_z,
    g,
    hid_v,
    heads_v,
    dpre,
    g_v,
    joint_v,
    dw_v,
    uw_v,
    qw_v,
    n_v,
    hid_t,
    heads_t,
    dh_v,
    cos_v,
    sin_v,
    own,
    to_sib,
    from_sib,
    from_x,
    came,
    dgrad,
    q_g,
    q_sib,
    q_group,
    o_g,
    o_sib,
    u_parts,
    g_sum,
    vec,
    loc,
    n_sem,
    g_sem,
    s_v,
    r_v,
    s_s,
    r_s,
    s_x,
    r_x,
    s_c,
    r_c,
    s_q,
    r_q,
    s_qb,
    r_qb,
    s_qz,
    r_qz,
    s_qa,
    r_qa,
    s_o,
    r_o,
    s_oa,
    r_oa,
    s_u,
    r_u,
    s_uz,
    r_uz,
    s_ua,
    r_ua,
    s_d,
    r_d,
    s_g,
    r_g,
    free,
):
    A, S, C, X, r, R = p.A, p.S, p.C, p.X, p.r, p.R
    dp, c, a, b, xh, core = place(p)
    me = dp * C + c
    t = a * C + c
    head = a * X + xh
    sib = (dp, xh * 2 + 1 - core)
    xnb = (dp, (1 - xh) * 2 + core)
    far = 1 - xh
    L = C * p.tok
    D, ffl = p.d, p.ffl
    half = A // 2
    ugrad = hid_v
    blk = C * r

    loads = [
        pltpu.make_async_copy(src, dst, loc.at[k])
        for k, (src, dst) in enumerate(
            (
                (hid, hid_v.at[pl.ds(0, p.rows)]),
                (dw, dw_v),
                (heads, heads_v),
                (joint, joint_v),
                (slope, dpre),
                (uw, uw_v),
                (qw, qw_v),
            )
        )
    ]
    for load in loads:
        load.start()
    vec[...] = jnp.zeros_like(vec)
    angle_tables(cos_v, sin_v)
    greet_all(p, me)
    last_slot = jnp.where(a < half, A - 1, 0)

    def g_rows(cc):
        return g.at[pl.ds(pl.multiple_of(last_slot * L + cc * p.tok, p.tok), p.tok)]

    remote(g_rows(c), g_rows(c), s_g.at[0], r_g.at[0], xnb).start()
    x_ctx = far * 2 + core

    def g_forward():
        drain(g_rows(x_ctx), r_g.at[0])
        remote(g_rows(x_ctx), g_rows(x_ctx), s_g.at[1], r_g.at[1], sib).start()

    low = a < half
    order = [
        jnp.where(low, A - 1, 0),
        jnp.where(low, A - 2, 1),
        jnp.where(low, 1 - a, A + 1 - a),
        a,
    ]
    inner = (a == 1) | (a == A - 2)

    def slot_rows(k):
        return pl.ds(pl.multiple_of(k * L, L), L)

    def blocks(src, base):
        rows = []
        for cc in (core, 1 - core):
            for side in range(X):
                at = pl.multiple_of(base + (side * 2 + cc) * p.tok, p.tok)
                rows.append(src[pl.ds(at, p.tok), :])
        return jnp.concatenate(rows, axis=0)

    def keep(j, k, n, acc):
        acc = acc.astype(BF)
        for side in range(X):
            own[j, k, side, :, pl.ds(n, TILE)] = acc[side * p.tok : (side + 1) * p.tok]
            to_sib[k, side, :, pl.ds(n, TILE)] = acc[
                (X + side) * p.tok : (X + side + 1) * p.tok
            ]

    def partial(j, i):
        k = order[i]
        mine = lax.div(k, half) == core
        base = pl.multiple_of(lax.rem(k, half) * L, L)
        if j == 0 and i == 0:
            for n in range(3):
                loads[n].wait()
        if j == 1:
            if i == 0:
                loads[5].wait()
                loads[6].wait()
                pl.semaphore_wait(free, 1)
            drain(from_sib.at[k], s_s.at[0, k])
        units = blocks(dpre if j else hid_v, k * L)

        @pl.when(mine)
        def _():
            heads_rows = blocks(joint_v if j else heads_v, base)

            def tile(n):
                at = pl.ds(n, TILE)
                if j == 0:
                    acc = dot(units, dw_v[0:ffl, at]) + dot(heads_rows, dw_v[ffl:, at])
                else:
                    acc = dot_t(units, uw_v[at, :]) * gains[2:3, at]
                    acc += dot_t(heads_rows, qw_v[at, :]) * gains[0:1, at]
                keep(j, k, n, acc)

            tiles(D, tile)

        @pl.when(jnp.logical_not(mine))
        def _():
            def tile(n):
                at = pl.ds(n, TILE)
                if j == 0:
                    acc = dot(units, dw_v[0:ffl, at])
                else:
                    acc = dot_t(units, uw_v[at, :]) * gains[2:3, at]
                keep(j, k, n, acc)

            tiles(D, tile)

        remote(to_sib.at[k], from_sib.at[k], s_s.at[j, k], r_s.at[j, k], sib).start()

    def chip_sum(j, k):
        drain(from_sib.at[k], r_s.at[j, k])
        mine = own.at[j, k, far]
        add_rows(mine, (mine, from_sib.at[k, far]), p.tok)
        remote(mine, from_x.at[j, k], s_x.at[j, k], r_x.at[j, k], xnb).start()
        mine = own.at[j, k, xh]
        add_rows(mine, (mine, from_sib.at[k, xh]), p.tok)

    def hop(j, i, joins):
        k = order[i]
        across = i < 2
        if joins:
            run = inner
        else:
            run = jnp.logical_not(inner) if across else a >= 0

        @pl.when(run)
        def _():
            drain(from_x.at[j, k], r_x.at[j, k])
            mine = own.at[j, k, xh]
            if joins:
                drain(came.at[j, 0], r_c.at[j, lax.rem(k, 2)])
                add_rows(mine, (mine, from_x.at[j, k], came.at[j, lax.rem(k, 2)]), p.tok)
                to, at = k, 2
            else:
                add_rows(mine, (mine, from_x.at[j, k]), p.tok)
                if across:
                    to, at = jnp.where(a == 0, 1, A - 2), lax.rem(k, 2)
                else:
                    to, at = k, 3
            dev = (to * S + b, c)
            remote(mine, came.at[j, at], s_c.at[j, k], r_c.at[j, at], dev).start()

    def last(j, total):
        drain(from_x.at[j, a], r_x.at[j, a])
        drain(came.at[j, 2], r_c.at[j, 2])
        drain(came.at[j, 3], r_c.at[j, 3])
        mine = own.at[j, a, xh]
        add_rows(total, (mine, from_x.at[j, a], came.at[j, 2], came.at[j, 3]), p.tok)

    def unit_grads():
        loads[4].wait()
        for k in range(A):
            rows = slice(k * L, (k + 1) * L)
            for f in range(ffl // TILE):
                at = slice(f * TILE, (f + 1) * TILE)
                hid_t[at, rows] = hid_v[rows, at].astype(F32).T.astype(BF)
        for k in range(half):
            rows = slice(k * L, (k + 1) * L)
            heads_t[:, rows] = heads_v[rows, :].astype(F32).T.astype(BF)

        def g_load(i, slot):
            at = pl.ds(pl.multiple_of(i * TILE, TILE), TILE)
            return pltpu.make_async_copy(g.at[at], g_v.at[slot], g_sem.at[slot])

        drain(g_rows(far * 2 + 1 - core), r_g.at[1])
        g_load(0, 0).start()

        def step(i, carry):
            slot = lax.rem(i, 2)
            g_load(i, slot).wait()

            @pl.when(i + 1 < p.rows // TILE)
            def _():
                g_load(i + 1, 1 - slot).start()

            rows = pl.ds(pl.multiple_of(i * TILE, TILE), TILE)
            for f in range(ffl // TILE):
                at = pl.ds(f * TILE, TILE)
                d_unit = dot_t(g_v[slot], dw_v[f * TILE : (f + 1) * TILE, :])
                dpre[rows, at] = (d_unit * dpre[rows, at].astype(F32)).astype(BF)
            first = core * half * L

            @pl.when((i * TILE >= first) & (i * TILE < first + half * L))
            def _():
                at = pl.ds(pl.multiple_of(i * TILE - first, TILE), TILE)
                dh_v[at, :] = dot_t(g_v[slot], dw_v[ffl:, :]).astype(BF)

            return carry

        lax.fori_loop(0, p.rows // TILE, step, 0)
        loads[3].wait()

    cols = [pl.ds(j * HEAD_DIM, HEAD_DIM) for j in range(3)]
    rows2 = L // 2

    def attend_back(i, carry):
        rows = pl.ds(pl.multiple_of(i * L, L), L)
        dq, dk, dv = [], [], []
        for h in range(2):
            at = pl.ds(pl.multiple_of(i * L + h * rows2, rows2), rows2)
            keys = pl.ds(pl.multiple_of(i * L, L), (h + 1) * rows2)
            q, k, v = joint_v[at, cols[0]], joint_v[keys, cols[1]], joint_v[keys, cols[2]]
            dh = dh_v[at, :]
            probs = probabilities(q, k, h * rows2, SCALE)
            d_probs = dot_t(dh, v)
            delta = jnp.sum(probs * d_probs, axis=1, keepdims=True)
            d_scores = (probs * (d_probs - delta)).astype(BF)
            dq.append(dot(d_scores, k) * SCALE)
            dk.append(t_dot(d_scores, q) * SCALE)
            dv.append(t_dot(probs.astype(BF), dh))
        dq = jnp.concatenate(dq, axis=0)
        dk = jnp.concatenate([dk[0] + dk[1][:rows2], dk[1][rows2:]], axis=0)
        dv = jnp.concatenate([dv[0] + dv[1][:rows2], dv[1][rows2:]], axis=0)
        cos, sin = cos_v[...], sin_v[...]
        for j, d_part in enumerate((turn(dq, cos, -sin), turn(dk, cos, -sin), dv)):
            low = d_part.astype(BF)
            joint_v[rows, cols[j]] = low
            sums = jnp.sum(low.astype(F32), axis=0, keepdims=True)
            for k in range(HEAD_DIM // LANES):
                at = j * (HEAD_DIM // LANES) + k
                vec[at : at + 1, :] += sums[:, k * LANES : (k + 1) * LANES]
        return carry

    def n_load(src, i, slot):
        count = src.shape[0]
        return pltpu.make_async_copy(
            src.at[:, pl.ds(pl.multiple_of(i * TILE, TILE), TILE)],
            n_v.at[slot, pl.ds(0, count)],
            n_sem.at[slot],
        )

    def stream(src, use, low, high):
        n_load(src, low, low % 2).start()

        def step(i, carry):
            slot = lax.rem(i, 2)
            n_load(src, i, slot).wait()

            @pl.when(i + 1 < high)
            def _():
                n_load(src, i + 1, 1 - slot).start()

            use(i, slot)
            return carry

        lax.fori_loop(low, high, step, 0)

    pairs = TILE // (2 * r)

    def q_tile(i, slot):
        for j in range(3):
            acc = t_dot(n_v[slot, 0 : p.rows // 2, :], joint_v[:, cols[j]]).astype(BF)
            for k in range(pairs):
                for kk in range(2):
                    at = (2 * k + kk) * r
                    q_g[i * pairs + k, kk, :, cols[j]] = acc[at : at + r]

    def up_tile(i, slot):
        at = pl.ds(pl.multiple_of(i * TILE, TILE), TILE)
        ugrad[at, :] = t_dot(n_v[slot], dpre[...]).astype(BF)

    def down_tile(i, slot):
        at = pl.ds(pl.multiple_of(i * TILE, TILE), TILE)
        g_sum[:, at] = jnp.sum(n_v[slot].astype(F32), axis=0, keepdims=True)
        for f in range(ffl // TILE):
            rows = slice(f * TILE, (f + 1) * TILE)
            dgrad[rows, at] = dot(hid_t[rows, :], n_v[slot]).astype(BF)
        first = pl.multiple_of(core * half * L, L)
        acc = dot(heads_t[...], n_v[slot, pl.ds(first, half * L), :]).astype(BF)
        for k in range(p.m):
            for kk in range(2):
                to = (2 * k + kk) * r
                o_g[k, kk, :, at] = acc[to : to + r]

    def down_owner(j):
        if p.P == 1:
            return j, c
        return 2 * (j // 2) + core, xh * 2 + j % 2

    def down_send():
        for j in range(S):
            own_b, own_c = down_owner(j)
            src = dgrad.at[pl.ds(j * R, R)]
            here = (own_b == b) & (own_c == c)

            @pl.when(jnp.logical_not(here))
            def _():
                remote(src, d_parts.at[b], s_d.at[j], r_d, (a * S + own_b, own_c)).start()

            @pl.when(here)
            def _():
                pltpu.make_async_copy(src, d_parts.at[b], r_d).start()

        remote(o_g.at[:, 1 - core], o_sib, s_o, r_o, sib).start()

    def u_rows(aa, bb):
        return ugrad.at[pl.ds(pl.multiple_of((aa * S + bb) * blk, blk), blk)]

    def up_send():
        def one(k, carry):
            bb = lax.rem(b + k, S)
            for aa in range(A):
                remote(u_rows(aa, bb), u_parts.at[k - 1, aa], s_u, r_u, (a * S + bb, c)).start()
            return carry

        lax.fori_loop(1, S, one, 0)

    def up_along():
        for k in range(1, S):
            drain(u_parts.at[k - 1], r_u)
        for k in range(1, S):

            def add(aa, carry):
                add_rows(u_rows(aa, b), (u_rows(aa, b), u_parts.at[k - 1, aa]), blk)
                return carry

            lax.fori_loop(0, A, add, 0)
        for k in range(1, A):
            aa = lax.rem(a + k, A)
            remote(u_rows(aa, b), u_z.at[k - 1], s_uz, r_uz, (aa * S + b, c)).start()

    def up_home():
        drain(u_z, r_uz)
        for k in range(A):
            source = lax.rem(a - k + A, A)
            for step in range(C):
                cc = lax.rem(c + 1 + step, C)
                row = pl.multiple_of(cc * r, r)
                for j in range(ffl // p.W):
                    at = pl.ds(j * p.W, p.W)
                    if k == 0:
                        src = ugrad.at[
                            pl.ds(pl.multiple_of((a * S + b) * blk + cc * r, r), r), at
                        ]
                    else:
                        src = u_z.at[k - 1, pl.ds(row, r), at]
                    col = pl.multiple_of(unit_run(p, source, c, j), LANES)
                    dst = u_out.at[:, pl.ds(col, p.W)]
                    if step < C - 1:
                        remote(src, dst, s_ua, r_ua, (dp, cc)).start()
                    else:
                        pltpu.make_async_copy(src, dst, r_ua).start()

    def q_rows(aa, bb):
        return q_g.at[pl.ds((aa * S + bb) * X, X), core]

    def q_cross():
        drain(q_sib, r_q)

        def add(i, carry):
            mine = q_g.at[i, core]
            add_rows(mine, (mine, q_sib.at[i]), r)
            return carry

        lax.fori_loop(0, A * S * X, add, 0)

        def one(k, carry):
            bb = lax.rem(b + k, S)
            for aa in range(A):
                remote(q_rows(aa, bb), q_group.at[k - 1, aa], s_qb, r_qb, (a * S + bb, c)).start()
            return carry

        lax.fori_loop(1, S, one, 0)

    def q_along():
        for k in range(1, S):
            drain(q_group.at[k - 1], r_qb)
        for k in range(1, S):

            def add(i, carry):
                aa, xx = lax.div(i, X), lax.rem(i, X)
                mine = q_g.at[(aa * S + b) * X + xx, core]
                add_rows(mine, (mine, q_group.at[k - 1, aa, xx]), r)
                return carry

            lax.fori_loop(0, A * X, add, 0)
        for k in range(1, A):
            aa = lax.rem(a + k, A)
            remote(q_rows(aa, b), q_z.at[k - 1], s_qz, r_qz, (aa * S + b, c)).start()

    def q_home():
        drain(q_z, r_qz)
        for k in range(A):
            source = lax.rem(a - k + A, A)
            for xx in (far, xh):
                for j in range(3):
                    if k == 0:
                        src = q_g.at[(a * S + b) * X + xx, core, :, cols[j]]
                    else:
                        src = q_z.at[k - 1, xx, :, cols[j]]
                    col = pl.multiple_of(j * D + (source * X + xh) * HEAD_DIM, HEAD_DIM)
                    dst = q_out.at[:, pl.ds(col, HEAD_DIM)]
                    if xx is far:
                        remote(src, dst, s_qa, r_qa, xnb).start()
                    else:
                        pltpu.make_async_copy(src, dst, r_qa).start()

    def out_owner(k):
        return lax.div(head * HEAD_DIM, r) + 2 * k + core

    def out_home():
        drain(o_sib, r_o)
        for k in range(p.m):
            mine = o_g.at[k, core]
            add_rows(mine, (mine, o_sib.at[k]), r)
            od, oc = lax.div(out_owner(k), C), lax.rem(out_owner(k), C)

            @pl.when(out_owner(k) != me)
            def _():
                remote(mine, o_parts.at[b], s_oa.at[k], r_oa, (od, oc)).start()

            @pl.when(out_owner(k) == me)
            def _():
                pltpu.make_async_copy(mine, o_parts.at[b], r_oa).start()

    own_v = pltpu.make_async_copy(vec, v_all.at[me], loc.at[7])

    def sums_send():
        up_row = p.hc // LANES

        def sum_rows(i, carry):
            at = pl.ds(pl.multiple_of(i * 64, 64), 64)
            return carry + jnp.sum(dpre[at, :].astype(F32), axis=0, keepdims=True)

        sums = lax.fori_loop(0, p.rows // 64, sum_rows, jnp.zeros((1, ffl), F32))
        for i in range(ffl // LANES):
            vec[up_row + i : up_row + i + 1, :] = sums[:, i * LANES : (i + 1) * LANES]
        share = D // (A * C)
        g_row = up_row + ffl // LANES
        vec[g_row : g_row + 1, :] = g_sum[:, pl.ds(pl.multiple_of(t * share, share), share)]
        own_v.start()

        def one(k, carry):
            other = lax.rem(me + k, p.n)
            dev = (lax.div(other, C), lax.rem(other, C))
            remote(vec, v_all.at[me], s_v, r_v, dev).start()
            return carry

        lax.fori_loop(1, p.n, one, 0)

    def give_back():
        pl.semaphore_signal(free, inc=1, device_id=sib, device_id_type=MESH)

    partial(0, 0)
    partial(0, 1)
    chip_sum(0, order[0])
    partial(0, 2)
    chip_sum(0, order[1])
    partial(0, 3)
    g_forward()
    chip_sum(0, order[2])
    chip_sum(0, order[3])
    give_back()
    unit_grads()
    hop(0, 0, False)
    stream(n2, up_tile, 0, 4)
    hop(0, 1, False)
    stream(n2, up_tile, 4, 8)
    up_send()
    lax.fori_loop(0, half, attend_back, 0)
    partial(1, 0)
    partial(1, 1)
    chip_sum(1, order[0])
    hop(0, 0, True)
    hop(0, 2, False)
    partial(1, 2)
    chip_sum(1, order[1])
    partial(1, 3)
    chip_sum(1, order[2])
    hop(0, 1, True)
    chip_sum(1, order[3])
    up_along()
    stream(n1, q_tile, 0, 4)
    hop(1, 0, False)
    stream(n1, q_tile, 4, 8)
    remote(q_g.at[:, 1 - core], q_sib, s_q, r_q, sib).start()
    q_cross()
    stream(g, down_tile, 0, 4)
    hop(1, 1, False)
    stream(g, down_tile, 4, 8)
    down_send()
    hop(1, 2, False)
    hop(1, 0, True)
    q_along()
    out_home()
    sums_send()
    hop(1, 1, True)
    up_home()
    q_home()
    last(0, o_sum)
    last(1, e_sum)

    drain(u_out, r_ua)
    drain(q_out, r_qa)
    drain(v_all.at[pl.ds(0, p.n - 1)], r_v)
    drain(d_parts, r_d)
    drain(o_parts, r_oa)

    own_v.wait()
    for k in range(2):
        drain(g_rows(c), s_g.at[k])
    drain(v_all.at[pl.ds(0, p.n - 1)], s_v)
    drain(q_sib, s_q)
    drain(o_sib, s_o)
    for k in range(1, S):
        drain(u_parts.at[0], s_u)
        drain(q_group.at[0], s_qb)
    drain(u_z, s_uz)
    drain(q_z, s_qz)
    for _ in range(A):
        drain(ugrad.at[pl.ds(0, (C - 1) * r)], s_ua)
        drain(q_g.at[0, 0], s_qa)
    for k in range(p.m):

        @pl.when(out_owner(k) != me)
        def _():
            drain(o_g.at[k, 0], s_oa.at[k])

    for j in range(S):
        own_b, own_c = down_owner(j)

        @pl.when(jnp.logical_not((own_b == b) & (own_c == c)))
        def _():
            drain(d_parts.at[0], s_d.at[j])

    for k in range(A):
        drain(from_sib.at[0], s_s.at[1, k])
    for j in range(2):
        for k in range(A):
            drain(from_x.at[0, 0], s_x.at[j, k])

            @pl.when(k != a)
            def _():
                drain(from_x.at[0, 0], s_c.at[j, k])


def back(p, *args):
    dma = pltpu.SemaphoreType.DMA
    A, S, C, X, r, R = p.A, p.S, p.C, p.X, p.r, p.R
    L = C * p.tok
    vm = pltpu.VMEM
    hbm = pl.BlockSpec(memory_space=pl.ANY)
    vmem = pl.BlockSpec(memory_space=pltpu.VMEM)
    groups = max(S - 1, 1)
    return pl.pallas_call(
        functools.partial(back_kernel, p),
        out_shape=(
            jax.ShapeDtypeStruct((p.tok, p.d), F32),
            jax.ShapeDtypeStruct((p.tok, p.d), F32),
            jax.ShapeDtypeStruct((r, 3 * p.d), BF),
            jax.ShapeDtypeStruct((r, p.ff), BF),
            jax.ShapeDtypeStruct((S, R, p.d), BF),
            jax.ShapeDtypeStruct((S, r, p.d), BF),
            jax.ShapeDtypeStruct((p.n, 16, LANES), F32),
            jax.ShapeDtypeStruct((A - 1, C * r, p.ffl), BF),
            jax.ShapeDtypeStruct((A - 1, X, r, p.hc), BF),
            jax.ShapeDtypeStruct((p.rows, p.d), BF),
        ),
        input_output_aliases={3: 9},
        in_specs=[hbm] * 10 + [vmem],
        out_specs=[vmem] * 2 + [hbm] * 8,
        scratch_shapes=[
            vm((max(p.rows, p.d), p.ffl), BF),
            vm((p.rows // 2, HEAD_DIM), BF),
            vm((p.rows, p.ffl), BF),
            vm((2, TILE, p.d), BF),
            vm((p.rows // 2, p.hc), BF),
            vm((p.ffl + HEAD_DIM, p.d), BF),
            vm((p.d, p.ffl), BF),
            vm((p.d, p.hc), BF),
            vm((2, p.rows, TILE), BF),
            vm((p.ffl, p.rows), BF),
            vm((HEAD_DIM, p.rows // 2), BF),
            vm((p.rows // 2, HEAD_DIM), BF),
            vm((L, LANES), F32),
            vm((L, LANES), F32),
            vm((2, A, X, p.tok, p.d), BF),
            vm((A, X, p.tok, p.d), BF),
            vm((A, X, p.tok, p.d), BF),
            vm((2, A, p.tok, p.d), BF),
            vm((2, 4, p.tok, p.d), BF),
            vm((p.ffl, p.d), BF),
            vm((A * S * X, 2, r, p.hc), BF),
            vm((A * S * X, r, p.hc), BF),
            vm((groups, A, X, r, p.hc), BF),
            vm((p.m, 2, r, p.d), BF),
            vm((p.m, r, p.d), BF),
            vm((groups, A, C * r, p.ffl), BF),
            vm((1, p.d), F32),
            vm((16, LANES), F32),
            dma((8,)),
            dma((2,)),
            dma((2,)),
            dma,
            dma,
            dma((2, A)),
            dma((2, A)),
            dma((2, A)),
            dma((2, A)),
            dma((2, A)),
            dma((2, 4)),
            dma,
            dma,
            dma,
            dma,
            dma,
            dma,
            dma,
            dma,
            dma,
            dma,
            dma((p.m,)),
            dma,
            dma,
            dma,
            dma,
            dma,
            dma,
            dma,
            dma((S,)),
            dma,
            dma((2,)),
            dma((2,)),
            pltpu.SemaphoreType.REGULAR,
        ],
        compiler_params=pltpu.CompilerParams(
            collective_id=1, has_side_effects=True, vmem_limit_bytes=67043328
        ),
        name="back",
    )(*args)


def norm_stats(values):
    center = jnp.mean(values, axis=-1, keepdims=True)
    spread = jnp.mean(jnp.square(values - center), axis=-1, keepdims=True)
    inv_std = lax.rsqrt(spread + EPS)
    return (values - center) * inv_std, inv_std


def local(
    dp_size,
    ctx_size,
    layer_input,
    lengths,
    cotangent,
    qkv_weight,
    qkv_bias,
    out_weight,
    out_bias,
    up_weight,
    up_bias,
    down_weight,
    down_bias,
    first_gain,
    first_bias,
    second_gain,
    second_bias,
):
    tok, d = layer_input.shape
    ff = up_weight.shape[1]
    p = Plan(dp_size, ctx_size, tok, d, ff)
    A, S, C, X, r, R = p.A, p.S, p.C, p.X, p.r, p.R
    dp, c, a, b, xh, core = place(p)
    me = dp * C + c
    t = a * C + c
    valid = (c * tok + jnp.arange(tok, dtype=jnp.int32) < lengths[0])[:, None]
    grad_out = jnp.where(valid, cotangent, jnp.zeros_like(cotangent))
    vectors = (
        qkv_bias,
        out_bias,
        up_bias,
        down_bias,
        first_gain,
        first_bias,
        second_gain,
        second_bias,
    )
    (_, g_all, qw, dw, uw, _, n1, n2, hid, slope, heads, joint, full) = front(
        p,
        layer_input,
        cotangent,
        qkv_weight,
        out_weight,
        up_weight,
        down_weight,
        lengths,
        *(v.reshape(1, -1) for v in vectors),
    )
    o_sum, e_sum, q_out, u_out, d_parts, o_parts, v_all, _, _, _ = back(
        p,
        hid,
        heads,
        slope,
        g_all.reshape(p.rows, d),
        joint,
        n1,
        n2,
        dw,
        uw.reshape(d, p.ffl),
        qw.reshape(d, p.hc),
        full,
    )
    g_cols = d // (A * C)
    o_out = jnp.sum(o_parts.astype(F32), axis=0)
    d_out = jnp.sum(d_parts.astype(F32), axis=0)

    xf = layer_input.astype(F32)
    output = jnp.where(valid, xf + o_sum + full[4:5], 0.0).astype(BF)
    xhat_o, inv = norm_stats(xf)
    dx = inv * (
        e_sum
        - jnp.mean(e_sum, axis=-1, keepdims=True)
        - xhat_o * jnp.mean(e_sum * xhat_o, axis=-1, keepdims=True)
    )
    input_grad = (grad_out.astype(F32) + dx).astype(BF)

    v_all = v_all.reshape(A, S, C, 2048)
    v_sum = jnp.sum(v_all, axis=1)
    q_bias = v_sum[..., : p.hc].reshape(A, X, 2, 3, HEAD_DIM).sum(axis=2)
    q_bias = q_bias.reshape(HEADS, 3, HEAD_DIM).transpose(1, 0, 2).reshape(-1)
    u_bias = v_sum[..., p.hc : p.hc + p.ffl]
    if p.P == 1:
        u_bias = u_bias.reshape(A, C, S, R).transpose(0, 2, 1, 3).reshape(-1)
    else:
        u_bias = u_bias.reshape(A, X, 2, S // 2, p.W).transpose(0, 3, 2, 1, 4).reshape(-1)
    g_bias = v_sum[..., p.hc + p.ffl : p.hc + p.ffl + g_cols].reshape(-1)

    def own(vector):
        size = vector.shape[0] // p.n
        return lax.dynamic_slice(vector, (me * size,), (size,))

    def norm_grads(weight, grad, bias_grad, gain, shift):
        weight = weight.astype(F32)
        shift_grad = jnp.sum(weight * bias_grad, axis=1)
        gain_grad = (jnp.sum(weight * grad, axis=1) - shift.astype(F32) * shift_grad) / gain.astype(
            F32
        )
        return gain_grad, shift_grad

    q_grad = q_out.astype(F32)
    u_grad = u_out.astype(F32)
    gain1_grad, bias1_grad = norm_grads(qkv_weight, q_grad, q_bias, first_gain, first_bias)
    gain2_grad, bias2_grad = norm_grads(up_weight, u_grad, u_bias, second_gain, second_bias)
    g_own = own(g_bias)
    return (
        output,
        input_grad,
        q_grad,
        own(q_bias),
        o_out,
        g_own,
        u_grad,
        own(u_bias),
        d_out,
        g_own,
        gain1_grad,
        bias1_grad,
        gain2_grad,
        bias2_grad,
    )


def solution(mesh):
    rows = P(("dp", "ctx"), None)
    vector = P(("dp", "ctx"))
    return jax.shard_map(
        functools.partial(local, mesh.shape["dp"], mesh.shape["ctx"]),
        mesh=mesh,
        in_specs=(
            rows,
            P("dp"),
            rows,
            rows,
            vector,
            rows,
            vector,
            rows,
            vector,
            rows,
            vector,
            vector,
            vector,
            vector,
            vector,
        ),
        out_specs=(
            rows,
            rows,
            rows,
            vector,
            rows,
            vector,
            rows,
            vector,
            rows,
            vector,
            vector,
            vector,
            vector,
            vector,
        ),
        check_vma=False,
    )
```

```python
import functools
import math

import jax
import jax.numpy as jnp
from jax import lax
from jax.experimental import pallas as pl
from jax.experimental.pallas import tpu as pltpu
from jax.sharding import PartitionSpec as P

HEADS = 8
HEAD_DIM = 256
ROT = 64
EPS = 1e-05
SCALE = 1.0 / math.sqrt(HEAD_DIM)
MESH = pl.DeviceIdType.MESH
BF = jnp.bfloat16
F32 = jnp.float32
TILE = 256
LANES = 128


class Plan:
    def __init__(self, dp, ctx, tok, d, ff):
        self.C = ctx
        self.X = ctx // 2
        self.A = HEADS // self.X
        self.S = dp // self.A
        self.n = dp * ctx
        self.tok = tok
        self.d = d
        self.ff = ff
        self.r = d // self.n
        self.R = ff // self.n
        self.ffl = self.S * self.R
        self.W = max(self.R, 128)
        self.P = self.W // self.R
        self.hc = 3 * HEAD_DIM
        self.m = HEAD_DIM // self.r // 2
        self.rows = self.A * self.C * tok


def remote(src, dst, send, recv, dev):
    return pltpu.make_async_remote_copy(
        src_ref=src, dst_ref=dst, send_sem=send, recv_sem=recv, device_id=dev, device_id_type=MESH
    )


def drain(ref, sem):
    pltpu.make_async_copy(ref, ref, sem).wait()


def unit_run(p, aa, cc, j):
    if p.P == 1:
        return p.R * ((aa * p.S + j) * p.C + cc)
    return p.R * ((aa * p.S + 2 * j + lax.rem(cc, 2)) * p.C + lax.div(cc, 2) * 2)


def unit_home(p, b, xh, core):
    if p.P == 1:
        return xh * 2 + core, b * p.R
    return xh * 2 + lax.rem(b, 2), (lax.div(b, 2) * 2 + core) * p.R


def place(p):
    dp = lax.axis_index("dp")
    c = lax.axis_index("ctx")
    a = lax.div(dp, p.S)
    b = lax.rem(dp, p.S)
    xh = lax.div(c, 2)
    core = lax.rem(c, 2)
    return dp, c, a, b, xh, core


def greet_all(p, me):
    barrier = pltpu.get_barrier_semaphore()

    def greet(k, carry):
        other = lax.rem(me + k, p.n)
        pl.semaphore_signal(
            barrier,
            inc=1,
            device_id=(lax.div(other, p.C), lax.rem(other, p.C)),
            device_id_type=MESH,
        )
        return carry

    lax.fori_loop(1, p.n, greet, 0)
    pl.semaphore_wait(barrier, p.n - 1)


def dot(x, y):
    return jnp.dot(x, y, preferred_element_type=F32)


def dot_t(x, y):
    return lax.dot_general(x, y, (((1,), (1,)), ((), ())), preferred_element_type=F32)


def t_dot(x, y):
    return lax.dot_general(x, y, (((0,), (0,)), ((), ())), preferred_element_type=F32)


def tiles(count, body, size=TILE):
    def run(i, carry):
        body(pl.multiple_of(i * size, size))
        return carry

    lax.fori_loop(0, count // size, run, 0)


def pick(values, i):
    out = values[0]
    for k in range(1, len(values)):
        out = jnp.where(i == k, values[k], out)
    return out


def far_order(p, a):
    order = []
    lo, hi = 0, p.A - 1
    for _ in range(p.A):
        up_far = hi - a >= a - lo
        order.append(jnp.where(up_far, hi, lo))
        lo = jnp.where(up_far, lo, lo + 1)
        hi = jnp.where(up_far, hi - 1, hi)
    return order


def add_rows(dst, parts, rows):
    step = 16

    def body(k, carry):
        at = pl.ds(pl.multiple_of(k * step, step), step)
        total = parts[0][at, :].astype(F32)
        for part in parts[1:]:
            total = total + part[at, :].astype(F32)
        dst[at, :] = total.astype(dst.dtype)
        return carry

    lax.fori_loop(0, rows // step, body, 0)


def angle_tables(cos_v, sin_v):
    rows = cos_v.shape[0]
    half = ROT // 2

    def body(at):
        shape = (64, LANES)
        lane = lax.broadcasted_iota(jnp.int32, shape, 1)
        pos = (lax.broadcasted_iota(jnp.int32, shape, 0) + at).astype(F32)
        exponent = lax.rem(lane, half).astype(F32) * (-2.0 * math.log(10000.0) / ROT)
        angle = pos * jnp.exp(exponent)
        turned = lane < ROT
        sign = jnp.where(lane < half, -1.0, 1.0)
        cos_v[pl.ds(at, 64), :] = jnp.where(turned, jnp.cos(angle), 1.0)
        sin_v[pl.ds(at, 64), :] = jnp.where(turned, jnp.sin(angle) * sign, 0.0)

    tiles(rows, body, 64)


def turn(v, cos, sin):
    first = v[:, :LANES]
    half = ROT // 2
    lane = lax.broadcasted_iota(jnp.int32, first.shape, 1)
    partner = jnp.where(
        lane < half, pltpu.roll(first, LANES - half, 1), pltpu.roll(first, half, 1)
    )
    return jnp.concatenate([first * cos + partner * sin, v[:, LANES:]], axis=1)


def probabilities(q, k, row0, scale):
    scores = dot_t(q, k) * scale
    row = lax.broadcasted_iota(jnp.int32, scores.shape, 0) + row0
    col = lax.broadcasted_iota(jnp.int32, scores.shape, 1)
    scores = jnp.where(col <= row, scores, -1e30)
    expo = jnp.exp(scores - jnp.max(scores, axis=1, keepdims=True))
    return expo / jnp.sum(expo, axis=1, keepdims=True)


def front_kernel(
    p,
    x,
    g,
    qkv,
    outw,
    up,
    down,
    lens,
    qkv_b,
    out_b,
    up_b,
    down_b,
    gain1,
    bias1,
    gain2,
    bias2,
    xa,
    ga,
    qw,
    dw,
    uw,
    sm,
    n1,
    n2,
    hid,
    slope,
    heads,
    joint,
    rows_out,
    small,
    pads,
    gm,
    sm_v,
    vecs,
    ub,
    qb,
    cos_v,
    sin_v,
    uw_v,
    qw_v,
    xs,
    n1_v,
    n2_v,
    hid_v,
    slope_v,
    heads_v,
    joint_v,
    ux,
    qx,
    loc,
    puts,
    s_ux,
    r_ux,
    s_qx,
    r_qx,
    s_sm,
    r_sm,
    s_up,
    r_up,
    s_upb,
    r_upb,
    s_q,
    r_q,
    s_qb,
    r_qb,
    s_qc,
    r_qc,
    s_o,
    r_o,
    s_ob,
    s_oc,
    r_oc,
    s_d,
    r_d,
    s_r,
    r_r,
    s_l,
    r_l,
    s_x,
    r_x,
    s_s,
    r_s,
):
    A, S, C, r, R = p.A, p.S, p.C, p.r, p.R
    dp, c, a, b, xh, core = place(p)
    me = dp * C + c
    t = a * C + c
    head = a * p.X + xh
    sib = (dp, xh * 2 + 1 - core)
    xnb = (dp, (1 - xh) * 2 + core)
    right = (dp + S, c)
    left = (dp - S, c)
    L = C * p.tok
    half = A // 2

    length = lens[0]

    def mask(at):
        row = lax.broadcasted_iota(jnp.int32, (32, p.d), 0) + (at + c * p.tok)
        rows = g[pl.ds(at, 32), :].astype(F32)
        gm[pl.ds(at, 32), :] = jnp.where(row < length, rows, 0.0).astype(BF)

    tiles(p.tok, mask, 32)

    pads[...] = jnp.zeros_like(pads)
    vectors = (qkv_b, up_b, gain1, bias1, gain2, bias2, out_b)
    for k, v in enumerate(vectors):
        value = v[...].astype(F32)
        if k == len(vectors) - 1:
            value = value + down_b[...].astype(F32)
        pads[k, 0 : v.shape[0]] = value
    for k, v in enumerate(vectors):
        placed = pltpu.roll(pads[k : k + 1, :], lax.rem(v.shape[0] * me, LANES), 1)
        small[2 * k : 2 * k + 1, :] = placed[:, :LANES]
        small[2 * k + 1 : 2 * k + 2, :] = placed[:, LANES:]
    small[2 * len(vectors) :, :] = jnp.zeros((2, LANES), F32)
    greet_all(p, me)

    own_small = pltpu.make_async_copy(small, sm.at[me], loc.at[0])
    own_small.start()
    own_x = pltpu.make_async_copy(x, xa.at[a, pl.ds(pl.multiple_of(c * p.tok, p.tok), p.tok)], loc.at[1])
    own_x.start()
    own_g = pltpu.make_async_copy(gm, ga.at[a, pl.ds(pl.multiple_of(c * p.tok, p.tok), p.tok)], loc.at[2])
    own_g.start()

    row_head = lax.div(me * r, HEAD_DIM)
    row_part = lax.div(lax.rem(me * r, HEAD_DIM), 2 * r)
    o_dp, o_ctx = lax.div(row_head, p.X) * S + b, lax.rem(row_head, p.X) * 2 + core
    o_here = (o_dp == dp) & (o_ctx == c)

    def o_rows(k, cc):
        return dw.at[pl.ds(pl.multiple_of(p.ffl + (2 * k + cc) * r, r), r)]

    def o_first(k):
        owner = lax.div(head * HEAD_DIM, r) + 2 * k + core
        return lax.rem(lax.div(owner, C), S) == b

    streams = ((x, xa), (gm, ga))

    def blk(j, k, cc):
        return streams[j][1].at[k, pl.ds(pl.multiple_of(cc * p.tok, p.tok), p.tok)]

    def send_z(j):
        own, slot = streams[j][0], blk(j, a, c)

        @pl.when(a < A - 1)
        def _():
            remote(own, slot, s_r.at[j, 0], r_r.at[j, 0], right).start()

        @pl.when(a > 0)
        def _():
            remote(own, slot, s_l.at[j, 0], r_l.at[j, 0], left).start()

    def send_x(j):
        own, slot = streams[j][0], blk(j, a, c)
        remote(own, slot, s_x.at[j, a], r_x.at[j, a], xnb).start()
        remote(own, slot, s_s.at[j, a], r_s.at[j, a], sib).start()

    last_slot = jnp.where(a < A // 2, A - 1, 0)

    def send_on(j, k, part):
        if j == 0:
            remote(part, part, s_x.at[j, k], r_x.at[j, k], xnb).start()
        else:

            @pl.when(k != last_slot)
            def _():
                remote(part, part, s_x.at[j, k], r_x.at[j, k], xnb).start()

        remote(part, part, s_s.at[j, k], r_s.at[j, k], sib).start()

    def z_step(j, s):
        @pl.when(a - 1 - s >= 0)
        def _():
            k = a - 1 - s
            part = blk(j, k, c)
            drain(part, r_r.at[j, s])

            @pl.when((s + 1 < A - 1) & (a < A - 1))
            def _():
                nxt = jnp.minimum(s + 1, A - 2)
                remote(part, part, s_r.at[j, nxt], r_r.at[j, nxt], right).start()

            send_on(j, k, part)

        @pl.when(a + 1 + s <= A - 1)
        def _():
            k = a + 1 + s
            part = blk(j, k, c)
            drain(part, r_l.at[j, s])

            @pl.when((s + 1 < A - 1) & (a > 0))
            def _():
                nxt = jnp.minimum(s + 1, A - 2)
                remote(part, part, s_l.at[j, nxt], r_l.at[j, nxt], left).start()

            send_on(j, k, part)

    xc = (1 - xh) * 2 + core

    def cross(j, k):
        part = blk(j, k, xc)
        drain(part, r_x.at[j, k])
        remote(part, part, s_s.at[j, k], r_s.at[j, k], sib).start()

    runs = p.ffl // p.W

    def up_cols(aa, cc, j):
        return up.at[:, pl.ds(pl.multiple_of(unit_run(p, aa, cc, j), LANES), p.W)]

    def up_over(i, carry):
        aa, kk = lax.div(i, 2), lax.rem(i, 2)
        for j in range(runs):
            dst = ux.at[aa, kk, :, pl.ds(j * p.W, p.W)]
            remote(up_cols(aa, (1 - xh) * 2 + kk, j), dst, s_ux, r_ux, xnb).start()
        return carry

    def up_along(i, carry):
        aa, kk = lax.rem(a + 1 + lax.div(i, 2), A), lax.rem(i, 2)
        cc = xh * 2 + kk
        here = (aa == a) & (kk == core)
        for j in range(runs):
            dst = uw.at[a, b, c, :, pl.ds(j * p.W, p.W)]

            @pl.when(jnp.logical_not(here))
            def _():
                remote(up_cols(aa, cc, j), dst, s_up, r_up, (aa * S + b, cc)).start()

            @pl.when(here)
            def _():
                pltpu.make_async_copy(up_cols(aa, cc, j), dst, r_up).start()

        return carry

    def up_onward(i, carry):
        aa, kk = lax.rem(a + 1 + lax.div(i, 2), A), lax.rem(i, 2)
        here = (aa == a) & (kk == core)
        src, dst = ux.at[aa, kk], uw.at[a, b, (1 - xh) * 2 + core]

        @pl.when(jnp.logical_not(here))
        def _():
            remote(src, dst, s_up, r_up, (aa * S + b, xh * 2 + kk)).start()

        @pl.when(here)
        def _():
            pltpu.make_async_copy(src, dst, r_up).start()

        return carry

    def q_cols(aa, xx, j):
        col = pl.multiple_of(j * p.d + (aa * p.X + xx) * HEAD_DIM, HEAD_DIM)
        return qkv.at[:, pl.ds(col, HEAD_DIM)]

    def q_over(aa, carry):
        for j in range(3):
            dst = qx.at[aa, :, pl.ds(j * HEAD_DIM, HEAD_DIM)]
            remote(q_cols(aa, 1 - xh, j), dst, s_qx, r_qx, xnb).start()
        return carry

    def q_along(i, carry):
        aa = lax.rem(a + 1 + i, A)
        for j in range(3):
            dst = qw.at[a, b, xh, core, :, pl.ds(j * HEAD_DIM, HEAD_DIM)]

            @pl.when(aa != a)
            def _():
                remote(q_cols(aa, xh, j), dst, s_q, r_q, (aa * S + b, c)).start()

            @pl.when(aa == a)
            def _():
                pltpu.make_async_copy(q_cols(aa, xh, j), dst, r_q).start()

        return carry

    def q_onward(i, carry):
        aa = lax.rem(a + 1 + i, A)
        src, dst = qx.at[aa], qw.at[a, b, 1 - xh, core]

        @pl.when(aa != a)
        def _():
            remote(src, dst, s_q, r_q, (aa * S + b, c)).start()

        @pl.when(aa == a)
        def _():
            pltpu.make_async_copy(src, dst, r_q).start()

        return carry

    def up_cross(k, carry):
        bb = lax.rem(b + k, S)
        remote(uw.at[:, b], uw.at[:, b], s_upb, r_upb, (a * S + bb, c)).start()
        return carry

    def q_cross(k, carry):
        bb = lax.rem(b + k, S)
        part = qw.at[:, b, :, core]
        remote(part, part, s_qb, r_qb, (a * S + bb, c)).start()
        return carry

    def slot_rows(k):
        return pl.ds(pl.multiple_of(k * L, L), L)

    near = far_order(p, a)[::-1]

    def norm_slot(i):
        k = near[i]
        drain(xa.at[k, pl.ds(0, p.X * p.tok)], r_s.at[0, k])
        get = pltpu.make_async_copy(xa.at[k], xs, loc.at[3])
        get.start()
        get.wait()
        mine = lax.div(k, half) == core
        step = 32

        def unit_rows(at):
            rows = xs[pl.ds(at, step), :].astype(F32)
            rows = rows - jnp.mean(rows, axis=1, keepdims=True)
            spread = jnp.mean(rows * rows, axis=1, keepdims=True)
            rows = rows * lax.rsqrt(spread + EPS)
            to = pl.multiple_of(k * L + at, step)
            n2_v[pl.ds(to, step), :] = (rows * vecs[2:3, :] + vecs[3:4, :]).astype(BF)
            return rows

        @pl.when(mine)
        def _():
            def both(at):
                rows = unit_rows(at)
                to = pl.multiple_of(lax.rem(k, half) * L + at, step)
                n1_v[pl.ds(to, step), :] = (rows * vecs[0:1, :] + vecs[1:2, :]).astype(BF)

            tiles(L, both, step)

        @pl.when(jnp.logical_not(mine))
        def _():
            def one(at):
                unit_rows(at)

            tiles(L, one, step)

        pltpu.make_async_copy(n2_v.at[slot_rows(k)], n2.at[slot_rows(k)], puts.at[i]).start()

    def units(i):
        k = near[i]

        def unit_tile(n):
            at = pl.ds(n, TILE)
            w = uw_v[:, :, :, :, at].reshape(p.d, TILE)
            v = dot(n2_v[slot_rows(k), :], w) + ub[:, at]
            phi = 0.5 * (1.0 + lax.erf(v * (1.0 / math.sqrt(2.0))))
            density = jnp.exp(-0.5 * v * v) * (1.0 / math.sqrt(2.0 * math.pi))
            hid_v[slot_rows(k), at] = (v * phi).astype(BF)
            slope_v[slot_rows(k), at] = (phi + v * density).astype(BF)

        tiles(p.ffl, unit_tile)

    d_ctx, d_row = unit_home(p, b, xh, core)
    d_dst = dw.at[pl.ds(pl.multiple_of(d_row, R), R)]
    def small_all():
        def small_send(k, carry):
            other = lax.rem(me + k, p.n)
            dev = (lax.div(other, C), lax.rem(other, C))
            remote(small, sm.at[me], s_sm, r_sm, dev).start()
            return carry

        lax.fori_loop(1, p.n, small_send, 0)

    def down_all():
        for bb in range(S):
            here = (bb == b) & (d_ctx == c)

            @pl.when(jnp.logical_not(here))
            def _():
                remote(down, d_dst, s_d.at[bb], r_d, (a * S + bb, d_ctx)).start()

            @pl.when(here)
            def _():
                pltpu.make_async_copy(down, d_dst, r_d).start()

    def out_send():
        @pl.when(jnp.logical_not(o_here))
        def _():
            remote(outw, o_rows(row_part, core), s_o, r_o.at[row_part], (o_dp, o_ctx)).start()

        @pl.when(o_here)
        def _():
            pltpu.make_async_copy(outw, o_rows(row_part, core), r_o.at[row_part]).start()

    def chunk(which, jj):
        size = vectors[which].shape[0]
        if size % LANES == 0:
            count = 1
        elif LANES % size == 0:
            count = LANES // size
        else:
            count = (LANES - 1) // size + 2
        total = jnp.zeros((1, LANES), F32)
        for o in range(count):
            i = lax.div(LANES * jj, size) + o
            row = jj - lax.div(i * size, LANES)
            good = ((row >= 0) & (row <= 1) & (i < p.n)).astype(F32)
            at = 2 * which + jnp.clip(row, 0, 1)
            total = total + good * sm_v[jnp.minimum(i, p.n - 1), pl.ds(at, 1), :]
        return total

    def vectors_whole():
        own_small.wait()
        drain(sm.at[pl.ds(0, p.n - 1)], r_sm)
        get_small = pltpu.make_async_copy(sm, sm_v, loc.at[0])
        get_small.start()
        get_small.wait()

        def fill(jj, carry):
            for k in range(5):
                vecs[k : k + 1, pl.ds(pl.multiple_of(jj * LANES, LANES), LANES)] = chunk(2 + k, jj)
            return carry

        lax.fori_loop(0, p.d // LANES, fill, 0)
        for j in range(p.ffl // LANES):
            run, rest = j * LANES // p.W, (j * LANES % p.W) // LANES
            first = lax.div(unit_run(p, a, c, run), LANES) + rest
            ub[:, j * LANES : (j + 1) * LANES] = chunk(1, first)
        for j in range(3):
            for k in range(HEAD_DIM // LANES):
                first = (j * p.d + head * HEAD_DIM) // LANES + k
                at = j * HEAD_DIM + k * LANES
                qb[:, at : at + LANES] = chunk(0, first)

    def out_onward(k):
        remote(o_rows(k, core), o_rows(k, core), s_oc.at[k], r_oc.at[k], sib).start()

    def out_first():
        for k in range(p.m):

            @pl.when(o_first(k))
            def _():
                drain(o_rows(k, core), r_o.at[k])

                def o_cross(kk, carry):
                    bb = lax.rem(b + kk, S)
                    rows = o_rows(k, core)
                    remote(rows, rows, s_ob.at[k], r_o.at[k], (a * S + bb, c)).start()
                    return carry

                lax.fori_loop(1, S, o_cross, 0)
                out_onward(k)

    def out_rest():
        for k in range(p.m):

            @pl.when(jnp.logical_not(o_first(k)))
            def _():
                drain(o_rows(k, core), r_o.at[k])
                out_onward(k)

    def load_uw():
        for _ in range(S - 1):
            drain(uw.at[:, b], r_upb)
        get = pltpu.make_async_copy(uw, uw_v, loc.at[3])
        get.start()
        get.wait()

    def send_half_qw():
        for _ in range(S - 1):
            drain(qw.at[:, b, :, core], r_qb)
        part = qw.at[:, :, :, core]
        remote(part, part, s_qc, r_qc, sib).start()

    def load_qw():
        drain(qw.at[:, :, :, 1 - core], r_qc)
        get = pltpu.make_async_copy(qw, qw_v, loc.at[3])
        get.start()
        get.wait()

    def attend(i):
        own = pl.ds(pl.multiple_of(i * L, L), L)
        cols = [pl.ds(j * HEAD_DIM, HEAD_DIM) for j in range(3)]
        for j in range(3):
            w = qw_v[:, :, :, :, :, cols[j]].reshape(p.d, HEAD_DIM)
            v = dot(n1_v[own, :], w) + qb[:, cols[j]]
            if j < 2:
                v = turn(v, cos_v[...], sin_v[...])
            joint_v[own, cols[j]] = v.astype(BF)
        rows = L // 2
        for h in range(2):
            at = pl.ds(pl.multiple_of(i * L + h * rows, rows), rows)
            keys = pl.ds(pl.multiple_of(i * L, L), (h + 1) * rows)
            probs = probabilities(joint_v[at, cols[0]], joint_v[keys, cols[1]], h * rows, SCALE)
            heads_v[at, :] = dot(probs.astype(BF), joint_v[keys, cols[2]]).astype(BF)

    send_z(0)
    send_x(0)
    angle_tables(cos_v, sin_v)
    small_all()
    lax.fori_loop(0, 2 * A, up_over, 0)
    z_step(0, 0)
    cross(0, near[0])
    lax.fori_loop(0, 2 * A, up_along, 0)
    down_all()
    z_step(0, 1)
    drain(ux, r_ux)
    lax.fori_loop(0, 2 * A, up_onward, 0)
    lax.fori_loop(0, A, q_over, 0)
    cross(0, near[1])
    vectors_whole()
    own_x.wait()
    norm_slot(0)
    lax.fori_loop(0, A, q_along, 0)
    send_x(1)
    norm_slot(1)
    drain(qx, r_qx)
    lax.fori_loop(0, A, q_onward, 0)
    out_send()
    cross(0, near[2])
    send_z(1)
    drain(uw.at[:, b], r_up)
    lax.fori_loop(1, S, up_cross, 0)
    drain(qw.at[:, b, :, core], r_q)
    lax.fori_loop(1, S, q_cross, 0)
    norm_slot(2)
    z_step(0, 2)
    cross(1, near[0])
    z_step(1, 0)
    out_first()
    cross(0, near[3])
    norm_slot(3)
    put_n1 = pltpu.make_async_copy(n1_v, n1, loc.at[6])
    put_n1.start()
    put_rows = pltpu.make_async_copy(vecs, rows_out, loc.at[7])
    put_rows.start()
    load_uw()
    send_half_qw()
    units(0)
    z_step(1, 1)
    cross(1, near[1])
    units(1)
    load_qw()
    attend(0)
    units(2)
    z_step(1, 2)
    attend(1)
    cross(1, near[2])
    units(3)
    put_hid = pltpu.make_async_copy(hid_v, hid, loc.at[4])
    put_hid.start()
    put_slope = pltpu.make_async_copy(slope_v, slope, loc.at[5])
    put_slope.start()
    out_rest()

    put_heads = pltpu.make_async_copy(heads_v, heads, loc.at[0])
    put_heads.start()
    put_joint = pltpu.make_async_copy(joint_v, joint, loc.at[1])
    put_joint.start()

    drain(dw.at[pl.ds(0, p.ffl)], r_d)
    for k in range(p.m):
        drain(dw.at[pl.ds(0, r)], r_oc.at[k])
    for k in range(A):

        @pl.when(k != last_slot)
        def _():
            drain(ga.at[k, pl.ds(0, p.X * p.tok)], r_s.at[1, k])

        @pl.when(k == last_slot)
        def _():
            drain(ga.at[k, pl.ds(0, p.tok)], r_s.at[1, k])


    own_g.wait()
    put_hid.wait()
    put_slope.wait()
    put_n1.wait()
    put_rows.wait()
    put_heads.wait()
    put_joint.wait()
    for i in range(A):
        drain(n2_v.at[pl.ds(0, L)], puts.at[i])
    drain(sm.at[pl.ds(0, p.n - 1)], s_sm)
    drain(ux, s_ux)
    drain(qx, s_qx)
    for _ in range(4 * A - 2):
        drain(uw.at[a, b, c], s_up)
    for _ in range(2 * A - 2):
        drain(qw.at[a, b, xh, core], s_q)
    for bb in range(S):

        @pl.when(jnp.logical_not((bb == b) & (d_ctx == c)))
        def _():
            drain(down, s_d.at[bb])

    @pl.when(jnp.logical_not(o_here))
    def _():
        drain(outw, s_o)

    for k in range(p.m):

        @pl.when(o_first(k))
        def _():
            for _ in range(S - 1):
                drain(outw, s_ob.at[k])

    for k in range(p.m):
        drain(dw.at[pl.ds(0, r)], s_oc.at[k])
    for _ in range(S - 1):
        drain(uw.at[:, b], s_upb)
        drain(qw.at[:, b, :, core], s_qb)
    drain(qw.at[:, :, :, core], s_qc)
    for j in range(2):
        for s in range(A - 1):

            @pl.when((a < A - 1) & (a - s >= 0))
            def _():
                drain(x, s_r.at[j, s])

            @pl.when((a > 0) & (a + s <= A - 1))
            def _():
                drain(x, s_l.at[j, s])

        for k in range(A):
            if j == 0:
                drain(x, s_x.at[j, k])
                drain(xa.at[k, pl.ds(0, p.X * p.tok)], s_s.at[j, k])
                continue

            @pl.when(k != last_slot)
            def _():
                drain(x, s_x.at[j, k])
                drain(xa.at[k, pl.ds(0, p.X * p.tok)], s_s.at[j, k])

            @pl.when(k == last_slot)
            def _():
                drain(x, s_s.at[j, k])


def front(p, x, g, qkv, outw, up, down, lens, *vectors):
    dma = pltpu.SemaphoreType.DMA
    A, S, C, r = p.A, p.S, p.C, p.r
    L = C * p.tok
    vm = pltpu.VMEM
    hbm = pl.BlockSpec(memory_space=pl.ANY)
    vmem = pl.BlockSpec(memory_space=pltpu.VMEM)
    half = p.rows // 2
    qw_shape = (A, S, p.X, 2, r, p.hc)
    uw_shape = (A, S, C, r, p.ffl)
    return pl.pallas_call(
        functools.partial(front_kernel, p),
        out_shape=(
            jax.ShapeDtypeStruct((A, L, p.d), BF),
            jax.ShapeDtypeStruct((A, L, p.d), BF),
            jax.ShapeDtypeStruct(qw_shape, BF),
            jax.ShapeDtypeStruct((p.ffl + HEAD_DIM, p.d), BF),
            jax.ShapeDtypeStruct(uw_shape, BF),
            jax.ShapeDtypeStruct((p.n, 16, LANES), F32),
            jax.ShapeDtypeStruct((half, p.d), BF),
            jax.ShapeDtypeStruct((p.rows, p.d), BF),
            jax.ShapeDtypeStruct((p.rows, p.ffl), BF),
            jax.ShapeDtypeStruct((p.rows, p.ffl), BF),
            jax.ShapeDtypeStruct((half, HEAD_DIM), BF),
            jax.ShapeDtypeStruct((half, p.hc), BF),
            jax.ShapeDtypeStruct((8, p.d), F32),
        ),
        in_specs=[vmem] * 6 + [pl.BlockSpec(memory_space=pltpu.SMEM)] + [vmem] * 8,
        out_specs=[hbm] * 13,
        scratch_shapes=[
            vm((16, LANES), F32),
            vm((8, 2 * LANES), F32),
            vm((p.tok, p.d), BF),
            vm((p.n, 16, LANES), F32),
            vm((8, p.d), F32),
            vm((1, p.ffl), F32),
            vm((1, p.hc), F32),
            vm((L, LANES), F32),
            vm((L, LANES), F32),
            vm(uw_shape, BF),
            vm(qw_shape, BF),
            vm((L, p.d), BF),
            vm((half, p.d), BF),
            vm((p.rows, p.d), BF),
            vm((p.rows, p.ffl), BF),
            vm((p.rows, p.ffl), BF),
            vm((half, HEAD_DIM), BF),
            vm((half, p.hc), BF),
            vm((A, 2, r, p.ffl), BF),
            vm((A, r, p.hc), BF),
            dma((8,)),
            dma((A,)),
            dma,
            dma,
            dma,
            dma,
            dma,
            dma,
            dma,
            dma,
            dma,
            dma,
            dma,
            dma,
            dma,
            dma,
            dma,
            dma,
            dma,
            dma((p.m,)),
            dma((p.m,)),
            dma((p.m,)),
            dma((p.m,)),
            dma((S,)),
            dma,
            dma((2, A - 1)),
            dma((2, A - 1)),
            dma((2, A - 1)),
            dma((2, A - 1)),
            dma((2, A)),
            dma((2, A)),
            dma((2, A)),
            dma((2, A)),
        ],
        compiler_params=pltpu.CompilerParams(
            collective_id=0, has_side_effects=True, vmem_limit_bytes=60 * 1024 * 1024
        ),
        name="front",
    )(x, g, qkv, outw, up, down, lens, *vectors)


def back_kernel(
    p,
    hid,
    heads,
    slope,
    g_in,
    joint,
    n1,
    n2,
    dw,
    uw,
    qw,
    gains,
    o_sum,
    e_sum,
    q_out,
    u_out,
    d_parts,
    o_parts,
    v_all,
    u_z,
    q_z,
    g,
    hid_v,
    heads_v,
    dpre,
    g_v,
    joint_v,
    dw_v,
    uw_v,
    qw_v,
    n_v,
    hid_t,
    heads_t,
    dh_v,
    cos_v,
    sin_v,
    own,
    to_sib,
    from_sib,
    from_x,
    came,
    dgrad,
    q_g,
    q_sib,
    q_group,
    o_g,
    o_sib,
    u_parts,
    g_sum,
    vec,
    loc,
    n_sem,
    g_sem,
    s_v,
    r_v,
    s_s,
    r_s,
    s_x,
    r_x,
    s_c,
    r_c,
    s_q,
    r_q,
    s_qb,
    r_qb,
    s_qz,
    r_qz,
    s_qa,
    r_qa,
    s_o,
    r_o,
    s_oa,
    r_oa,
    s_u,
    r_u,
    s_uz,
    r_uz,
    s_ua,
    r_ua,
    s_d,
    r_d,
    s_g,
    r_g,
    free,
):
    A, S, C, X, r, R = p.A, p.S, p.C, p.X, p.r, p.R
    dp, c, a, b, xh, core = place(p)
    me = dp * C + c
    t = a * C + c
    head = a * X + xh
    sib = (dp, xh * 2 + 1 - core)
    xnb = (dp, (1 - xh) * 2 + core)
    far = 1 - xh
    L = C * p.tok
    D, ffl = p.d, p.ffl
    half = A // 2
    ugrad = hid_v
    blk = C * r

    loads = [
        pltpu.make_async_copy(src, dst, loc.at[k])
        for k, (src, dst) in enumerate(
            (
                (hid, hid_v.at[pl.ds(0, p.rows)]),
                (dw, dw_v),
                (heads, heads_v),
                (joint, joint_v),
                (slope, dpre),
                (uw, uw_v),
                (qw, qw_v),
            )
        )
    ]
    for load in loads:
        load.start()
    vec[...] = jnp.zeros_like(vec)
    angle_tables(cos_v, sin_v)
    greet_all(p, me)
    last_slot = jnp.where(a < half, A - 1, 0)

    def g_rows(cc):
        return g.at[pl.ds(pl.multiple_of(last_slot * L + cc * p.tok, p.tok), p.tok)]

    remote(g_rows(c), g_rows(c), s_g.at[0], r_g.at[0], xnb).start()
    x_ctx = far * 2 + core

    def g_forward():
        drain(g_rows(x_ctx), r_g.at[0])
        remote(g_rows(x_ctx), g_rows(x_ctx), s_g.at[1], r_g.at[1], sib).start()

    low = a < half
    order = [
        jnp.where(low, A - 1, 0),
        jnp.where(low, A - 2, 1),
        jnp.where(low, 1 - a, A + 1 - a),
        a,
    ]
    inner = (a == 1) | (a == A - 2)

    def slot_rows(k):
        return pl.ds(pl.multiple_of(k * L, L), L)

    def blocks(src, base):
        rows = []
        for cc in (core, 1 - core):
            for side in range(X):
                at = pl.multiple_of(base + (side * 2 + cc) * p.tok, p.tok)
                rows.append(src[pl.ds(at, p.tok), :])
        return jnp.concatenate(rows, axis=0)

    def keep(j, k, n, acc):
        acc = acc.astype(BF)
        for side in range(X):
            own[j, k, side, :, pl.ds(n, TILE)] = acc[side * p.tok : (side + 1) * p.tok]
            to_sib[k, side, :, pl.ds(n, TILE)] = acc[
                (X + side) * p.tok : (X + side + 1) * p.tok
            ]

    def partial(j, i):
        k = order[i]
        mine = lax.div(k, half) == core
        base = pl.multiple_of(lax.rem(k, half) * L, L)
        if j == 0 and i == 0:
            for n in range(3):
                loads[n].wait()
        if j == 1:
            if i == 0:
                loads[5].wait()
                loads[6].wait()
                pl.semaphore_wait(free, 1)
            drain(from_sib.at[k], s_s.at[0, k])
        units = blocks(dpre if j else hid_v, k * L)

        @pl.when(mine)
        def _():
            heads_rows = blocks(joint_v if j else heads_v, base)

            def tile(n):
                at = pl.ds(n, TILE)
                if j == 0:
                    acc = dot(units, dw_v[0:ffl, at]) + dot(heads_rows, dw_v[ffl:, at])
                else:
                    acc = dot_t(units, uw_v[at, :]) * gains[2:3, at]
                    acc += dot_t(heads_rows, qw_v[at, :]) * gains[0:1, at]
                keep(j, k, n, acc)

            tiles(D, tile)

        @pl.when(jnp.logical_not(mine))
        def _():
            def tile(n):
                at = pl.ds(n, TILE)
                if j == 0:
                    acc = dot(units, dw_v[0:ffl, at])
                else:
                    acc = dot_t(units, uw_v[at, :]) * gains[2:3, at]
                keep(j, k, n, acc)

            tiles(D, tile)

        remote(to_sib.at[k], from_sib.at[k], s_s.at[j, k], r_s.at[j, k], sib).start()

    def chip_sum(j, k):
        drain(from_sib.at[k], r_s.at[j, k])
        mine = own.at[j, k, far]
        add_rows(mine, (mine, from_sib.at[k, far]), p.tok)
        remote(mine, from_x.at[j, k], s_x.at[j, k], r_x.at[j, k], xnb).start()
        mine = own.at[j, k, xh]
        add_rows(mine, (mine, from_sib.at[k, xh]), p.tok)

    def hop(j, i, joins):
        k = order[i]
        across = i < 2
        if joins:
            run = inner
        else:
            run = jnp.logical_not(inner) if across else a >= 0

        @pl.when(run)
        def _():
            drain(from_x.at[j, k], r_x.at[j, k])
            mine = own.at[j, k, xh]
            if joins:
                drain(came.at[j, 0], r_c.at[j, lax.rem(k, 2)])
                add_rows(mine, (mine, from_x.at[j, k], came.at[j, lax.rem(k, 2)]), p.tok)
                to, at = k, 2
            else:
                add_rows(mine, (mine, from_x.at[j, k]), p.tok)
                if across:
                    to, at = jnp.where(a == 0, 1, A - 2), lax.rem(k, 2)
                else:
                    to, at = k, 3
            dev = (to * S + b, c)
            remote(mine, came.at[j, at], s_c.at[j, k], r_c.at[j, at], dev).start()

    def last(j, total):
        drain(from_x.at[j, a], r_x.at[j, a])
        drain(came.at[j, 2], r_c.at[j, 2])
        drain(came.at[j, 3], r_c.at[j, 3])
        mine = own.at[j, a, xh]
        add_rows(total, (mine, from_x.at[j, a], came.at[j, 2], came.at[j, 3]), p.tok)

    def unit_grads():
        loads[4].wait()
        for k in range(A):
            rows = slice(k * L, (k + 1) * L)
            for f in range(ffl // TILE):
                at = slice(f * TILE, (f + 1) * TILE)
                hid_t[at, rows] = hid_v[rows, at].astype(F32).T.astype(BF)
        for k in range(half):
            rows = slice(k * L, (k + 1) * L)
            heads_t[:, rows] = heads_v[rows, :].astype(F32).T.astype(BF)

        def g_load(i, slot):
            at = pl.ds(pl.multiple_of(i * TILE, TILE), TILE)
            return pltpu.make_async_copy(g.at[at], g_v.at[slot], g_sem.at[slot])

        drain(g_rows(far * 2 + 1 - core), r_g.at[1])
        g_load(0, 0).start()

        def step(i, carry):
            slot = lax.rem(i, 2)
            g_load(i, slot).wait()

            @pl.when(i + 1 < p.rows // TILE)
            def _():
                g_load(i + 1, 1 - slot).start()

            rows = pl.ds(pl.multiple_of(i * TILE, TILE), TILE)
            for f in range(ffl // TILE):
                at = pl.ds(f * TILE, TILE)
                d_unit = dot_t(g_v[slot], dw_v[f * TILE : (f + 1) * TILE, :])
                dpre[rows, at] = (d_unit * dpre[rows, at].astype(F32)).astype(BF)
            first = core * half * L

            @pl.when((i * TILE >= first) & (i * TILE < first + half * L))
            def _():
                at = pl.ds(pl.multiple_of(i * TILE - first, TILE), TILE)
                dh_v[at, :] = dot_t(g_v[slot], dw_v[ffl:, :]).astype(BF)

            return carry

        lax.fori_loop(0, p.rows // TILE, step, 0)
        loads[3].wait()

    cols = [pl.ds(j * HEAD_DIM, HEAD_DIM) for j in range(3)]
    rows2 = L // 2

    def attend_back(i, carry):
        rows = pl.ds(pl.multiple_of(i * L, L), L)
        dq, dk, dv = [], [], []
        for h in range(2):
            at = pl.ds(pl.multiple_of(i * L + h * rows2, rows2), rows2)
            keys = pl.ds(pl.multiple_of(i * L, L), (h + 1) * rows2)
            q, k, v = joint_v[at, cols[0]], joint_v[keys, cols[1]], joint_v[keys, cols[2]]
            dh = dh_v[at, :]
            probs = probabilities(q, k, h * rows2, SCALE)
            d_probs = dot_t(dh, v)
            delta = jnp.sum(probs * d_probs, axis=1, keepdims=True)
            d_scores = (probs * (d_probs - delta)).astype(BF)
            dq.append(dot(d_scores, k) * SCALE)
            dk.append(t_dot(d_scores, q) * SCALE)
            dv.append(t_dot(probs.astype(BF), dh))
        dq = jnp.concatenate(dq, axis=0)
        dk = jnp.concatenate([dk[0] + dk[1][:rows2], dk[1][rows2:]], axis=0)
        dv = jnp.concatenate([dv[0] + dv[1][:rows2], dv[1][rows2:]], axis=0)
        cos, sin = cos_v[...], sin_v[...]
        for j, d_part in enumerate((turn(dq, cos, -sin), turn(dk, cos, -sin), dv)):
            low = d_part.astype(BF)
            joint_v[rows, cols[j]] = low
            sums = jnp.sum(low.astype(F32), axis=0, keepdims=True)
            for k in range(HEAD_DIM // LANES):
                at = j * (HEAD_DIM // LANES) + k
                vec[at : at + 1, :] += sums[:, k * LANES : (k + 1) * LANES]
        return carry

    def n_load(src, i, slot):
        count = src.shape[0]
        return pltpu.make_async_copy(
            src.at[:, pl.ds(pl.multiple_of(i * TILE, TILE), TILE)],
            n_v.at[slot, pl.ds(0, count)],
            n_sem.at[slot],
        )

    def stream(src, use, low, high):
        n_load(src, low, low % 2).start()

        def step(i, carry):
            slot = lax.rem(i, 2)
            n_load(src, i, slot).wait()

            @pl.when(i + 1 < high)
            def _():
                n_load(src, i + 1, 1 - slot).start()

            use(i, slot)
            return carry

        lax.fori_loop(low, high, step, 0)

    pairs = TILE // (2 * r)

    def q_tile(i, slot):
        for j in range(3):
            acc = t_dot(n_v[slot, 0 : p.rows // 2, :], joint_v[:, cols[j]]).astype(BF)
            for k in range(pairs):
                for kk in range(2):
                    at = (2 * k + kk) * r
                    q_g[i * pairs + k, kk, :, cols[j]] = acc[at : at + r]

    def up_tile(i, slot):
        at = pl.ds(pl.multiple_of(i * TILE, TILE), TILE)
        ugrad[at, :] = t_dot(n_v[slot], dpre[...]).astype(BF)

    def down_tile(i, slot):
        at = pl.ds(pl.multiple_of(i * TILE, TILE), TILE)
        g_sum[:, at] = jnp.sum(n_v[slot].astype(F32), axis=0, keepdims=True)
        for f in range(ffl // TILE):
            rows = slice(f * TILE, (f + 1) * TILE)
            dgrad[rows, at] = dot(hid_t[rows, :], n_v[slot]).astype(BF)
        first = pl.multiple_of(core * half * L, L)
        acc = dot(heads_t[...], n_v[slot, pl.ds(first, half * L), :]).astype(BF)
        for k in range(p.m):
            for kk in range(2):
                to = (2 * k + kk) * r
                o_g[k, kk, :, at] = acc[to : to + r]

    def down_owner(j):
        if p.P == 1:
            return j, c
        return 2 * (j // 2) + core, xh * 2 + j % 2

    def down_send():
        for j in range(S):
            own_b, own_c = down_owner(j)
            src = dgrad.at[pl.ds(j * R, R)]
            here = (own_b == b) & (own_c == c)

            @pl.when(jnp.logical_not(here))
            def _():
                remote(src, d_parts.at[b], s_d.at[j], r_d, (a * S + own_b, own_c)).start()

            @pl.when(here)
            def _():
                pltpu.make_async_copy(src, d_parts.at[b], r_d).start()

        remote(o_g.at[:, 1 - core], o_sib, s_o, r_o, sib).start()

    def u_rows(aa, bb):
        return ugrad.at[pl.ds(pl.multiple_of((aa * S + bb) * blk, blk), blk)]

    def up_send():
        def one(k, carry):
            bb = lax.rem(b + k, S)
            for aa in range(A):
                remote(u_rows(aa, bb), u_parts.at[k - 1, aa], s_u, r_u, (a * S + bb, c)).start()
            return carry

        lax.fori_loop(1, S, one, 0)

    def up_along():
        for k in range(1, S):
            drain(u_parts.at[k - 1], r_u)
        for k in range(1, S):

            def add(aa, carry):
                add_rows(u_rows(aa, b), (u_rows(aa, b), u_parts.at[k - 1, aa]), blk)
                return carry

            lax.fori_loop(0, A, add, 0)
        for k in range(1, A):
            aa = lax.rem(a + k, A)
            remote(u_rows(aa, b), u_z.at[k - 1], s_uz, r_uz, (aa * S + b, c)).start()

    def up_home():
        drain(u_z, r_uz)
        for k in range(A):
            source = lax.rem(a - k + A, A)
            for step in range(C):
                cc = lax.rem(c + 1 + step, C)
                row = pl.multiple_of(cc * r, r)
                for j in range(ffl // p.W):
                    at = pl.ds(j * p.W, p.W)
                    if k == 0:
                        src = ugrad.at[
                            pl.ds(pl.multiple_of((a * S + b) * blk + cc * r, r), r), at
                        ]
                    else:
                        src = u_z.at[k - 1, pl.ds(row, r), at]
                    col = pl.multiple_of(unit_run(p, source, c, j), LANES)
                    dst = u_out.at[:, pl.ds(col, p.W)]
                    if step < C - 1:
                        remote(src, dst, s_ua, r_ua, (dp, cc)).start()
                    else:
                        pltpu.make_async_copy(src, dst, r_ua).start()

    def q_rows(aa, bb):
        return q_g.at[pl.ds((aa * S + bb) * X, X), core]

    def q_cross():
        drain(q_sib, r_q)

        def add(i, carry):
            mine = q_g.at[i, core]
            add_rows(mine, (mine, q_sib.at[i]), r)
            return carry

        lax.fori_loop(0, A * S * X, add, 0)

        def one(k, carry):
            bb = lax.rem(b + k, S)
            for aa in range(A):
                remote(q_rows(aa, bb), q_group.at[k - 1, aa], s_qb, r_qb, (a * S + bb, c)).start()
            return carry

        lax.fori_loop(1, S, one, 0)

    def q_along():
        for k in range(1, S):
            drain(q_group.at[k - 1], r_qb)
        for k in range(1, S):

            def add(i, carry):
                aa, xx = lax.div(i, X), lax.rem(i, X)
                mine = q_g.at[(aa * S + b) * X + xx, core]
                add_rows(mine, (mine, q_group.at[k - 1, aa, xx]), r)
                return carry

            lax.fori_loop(0, A * X, add, 0)
        for k in range(1, A):
            aa = lax.rem(a + k, A)
            remote(q_rows(aa, b), q_z.at[k - 1], s_qz, r_qz, (aa * S + b, c)).start()

    def q_home():
        drain(q_z, r_qz)
        for k in range(A):
            source = lax.rem(a - k + A, A)
            for xx in (far, xh):
                for j in range(3):
                    if k == 0:
                        src = q_g.at[(a * S + b) * X + xx, core, :, cols[j]]
                    else:
                        src = q_z.at[k - 1, xx, :, cols[j]]
                    col = pl.multiple_of(j * D + (source * X + xh) * HEAD_DIM, HEAD_DIM)
                    dst = q_out.at[:, pl.ds(col, HEAD_DIM)]
                    if xx is far:
                        remote(src, dst, s_qa, r_qa, xnb).start()
                    else:
                        pltpu.make_async_copy(src, dst, r_qa).start()

    def out_owner(k):
        return lax.div(head * HEAD_DIM, r) + 2 * k + core

    def out_home():
        drain(o_sib, r_o)
        for k in range(p.m):
            mine = o_g.at[k, core]
            add_rows(mine, (mine, o_sib.at[k]), r)
            od, oc = lax.div(out_owner(k), C), lax.rem(out_owner(k), C)

            @pl.when(out_owner(k) != me)
            def _():
                remote(mine, o_parts.at[b], s_oa.at[k], r_oa, (od, oc)).start()

            @pl.when(out_owner(k) == me)
            def _():
                pltpu.make_async_copy(mine, o_parts.at[b], r_oa).start()

    own_v = pltpu.make_async_copy(vec, v_all.at[me], loc.at[7])

    def sums_send():
        up_row = p.hc // LANES

        def sum_rows(i, carry):
            at = pl.ds(pl.multiple_of(i * 64, 64), 64)
            return carry + jnp.sum(dpre[at, :].astype(F32), axis=0, keepdims=True)

        sums = lax.fori_loop(0, p.rows // 64, sum_rows, jnp.zeros((1, ffl), F32))
        for i in range(ffl // LANES):
            vec[up_row + i : up_row + i + 1, :] = sums[:, i * LANES : (i + 1) * LANES]
        share = D // (A * C)
        g_row = up_row + ffl // LANES
        vec[g_row : g_row + 1, :] = g_sum[:, pl.ds(pl.multiple_of(t * share, share), share)]
        own_v.start()

        def one(k, carry):
            other = lax.rem(me + k, p.n)
            dev = (lax.div(other, C), lax.rem(other, C))
            remote(vec, v_all.at[me], s_v, r_v, dev).start()
            return carry

        lax.fori_loop(1, p.n, one, 0)

    def give_back():
        pl.semaphore_signal(free, inc=1, device_id=sib, device_id_type=MESH)

    partial(0, 0)
    partial(0, 1)
    chip_sum(0, order[0])
    partial(0, 2)
    chip_sum(0, order[1])
    partial(0, 3)
    g_forward()
    chip_sum(0, order[2])
    chip_sum(0, order[3])
    give_back()
    unit_grads()
    hop(0, 0, False)
    stream(n2, up_tile, 0, 4)
    hop(0, 1, False)
    stream(n2, up_tile, 4, 8)
    up_send()
    lax.fori_loop(0, half, attend_back, 0)
    partial(1, 0)
    partial(1, 1)
    chip_sum(1, order[0])
    hop(0, 0, True)
    hop(0, 2, False)
    partial(1, 2)
    chip_sum(1, order[1])
    partial(1, 3)
    chip_sum(1, order[2])
    hop(0, 1, True)
    chip_sum(1, order[3])
    up_along()
    stream(n1, q_tile, 0, 4)
    hop(1, 0, False)
    stream(n1, q_tile, 4, 8)
    remote(q_g.at[:, 1 - core], q_sib, s_q, r_q, sib).start()
    q_cross()
    stream(g, down_tile, 0, 4)
    hop(1, 1, False)
    stream(g, down_tile, 4, 8)
    down_send()
    hop(1, 2, False)
    hop(1, 0, True)
    q_along()
    out_home()
    sums_send()
    hop(1, 1, True)
    up_home()
    q_home()
    last(0, o_sum)
    last(1, e_sum)

    drain(u_out, r_ua)
    drain(q_out, r_qa)
    drain(v_all.at[pl.ds(0, p.n - 1)], r_v)
    drain(d_parts, r_d)
    drain(o_parts, r_oa)

    own_v.wait()
    for k in range(2):
        drain(g_rows(c), s_g.at[k])
    drain(v_all.at[pl.ds(0, p.n - 1)], s_v)
    drain(q_sib, s_q)
    drain(o_sib, s_o)
    for k in range(1, S):
        drain(u_parts.at[0], s_u)
        drain(q_group.at[0], s_qb)
    drain(u_z, s_uz)
    drain(q_z, s_qz)
    for _ in range(A):
        drain(ugrad.at[pl.ds(0, (C - 1) * r)], s_ua)
        drain(q_g.at[0, 0], s_qa)
    for k in range(p.m):

        @pl.when(out_owner(k) != me)
        def _():
            drain(o_g.at[k, 0], s_oa.at[k])

    for j in range(S):
        own_b, own_c = down_owner(j)

        @pl.when(jnp.logical_not((own_b == b) & (own_c == c)))
        def _():
            drain(d_parts.at[0], s_d.at[j])

    for k in range(A):
        drain(from_sib.at[0], s_s.at[1, k])
    for j in range(2):
        for k in range(A):
            drain(from_x.at[0, 0], s_x.at[j, k])

            @pl.when(k != a)
            def _():
                drain(from_x.at[0, 0], s_c.at[j, k])


def back(p, *args):
    dma = pltpu.SemaphoreType.DMA
    A, S, C, X, r, R = p.A, p.S, p.C, p.X, p.r, p.R
    L = C * p.tok
    vm = pltpu.VMEM
    hbm = pl.BlockSpec(memory_space=pl.ANY)
    vmem = pl.BlockSpec(memory_space=pltpu.VMEM)
    groups = max(S - 1, 1)
    return pl.pallas_call(
        functools.partial(back_kernel, p),
        out_shape=(
            jax.ShapeDtypeStruct((p.tok, p.d), F32),
            jax.ShapeDtypeStruct((p.tok, p.d), F32),
            jax.ShapeDtypeStruct((r, 3 * p.d), BF),
            jax.ShapeDtypeStruct((r, p.ff), BF),
            jax.ShapeDtypeStruct((S, R, p.d), BF),
            jax.ShapeDtypeStruct((S, r, p.d), BF),
            jax.ShapeDtypeStruct((p.n, 16, LANES), F32),
            jax.ShapeDtypeStruct((A - 1, C * r, p.ffl), BF),
            jax.ShapeDtypeStruct((A - 1, X, r, p.hc), BF),
            jax.ShapeDtypeStruct((p.rows, p.d), BF),
        ),
        input_output_aliases={3: 9},
        in_specs=[hbm] * 10 + [vmem],
        out_specs=[vmem] * 2 + [hbm] * 8,
        scratch_shapes=[
            vm((max(p.rows, p.d), p.ffl), BF),
            vm((p.rows // 2, HEAD_DIM), BF),
            vm((p.rows, p.ffl), BF),
            vm((2, TILE, p.d), BF),
            vm((p.rows // 2, p.hc), BF),
            vm((p.ffl + HEAD_DIM, p.d), BF),
            vm((p.d, p.ffl), BF),
            vm((p.d, p.hc), BF),
            vm((2, p.rows, TILE), BF),
            vm((p.ffl, p.rows), BF),
            vm((HEAD_DIM, p.rows // 2), BF),
            vm((p.rows // 2, HEAD_DIM), BF),
            vm((L, LANES), F32),
            vm((L, LANES), F32),
            vm((2, A, X, p.tok, p.d), BF),
            vm((A, X, p.tok, p.d), BF),
            vm((A, X, p.tok, p.d), BF),
            vm((2, A, p.tok, p.d), BF),
            vm((2, 4, p.tok, p.d), BF),
            vm((p.ffl, p.d), BF),
            vm((A * S * X, 2, r, p.hc), BF),
            vm((A * S * X, r, p.hc), BF),
            vm((groups, A, X, r, p.hc), BF),
            vm((p.m, 2, r, p.d), BF),
            vm((p.m, r, p.d), BF),
            vm((groups, A, C * r, p.ffl), BF),
            vm((1, p.d), F32),
            vm((16, LANES), F32),
            dma((8,)),
            dma((2,)),
            dma((2,)),
            dma,
            dma,
            dma((2, A)),
            dma((2, A)),
            dma((2, A)),
            dma((2, A)),
            dma((2, A)),
            dma((2, 4)),
            dma,
            dma,
            dma,
            dma,
            dma,
            dma,
            dma,
            dma,
            dma,
            dma,
            dma((p.m,)),
            dma,
            dma,
            dma,
            dma,
            dma,
            dma,
            dma,
            dma((S,)),
            dma,
            dma((2,)),
            dma((2,)),
            pltpu.SemaphoreType.REGULAR,
        ],
        compiler_params=pltpu.CompilerParams(
            collective_id=1, has_side_effects=True, vmem_limit_bytes=67043328
        ),
        name="back",
    )(*args)


def finish_kernel(
    p,
    lens,
    x,
    g,
    o_sum,
    e_sum,
    full,
    q_part,
    u_part,
    d_parts,
    o_parts,
    sums,
    qkv_w,
    up_w,
    gain1,
    bias1,
    gain2,
    bias2,
    out,
    grad,
    q_grad,
    u_grad,
    d_grad,
    o_grad,
    q_own,
    u_own,
    g_own,
    g_same,
    gain1_grad,
    bias1_grad,
    gain2_grad,
    bias2_grad,
    q_bias,
    u_bias,
    g_bias,
    row_sums,
):
    A, S, C, X = p.A, p.S, p.C, p.X
    step = pl.program_id(0)

    @pl.when(step == 0)
    def _():
        up_row = p.hc // LANES
        g_row = up_row + p.ffl // LANES
        share = p.d // (A * C)
        for aa in range(A):
            for cc in range(C):
                for row in range(up_row, g_row + 1):
                    total = sums[aa * S * C + cc, row : row + 1, :]
                    for bb in range(1, S):
                        total = total + sums[(aa * S + bb) * C + cc, row : row + 1, :]
                    if row == g_row:
                        at = (aa * C + cc) * share
                        g_bias[:, at : at + share] = total[:, :share]
                        continue
                    unit = (row - up_row) * LANES
                    run = unit // p.W
                    if p.P == 1:
                        first = p.R * ((aa * S + run) * C + cc)
                    else:
                        first = p.R * ((aa * S + 2 * run + cc % 2) * C + cc // 2 * 2)
                    at = first + unit % p.W
                    u_bias[:, at : at + LANES] = total
            for xx in range(X):
                for row in range(up_row):
                    total = jnp.zeros((1, LANES), F32)
                    for bb in range(S):
                        for kk in range(2):
                            total = total + sums[(aa * S + bb) * C + xx * 2 + kk, row : row + 1, :]
                    j, rest = row * LANES // HEAD_DIM, row * LANES % HEAD_DIM
                    at = j * p.d + (aa * X + xx) * HEAD_DIM + rest
                    q_bias[:, at : at + LANES] = total
        me = lax.axis_index("dp") * C + lax.axis_index("ctx")

        def own(vector, size):
            span = max(size * i % LANES + size for i in range(p.n))
            span = (span + LANES - 1) // LANES * LANES
            rest = lax.rem(size * me, LANES)
            at = pl.multiple_of(size * me - rest, LANES)
            piece = pltpu.roll(vector[:, pl.ds(at, span)], lax.rem(span - rest, span), 1)
            return piece[0, :size]

        q_own[...] = own(q_bias, 3 * p.d // p.n)
        u_own[...] = own(u_bias, p.ff // p.n)
        g_own[...] = own(g_bias, p.d // p.n)
        g_same[...] = own(g_bias, p.d // p.n)

    rows = x.shape[0]
    sub = 16
    first = lax.axis_index("ctx") * p.tok + step * rows
    length = lens[0]

    def tokens(at):
        here = pl.ds(at, sub)
        row = lax.broadcasted_iota(jnp.int32, (sub, p.d), 0) + (at + first)
        live = row < length
        xf = x[here, :].astype(F32)
        total = xf + o_sum[here, :] + full[4:5, :]
        out[here, :] = jnp.where(live, total, 0.0).astype(BF)
        mid = xf - jnp.mean(xf, axis=1, keepdims=True)
        inv = lax.rsqrt(jnp.mean(mid * mid, axis=1, keepdims=True) + EPS)
        xhat = mid * inv
        e = e_sum[here, :]
        e_mean = jnp.mean(e, axis=1, keepdims=True)
        dx = inv * (e - e_mean - xhat * jnp.mean(e * xhat, axis=1, keepdims=True))
        go = jnp.where(live, g[here, :].astype(F32), 0.0)
        grad[here, :] = (go + dx).astype(BF)

    tiles(rows, tokens, sub)

    count = q_part.shape[0]
    lane = lax.broadcasted_iota(jnp.int32, (count, LANES), 1)
    kept = jnp.zeros((count, LANES), F32)
    for k, (part, weight, bias, result) in enumerate(
        ((q_part, qkv_w, q_bias, q_grad), (u_part, up_w, u_bias, u_grad))
    ):
        with_grad = jnp.zeros((part.shape[0], LANES), F32)
        with_bias = jnp.zeros((part.shape[0], LANES), F32)
        for n in range(0, part.shape[1], LANES):
            at = slice(n, n + LANES)
            value = part[:, at].astype(F32)
            result[:, at] = value
            w = weight[:, at].astype(F32)
            with_grad = with_grad + w * value
            with_bias = with_bias + w * bias[:, at]
        for o, t in enumerate((with_grad, with_bias)):
            kept = jnp.where(lane == 2 * k + o, jnp.sum(t, axis=1, keepdims=True), kept)
    row_sums[pl.ds(pl.multiple_of(step * count, count), count), :] = kept

    @pl.when(step == pl.num_programs(0) - 1)
    def _():
        turned = row_sums[...].T
        for k, (gain, shift, to_gain, to_shift) in enumerate(
            ((gain1, bias1, gain1_grad, bias1_grad), (gain2, bias2, gain2_grad, bias2_grad))
        ):
            with_grad, with_bias = turned[2 * k, : p.r], turned[2 * k + 1, : p.r]
            to_gain[...] = (with_grad - shift[...].astype(F32) * with_bias) / gain[...].astype(F32)
            to_shift[...] = with_bias

    for parts, result in ((d_parts, d_grad), (o_parts, o_grad)):

        def add(at):
            here = pl.ds(at, sub)
            total = parts[0, here, :].astype(F32)
            for k in range(1, S):
                total = total + parts[k, here, :].astype(F32)
            result[here, :] = total

        tiles(result.shape[0], add, sub)


def finish(p, *args):
    steps = max(1, p.r // 16)
    D, r, R = p.d, p.r, p.R

    def rows(count, width):
        return pl.BlockSpec((count // steps, width), lambda i: (i, 0))

    def parts(count):
        return pl.BlockSpec((p.S, count // steps, D), lambda i: (0, i, 0))

    def whole(*shape):
        return pl.BlockSpec(shape, lambda i: (0,) * len(shape))

    tok = rows(p.tok, D)
    return pl.pallas_call(
        functools.partial(finish_kernel, p),
        grid=(steps,),
        out_shape=(
            jax.ShapeDtypeStruct((p.tok, D), BF),
            jax.ShapeDtypeStruct((p.tok, D), BF),
            jax.ShapeDtypeStruct((r, 3 * D), F32),
            jax.ShapeDtypeStruct((r, p.ff), F32),
            jax.ShapeDtypeStruct((R, D), F32),
            jax.ShapeDtypeStruct((r, D), F32),
            jax.ShapeDtypeStruct((3 * D // p.n,), F32),
            jax.ShapeDtypeStruct((p.ff // p.n,), F32),
            *[jax.ShapeDtypeStruct((r,), F32)] * 6,
        ),
        in_specs=[
            pl.BlockSpec(memory_space=pltpu.SMEM),
            tok,
            tok,
            tok,
            tok,
            whole(8, D),
            rows(r, 3 * D),
            rows(r, p.ff),
            parts(R),
            parts(r),
            whole(p.n, 16, LANES),
            rows(r, 3 * D),
            rows(r, p.ff),
            *[whole(r)] * 4,
        ],
        out_specs=[
            tok,
            tok,
            rows(r, 3 * D),
            rows(r, p.ff),
            rows(R, D),
            rows(r, D),
            whole(3 * D // p.n),
            whole(p.ff // p.n),
            *[whole(r)] * 6,
        ],
        scratch_shapes=[
            pltpu.VMEM((1, 3 * D), F32),
            pltpu.VMEM((1, p.ff), F32),
            pltpu.VMEM((1, D), F32),
            pltpu.VMEM((r, LANES), F32),
        ],
        compiler_params=pltpu.CompilerParams(dimension_semantics=("arbitrary",)),
        name="finish",
    )(*args)


def local(
    dp_size,
    ctx_size,
    layer_input,
    lengths,
    cotangent,
    qkv_weight,
    qkv_bias,
    out_weight,
    out_bias,
    up_weight,
    up_bias,
    down_weight,
    down_bias,
    first_gain,
    first_bias,
    second_gain,
    second_bias,
):
    tok, d = layer_input.shape
    ff = up_weight.shape[1]
    p = Plan(dp_size, ctx_size, tok, d, ff)
    A, S, C, X, r, R = p.A, p.S, p.C, p.X, p.r, p.R
    dp, c, a, b, xh, core = place(p)
    me = dp * C + c
    t = a * C + c
    vectors = (
        qkv_bias,
        out_bias,
        up_bias,
        down_bias,
        first_gain,
        first_bias,
        second_gain,
        second_bias,
    )
    (_, g_all, qw, dw, uw, _, n1, n2, hid, slope, heads, joint, full) = front(
        p,
        layer_input,
        cotangent,
        qkv_weight,
        out_weight,
        up_weight,
        down_weight,
        lengths,
        *vectors,
    )
    o_sum, e_sum, q_out, u_out, d_parts, o_parts, v_all, _, _, _ = back(
        p,
        hid,
        heads,
        slope,
        g_all.reshape(p.rows, d),
        joint,
        n1,
        n2,
        dw,
        uw.reshape(d, p.ffl),
        qw.reshape(d, p.hc),
        full,
    )
    (
        output,
        input_grad,
        q_grad,
        u_grad,
        d_grad,
        o_grad,
        q_bias,
        u_bias,
        g_bias,
        g_same,
        gain1_grad,
        bias1_grad,
        gain2_grad,
        bias2_grad,
    ) = finish(
        p,
        lengths,
        layer_input,
        cotangent,
        o_sum,
        e_sum,
        full,
        q_out,
        u_out,
        d_parts,
        o_parts,
        v_all,
        qkv_weight,
        up_weight,
        first_gain,
        first_bias,
        second_gain,
        second_bias,
    )
    return (
        output,
        input_grad,
        q_grad,
        q_bias,
        o_grad,
        g_bias,
        u_grad,
        u_bias,
        d_grad,
        g_same,
        gain1_grad,
        bias1_grad,
        gain2_grad,
        bias2_grad,
    )


def solution(mesh):
    rows = P(("dp", "ctx"), None)
    vector = P(("dp", "ctx"))
    return jax.shard_map(
        functools.partial(local, mesh.shape["dp"], mesh.shape["ctx"]),
        mesh=mesh,
        in_specs=(
            rows,
            P("dp"),
            rows,
            rows,
            vector,
            rows,
            vector,
            rows,
            vector,
            rows,
            vector,
            vector,
            vector,
            vector,
            vector,
        ),
        out_specs=(
            rows,
            rows,
            rows,
            vector,
            rows,
            vector,
            rows,
            vector,
            rows,
            vector,
            vector,
            vector,
            vector,
            vector,
        ),
        check_vma=False,
    )
```

```python
import functools
import math

import jax
import jax.numpy as jnp
from jax import lax
from jax.experimental import pallas as pl
from jax.experimental.pallas import tpu as pltpu
from jax.sharding import PartitionSpec as P

HEADS = 8
HEAD_DIM = 256
ROT = 64
EPS = 1e-05
SCALE = 1.0 / math.sqrt(HEAD_DIM)
MESH = pl.DeviceIdType.MESH
BF = jnp.bfloat16
F32 = jnp.float32
TILE = 256
LANES = 128


class Plan:
    def __init__(self, dp, ctx, tok, d, ff):
        self.C = ctx
        self.X = ctx // 2
        self.A = HEADS // self.X
        self.S = dp // self.A
        self.n = dp * ctx
        self.tok = tok
        self.d = d
        self.ff = ff
        self.r = d // self.n
        self.R = ff // self.n
        self.ffl = self.S * self.R
        self.W = max(self.R, 128)
        self.P = self.W // self.R
        self.hc = 3 * HEAD_DIM
        self.m = HEAD_DIM // self.r // 2
        self.rows = self.A * self.C * tok


def remote(src, dst, send, recv, dev):
    return pltpu.make_async_remote_copy(
        src_ref=src, dst_ref=dst, send_sem=send, recv_sem=recv, device_id=dev, device_id_type=MESH
    )


def drain(ref, sem):
    pltpu.make_async_copy(ref, ref, sem).wait()


def unit_run(p, aa, cc, j):
    if p.P == 1:
        return p.R * ((aa * p.S + j) * p.C + cc)
    return p.R * ((aa * p.S + 2 * j + lax.rem(cc, 2)) * p.C + lax.div(cc, 2) * 2)


def unit_home(p, b, xh, core):
    if p.P == 1:
        return xh * 2 + core, b * p.R
    return xh * 2 + lax.rem(b, 2), (lax.div(b, 2) * 2 + core) * p.R


def place(p):
    dp = lax.axis_index("dp")
    c = lax.axis_index("ctx")
    a = lax.div(dp, p.S)
    b = lax.rem(dp, p.S)
    xh = lax.div(c, 2)
    core = lax.rem(c, 2)
    return dp, c, a, b, xh, core


def greet_all(p, me):
    barrier = pltpu.get_barrier_semaphore()

    def greet(k, carry):
        other = lax.rem(me + k, p.n)
        pl.semaphore_signal(
            barrier,
            inc=1,
            device_id=(lax.div(other, p.C), lax.rem(other, p.C)),
            device_id_type=MESH,
        )
        return carry

    lax.fori_loop(1, p.n, greet, 0)
    pl.semaphore_wait(barrier, p.n - 1)


def dot(x, y):
    return jnp.dot(x, y, preferred_element_type=F32)


def dot_t(x, y):
    return lax.dot_general(x, y, (((1,), (1,)), ((), ())), preferred_element_type=F32)


def t_dot(x, y):
    return lax.dot_general(x, y, (((0,), (0,)), ((), ())), preferred_element_type=F32)


def tiles(count, body, size=TILE):
    def run(i, carry):
        body(pl.multiple_of(i * size, size))
        return carry

    lax.fori_loop(0, count // size, run, 0)


def pick(values, i):
    out = values[0]
    for k in range(1, len(values)):
        out = jnp.where(i == k, values[k], out)
    return out


def far_order(p, a):
    order = []
    lo, hi = 0, p.A - 1
    for _ in range(p.A):
        up_far = hi - a >= a - lo
        order.append(jnp.where(up_far, hi, lo))
        lo = jnp.where(up_far, lo, lo + 1)
        hi = jnp.where(up_far, hi - 1, hi)
    return order


def add_rows(dst, parts, rows):
    step = 16

    def body(k, carry):
        at = pl.ds(pl.multiple_of(k * step, step), step)
        total = parts[0][at, :].astype(F32)
        for part in parts[1:]:
            total = total + part[at, :].astype(F32)
        dst[at, :] = total.astype(dst.dtype)
        return carry

    lax.fori_loop(0, rows // step, body, 0)


def angle_tables(cos_v, sin_v):
    rows = cos_v.shape[0]
    half = ROT // 2

    def body(at):
        shape = (64, LANES)
        lane = lax.broadcasted_iota(jnp.int32, shape, 1)
        pos = (lax.broadcasted_iota(jnp.int32, shape, 0) + at).astype(F32)
        exponent = lax.rem(lane, half).astype(F32) * (-2.0 * math.log(10000.0) / ROT)
        angle = pos * jnp.exp(exponent)
        turned = lane < ROT
        sign = jnp.where(lane < half, -1.0, 1.0)
        cos_v[pl.ds(at, 64), :] = jnp.where(turned, jnp.cos(angle), 1.0)
        sin_v[pl.ds(at, 64), :] = jnp.where(turned, jnp.sin(angle) * sign, 0.0)

    tiles(rows, body, 64)


def turn(v, cos, sin):
    first = v[:, :LANES]
    half = ROT // 2
    lane = lax.broadcasted_iota(jnp.int32, first.shape, 1)
    partner = jnp.where(
        lane < half, pltpu.roll(first, LANES - half, 1), pltpu.roll(first, half, 1)
    )
    return jnp.concatenate([first * cos + partner * sin, v[:, LANES:]], axis=1)


def probabilities(q, k, row0, scale):
    scores = dot_t(q, k) * scale
    row = lax.broadcasted_iota(jnp.int32, scores.shape, 0) + row0
    col = lax.broadcasted_iota(jnp.int32, scores.shape, 1)
    scores = jnp.where(col <= row, scores, -1e30)
    expo = jnp.exp(scores - jnp.max(scores, axis=1, keepdims=True))
    return expo / jnp.sum(expo, axis=1, keepdims=True)


def front_kernel(
    p,
    x,
    g,
    qkv,
    outw,
    up,
    down,
    lens,
    qkv_b,
    out_b,
    up_b,
    down_b,
    gain1,
    bias1,
    gain2,
    bias2,
    xa,
    ga,
    qw,
    dw,
    uw,
    sm,
    n1,
    n2,
    hid,
    slope,
    heads,
    joint,
    rows_out,
    small,
    pads,
    g_v,
    gm,
    sm_v,
    vecs,
    ub,
    qb,
    cos_v,
    sin_v,
    uw_v,
    qw_v,
    xs,
    n1_v,
    n2_v,
    hid_v,
    slope_v,
    heads_v,
    joint_v,
    ux,
    qx,
    loc,
    puts,
    s_ux,
    r_ux,
    s_qx,
    r_qx,
    s_sm,
    r_sm,
    s_up,
    r_up,
    s_upb,
    r_upb,
    s_q,
    r_q,
    s_qb,
    r_qb,
    s_qc,
    r_qc,
    s_o,
    r_o,
    s_ob,
    s_oc,
    r_oc,
    s_d,
    r_d,
    s_r,
    r_r,
    s_l,
    r_l,
    s_x,
    r_x,
    s_s,
    r_s,
):
    A, S, C, r, R = p.A, p.S, p.C, p.r, p.R
    dp, c, a, b, xh, core = place(p)
    me = dp * C + c
    t = a * C + c
    head = a * p.X + xh
    sib = (dp, xh * 2 + 1 - core)
    xnb = (dp, (1 - xh) * 2 + core)
    right = (dp + S, c)
    left = (dp - S, c)
    L = C * p.tok
    half = A // 2

    get_g = pltpu.make_async_copy(g, g_v, loc.at[2])
    get_g.start()
    vectors = (qkv_b, up_b, gain1, bias1, gain2, bias2, out_b)
    greet_all(p, me)

    own_small = pltpu.make_async_copy(small, sm.at[me], loc.at[0])
    own_x = pltpu.make_async_copy(x, xa.at[a, pl.ds(pl.multiple_of(c * p.tok, p.tok), p.tok)], loc.at[1])
    own_x.start()
    own_g = pltpu.make_async_copy(gm, ga.at[a, pl.ds(pl.multiple_of(c * p.tok, p.tok), p.tok)], loc.at[2])

    row_head = lax.div(me * r, HEAD_DIM)
    row_part = lax.div(lax.rem(me * r, HEAD_DIM), 2 * r)
    o_dp, o_ctx = lax.div(row_head, p.X) * S + b, lax.rem(row_head, p.X) * 2 + core
    o_here = (o_dp == dp) & (o_ctx == c)

    def o_rows(k, cc):
        return dw.at[pl.ds(pl.multiple_of(p.ffl + (2 * k + cc) * r, r), r)]

    def o_first(k):
        owner = lax.div(head * HEAD_DIM, r) + 2 * k + core
        return lax.rem(lax.div(owner, C), S) == b

    streams = ((x, xa), (gm, ga))

    def blk(j, k, cc):
        return streams[j][1].at[k, pl.ds(pl.multiple_of(cc * p.tok, p.tok), p.tok)]

    def send_z(j):
        own, slot = streams[j][0], blk(j, a, c)

        @pl.when(a < A - 1)
        def _():
            remote(own, slot, s_r.at[j, 0], r_r.at[j, 0], right).start()

        @pl.when(a > 0)
        def _():
            remote(own, slot, s_l.at[j, 0], r_l.at[j, 0], left).start()

    def send_x(j):
        own, slot = streams[j][0], blk(j, a, c)
        remote(own, slot, s_x.at[j, a], r_x.at[j, a], xnb).start()
        remote(own, slot, s_s.at[j, a], r_s.at[j, a], sib).start()

    last_slot = jnp.where(a < A // 2, A - 1, 0)

    def send_on(j, k, part):
        if j == 0:
            remote(part, part, s_x.at[j, k], r_x.at[j, k], xnb).start()
        else:

            @pl.when(k != last_slot)
            def _():
                remote(part, part, s_x.at[j, k], r_x.at[j, k], xnb).start()

        remote(part, part, s_s.at[j, k], r_s.at[j, k], sib).start()

    def z_step(j, s):
        @pl.when(a - 1 - s >= 0)
        def _():
            k = a - 1 - s
            part = blk(j, k, c)
            drain(part, r_r.at[j, s])

            @pl.when((s + 1 < A - 1) & (a < A - 1))
            def _():
                nxt = jnp.minimum(s + 1, A - 2)
                remote(part, part, s_r.at[j, nxt], r_r.at[j, nxt], right).start()

            send_on(j, k, part)

        @pl.when(a + 1 + s <= A - 1)
        def _():
            k = a + 1 + s
            part = blk(j, k, c)
            drain(part, r_l.at[j, s])

            @pl.when((s + 1 < A - 1) & (a > 0))
            def _():
                nxt = jnp.minimum(s + 1, A - 2)
                remote(part, part, s_l.at[j, nxt], r_l.at[j, nxt], left).start()

            send_on(j, k, part)

    xc = (1 - xh) * 2 + core

    def cross(j, k):
        part = blk(j, k, xc)
        drain(part, r_x.at[j, k])
        remote(part, part, s_s.at[j, k], r_s.at[j, k], sib).start()

    runs = p.ffl // p.W

    def up_cols(aa, cc, j):
        return up.at[:, pl.ds(pl.multiple_of(unit_run(p, aa, cc, j), LANES), p.W)]

    def up_over(i, carry):
        aa, kk = lax.div(i, 2), lax.rem(i, 2)
        for j in range(runs):
            dst = ux.at[aa, kk, :, pl.ds(j * p.W, p.W)]
            remote(up_cols(aa, (1 - xh) * 2 + kk, j), dst, s_ux, r_ux, xnb).start()
        return carry

    def up_along(i, carry):
        aa, kk = lax.rem(a + 1 + lax.div(i, 2), A), lax.rem(i, 2)
        cc = xh * 2 + kk
        here = (aa == a) & (kk == core)
        for j in range(runs):
            dst = uw.at[a, b, c, :, pl.ds(j * p.W, p.W)]

            @pl.when(jnp.logical_not(here))
            def _():
                remote(up_cols(aa, cc, j), dst, s_up, r_up, (aa * S + b, cc)).start()

            @pl.when(here)
            def _():
                pltpu.make_async_copy(up_cols(aa, cc, j), dst, r_up).start()

        return carry

    def up_onward(i, carry):
        aa, kk = lax.rem(a + 1 + lax.div(i, 2), A), lax.rem(i, 2)
        here = (aa == a) & (kk == core)
        src, dst = ux.at[aa, kk], uw.at[a, b, (1 - xh) * 2 + core]

        @pl.when(jnp.logical_not(here))
        def _():
            remote(src, dst, s_up, r_up, (aa * S + b, xh * 2 + kk)).start()

        @pl.when(here)
        def _():
            pltpu.make_async_copy(src, dst, r_up).start()

        return carry

    def q_cols(aa, xx, j):
        col = pl.multiple_of(j * p.d + (aa * p.X + xx) * HEAD_DIM, HEAD_DIM)
        return qkv.at[:, pl.ds(col, HEAD_DIM)]

    def q_over(aa, carry):
        for j in range(3):
            dst = qx.at[aa, :, pl.ds(j * HEAD_DIM, HEAD_DIM)]
            remote(q_cols(aa, 1 - xh, j), dst, s_qx, r_qx, xnb).start()
        return carry

    def q_along(i, carry):
        aa = lax.rem(a + 1 + i, A)
        for j in range(3):
            dst = qw.at[a, b, xh, core, :, pl.ds(j * HEAD_DIM, HEAD_DIM)]

            @pl.when(aa != a)
            def _():
                remote(q_cols(aa, xh, j), dst, s_q, r_q, (aa * S + b, c)).start()

            @pl.when(aa == a)
            def _():
                pltpu.make_async_copy(q_cols(aa, xh, j), dst, r_q).start()

        return carry

    def q_onward(i, carry):
        aa = lax.rem(a + 1 + i, A)
        src, dst = qx.at[aa], qw.at[a, b, 1 - xh, core]

        @pl.when(aa != a)
        def _():
            remote(src, dst, s_q, r_q, (aa * S + b, c)).start()

        @pl.when(aa == a)
        def _():
            pltpu.make_async_copy(src, dst, r_q).start()

        return carry

    def up_cross(k, carry):
        bb = lax.rem(b + k, S)
        remote(uw.at[:, b], uw.at[:, b], s_upb, r_upb, (a * S + bb, c)).start()
        return carry

    def q_cross(k, carry):
        bb = lax.rem(b + k, S)
        part = qw.at[:, b, :, core]
        remote(part, part, s_qb, r_qb, (a * S + bb, c)).start()
        return carry

    def slot_rows(k):
        return pl.ds(pl.multiple_of(k * L, L), L)

    near = far_order(p, a)[::-1]

    def norm_slot(i):
        k = near[i]
        drain(xa.at[k, pl.ds(0, p.X * p.tok)], r_s.at[0, k])
        get = pltpu.make_async_copy(xa.at[k], xs, loc.at[3])
        get.start()
        get.wait()
        mine = lax.div(k, half) == core
        step = 32

        def unit_rows(at):
            rows = xs[pl.ds(at, step), :].astype(F32)
            rows = rows - jnp.mean(rows, axis=1, keepdims=True)
            spread = jnp.mean(rows * rows, axis=1, keepdims=True)
            rows = rows * lax.rsqrt(spread + EPS)
            to = pl.multiple_of(k * L + at, step)
            n2_v[pl.ds(to, step), :] = (rows * vecs[2:3, :] + vecs[3:4, :]).astype(BF)
            return rows

        @pl.when(mine)
        def _():
            def both(at):
                rows = unit_rows(at)
                to = pl.multiple_of(lax.rem(k, half) * L + at, step)
                n1_v[pl.ds(to, step), :] = (rows * vecs[0:1, :] + vecs[1:2, :]).astype(BF)

            tiles(L, both, step)

        @pl.when(jnp.logical_not(mine))
        def _():
            def one(at):
                unit_rows(at)

            tiles(L, one, step)

        pltpu.make_async_copy(n2_v.at[slot_rows(k)], n2.at[slot_rows(k)], puts.at[i]).start()

    def units(i):
        k = near[i]

        def unit_tile(n):
            at = pl.ds(n, TILE)
            w = uw_v[:, :, :, :, at].reshape(p.d, TILE)
            v = dot(n2_v[slot_rows(k), :], w) + ub[:, at]
            phi = 0.5 * (1.0 + lax.erf(v * (1.0 / math.sqrt(2.0))))
            density = jnp.exp(-0.5 * v * v) * (1.0 / math.sqrt(2.0 * math.pi))
            hid_v[slot_rows(k), at] = (v * phi).astype(BF)
            slope_v[slot_rows(k), at] = (phi + v * density).astype(BF)

        tiles(p.ffl, unit_tile)

    d_ctx, d_row = unit_home(p, b, xh, core)
    d_dst = dw.at[pl.ds(pl.multiple_of(d_row, R), R)]
    def small_all():
        def small_send(k, carry):
            other = lax.rem(me + k, p.n)
            dev = (lax.div(other, C), lax.rem(other, C))
            remote(small, sm.at[me], s_sm, r_sm, dev).start()
            return carry

        lax.fori_loop(1, p.n, small_send, 0)

    def down_all():
        for bb in range(S):
            here = (bb == b) & (d_ctx == c)

            @pl.when(jnp.logical_not(here))
            def _():
                remote(down, d_dst, s_d.at[bb], r_d, (a * S + bb, d_ctx)).start()

            @pl.when(here)
            def _():
                pltpu.make_async_copy(down, d_dst, r_d).start()

    def out_send():
        @pl.when(jnp.logical_not(o_here))
        def _():
            remote(outw, o_rows(row_part, core), s_o, r_o.at[row_part], (o_dp, o_ctx)).start()

        @pl.when(o_here)
        def _():
            pltpu.make_async_copy(outw, o_rows(row_part, core), r_o.at[row_part]).start()

    def chunk(which, jj):
        size = vectors[which].shape[0]
        if size % LANES == 0:
            count = 1
        elif LANES % size == 0:
            count = LANES // size
        else:
            count = (LANES - 1) // size + 2
        total = jnp.zeros((1, LANES), F32)
        for o in range(count):
            i = lax.div(LANES * jj, size) + o
            row = jj - lax.div(i * size, LANES)
            good = ((row >= 0) & (row <= 1) & (i < p.n)).astype(F32)
            at = 2 * which + jnp.clip(row, 0, 1)
            total = total + good * sm_v[jnp.minimum(i, p.n - 1), pl.ds(at, 1), :]
        return total

    def vectors_whole():
        own_small.wait()
        drain(sm.at[pl.ds(0, p.n - 1)], r_sm)
        get_small = pltpu.make_async_copy(sm, sm_v, loc.at[0])
        get_small.start()
        get_small.wait()

        def fill(jj, carry):
            for k in range(5):
                vecs[k : k + 1, pl.ds(pl.multiple_of(jj * LANES, LANES), LANES)] = chunk(2 + k, jj)
            return carry

        lax.fori_loop(0, p.d // LANES, fill, 0)
        for j in range(p.ffl // LANES):
            run, rest = j * LANES // p.W, (j * LANES % p.W) // LANES
            first = lax.div(unit_run(p, a, c, run), LANES) + rest
            ub[:, j * LANES : (j + 1) * LANES] = chunk(1, first)
        for j in range(3):
            for k in range(HEAD_DIM // LANES):
                first = (j * p.d + head * HEAD_DIM) // LANES + k
                at = j * HEAD_DIM + k * LANES
                qb[:, at : at + LANES] = chunk(0, first)

    def out_onward(k):
        remote(o_rows(k, core), o_rows(k, core), s_oc.at[k], r_oc.at[k], sib).start()

    def out_first():
        for k in range(p.m):

            @pl.when(o_first(k))
            def _():
                drain(o_rows(k, core), r_o.at[k])

                def o_cross(kk, carry):
                    bb = lax.rem(b + kk, S)
                    rows = o_rows(k, core)
                    remote(rows, rows, s_ob.at[k], r_o.at[k], (a * S + bb, c)).start()
                    return carry

                lax.fori_loop(1, S, o_cross, 0)
                out_onward(k)

    def out_rest():
        for k in range(p.m):

            @pl.when(jnp.logical_not(o_first(k)))
            def _():
                drain(o_rows(k, core), r_o.at[k])
                out_onward(k)

    def load_uw():
        for _ in range(S - 1):
            drain(uw.at[:, b], r_upb)
        get = pltpu.make_async_copy(uw, uw_v, loc.at[3])
        get.start()
        get.wait()

    def send_half_qw():
        for _ in range(S - 1):
            drain(qw.at[:, b, :, core], r_qb)
        part = qw.at[:, :, :, core]
        remote(part, part, s_qc, r_qc, sib).start()

    def load_qw():
        drain(qw.at[:, :, :, 1 - core], r_qc)
        get = pltpu.make_async_copy(qw, qw_v, loc.at[3])
        get.start()
        get.wait()

    def attend(i):
        own = pl.ds(pl.multiple_of(i * L, L), L)
        cols = [pl.ds(j * HEAD_DIM, HEAD_DIM) for j in range(3)]
        for j in range(3):
            w = qw_v[:, :, :, :, :, cols[j]].reshape(p.d, HEAD_DIM)
            v = dot(n1_v[own, :], w) + qb[:, cols[j]]
            if j < 2:
                v = turn(v, cos_v[...], sin_v[...])
            joint_v[own, cols[j]] = v.astype(BF)
        rows = L // 2
        for h in range(2):
            at = pl.ds(pl.multiple_of(i * L + h * rows, rows), rows)
            keys = pl.ds(pl.multiple_of(i * L, L), (h + 1) * rows)
            probs = probabilities(joint_v[at, cols[0]], joint_v[keys, cols[1]], h * rows, SCALE)
            heads_v[at, :] = dot(probs.astype(BF), joint_v[keys, cols[2]]).astype(BF)

    send_z(0)
    send_x(0)

    get_g.wait()
    length = lens[0]

    def mask(at):
        row = lax.broadcasted_iota(jnp.int32, (32, p.d), 0) + (at + c * p.tok)
        rows = g_v[pl.ds(at, 32), :].astype(F32)
        gm[pl.ds(at, 32), :] = jnp.where(row < length, rows, 0.0).astype(BF)

    tiles(p.tok, mask, 32)

    pads[...] = jnp.zeros_like(pads)
    for k, v in enumerate(vectors):
        value = v[...].astype(F32)
        if k == len(vectors) - 1:
            value = value + down_b[...].astype(F32)
        pads[k, 0 : v.shape[0]] = value
    for k, v in enumerate(vectors):
        placed = pltpu.roll(pads[k : k + 1, :], lax.rem(v.shape[0] * me, LANES), 1)
        small[2 * k : 2 * k + 1, :] = placed[:, :LANES]
        small[2 * k + 1 : 2 * k + 2, :] = placed[:, LANES:]
    small[2 * len(vectors) :, :] = jnp.zeros((2, LANES), F32)
    own_small.start()
    own_g.start()
    small_all()
    lax.fori_loop(0, 2 * A, up_over, 0)
    angle_tables(cos_v, sin_v)
    z_step(0, 0)
    cross(0, near[0])
    lax.fori_loop(0, 2 * A, up_along, 0)
    down_all()
    z_step(0, 1)
    drain(ux, r_ux)
    lax.fori_loop(0, 2 * A, up_onward, 0)
    lax.fori_loop(0, A, q_over, 0)
    cross(0, near[1])
    vectors_whole()
    own_x.wait()
    norm_slot(0)
    lax.fori_loop(0, A, q_along, 0)
    send_x(1)
    norm_slot(1)
    drain(qx, r_qx)
    lax.fori_loop(0, A, q_onward, 0)
    out_send()
    cross(0, near[2])
    send_z(1)
    drain(uw.at[:, b], r_up)
    lax.fori_loop(1, S, up_cross, 0)
    drain(qw.at[:, b, :, core], r_q)
    lax.fori_loop(1, S, q_cross, 0)
    norm_slot(2)
    z_step(0, 2)
    cross(1, near[0])
    z_step(1, 0)
    out_first()
    cross(0, near[3])
    norm_slot(3)
    put_n1 = pltpu.make_async_copy(n1_v, n1, loc.at[6])
    put_n1.start()
    put_rows = pltpu.make_async_copy(vecs, rows_out, loc.at[7])
    put_rows.start()
    load_uw()
    send_half_qw()
    units(0)
    z_step(1, 1)
    cross(1, near[1])
    units(1)
    load_qw()
    attend(0)
    units(2)
    z_step(1, 2)
    attend(1)
    cross(1, near[2])
    units(3)
    put_hid = pltpu.make_async_copy(hid_v, hid, loc.at[4])
    put_hid.start()
    put_slope = pltpu.make_async_copy(slope_v, slope, loc.at[5])
    put_slope.start()
    out_rest()

    put_heads = pltpu.make_async_copy(heads_v, heads, loc.at[0])
    put_heads.start()
    put_joint = pltpu.make_async_copy(joint_v, joint, loc.at[1])
    put_joint.start()

    drain(dw.at[pl.ds(0, p.ffl)], r_d)
    for k in range(p.m):
        drain(dw.at[pl.ds(0, r)], r_oc.at[k])
    for k in range(A):

        @pl.when(k != last_slot)
        def _():
            drain(ga.at[k, pl.ds(0, p.X * p.tok)], r_s.at[1, k])

        @pl.when(k == last_slot)
        def _():
            drain(ga.at[k, pl.ds(0, p.tok)], r_s.at[1, k])


    own_g.wait()
    put_hid.wait()
    put_slope.wait()
    put_n1.wait()
    put_rows.wait()
    put_heads.wait()
    put_joint.wait()
    for i in range(A):
        drain(n2_v.at[pl.ds(0, L)], puts.at[i])
    drain(sm.at[pl.ds(0, p.n - 1)], s_sm)
    drain(ux, s_ux)
    drain(qx, s_qx)
    for _ in range(4 * A - 2):
        drain(uw.at[a, b, c], s_up)
    for _ in range(2 * A - 2):
        drain(qw.at[a, b, xh, core], s_q)
    for bb in range(S):

        @pl.when(jnp.logical_not((bb == b) & (d_ctx == c)))
        def _():
            drain(down, s_d.at[bb])

    @pl.when(jnp.logical_not(o_here))
    def _():
        drain(outw, s_o)

    for k in range(p.m):

        @pl.when(o_first(k))
        def _():
            for _ in range(S - 1):
                drain(outw, s_ob.at[k])

    for k in range(p.m):
        drain(dw.at[pl.ds(0, r)], s_oc.at[k])
    for _ in range(S - 1):
        drain(uw.at[:, b], s_upb)
        drain(qw.at[:, b, :, core], s_qb)
    drain(qw.at[:, :, :, core], s_qc)
    for j in range(2):
        for s in range(A - 1):

            @pl.when((a < A - 1) & (a - s >= 0))
            def _():
                drain(x, s_r.at[j, s])

            @pl.when((a > 0) & (a + s <= A - 1))
            def _():
                drain(x, s_l.at[j, s])

        for k in range(A):
            if j == 0:
                drain(x, s_x.at[j, k])
                drain(xa.at[k, pl.ds(0, p.X * p.tok)], s_s.at[j, k])
                continue

            @pl.when(k != last_slot)
            def _():
                drain(x, s_x.at[j, k])
                drain(xa.at[k, pl.ds(0, p.X * p.tok)], s_s.at[j, k])

            @pl.when(k == last_slot)
            def _():
                drain(x, s_s.at[j, k])


def front(p, x, g, qkv, outw, up, down, lens, *vectors):
    dma = pltpu.SemaphoreType.DMA
    A, S, C, r = p.A, p.S, p.C, p.r
    L = C * p.tok
    vm = pltpu.VMEM
    hbm = pl.BlockSpec(memory_space=pl.ANY)
    vmem = pl.BlockSpec(memory_space=pltpu.VMEM)
    half = p.rows // 2
    qw_shape = (A, S, p.X, 2, r, p.hc)
    uw_shape = (A, S, C, r, p.ffl)
    return pl.pallas_call(
        functools.partial(front_kernel, p),
        out_shape=(
            jax.ShapeDtypeStruct((A, L, p.d), BF),
            jax.ShapeDtypeStruct((A, L, p.d), BF),
            jax.ShapeDtypeStruct(qw_shape, BF),
            jax.ShapeDtypeStruct((p.ffl + HEAD_DIM, p.d), BF),
            jax.ShapeDtypeStruct(uw_shape, BF),
            jax.ShapeDtypeStruct((p.n, 16, LANES), F32),
            jax.ShapeDtypeStruct((half, p.d), BF),
            jax.ShapeDtypeStruct((p.rows, p.d), BF),
            jax.ShapeDtypeStruct((p.rows, p.ffl), BF),
            jax.ShapeDtypeStruct((p.rows, p.ffl), BF),
            jax.ShapeDtypeStruct((half, HEAD_DIM), BF),
            jax.ShapeDtypeStruct((half, p.hc), BF),
            jax.ShapeDtypeStruct((8, p.d), F32),
        ),
        in_specs=[hbm] * 6 + [pl.BlockSpec(memory_space=pltpu.SMEM)] + [vmem] * 8,
        out_specs=[hbm] * 13,
        scratch_shapes=[
            vm((16, LANES), F32),
            vm((8, 2 * LANES), F32),
            vm((p.tok, p.d), BF),
            vm((p.tok, p.d), BF),
            vm((p.n, 16, LANES), F32),
            vm((8, p.d), F32),
            vm((1, p.ffl), F32),
            vm((1, p.hc), F32),
            vm((L, LANES), F32),
            vm((L, LANES), F32),
            vm(uw_shape, BF),
            vm(qw_shape, BF),
            vm((L, p.d), BF),
            vm((half, p.d), BF),
            vm((p.rows, p.d), BF),
            vm((p.rows, p.ffl), BF),
            vm((p.rows, p.ffl), BF),
            vm((half, HEAD_DIM), BF),
            vm((half, p.hc), BF),
            vm((A, 2, r, p.ffl), BF),
            vm((A, r, p.hc), BF),
            dma((8,)),
            dma((A,)),
            dma,
            dma,
            dma,
            dma,
            dma,
            dma,
            dma,
            dma,
            dma,
            dma,
            dma,
            dma,
            dma,
            dma,
            dma,
            dma,
            dma,
            dma((p.m,)),
            dma((p.m,)),
            dma((p.m,)),
            dma((p.m,)),
            dma((S,)),
            dma,
            dma((2, A - 1)),
            dma((2, A - 1)),
            dma((2, A - 1)),
            dma((2, A - 1)),
            dma((2, A)),
            dma((2, A)),
            dma((2, A)),
            dma((2, A)),
        ],
        compiler_params=pltpu.CompilerParams(
            collective_id=0, has_side_effects=True, vmem_limit_bytes=60 * 1024 * 1024
        ),
        name="front",
    )(x, g, qkv, outw, up, down, lens, *vectors)


def back_kernel(
    p,
    hid,
    heads,
    slope,
    g_in,
    joint,
    n1,
    n2,
    dw,
    uw,
    qw,
    gains,
    o_sum,
    e_sum,
    q_out,
    u_out,
    d_parts,
    o_parts,
    v_all,
    u_z,
    q_z,
    g,
    hid_v,
    heads_v,
    dpre,
    g_v,
    joint_v,
    dw_v,
    uw_v,
    qw_v,
    n_v,
    hid_t,
    heads_t,
    dh_v,
    cos_v,
    sin_v,
    own,
    to_sib,
    from_sib,
    from_x,
    came,
    dgrad,
    q_g,
    q_sib,
    q_group,
    o_g,
    o_sib,
    u_parts,
    g_sum,
    vec,
    loc,
    n_sem,
    g_sem,
    s_v,
    r_v,
    s_s,
    r_s,
    s_x,
    r_x,
    s_c,
    r_c,
    s_q,
    r_q,
    s_qb,
    r_qb,
    s_qz,
    r_qz,
    s_qa,
    r_qa,
    s_o,
    r_o,
    s_oa,
    r_oa,
    s_u,
    r_u,
    s_uz,
    r_uz,
    s_ua,
    r_ua,
    s_d,
    r_d,
    s_g,
    r_g,
    free,
):
    A, S, C, X, r, R = p.A, p.S, p.C, p.X, p.r, p.R
    dp, c, a, b, xh, core = place(p)
    me = dp * C + c
    t = a * C + c
    head = a * X + xh
    sib = (dp, xh * 2 + 1 - core)
    xnb = (dp, (1 - xh) * 2 + core)
    far = 1 - xh
    L = C * p.tok
    D, ffl = p.d, p.ffl
    half = A // 2
    ugrad = hid_v
    blk = C * r

    loads = [
        pltpu.make_async_copy(src, dst, loc.at[k])
        for k, (src, dst) in enumerate(
            (
                (hid, hid_v.at[pl.ds(0, p.rows)]),
                (dw, dw_v),
                (heads, heads_v),
                (joint, joint_v),
                (slope, dpre),
                (uw, uw_v),
                (qw, qw_v),
            )
        )
    ]
    for load in loads:
        load.start()
    greet_all(p, me)
    last_slot = jnp.where(a < half, A - 1, 0)

    def g_rows(cc):
        return g.at[pl.ds(pl.multiple_of(last_slot * L + cc * p.tok, p.tok), p.tok)]

    remote(g_rows(c), g_rows(c), s_g.at[0], r_g.at[0], xnb).start()
    x_ctx = far * 2 + core
    vec[...] = jnp.zeros_like(vec)
    angle_tables(cos_v, sin_v)

    def g_forward():
        drain(g_rows(x_ctx), r_g.at[0])
        remote(g_rows(x_ctx), g_rows(x_ctx), s_g.at[1], r_g.at[1], sib).start()

    low = a < half
    order = [
        jnp.where(low, A - 1, 0),
        jnp.where(low, A - 2, 1),
        jnp.where(low, 1 - a, A + 1 - a),
        a,
    ]
    inner = (a == 1) | (a == A - 2)

    def slot_rows(k):
        return pl.ds(pl.multiple_of(k * L, L), L)

    def blocks(src, base):
        rows = []
        for cc in (core, 1 - core):
            for side in range(X):
                at = pl.multiple_of(base + (side * 2 + cc) * p.tok, p.tok)
                rows.append(src[pl.ds(at, p.tok), :])
        return jnp.concatenate(rows, axis=0)

    def keep(j, k, n, acc):
        acc = acc.astype(BF)
        for side in range(X):
            own[j, k, side, :, pl.ds(n, TILE)] = acc[side * p.tok : (side + 1) * p.tok]
            to_sib[k, side, :, pl.ds(n, TILE)] = acc[
                (X + side) * p.tok : (X + side + 1) * p.tok
            ]

    def partial(j, i):
        k = order[i]
        mine = lax.div(k, half) == core
        base = pl.multiple_of(lax.rem(k, half) * L, L)
        if j == 0 and i == 0:
            for n in range(3):
                loads[n].wait()
        if j == 1:
            if i == 0:
                loads[5].wait()
                loads[6].wait()
                pl.semaphore_wait(free, 1)
            drain(from_sib.at[k], s_s.at[0, k])
        units = blocks(dpre if j else hid_v, k * L)

        @pl.when(mine)
        def _():
            heads_rows = blocks(joint_v if j else heads_v, base)

            def tile(n):
                at = pl.ds(n, TILE)
                if j == 0:
                    acc = dot(units, dw_v[0:ffl, at]) + dot(heads_rows, dw_v[ffl:, at])
                else:
                    acc = dot_t(units, uw_v[at, :]) * gains[2:3, at]
                    acc += dot_t(heads_rows, qw_v[at, :]) * gains[0:1, at]
                keep(j, k, n, acc)

            tiles(D, tile)

        @pl.when(jnp.logical_not(mine))
        def _():
            def tile(n):
                at = pl.ds(n, TILE)
                if j == 0:
                    acc = dot(units, dw_v[0:ffl, at])
                else:
                    acc = dot_t(units, uw_v[at, :]) * gains[2:3, at]
                keep(j, k, n, acc)

            tiles(D, tile)

        remote(to_sib.at[k], from_sib.at[k], s_s.at[j, k], r_s.at[j, k], sib).start()

    def chip_sum(j, k):
        drain(from_sib.at[k], r_s.at[j, k])
        mine = own.at[j, k, far]
        add_rows(mine, (mine, from_sib.at[k, far]), p.tok)
        remote(mine, from_x.at[j, k], s_x.at[j, k], r_x.at[j, k], xnb).start()
        mine = own.at[j, k, xh]
        add_rows(mine, (mine, from_sib.at[k, xh]), p.tok)

    def hop(j, i, joins):
        k = order[i]
        across = i < 2
        if joins:
            run = inner
        else:
            run = jnp.logical_not(inner) if across else a >= 0

        @pl.when(run)
        def _():
            drain(from_x.at[j, k], r_x.at[j, k])
            mine = own.at[j, k, xh]
            if joins:
                drain(came.at[j, 0], r_c.at[j, lax.rem(k, 2)])
                add_rows(mine, (mine, from_x.at[j, k], came.at[j, lax.rem(k, 2)]), p.tok)
                to, at = k, 2
            else:
                add_rows(mine, (mine, from_x.at[j, k]), p.tok)
                if across:
                    to, at = jnp.where(a == 0, 1, A - 2), lax.rem(k, 2)
                else:
                    to, at = k, 3
            dev = (to * S + b, c)
            remote(mine, came.at[j, at], s_c.at[j, k], r_c.at[j, at], dev).start()

    def last(j, total):
        drain(from_x.at[j, a], r_x.at[j, a])
        drain(came.at[j, 2], r_c.at[j, 2])
        drain(came.at[j, 3], r_c.at[j, 3])
        mine = own.at[j, a, xh]
        add_rows(total, (mine, from_x.at[j, a], came.at[j, 2], came.at[j, 3]), p.tok)

    def unit_grads():
        loads[4].wait()
        for k in range(A):
            rows = slice(k * L, (k + 1) * L)
            for f in range(ffl // TILE):
                at = slice(f * TILE, (f + 1) * TILE)
                hid_t[at, rows] = hid_v[rows, at].astype(F32).T.astype(BF)
        for k in range(half):
            rows = slice(k * L, (k + 1) * L)
            heads_t[:, rows] = heads_v[rows, :].astype(F32).T.astype(BF)

        def g_load(i, slot):
            at = pl.ds(pl.multiple_of(i * TILE, TILE), TILE)
            return pltpu.make_async_copy(g.at[at], g_v.at[slot], g_sem.at[slot])

        drain(g_rows(far * 2 + 1 - core), r_g.at[1])
        g_load(0, 0).start()

        def step(i, carry):
            slot = lax.rem(i, 2)
            g_load(i, slot).wait()

            @pl.when(i + 1 < p.rows // TILE)
            def _():
                g_load(i + 1, 1 - slot).start()

            rows = pl.ds(pl.multiple_of(i * TILE, TILE), TILE)
            for f in range(ffl // TILE):
                at = pl.ds(f * TILE, TILE)
                d_unit = dot_t(g_v[slot], dw_v[f * TILE : (f + 1) * TILE, :])
                dpre[rows, at] = (d_unit * dpre[rows, at].astype(F32)).astype(BF)
            first = core * half * L

            @pl.when((i * TILE >= first) & (i * TILE < first + half * L))
            def _():
                at = pl.ds(pl.multiple_of(i * TILE - first, TILE), TILE)
                dh_v[at, :] = dot_t(g_v[slot], dw_v[ffl:, :]).astype(BF)

            return carry

        lax.fori_loop(0, p.rows // TILE, step, 0)
        loads[3].wait()

    cols = [pl.ds(j * HEAD_DIM, HEAD_DIM) for j in range(3)]
    rows2 = L // 2

    def attend_back(i, carry):
        rows = pl.ds(pl.multiple_of(i * L, L), L)
        dq, dk, dv = [], [], []
        for h in range(2):
            at = pl.ds(pl.multiple_of(i * L + h * rows2, rows2), rows2)
            keys = pl.ds(pl.multiple_of(i * L, L), (h + 1) * rows2)
            q, k, v = joint_v[at, cols[0]], joint_v[keys, cols[1]], joint_v[keys, cols[2]]
            dh = dh_v[at, :]
            probs = probabilities(q, k, h * rows2, SCALE)
            d_probs = dot_t(dh, v)
            delta = jnp.sum(probs * d_probs, axis=1, keepdims=True)
            d_scores = (probs * (d_probs - delta)).astype(BF)
            dq.append(dot(d_scores, k) * SCALE)
            dk.append(t_dot(d_scores, q) * SCALE)
            dv.append(t_dot(probs.astype(BF), dh))
        dq = jnp.concatenate(dq, axis=0)
        dk = jnp.concatenate([dk[0] + dk[1][:rows2], dk[1][rows2:]], axis=0)
        dv = jnp.concatenate([dv[0] + dv[1][:rows2], dv[1][rows2:]], axis=0)
        cos, sin = cos_v[...], sin_v[...]
        for j, d_part in enumerate((turn(dq, cos, -sin), turn(dk, cos, -sin), dv)):
            low = d_part.astype(BF)
            joint_v[rows, cols[j]] = low
            sums = jnp.sum(low.astype(F32), axis=0, keepdims=True)
            for k in range(HEAD_DIM // LANES):
                at = j * (HEAD_DIM // LANES) + k
                vec[at : at + 1, :] += sums[:, k * LANES : (k + 1) * LANES]
        return carry

    def n_load(src, i, slot):
        count = src.shape[0]
        return pltpu.make_async_copy(
            src.at[:, pl.ds(pl.multiple_of(i * TILE, TILE), TILE)],
            n_v.at[slot, pl.ds(0, count)],
            n_sem.at[slot],
        )

    def stream(src, use, low, high):
        n_load(src, low, low % 2).start()

        def step(i, carry):
            slot = lax.rem(i, 2)
            n_load(src, i, slot).wait()

            @pl.when(i + 1 < high)
            def _():
                n_load(src, i + 1, 1 - slot).start()

            use(i, slot)
            return carry

        lax.fori_loop(low, high, step, 0)

    pairs = TILE // (2 * r)

    def q_tile(i, slot):
        for j in range(3):
            acc = t_dot(n_v[slot, 0 : p.rows // 2, :], joint_v[:, cols[j]]).astype(BF)
            for k in range(pairs):
                for kk in range(2):
                    at = (2 * k + kk) * r
                    q_g[i * pairs + k, kk, :, cols[j]] = acc[at : at + r]

    def up_tile(i, slot):
        at = pl.ds(pl.multiple_of(i * TILE, TILE), TILE)
        ugrad[at, :] = t_dot(n_v[slot], dpre[...]).astype(BF)

    def down_tile(i, slot):
        at = pl.ds(pl.multiple_of(i * TILE, TILE), TILE)
        g_sum[:, at] = jnp.sum(n_v[slot].astype(F32), axis=0, keepdims=True)
        for f in range(ffl // TILE):
            rows = slice(f * TILE, (f + 1) * TILE)
            dgrad[rows, at] = dot(hid_t[rows, :], n_v[slot]).astype(BF)
        first = pl.multiple_of(core * half * L, L)
        acc = dot(heads_t[...], n_v[slot, pl.ds(first, half * L), :]).astype(BF)
        for k in range(p.m):
            for kk in range(2):
                to = (2 * k + kk) * r
                o_g[k, kk, :, at] = acc[to : to + r]

    def down_owner(j):
        if p.P == 1:
            return j, c
        return 2 * (j // 2) + core, xh * 2 + j % 2

    def down_send():
        for j in range(S):
            own_b, own_c = down_owner(j)
            src = dgrad.at[pl.ds(j * R, R)]
            here = (own_b == b) & (own_c == c)

            @pl.when(jnp.logical_not(here))
            def _():
                remote(src, d_parts.at[b], s_d.at[j], r_d, (a * S + own_b, own_c)).start()

            @pl.when(here)
            def _():
                pltpu.make_async_copy(src, d_parts.at[b], r_d).start()

        remote(o_g.at[:, 1 - core], o_sib, s_o, r_o, sib).start()

    def u_rows(aa, bb):
        return ugrad.at[pl.ds(pl.multiple_of((aa * S + bb) * blk, blk), blk)]

    def up_send():
        def one(k, carry):
            bb = lax.rem(b + k, S)
            for aa in range(A):
                remote(u_rows(aa, bb), u_parts.at[k - 1, aa], s_u, r_u, (a * S + bb, c)).start()
            return carry

        lax.fori_loop(1, S, one, 0)

    def up_along():
        for k in range(1, S):
            drain(u_parts.at[k - 1], r_u)
        for k in range(1, S):

            def add(aa, carry):
                add_rows(u_rows(aa, b), (u_rows(aa, b), u_parts.at[k - 1, aa]), blk)
                return carry

            lax.fori_loop(0, A, add, 0)
        for k in range(1, A):
            aa = lax.rem(a + k, A)
            remote(u_rows(aa, b), u_z.at[k - 1], s_uz, r_uz, (aa * S + b, c)).start()

    def up_home():
        drain(u_z, r_uz)
        for k in range(A):
            source = lax.rem(a - k + A, A)
            for step in range(C):
                cc = lax.rem(c + 1 + step, C)
                row = pl.multiple_of(cc * r, r)
                for j in range(ffl // p.W):
                    at = pl.ds(j * p.W, p.W)
                    if k == 0:
                        src = ugrad.at[
                            pl.ds(pl.multiple_of((a * S + b) * blk + cc * r, r), r), at
                        ]
                    else:
                        src = u_z.at[k - 1, pl.ds(row, r), at]
                    col = pl.multiple_of(unit_run(p, source, c, j), LANES)
                    dst = u_out.at[:, pl.ds(col, p.W)]
                    if step < C - 1:
                        remote(src, dst, s_ua, r_ua, (dp, cc)).start()
                    else:
                        pltpu.make_async_copy(src, dst, r_ua).start()

    def q_rows(aa, bb):
        return q_g.at[pl.ds((aa * S + bb) * X, X), core]

    def q_cross():
        drain(q_sib, r_q)

        def add(i, carry):
            mine = q_g.at[i, core]
            add_rows(mine, (mine, q_sib.at[i]), r)
            return carry

        lax.fori_loop(0, A * S * X, add, 0)

        def one(k, carry):
            bb = lax.rem(b + k, S)
            for aa in range(A):
                remote(q_rows(aa, bb), q_group.at[k - 1, aa], s_qb, r_qb, (a * S + bb, c)).start()
            return carry

        lax.fori_loop(1, S, one, 0)

    def q_along():
        for k in range(1, S):
            drain(q_group.at[k - 1], r_qb)
        for k in range(1, S):

            def add(i, carry):
                aa, xx = lax.div(i, X), lax.rem(i, X)
                mine = q_g.at[(aa * S + b) * X + xx, core]
                add_rows(mine, (mine, q_group.at[k - 1, aa, xx]), r)
                return carry

            lax.fori_loop(0, A * X, add, 0)
        for k in range(1, A):
            aa = lax.rem(a + k, A)
            remote(q_rows(aa, b), q_z.at[k - 1], s_qz, r_qz, (aa * S + b, c)).start()

    def q_home():
        drain(q_z, r_qz)
        for k in range(A):
            source = lax.rem(a - k + A, A)
            for xx in (far, xh):
                for j in range(3):
                    if k == 0:
                        src = q_g.at[(a * S + b) * X + xx, core, :, cols[j]]
                    else:
                        src = q_z.at[k - 1, xx, :, cols[j]]
                    col = pl.multiple_of(j * D + (source * X + xh) * HEAD_DIM, HEAD_DIM)
                    dst = q_out.at[:, pl.ds(col, HEAD_DIM)]
                    if xx is far:
                        remote(src, dst, s_qa, r_qa, xnb).start()
                    else:
                        pltpu.make_async_copy(src, dst, r_qa).start()

    def out_owner(k):
        return lax.div(head * HEAD_DIM, r) + 2 * k + core

    def out_home():
        drain(o_sib, r_o)
        for k in range(p.m):
            mine = o_g.at[k, core]
            add_rows(mine, (mine, o_sib.at[k]), r)
            od, oc = lax.div(out_owner(k), C), lax.rem(out_owner(k), C)

            @pl.when(out_owner(k) != me)
            def _():
                remote(mine, o_parts.at[b], s_oa.at[k], r_oa, (od, oc)).start()

            @pl.when(out_owner(k) == me)
            def _():
                pltpu.make_async_copy(mine, o_parts.at[b], r_oa).start()

    own_v = pltpu.make_async_copy(vec, v_all.at[me], loc.at[7])

    def sums_send():
        up_row = p.hc // LANES

        def sum_rows(i, carry):
            at = pl.ds(pl.multiple_of(i * 64, 64), 64)
            return carry + jnp.sum(dpre[at, :].astype(F32), axis=0, keepdims=True)

        sums = lax.fori_loop(0, p.rows // 64, sum_rows, jnp.zeros((1, ffl), F32))
        for i in range(ffl // LANES):
            vec[up_row + i : up_row + i + 1, :] = sums[:, i * LANES : (i + 1) * LANES]
        share = D // (A * C)
        g_row = up_row + ffl // LANES
        vec[g_row : g_row + 1, :] = g_sum[:, pl.ds(pl.multiple_of(t * share, share), share)]
        own_v.start()

        def one(k, carry):
            other = lax.rem(me + k, p.n)
            dev = (lax.div(other, C), lax.rem(other, C))
            remote(vec, v_all.at[me], s_v, r_v, dev).start()
            return carry

        lax.fori_loop(1, p.n, one, 0)

    def give_back():
        pl.semaphore_signal(free, inc=1, device_id=sib, device_id_type=MESH)

    partial(0, 0)
    partial(0, 1)
    chip_sum(0, order[0])
    partial(0, 2)
    chip_sum(0, order[1])
    partial(0, 3)
    g_forward()
    chip_sum(0, order[2])
    chip_sum(0, order[3])
    give_back()
    unit_grads()
    hop(0, 0, False)
    stream(n2, up_tile, 0, 4)
    hop(0, 1, False)
    stream(n2, up_tile, 4, 8)
    up_send()
    lax.fori_loop(0, half, attend_back, 0)
    partial(1, 0)
    partial(1, 1)
    chip_sum(1, order[0])
    hop(0, 0, True)
    hop(0, 2, False)
    partial(1, 2)
    chip_sum(1, order[1])
    partial(1, 3)
    chip_sum(1, order[2])
    hop(0, 1, True)
    chip_sum(1, order[3])
    up_along()
    stream(n1, q_tile, 0, 4)
    hop(1, 0, False)
    stream(n1, q_tile, 4, 8)
    remote(q_g.at[:, 1 - core], q_sib, s_q, r_q, sib).start()
    q_cross()
    stream(g, down_tile, 0, 4)
    hop(1, 1, False)
    stream(g, down_tile, 4, 8)
    down_send()
    hop(1, 2, False)
    hop(1, 0, True)
    q_along()
    out_home()
    sums_send()
    hop(1, 1, True)
    up_home()
    q_home()
    last(0, o_sum)
    last(1, e_sum)

    drain(u_out, r_ua)
    drain(q_out, r_qa)
    drain(v_all.at[pl.ds(0, p.n - 1)], r_v)
    drain(d_parts, r_d)
    drain(o_parts, r_oa)

    own_v.wait()
    for k in range(2):
        drain(g_rows(c), s_g.at[k])
    drain(v_all.at[pl.ds(0, p.n - 1)], s_v)
    drain(q_sib, s_q)
    drain(o_sib, s_o)
    for k in range(1, S):
        drain(u_parts.at[0], s_u)
        drain(q_group.at[0], s_qb)
    drain(u_z, s_uz)
    drain(q_z, s_qz)
    for _ in range(A):
        drain(ugrad.at[pl.ds(0, (C - 1) * r)], s_ua)
        drain(q_g.at[0, 0], s_qa)
    for k in range(p.m):

        @pl.when(out_owner(k) != me)
        def _():
            drain(o_g.at[k, 0], s_oa.at[k])

    for j in range(S):
        own_b, own_c = down_owner(j)

        @pl.when(jnp.logical_not((own_b == b) & (own_c == c)))
        def _():
            drain(d_parts.at[0], s_d.at[j])

    for k in range(A):
        drain(from_sib.at[0], s_s.at[1, k])
    for j in range(2):
        for k in range(A):
            drain(from_x.at[0, 0], s_x.at[j, k])

            @pl.when(k != a)
            def _():
                drain(from_x.at[0, 0], s_c.at[j, k])


def back(p, *args):
    dma = pltpu.SemaphoreType.DMA
    A, S, C, X, r, R = p.A, p.S, p.C, p.X, p.r, p.R
    L = C * p.tok
    vm = pltpu.VMEM
    hbm = pl.BlockSpec(memory_space=pl.ANY)
    vmem = pl.BlockSpec(memory_space=pltpu.VMEM)
    groups = max(S - 1, 1)
    return pl.pallas_call(
        functools.partial(back_kernel, p),
        out_shape=(
            jax.ShapeDtypeStruct((p.tok, p.d), F32),
            jax.ShapeDtypeStruct((p.tok, p.d), F32),
            jax.ShapeDtypeStruct((r, 3 * p.d), BF),
            jax.ShapeDtypeStruct((r, p.ff), BF),
            jax.ShapeDtypeStruct((S, R, p.d), BF),
            jax.ShapeDtypeStruct((S, r, p.d), BF),
            jax.ShapeDtypeStruct((p.n, 16, LANES), F32),
            jax.ShapeDtypeStruct((A - 1, C * r, p.ffl), BF),
            jax.ShapeDtypeStruct((A - 1, X, r, p.hc), BF),
            jax.ShapeDtypeStruct((p.rows, p.d), BF),
        ),
        input_output_aliases={3: 9},
        in_specs=[hbm] * 10 + [vmem],
        out_specs=[vmem] * 2 + [hbm] * 8,
        scratch_shapes=[
            vm((max(p.rows, p.d), p.ffl), BF),
            vm((p.rows // 2, HEAD_DIM), BF),
            vm((p.rows, p.ffl), BF),
            vm((2, TILE, p.d), BF),
            vm((p.rows // 2, p.hc), BF),
            vm((p.ffl + HEAD_DIM, p.d), BF),
            vm((p.d, p.ffl), BF),
            vm((p.d, p.hc), BF),
            vm((2, p.rows, TILE), BF),
            vm((p.ffl, p.rows), BF),
            vm((HEAD_DIM, p.rows // 2), BF),
            vm((p.rows // 2, HEAD_DIM), BF),
            vm((L, LANES), F32),
            vm((L, LANES), F32),
            vm((2, A, X, p.tok, p.d), BF),
            vm((A, X, p.tok, p.d), BF),
            vm((A, X, p.tok, p.d), BF),
            vm((2, A, p.tok, p.d), BF),
            vm((2, 4, p.tok, p.d), BF),
            vm((p.ffl, p.d), BF),
            vm((A * S * X, 2, r, p.hc), BF),
            vm((A * S * X, r, p.hc), BF),
            vm((groups, A, X, r, p.hc), BF),
            vm((p.m, 2, r, p.d), BF),
            vm((p.m, r, p.d), BF),
            vm((groups, A, C * r, p.ffl), BF),
            vm((1, p.d), F32),
            vm((16, LANES), F32),
            dma((8,)),
            dma((2,)),
            dma((2,)),
            dma,
            dma,
            dma((2, A)),
            dma((2, A)),
            dma((2, A)),
            dma((2, A)),
            dma((2, A)),
            dma((2, 4)),
            dma,
            dma,
            dma,
            dma,
            dma,
            dma,
            dma,
            dma,
            dma,
            dma,
            dma((p.m,)),
            dma,
            dma,
            dma,
            dma,
            dma,
            dma,
            dma,
            dma((S,)),
            dma,
            dma((2,)),
            dma((2,)),
            pltpu.SemaphoreType.REGULAR,
        ],
        compiler_params=pltpu.CompilerParams(
            collective_id=1, has_side_effects=True, vmem_limit_bytes=67043328
        ),
        name="back",
    )(*args)


def finish_kernel(
    p,
    lens,
    x,
    g,
    o_sum,
    e_sum,
    full,
    q_part,
    u_part,
    d_parts,
    o_parts,
    sums,
    qkv_w,
    up_w,
    gain1,
    bias1,
    gain2,
    bias2,
    out,
    grad,
    q_grad,
    u_grad,
    d_grad,
    o_grad,
    q_own,
    u_own,
    g_own,
    g_same,
    gain1_grad,
    bias1_grad,
    gain2_grad,
    bias2_grad,
    q_bias,
    u_bias,
    g_bias,
    row_sums,
):
    A, S, C, X = p.A, p.S, p.C, p.X
    step = pl.program_id(0)

    @pl.when(step == 0)
    def _():
        up_row = p.hc // LANES
        g_row = up_row + p.ffl // LANES
        share = p.d // (A * C)
        for aa in range(A):
            for cc in range(C):
                for row in range(up_row, g_row + 1):
                    total = sums[aa * S * C + cc, row : row + 1, :]
                    for bb in range(1, S):
                        total = total + sums[(aa * S + bb) * C + cc, row : row + 1, :]
                    if row == g_row:
                        at = (aa * C + cc) * share
                        g_bias[:, at : at + share] = total[:, :share]
                        continue
                    unit = (row - up_row) * LANES
                    run = unit // p.W
                    if p.P == 1:
                        first = p.R * ((aa * S + run) * C + cc)
                    else:
                        first = p.R * ((aa * S + 2 * run + cc % 2) * C + cc // 2 * 2)
                    at = first + unit % p.W
                    u_bias[:, at : at + LANES] = total
            for xx in range(X):
                for row in range(up_row):
                    total = jnp.zeros((1, LANES), F32)
                    for bb in range(S):
                        for kk in range(2):
                            total = total + sums[(aa * S + bb) * C + xx * 2 + kk, row : row + 1, :]
                    j, rest = row * LANES // HEAD_DIM, row * LANES % HEAD_DIM
                    at = j * p.d + (aa * X + xx) * HEAD_DIM + rest
                    q_bias[:, at : at + LANES] = total
        me = lax.axis_index("dp") * C + lax.axis_index("ctx")

        def own(vector, size):
            span = max(size * i % LANES + size for i in range(p.n))
            span = (span + LANES - 1) // LANES * LANES
            rest = lax.rem(size * me, LANES)
            at = pl.multiple_of(size * me - rest, LANES)
            piece = pltpu.roll(vector[:, pl.ds(at, span)], lax.rem(span - rest, span), 1)
            return piece[0, :size]

        q_own[...] = own(q_bias, 3 * p.d // p.n)
        u_own[...] = own(u_bias, p.ff // p.n)
        g_own[...] = own(g_bias, p.d // p.n)
        g_same[...] = own(g_bias, p.d // p.n)

    rows = x.shape[0]
    sub = 32
    first = lax.axis_index("ctx") * p.tok + step * rows
    length = lens[0]

    def tokens(at):
        here = pl.ds(at, sub)
        row = lax.broadcasted_iota(jnp.int32, (sub, p.d), 0) + (at + first)
        live = row < length
        xf = x[here, :].astype(F32)
        total = xf + o_sum[here, :] + full[4:5, :]
        out[here, :] = jnp.where(live, total, 0.0).astype(BF)
        mid = xf - jnp.mean(xf, axis=1, keepdims=True)
        inv = lax.rsqrt(jnp.mean(mid * mid, axis=1, keepdims=True) + EPS)
        xhat = mid * inv
        e = e_sum[here, :]
        e_mean = jnp.mean(e, axis=1, keepdims=True)
        dx = inv * (e - e_mean - xhat * jnp.mean(e * xhat, axis=1, keepdims=True))
        go = jnp.where(live, g[here, :].astype(F32), 0.0)
        grad[here, :] = (go + dx).astype(BF)

    tiles(rows, tokens, sub)

    count = q_part.shape[0]
    lane = lax.broadcasted_iota(jnp.int32, (count, LANES), 1)
    kept = jnp.zeros((count, LANES), F32)
    for k, (part, weight, bias, result) in enumerate(
        ((q_part, qkv_w, q_bias, q_grad), (u_part, up_w, u_bias, u_grad))
    ):
        with_grad = jnp.zeros((part.shape[0], LANES), F32)
        with_bias = jnp.zeros((part.shape[0], LANES), F32)
        for n in range(0, part.shape[1], LANES):
            at = slice(n, n + LANES)
            value = part[:, at].astype(F32)
            result[:, at] = value
            w = weight[:, at].astype(F32)
            with_grad = with_grad + w * value
            with_bias = with_bias + w * bias[:, at]
        for o, t in enumerate((with_grad, with_bias)):
            kept = jnp.where(lane == 2 * k + o, jnp.sum(t, axis=1, keepdims=True), kept)
    row_sums[pl.ds(pl.multiple_of(step * count, count), count), :] = kept

    @pl.when(step == pl.num_programs(0) - 1)
    def _():
        turned = row_sums[...].T
        for k, (gain, shift, to_gain, to_shift) in enumerate(
            ((gain1, bias1, gain1_grad, bias1_grad), (gain2, bias2, gain2_grad, bias2_grad))
        ):
            with_grad, with_bias = turned[2 * k, : p.r], turned[2 * k + 1, : p.r]
            to_gain[...] = (with_grad - shift[...].astype(F32) * with_bias) / gain[...].astype(F32)
            to_shift[...] = with_bias

    for parts, result in ((d_parts, d_grad), (o_parts, o_grad)):

        size = min(sub, result.shape[0])

        def add(at):
            here = pl.ds(at, size)
            total = parts[0, here, :].astype(F32)
            for k in range(1, S):
                total = total + parts[k, here, :].astype(F32)
            result[here, :] = total

        tiles(result.shape[0], add, size)


def finish(p, *args):
    steps = max(1, p.r // 32)
    D, r, R = p.d, p.r, p.R

    def rows(count, width):
        return pl.BlockSpec((count // steps, width), lambda i: (i, 0))

    def parts(count):
        return pl.BlockSpec((p.S, count // steps, D), lambda i: (0, i, 0))

    def whole(*shape):
        return pl.BlockSpec(shape, lambda i: (0,) * len(shape))

    tok = rows(p.tok, D)
    return pl.pallas_call(
        functools.partial(finish_kernel, p),
        grid=(steps,),
        out_shape=(
            jax.ShapeDtypeStruct((p.tok, D), BF),
            jax.ShapeDtypeStruct((p.tok, D), BF),
            jax.ShapeDtypeStruct((r, 3 * D), F32),
            jax.ShapeDtypeStruct((r, p.ff), F32),
            jax.ShapeDtypeStruct((R, D), F32),
            jax.ShapeDtypeStruct((r, D), F32),
            jax.ShapeDtypeStruct((3 * D // p.n,), F32),
            jax.ShapeDtypeStruct((p.ff // p.n,), F32),
            *[jax.ShapeDtypeStruct((r,), F32)] * 6,
        ),
        in_specs=[
            pl.BlockSpec(memory_space=pltpu.SMEM),
            tok,
            tok,
            tok,
            tok,
            whole(8, D),
            rows(r, 3 * D),
            rows(r, p.ff),
            parts(R),
            parts(r),
            whole(p.n, 16, LANES),
            rows(r, 3 * D),
            rows(r, p.ff),
            *[whole(r)] * 4,
        ],
        out_specs=[
            tok,
            tok,
            rows(r, 3 * D),
            rows(r, p.ff),
            rows(R, D),
            rows(r, D),
            whole(3 * D // p.n),
            whole(p.ff // p.n),
            *[whole(r)] * 6,
        ],
        scratch_shapes=[
            pltpu.VMEM((1, 3 * D), F32),
            pltpu.VMEM((1, p.ff), F32),
            pltpu.VMEM((1, D), F32),
            pltpu.VMEM((r, LANES), F32),
        ],
        compiler_params=pltpu.CompilerParams(dimension_semantics=("arbitrary",)),
        name="finish",
    )(*args)


def local(
    dp_size,
    ctx_size,
    layer_input,
    lengths,
    cotangent,
    qkv_weight,
    qkv_bias,
    out_weight,
    out_bias,
    up_weight,
    up_bias,
    down_weight,
    down_bias,
    first_gain,
    first_bias,
    second_gain,
    second_bias,
):
    tok, d = layer_input.shape
    ff = up_weight.shape[1]
    p = Plan(dp_size, ctx_size, tok, d, ff)
    A, S, C, X, r, R = p.A, p.S, p.C, p.X, p.r, p.R
    dp, c, a, b, xh, core = place(p)
    me = dp * C + c
    t = a * C + c
    vectors = (
        qkv_bias,
        out_bias,
        up_bias,
        down_bias,
        first_gain,
        first_bias,
        second_gain,
        second_bias,
    )
    (_, g_all, qw, dw, uw, _, n1, n2, hid, slope, heads, joint, full) = front(
        p,
        layer_input,
        cotangent,
        qkv_weight,
        out_weight,
        up_weight,
        down_weight,
        lengths,
        *vectors,
    )
    o_sum, e_sum, q_out, u_out, d_parts, o_parts, v_all, _, _, _ = back(
        p,
        hid,
        heads,
        slope,
        g_all.reshape(p.rows, d),
        joint,
        n1,
        n2,
        dw,
        uw.reshape(d, p.ffl),
        qw.reshape(d, p.hc),
        full,
    )
    (
        output,
        input_grad,
        q_grad,
        u_grad,
        d_grad,
        o_grad,
        q_bias,
        u_bias,
        g_bias,
        g_same,
        gain1_grad,
        bias1_grad,
        gain2_grad,
        bias2_grad,
    ) = finish(
        p,
        lengths,
        layer_input,
        cotangent,
        o_sum,
        e_sum,
        full,
        q_out,
        u_out,
        d_parts,
        o_parts,
        v_all,
        qkv_weight,
        up_weight,
        first_gain,
        first_bias,
        second_gain,
        second_bias,
    )
    return (
        output,
        input_grad,
        q_grad,
        q_bias,
        o_grad,
        g_bias,
        u_grad,
        u_bias,
        d_grad,
        g_same,
        gain1_grad,
        bias1_grad,
        gain2_grad,
        bias2_grad,
    )


def solution(mesh):
    rows = P(("dp", "ctx"), None)
    vector = P(("dp", "ctx"))
    return jax.shard_map(
        functools.partial(local, mesh.shape["dp"], mesh.shape["ctx"]),
        mesh=mesh,
        in_specs=(
            rows,
            P("dp"),
            rows,
            rows,
            vector,
            rows,
            vector,
            rows,
            vector,
            rows,
            vector,
            vector,
            vector,
            vector,
            vector,
        ),
        out_specs=(
            rows,
            rows,
            rows,
            vector,
            rows,
            vector,
            rows,
            vector,
            rows,
            vector,
            vector,
            vector,
            vector,
            vector,
        ),
        check_vma=False,
    )
```

```python
import functools
import math

import jax
import jax.numpy as jnp
from jax import lax
from jax.experimental import pallas as pl
from jax.experimental.pallas import tpu as pltpu
from jax.sharding import PartitionSpec as P

HEADS = 8
HEAD_DIM = 256
ROT = 64
EPS = 1e-05
SCALE = 1.0 / math.sqrt(HEAD_DIM)
MESH = pl.DeviceIdType.MESH
BF = jnp.bfloat16
F32 = jnp.float32
TILE = 256
LANES = 128


class Plan:
    def __init__(self, dp, ctx, tok, d, ff):
        self.C = ctx
        self.X = ctx // 2
        self.A = HEADS // self.X
        self.S = dp // self.A
        self.n = dp * ctx
        self.tok = tok
        self.d = d
        self.ff = ff
        self.r = d // self.n
        self.R = ff // self.n
        self.ffl = self.S * self.R
        self.W = max(self.R, 128)
        self.P = self.W // self.R
        self.hc = 3 * HEAD_DIM
        self.m = HEAD_DIM // self.r // 2
        self.rows = self.A * self.C * tok


def remote(src, dst, send, recv, dev):
    return pltpu.make_async_remote_copy(
        src_ref=src, dst_ref=dst, send_sem=send, recv_sem=recv, device_id=dev, device_id_type=MESH
    )


def drain(ref, sem):
    pltpu.make_async_copy(ref, ref, sem).wait()


def unit_run(p, aa, cc, j):
    if p.P == 1:
        return p.R * ((aa * p.S + j) * p.C + cc)
    return p.R * ((aa * p.S + 2 * j + lax.rem(cc, 2)) * p.C + lax.div(cc, 2) * 2)


def unit_home(p, b, xh, core):
    if p.P == 1:
        return xh * 2 + core, b * p.R
    return xh * 2 + lax.rem(b, 2), (lax.div(b, 2) * 2 + core) * p.R


def place(p):
    dp = lax.axis_index("dp")
    c = lax.axis_index("ctx")
    a = lax.div(dp, p.S)
    b = lax.rem(dp, p.S)
    xh = lax.div(c, 2)
    core = lax.rem(c, 2)
    return dp, c, a, b, xh, core


def greet_all(p, me):
    barrier = pltpu.get_barrier_semaphore()

    def greet(k, carry):
        other = lax.rem(me + k, p.n)
        pl.semaphore_signal(
            barrier,
            inc=1,
            device_id=(lax.div(other, p.C), lax.rem(other, p.C)),
            device_id_type=MESH,
        )
        return carry

    lax.fori_loop(1, p.n, greet, 0)
    pl.semaphore_wait(barrier, p.n - 1)


def dot(x, y):
    return jnp.dot(x, y, preferred_element_type=F32)


def dot_t(x, y):
    return lax.dot_general(x, y, (((1,), (1,)), ((), ())), preferred_element_type=F32)


def t_dot(x, y):
    return lax.dot_general(x, y, (((0,), (0,)), ((), ())), preferred_element_type=F32)


def tiles(count, body, size=TILE):
    def run(i, carry):
        body(pl.multiple_of(i * size, size))
        return carry

    lax.fori_loop(0, count // size, run, 0)


def pick(values, i):
    out = values[0]
    for k in range(1, len(values)):
        out = jnp.where(i == k, values[k], out)
    return out


def far_order(p, a):
    order = []
    lo, hi = 0, p.A - 1
    for _ in range(p.A):
        up_far = hi - a >= a - lo
        order.append(jnp.where(up_far, hi, lo))
        lo = jnp.where(up_far, lo, lo + 1)
        hi = jnp.where(up_far, hi - 1, hi)
    return order


def add_rows(dst, parts, rows):
    step = 16

    def body(k, carry):
        at = pl.ds(pl.multiple_of(k * step, step), step)
        total = parts[0][at, :].astype(F32)
        for part in parts[1:]:
            total = total + part[at, :].astype(F32)
        dst[at, :] = total.astype(dst.dtype)
        return carry

    lax.fori_loop(0, rows // step, body, 0)


def angle_tables(cos_v, sin_v):
    rows = cos_v.shape[0]
    half = ROT // 2

    def body(at):
        shape = (64, LANES)
        lane = lax.broadcasted_iota(jnp.int32, shape, 1)
        pos = (lax.broadcasted_iota(jnp.int32, shape, 0) + at).astype(F32)
        exponent = lax.rem(lane, half).astype(F32) * (-2.0 * math.log(10000.0) / ROT)
        angle = pos * jnp.exp(exponent)
        turned = lane < ROT
        sign = jnp.where(lane < half, -1.0, 1.0)
        cos_v[pl.ds(at, 64), :] = jnp.where(turned, jnp.cos(angle), 1.0)
        sin_v[pl.ds(at, 64), :] = jnp.where(turned, jnp.sin(angle) * sign, 0.0)

    tiles(rows, body, 64)


def turn(v, cos, sin):
    first = v[:, :LANES]
    half = ROT // 2
    lane = lax.broadcasted_iota(jnp.int32, first.shape, 1)
    partner = jnp.where(
        lane < half, pltpu.roll(first, LANES - half, 1), pltpu.roll(first, half, 1)
    )
    return jnp.concatenate([first * cos + partner * sin, v[:, LANES:]], axis=1)


def probabilities(q, k, row0, scale):
    scores = dot_t(q, k) * scale
    row = lax.broadcasted_iota(jnp.int32, scores.shape, 0) + row0
    col = lax.broadcasted_iota(jnp.int32, scores.shape, 1)
    scores = jnp.where(col <= row, scores, -1e30)
    expo = jnp.exp(scores - jnp.max(scores, axis=1, keepdims=True))
    return expo / jnp.sum(expo, axis=1, keepdims=True)


def front_kernel(
    p,
    x,
    g,
    qkv,
    outw,
    up,
    down,
    lens,
    qkv_b,
    out_b,
    up_b,
    down_b,
    gain1,
    bias1,
    gain2,
    bias2,
    xa,
    ga,
    qw,
    dw,
    uw,
    sm,
    n1,
    n2,
    hid,
    slope,
    heads,
    joint,
    rows_out,
    small,
    pads,
    g_v,
    gm,
    sm_v,
    vecs,
    ub,
    qb,
    cos_v,
    sin_v,
    uw_v,
    qw_v,
    xs,
    n1_v,
    n2_v,
    hid_v,
    slope_v,
    heads_v,
    joint_v,
    ux,
    qx,
    loc,
    puts,
    s_ux,
    r_ux,
    s_qx,
    r_qx,
    s_sm,
    r_sm,
    s_up,
    r_up,
    s_upb,
    r_upb,
    s_q,
    r_q,
    s_qb,
    r_qb,
    s_qc,
    r_qc,
    s_o,
    r_o,
    s_ob,
    s_oc,
    r_oc,
    s_d,
    r_d,
    s_r,
    r_r,
    s_l,
    r_l,
    s_x,
    r_x,
    s_s,
    r_s,
):
    A, S, C, r, R = p.A, p.S, p.C, p.r, p.R
    dp, c, a, b, xh, core = place(p)
    me = dp * C + c
    t = a * C + c
    head = a * p.X + xh
    sib = (dp, xh * 2 + 1 - core)
    xnb = (dp, (1 - xh) * 2 + core)
    right = (dp + S, c)
    left = (dp - S, c)
    L = C * p.tok
    half = A // 2

    get_g = pltpu.make_async_copy(g, g_v, loc.at[2])
    get_g.start()
    vectors = (qkv_b, up_b, gain1, bias1, gain2, bias2, out_b)
    greet_all(p, me)

    own_small = pltpu.make_async_copy(small, sm.at[me], loc.at[0])
    own_x = pltpu.make_async_copy(x, xa.at[a, pl.ds(pl.multiple_of(c * p.tok, p.tok), p.tok)], loc.at[1])
    own_x.start()
    own_g = pltpu.make_async_copy(gm, ga.at[a, pl.ds(pl.multiple_of(c * p.tok, p.tok), p.tok)], loc.at[2])

    row_head = lax.div(me * r, HEAD_DIM)
    row_part = lax.div(lax.rem(me * r, HEAD_DIM), 2 * r)
    o_dp, o_ctx = lax.div(row_head, p.X) * S + b, lax.rem(row_head, p.X) * 2 + core
    o_here = (o_dp == dp) & (o_ctx == c)

    def o_rows(k, cc):
        return dw.at[pl.ds(pl.multiple_of(p.ffl + (2 * k + cc) * r, r), r)]

    def o_first(k):
        owner = lax.div(head * HEAD_DIM, r) + 2 * k + core
        return lax.rem(lax.div(owner, C), S) == b

    streams = ((x, xa), (gm, ga))

    def blk(j, k, cc):
        return streams[j][1].at[k, pl.ds(pl.multiple_of(cc * p.tok, p.tok), p.tok)]

    def send_z(j):
        own, slot = streams[j][0], blk(j, a, c)

        @pl.when(a < A - 1)
        def _():
            remote(own, slot, s_r.at[j, 0], r_r.at[j, 0], right).start()

        @pl.when(a > 0)
        def _():
            remote(own, slot, s_l.at[j, 0], r_l.at[j, 0], left).start()

    def send_x(j):
        own, slot = streams[j][0], blk(j, a, c)
        remote(own, slot, s_x.at[j, a], r_x.at[j, a], xnb).start()
        remote(own, slot, s_s.at[j, a], r_s.at[j, a], sib).start()

    last_slot = jnp.where(a < A // 2, A - 1, 0)

    def send_on(j, k, part):
        if j == 0:
            remote(part, part, s_x.at[j, k], r_x.at[j, k], xnb).start()
        else:

            @pl.when(k != last_slot)
            def _():
                remote(part, part, s_x.at[j, k], r_x.at[j, k], xnb).start()

        remote(part, part, s_s.at[j, k], r_s.at[j, k], sib).start()

    def z_step(j, s):
        @pl.when(a - 1 - s >= 0)
        def _():
            k = a - 1 - s
            part = blk(j, k, c)
            drain(part, r_r.at[j, s])

            @pl.when((s + 1 < A - 1) & (a < A - 1))
            def _():
                nxt = jnp.minimum(s + 1, A - 2)
                remote(part, part, s_r.at[j, nxt], r_r.at[j, nxt], right).start()

            send_on(j, k, part)

        @pl.when(a + 1 + s <= A - 1)
        def _():
            k = a + 1 + s
            part = blk(j, k, c)
            drain(part, r_l.at[j, s])

            @pl.when((s + 1 < A - 1) & (a > 0))
            def _():
                nxt = jnp.minimum(s + 1, A - 2)
                remote(part, part, s_l.at[j, nxt], r_l.at[j, nxt], left).start()

            send_on(j, k, part)

    xc = (1 - xh) * 2 + core

    def cross(j, k):
        part = blk(j, k, xc)
        drain(part, r_x.at[j, k])
        remote(part, part, s_s.at[j, k], r_s.at[j, k], sib).start()

    runs = p.ffl // p.W

    def up_cols(aa, cc, j):
        return up.at[:, pl.ds(pl.multiple_of(unit_run(p, aa, cc, j), LANES), p.W)]

    def up_over(i, carry):
        aa, kk = lax.div(i, 2), lax.rem(i, 2)
        for j in range(runs):
            dst = ux.at[aa, kk, :, pl.ds(j * p.W, p.W)]
            remote(up_cols(aa, (1 - xh) * 2 + kk, j), dst, s_ux, r_ux, xnb).start()
        return carry

    def up_along(i, carry):
        aa, kk = lax.rem(a + 1 + lax.div(i, 2), A), lax.rem(i, 2)
        cc = xh * 2 + kk
        here = (aa == a) & (kk == core)
        for j in range(runs):
            dst = uw.at[a, b, c, :, pl.ds(j * p.W, p.W)]

            @pl.when(jnp.logical_not(here))
            def _():
                remote(up_cols(aa, cc, j), dst, s_up, r_up, (aa * S + b, cc)).start()

            @pl.when(here)
            def _():
                pltpu.make_async_copy(up_cols(aa, cc, j), dst, r_up).start()

        return carry

    def up_onward(i, carry):
        aa, kk = lax.rem(a + 1 + lax.div(i, 2), A), lax.rem(i, 2)
        here = (aa == a) & (kk == core)
        src, dst = ux.at[aa, kk], uw.at[a, b, (1 - xh) * 2 + core]

        @pl.when(jnp.logical_not(here))
        def _():
            remote(src, dst, s_up, r_up, (aa * S + b, xh * 2 + kk)).start()

        @pl.when(here)
        def _():
            pltpu.make_async_copy(src, dst, r_up).start()

        return carry

    def q_cols(aa, xx, j):
        col = pl.multiple_of(j * p.d + (aa * p.X + xx) * HEAD_DIM, HEAD_DIM)
        return qkv.at[:, pl.ds(col, HEAD_DIM)]

    def q_over(aa, carry):
        for j in range(3):
            dst = qx.at[aa, :, pl.ds(j * HEAD_DIM, HEAD_DIM)]
            remote(q_cols(aa, 1 - xh, j), dst, s_qx, r_qx, xnb).start()
        return carry

    def q_along(i, carry):
        aa = lax.rem(a + 1 + i, A)
        for j in range(3):
            dst = qw.at[a, b, xh, core, :, pl.ds(j * HEAD_DIM, HEAD_DIM)]

            @pl.when(aa != a)
            def _():
                remote(q_cols(aa, xh, j), dst, s_q, r_q, (aa * S + b, c)).start()

            @pl.when(aa == a)
            def _():
                pltpu.make_async_copy(q_cols(aa, xh, j), dst, r_q).start()

        return carry

    def q_onward(i, carry):
        aa = lax.rem(a + 1 + i, A)
        src, dst = qx.at[aa], qw.at[a, b, 1 - xh, core]

        @pl.when(aa != a)
        def _():
            remote(src, dst, s_q, r_q, (aa * S + b, c)).start()

        @pl.when(aa == a)
        def _():
            pltpu.make_async_copy(src, dst, r_q).start()

        return carry

    def up_cross(k, carry):
        bb = lax.rem(b + k, S)
        remote(uw.at[:, b], uw.at[:, b], s_upb, r_upb, (a * S + bb, c)).start()
        return carry

    def q_cross(k, carry):
        bb = lax.rem(b + k, S)
        part = qw.at[:, b, :, core]
        remote(part, part, s_qb, r_qb, (a * S + bb, c)).start()
        return carry

    def slot_rows(k):
        return pl.ds(pl.multiple_of(k * L, L), L)

    near = far_order(p, a)[::-1]

    def norm_slot(i):
        k = near[i]
        drain(xa.at[k, pl.ds(0, p.X * p.tok)], r_s.at[0, k])
        get = pltpu.make_async_copy(xa.at[k], xs, loc.at[3])
        get.start()
        get.wait()
        mine = lax.div(k, half) == core
        step = 32

        def unit_rows(at):
            rows = xs[pl.ds(at, step), :].astype(F32)
            rows = rows - jnp.mean(rows, axis=1, keepdims=True)
            spread = jnp.mean(rows * rows, axis=1, keepdims=True)
            rows = rows * lax.rsqrt(spread + EPS)
            to = pl.multiple_of(k * L + at, step)
            n2_v[pl.ds(to, step), :] = (rows * vecs[2:3, :] + vecs[3:4, :]).astype(BF)
            return rows

        @pl.when(mine)
        def _():
            def both(at):
                rows = unit_rows(at)
                to = pl.multiple_of(lax.rem(k, half) * L + at, step)
                n1_v[pl.ds(to, step), :] = (rows * vecs[0:1, :] + vecs[1:2, :]).astype(BF)

            tiles(L, both, step)

        @pl.when(jnp.logical_not(mine))
        def _():
            def one(at):
                unit_rows(at)

            tiles(L, one, step)

        pltpu.make_async_copy(n2_v.at[slot_rows(k)], n2.at[slot_rows(k)], puts.at[i]).start()

    def units(i):
        k = near[i]

        def unit_tile(n):
            at = pl.ds(n, TILE)
            w = uw_v[:, :, :, :, at].reshape(p.d, TILE)
            v = dot(n2_v[slot_rows(k), :], w) + ub[:, at]
            phi = 0.5 * (1.0 + lax.erf(v * (1.0 / math.sqrt(2.0))))
            density = jnp.exp(-0.5 * v * v) * (1.0 / math.sqrt(2.0 * math.pi))
            hid_v[slot_rows(k), at] = (v * phi).astype(BF)
            slope_v[slot_rows(k), at] = (phi + v * density).astype(BF)

        tiles(p.ffl, unit_tile)

    d_ctx, d_row = unit_home(p, b, xh, core)
    d_dst = dw.at[pl.ds(pl.multiple_of(d_row, R), R)]
    def small_all():
        def small_send(k, carry):
            other = lax.rem(me + k, p.n)
            dev = (lax.div(other, C), lax.rem(other, C))
            remote(small, sm.at[me], s_sm, r_sm, dev).start()
            return carry

        lax.fori_loop(1, p.n, small_send, 0)

    def down_all():
        for bb in range(S):
            here = (bb == b) & (d_ctx == c)

            @pl.when(jnp.logical_not(here))
            def _():
                remote(down, d_dst, s_d.at[bb], r_d, (a * S + bb, d_ctx)).start()

            @pl.when(here)
            def _():
                pltpu.make_async_copy(down, d_dst, r_d).start()

    def out_send():
        @pl.when(jnp.logical_not(o_here))
        def _():
            remote(outw, o_rows(row_part, core), s_o, r_o.at[row_part], (o_dp, o_ctx)).start()

        @pl.when(o_here)
        def _():
            pltpu.make_async_copy(outw, o_rows(row_part, core), r_o.at[row_part]).start()

    def chunk(which, jj):
        size = vectors[which].shape[0]
        if size % LANES == 0:
            count = 1
        elif LANES % size == 0:
            count = LANES // size
        else:
            count = (LANES - 1) // size + 2
        total = jnp.zeros((1, LANES), F32)
        for o in range(count):
            i = lax.div(LANES * jj, size) + o
            row = jj - lax.div(i * size, LANES)
            good = ((row >= 0) & (row <= 1) & (i < p.n)).astype(F32)
            at = 2 * which + jnp.clip(row, 0, 1)
            total = total + good * sm_v[jnp.minimum(i, p.n - 1), pl.ds(at, 1), :]
        return total

    def vectors_whole():
        own_small.wait()
        drain(sm.at[pl.ds(0, p.n - 1)], r_sm)
        get_small = pltpu.make_async_copy(sm, sm_v, loc.at[0])
        get_small.start()
        get_small.wait()

        def fill(jj, carry):
            for k in range(5):
                vecs[k : k + 1, pl.ds(pl.multiple_of(jj * LANES, LANES), LANES)] = chunk(2 + k, jj)
            return carry

        lax.fori_loop(0, p.d // LANES, fill, 0)
        for j in range(p.ffl // LANES):
            run, rest = j * LANES // p.W, (j * LANES % p.W) // LANES
            first = lax.div(unit_run(p, a, c, run), LANES) + rest
            ub[:, j * LANES : (j + 1) * LANES] = chunk(1, first)
        for j in range(3):
            for k in range(HEAD_DIM // LANES):
                first = (j * p.d + head * HEAD_DIM) // LANES + k
                at = j * HEAD_DIM + k * LANES
                qb[:, at : at + LANES] = chunk(0, first)

    def out_onward(k):
        remote(o_rows(k, core), o_rows(k, core), s_oc.at[k], r_oc.at[k], sib).start()

    def out_first():
        for k in range(p.m):

            @pl.when(o_first(k))
            def _():
                drain(o_rows(k, core), r_o.at[k])

                def o_cross(kk, carry):
                    bb = lax.rem(b + kk, S)
                    rows = o_rows(k, core)
                    remote(rows, rows, s_ob.at[k], r_o.at[k], (a * S + bb, c)).start()
                    return carry

                lax.fori_loop(1, S, o_cross, 0)
                out_onward(k)

    def out_rest():
        for k in range(p.m):

            @pl.when(jnp.logical_not(o_first(k)))
            def _():
                drain(o_rows(k, core), r_o.at[k])
                out_onward(k)

    def load_uw():
        for _ in range(S - 1):
            drain(uw.at[:, b], r_upb)
        get = pltpu.make_async_copy(uw, uw_v, loc.at[3])
        get.start()
        get.wait()

    def send_half_qw():
        for _ in range(S - 1):
            drain(qw.at[:, b, :, core], r_qb)
        part = qw.at[:, :, :, core]
        remote(part, part, s_qc, r_qc, sib).start()

    def load_qw():
        drain(qw.at[:, :, :, 1 - core], r_qc)
        get = pltpu.make_async_copy(qw, qw_v, loc.at[3])
        get.start()
        get.wait()

    def attend(i):
        own = pl.ds(pl.multiple_of(i * L, L), L)
        cols = [pl.ds(j * HEAD_DIM, HEAD_DIM) for j in range(3)]
        for j in range(3):
            w = qw_v[:, :, :, :, :, cols[j]].reshape(p.d, HEAD_DIM)
            v = dot(n1_v[own, :], w) + qb[:, cols[j]]
            if j < 2:
                v = turn(v, cos_v[...], sin_v[...])
            joint_v[own, cols[j]] = v.astype(BF)
        rows = L // 2
        for h in range(2):
            at = pl.ds(pl.multiple_of(i * L + h * rows, rows), rows)
            keys = pl.ds(pl.multiple_of(i * L, L), (h + 1) * rows)
            probs = probabilities(joint_v[at, cols[0]], joint_v[keys, cols[1]], h * rows, SCALE)
            heads_v[at, :] = dot(probs.astype(BF), joint_v[keys, cols[2]]).astype(BF)

    send_z(0)
    send_x(0)

    get_g.wait()
    length = lens[0]

    def mask(at):
        row = lax.broadcasted_iota(jnp.int32, (32, p.d), 0) + (at + c * p.tok)
        rows = g_v[pl.ds(at, 32), :].astype(F32)
        gm[pl.ds(at, 32), :] = jnp.where(row < length, rows, 0.0).astype(BF)

    tiles(p.tok, mask, 32)

    pads[...] = jnp.zeros_like(pads)
    for k, v in enumerate(vectors):
        value = v[...].astype(F32)
        if k == len(vectors) - 1:
            value = value + down_b[...].astype(F32)
        pads[k, 0 : v.shape[0]] = value
    for k, v in enumerate(vectors):
        placed = pltpu.roll(pads[k : k + 1, :], lax.rem(v.shape[0] * me, LANES), 1)
        small[2 * k : 2 * k + 1, :] = placed[:, :LANES]
        small[2 * k + 1 : 2 * k + 2, :] = placed[:, LANES:]
    small[2 * len(vectors) :, :] = jnp.zeros((2, LANES), F32)
    own_small.start()
    own_g.start()
    small_all()
    lax.fori_loop(0, 2 * A, up_over, 0)
    angle_tables(cos_v, sin_v)
    z_step(0, 0)
    cross(0, near[0])
    lax.fori_loop(0, 2 * A, up_along, 0)
    down_all()
    drain(ux, r_ux)
    lax.fori_loop(0, 2 * A, up_onward, 0)
    lax.fori_loop(0, A, q_over, 0)
    z_step(0, 1)
    cross(0, near[1])
    vectors_whole()
    own_x.wait()
    norm_slot(0)
    lax.fori_loop(0, A, q_along, 0)
    send_x(1)
    norm_slot(1)
    drain(qx, r_qx)
    lax.fori_loop(0, A, q_onward, 0)
    out_send()
    cross(0, near[2])
    send_z(1)
    drain(uw.at[:, b], r_up)
    lax.fori_loop(1, S, up_cross, 0)
    drain(qw.at[:, b, :, core], r_q)
    lax.fori_loop(1, S, q_cross, 0)
    norm_slot(2)
    z_step(0, 2)
    cross(1, near[0])
    out_first()
    cross(0, near[3])
    z_step(1, 0)
    norm_slot(3)
    put_n1 = pltpu.make_async_copy(n1_v, n1, loc.at[6])
    put_n1.start()
    put_rows = pltpu.make_async_copy(vecs, rows_out, loc.at[7])
    put_rows.start()
    load_uw()
    send_half_qw()
    units(0)
    z_step(1, 1)
    cross(1, near[1])
    units(1)
    load_qw()
    attend(0)
    units(2)
    z_step(1, 2)
    attend(1)
    cross(1, near[2])
    units(3)
    put_hid = pltpu.make_async_copy(hid_v, hid, loc.at[4])
    put_hid.start()
    put_slope = pltpu.make_async_copy(slope_v, slope, loc.at[5])
    put_slope.start()
    out_rest()

    put_heads = pltpu.make_async_copy(heads_v, heads, loc.at[0])
    put_heads.start()
    put_joint = pltpu.make_async_copy(joint_v, joint, loc.at[1])
    put_joint.start()

    drain(dw.at[pl.ds(0, p.ffl)], r_d)
    for k in range(p.m):
        drain(dw.at[pl.ds(0, r)], r_oc.at[k])
    for k in range(A):

        @pl.when(k != last_slot)
        def _():
            drain(ga.at[k, pl.ds(0, p.X * p.tok)], r_s.at[1, k])

        @pl.when(k == last_slot)
        def _():
            drain(ga.at[k, pl.ds(0, p.tok)], r_s.at[1, k])


    own_g.wait()
    put_hid.wait()
    put_slope.wait()
    put_n1.wait()
    put_rows.wait()
    put_heads.wait()
    put_joint.wait()
    for i in range(A):
        drain(n2_v.at[pl.ds(0, L)], puts.at[i])
    drain(sm.at[pl.ds(0, p.n - 1)], s_sm)
    drain(ux, s_ux)
    drain(qx, s_qx)
    for _ in range(4 * A - 2):
        drain(uw.at[a, b, c], s_up)
    for _ in range(2 * A - 2):
        drain(qw.at[a, b, xh, core], s_q)
    for bb in range(S):

        @pl.when(jnp.logical_not((bb == b) & (d_ctx == c)))
        def _():
            drain(down, s_d.at[bb])

    @pl.when(jnp.logical_not(o_here))
    def _():
        drain(outw, s_o)

    for k in range(p.m):

        @pl.when(o_first(k))
        def _():
            for _ in range(S - 1):
                drain(outw, s_ob.at[k])

    for k in range(p.m):
        drain(dw.at[pl.ds(0, r)], s_oc.at[k])
    for _ in range(S - 1):
        drain(uw.at[:, b], s_upb)
        drain(qw.at[:, b, :, core], s_qb)
    drain(qw.at[:, :, :, core], s_qc)
    for j in range(2):
        for s in range(A - 1):

            @pl.when((a < A - 1) & (a - s >= 0))
            def _():
                drain(x, s_r.at[j, s])

            @pl.when((a > 0) & (a + s <= A - 1))
            def _():
                drain(x, s_l.at[j, s])

        for k in range(A):
            if j == 0:
                drain(x, s_x.at[j, k])
                drain(xa.at[k, pl.ds(0, p.X * p.tok)], s_s.at[j, k])
                continue

            @pl.when(k != last_slot)
            def _():
                drain(x, s_x.at[j, k])
                drain(xa.at[k, pl.ds(0, p.X * p.tok)], s_s.at[j, k])

            @pl.when(k == last_slot)
            def _():
                drain(x, s_s.at[j, k])


def front(p, x, g, qkv, outw, up, down, lens, *vectors):
    dma = pltpu.SemaphoreType.DMA
    A, S, C, r = p.A, p.S, p.C, p.r
    L = C * p.tok
    vm = pltpu.VMEM
    hbm = pl.BlockSpec(memory_space=pl.ANY)
    vmem = pl.BlockSpec(memory_space=pltpu.VMEM)
    half = p.rows // 2
    qw_shape = (A, S, p.X, 2, r, p.hc)
    uw_shape = (A, S, C, r, p.ffl)
    return pl.pallas_call(
        functools.partial(front_kernel, p),
        out_shape=(
            jax.ShapeDtypeStruct((A, L, p.d), BF),
            jax.ShapeDtypeStruct((A, L, p.d), BF),
            jax.ShapeDtypeStruct(qw_shape, BF),
            jax.ShapeDtypeStruct((p.ffl + HEAD_DIM, p.d), BF),
            jax.ShapeDtypeStruct(uw_shape, BF),
            jax.ShapeDtypeStruct((p.n, 16, LANES), F32),
            jax.ShapeDtypeStruct((half, p.d), BF),
            jax.ShapeDtypeStruct((p.rows, p.d), BF),
            jax.ShapeDtypeStruct((p.rows, p.ffl), BF),
            jax.ShapeDtypeStruct((p.rows, p.ffl), BF),
            jax.ShapeDtypeStruct((half, HEAD_DIM), BF),
            jax.ShapeDtypeStruct((half, p.hc), BF),
            jax.ShapeDtypeStruct((8, p.d), F32),
        ),
        in_specs=[hbm] * 6 + [pl.BlockSpec(memory_space=pltpu.SMEM)] + [vmem] * 8,
        out_specs=[hbm] * 13,
        scratch_shapes=[
            vm((16, LANES), F32),
            vm((8, 2 * LANES), F32),
            vm((p.tok, p.d), BF),
            vm((p.tok, p.d), BF),
            vm((p.n, 16, LANES), F32),
            vm((8, p.d), F32),
            vm((1, p.ffl), F32),
            vm((1, p.hc), F32),
            vm((L, LANES), F32),
            vm((L, LANES), F32),
            vm(uw_shape, BF),
            vm(qw_shape, BF),
            vm((L, p.d), BF),
            vm((half, p.d), BF),
            vm((p.rows, p.d), BF),
            vm((p.rows, p.ffl), BF),
            vm((p.rows, p.ffl), BF),
            vm((half, HEAD_DIM), BF),
            vm((half, p.hc), BF),
            vm((A, 2, r, p.ffl), BF),
            vm((A, r, p.hc), BF),
            dma((8,)),
            dma((A,)),
            dma,
            dma,
            dma,
            dma,
            dma,
            dma,
            dma,
            dma,
            dma,
            dma,
            dma,
            dma,
            dma,
            dma,
            dma,
            dma,
            dma,
            dma((p.m,)),
            dma((p.m,)),
            dma((p.m,)),
            dma((p.m,)),
            dma((S,)),
            dma,
            dma((2, A - 1)),
            dma((2, A - 1)),
            dma((2, A - 1)),
            dma((2, A - 1)),
            dma((2, A)),
            dma((2, A)),
            dma((2, A)),
            dma((2, A)),
        ],
        compiler_params=pltpu.CompilerParams(
            collective_id=0, has_side_effects=True, vmem_limit_bytes=60 * 1024 * 1024
        ),
        name="front",
    )(x, g, qkv, outw, up, down, lens, *vectors)


def back_kernel(
    p,
    hid,
    heads,
    slope,
    g_in,
    joint,
    n1,
    n2,
    dw,
    uw,
    qw,
    gains,
    o_sum,
    e_sum,
    q_out,
    u_out,
    d_parts,
    o_parts,
    v_all,
    u_z,
    q_z,
    g,
    hid_v,
    heads_v,
    dpre,
    g_v,
    joint_v,
    dw_v,
    uw_v,
    qw_v,
    n_v,
    hid_t,
    heads_t,
    dh_v,
    cos_v,
    sin_v,
    own,
    to_sib,
    from_sib,
    from_x,
    came,
    dgrad,
    q_g,
    q_sib,
    q_group,
    o_g,
    o_sib,
    u_parts,
    g_sum,
    vec,
    loc,
    n_sem,
    g_sem,
    s_v,
    r_v,
    s_s,
    r_s,
    s_x,
    r_x,
    s_c,
    r_c,
    s_q,
    r_q,
    s_qb,
    r_qb,
    s_qz,
    r_qz,
    s_qa,
    r_qa,
    s_o,
    r_o,
    s_oa,
    r_oa,
    s_u,
    r_u,
    s_uz,
    r_uz,
    s_ua,
    r_ua,
    s_d,
    r_d,
    s_g,
    r_g,
    free,
):
    A, S, C, X, r, R = p.A, p.S, p.C, p.X, p.r, p.R
    dp, c, a, b, xh, core = place(p)
    me = dp * C + c
    t = a * C + c
    head = a * X + xh
    sib = (dp, xh * 2 + 1 - core)
    xnb = (dp, (1 - xh) * 2 + core)
    far = 1 - xh
    L = C * p.tok
    D, ffl = p.d, p.ffl
    half = A // 2
    ugrad = hid_v
    blk = C * r

    loads = [
        pltpu.make_async_copy(src, dst, loc.at[k])
        for k, (src, dst) in enumerate(
            (
                (hid, hid_v.at[pl.ds(0, p.rows)]),
                (dw, dw_v),
                (heads, heads_v),
                (joint, joint_v),
                (slope, dpre),
                (uw, uw_v),
                (qw, qw_v),
            )
        )
    ]
    for load in loads:
        load.start()
    greet_all(p, me)
    last_slot = jnp.where(a < half, A - 1, 0)

    def g_rows(cc):
        return g.at[pl.ds(pl.multiple_of(last_slot * L + cc * p.tok, p.tok), p.tok)]

    remote(g_rows(c), g_rows(c), s_g.at[0], r_g.at[0], xnb).start()
    x_ctx = far * 2 + core
    vec[...] = jnp.zeros_like(vec)
    angle_tables(cos_v, sin_v)

    def g_forward():
        drain(g_rows(x_ctx), r_g.at[0])
        remote(g_rows(x_ctx), g_rows(x_ctx), s_g.at[1], r_g.at[1], sib).start()

    low = a < half
    order = [
        jnp.where(low, A - 1, 0),
        jnp.where(low, A - 2, 1),
        jnp.where(low, 1 - a, A + 1 - a),
        a,
    ]
    inner = (a == 1) | (a == A - 2)

    def slot_rows(k):
        return pl.ds(pl.multiple_of(k * L, L), L)

    def blocks(src, base):
        rows = []
        for cc in (core, 1 - core):
            for side in range(X):
                at = pl.multiple_of(base + (side * 2 + cc) * p.tok, p.tok)
                rows.append(src[pl.ds(at, p.tok), :])
        return jnp.concatenate(rows, axis=0)

    def keep(j, k, n, acc):
        acc = acc.astype(BF)
        for side in range(X):
            own[j, k, side, :, pl.ds(n, TILE)] = acc[side * p.tok : (side + 1) * p.tok]
            to_sib[k, side, :, pl.ds(n, TILE)] = acc[
                (X + side) * p.tok : (X + side + 1) * p.tok
            ]

    def partial(j, i):
        k = order[i]
        mine = lax.div(k, half) == core
        base = pl.multiple_of(lax.rem(k, half) * L, L)
        if j == 0 and i == 0:
            for n in range(3):
                loads[n].wait()
        if j == 1:
            if i == 0:
                loads[5].wait()
                loads[6].wait()
                pl.semaphore_wait(free, 1)
            drain(from_sib.at[k], s_s.at[0, k])
        units = blocks(dpre if j else hid_v, k * L)

        @pl.when(mine)
        def _():
            heads_rows = blocks(joint_v if j else heads_v, base)

            def tile(n):
                at = pl.ds(n, TILE)
                if j == 0:
                    acc = dot(units, dw_v[0:ffl, at]) + dot(heads_rows, dw_v[ffl:, at])
                else:
                    acc = dot_t(units, uw_v[at, :]) * gains[2:3, at]
                    acc += dot_t(heads_rows, qw_v[at, :]) * gains[0:1, at]
                keep(j, k, n, acc)

            tiles(D, tile)

        @pl.when(jnp.logical_not(mine))
        def _():
            def tile(n):
                at = pl.ds(n, TILE)
                if j == 0:
                    acc = dot(units, dw_v[0:ffl, at])
                else:
                    acc = dot_t(units, uw_v[at, :]) * gains[2:3, at]
                keep(j, k, n, acc)

            tiles(D, tile)

        remote(to_sib.at[k], from_sib.at[k], s_s.at[j, k], r_s.at[j, k], sib).start()

    def chip_sum(j, k):
        drain(from_sib.at[k], r_s.at[j, k])
        mine = own.at[j, k, far]
        add_rows(mine, (mine, from_sib.at[k, far]), p.tok)
        remote(mine, from_x.at[j, k], s_x.at[j, k], r_x.at[j, k], xnb).start()
        mine = own.at[j, k, xh]
        add_rows(mine, (mine, from_sib.at[k, xh]), p.tok)

    def hop(j, i, joins):
        k = order[i]
        across = i < 2
        if joins:
            run = inner
        else:
            run = jnp.logical_not(inner) if across else a >= 0

        @pl.when(run)
        def _():
            drain(from_x.at[j, k], r_x.at[j, k])
            mine = own.at[j, k, xh]
            if joins:
                drain(came.at[j, 0], r_c.at[j, lax.rem(k, 2)])
                add_rows(mine, (mine, from_x.at[j, k], came.at[j, lax.rem(k, 2)]), p.tok)
                to, at = k, 2
            else:
                add_rows(mine, (mine, from_x.at[j, k]), p.tok)
                if across:
                    to, at = jnp.where(a == 0, 1, A - 2), lax.rem(k, 2)
                else:
                    to, at = k, 3
            dev = (to * S + b, c)
            remote(mine, came.at[j, at], s_c.at[j, k], r_c.at[j, at], dev).start()

    def last(j, total):
        drain(from_x.at[j, a], r_x.at[j, a])
        drain(came.at[j, 2], r_c.at[j, 2])
        drain(came.at[j, 3], r_c.at[j, 3])
        mine = own.at[j, a, xh]
        add_rows(total, (mine, from_x.at[j, a], came.at[j, 2], came.at[j, 3]), p.tok)

    def unit_grads():
        loads[4].wait()
        for k in range(A):
            rows = slice(k * L, (k + 1) * L)
            for f in range(ffl // TILE):
                at = slice(f * TILE, (f + 1) * TILE)
                hid_t[at, rows] = hid_v[rows, at].astype(F32).T.astype(BF)
        for k in range(half):
            rows = slice(k * L, (k + 1) * L)
            heads_t[:, rows] = heads_v[rows, :].astype(F32).T.astype(BF)

        def g_load(i, slot):
            at = pl.ds(pl.multiple_of(i * TILE, TILE), TILE)
            return pltpu.make_async_copy(g.at[at], g_v.at[slot], g_sem.at[slot])

        drain(g_rows(far * 2 + 1 - core), r_g.at[1])
        g_load(0, 0).start()

        def step(i, carry):
            slot = lax.rem(i, 2)
            g_load(i, slot).wait()

            @pl.when(i + 1 < p.rows // TILE)
            def _():
                g_load(i + 1, 1 - slot).start()

            rows = pl.ds(pl.multiple_of(i * TILE, TILE), TILE)
            for f in range(ffl // TILE):
                at = pl.ds(f * TILE, TILE)
                d_unit = dot_t(g_v[slot], dw_v[f * TILE : (f + 1) * TILE, :])
                dpre[rows, at] = (d_unit * dpre[rows, at].astype(F32)).astype(BF)
            first = core * half * L

            @pl.when((i * TILE >= first) & (i * TILE < first + half * L))
            def _():
                at = pl.ds(pl.multiple_of(i * TILE - first, TILE), TILE)
                dh_v[at, :] = dot_t(g_v[slot], dw_v[ffl:, :]).astype(BF)

            return carry

        lax.fori_loop(0, p.rows // TILE, step, 0)
        loads[3].wait()

    cols = [pl.ds(j * HEAD_DIM, HEAD_DIM) for j in range(3)]
    rows2 = L // 2

    def attend_back(i, carry):
        rows = pl.ds(pl.multiple_of(i * L, L), L)
        dq, dk, dv = [], [], []
        for h in range(2):
            at = pl.ds(pl.multiple_of(i * L + h * rows2, rows2), rows2)
            keys = pl.ds(pl.multiple_of(i * L, L), (h + 1) * rows2)
            q, k, v = joint_v[at, cols[0]], joint_v[keys, cols[1]], joint_v[keys, cols[2]]
            dh = dh_v[at, :]
            probs = probabilities(q, k, h * rows2, SCALE)
            d_probs = dot_t(dh, v)
            delta = jnp.sum(probs * d_probs, axis=1, keepdims=True)
            d_scores = (probs * (d_probs - delta)).astype(BF)
            dq.append(dot(d_scores, k) * SCALE)
            dk.append(t_dot(d_scores, q) * SCALE)
            dv.append(t_dot(probs.astype(BF), dh))
        dq = jnp.concatenate(dq, axis=0)
        dk = jnp.concatenate([dk[0] + dk[1][:rows2], dk[1][rows2:]], axis=0)
        dv = jnp.concatenate([dv[0] + dv[1][:rows2], dv[1][rows2:]], axis=0)
        cos, sin = cos_v[...], sin_v[...]
        for j, d_part in enumerate((turn(dq, cos, -sin), turn(dk, cos, -sin), dv)):
            low = d_part.astype(BF)
            joint_v[rows, cols[j]] = low
            sums = jnp.sum(low.astype(F32), axis=0, keepdims=True)
            for k in range(HEAD_DIM // LANES):
                at = j * (HEAD_DIM // LANES) + k
                vec[at : at + 1, :] += sums[:, k * LANES : (k + 1) * LANES]
        return carry

    def n_load(src, i, slot):
        count = src.shape[0]
        return pltpu.make_async_copy(
            src.at[:, pl.ds(pl.multiple_of(i * TILE, TILE), TILE)],
            n_v.at[slot, pl.ds(0, count)],
            n_sem.at[slot],
        )

    def stream(src, use, low, high):
        n_load(src, low, low % 2).start()

        def step(i, carry):
            slot = lax.rem(i, 2)
            n_load(src, i, slot).wait()

            @pl.when(i + 1 < high)
            def _():
                n_load(src, i + 1, 1 - slot).start()

            use(i, slot)
            return carry

        lax.fori_loop(low, high, step, 0)

    pairs = TILE // (2 * r)

    def q_tile(i, slot):
        for j in range(3):
            acc = t_dot(n_v[slot, 0 : p.rows // 2, :], joint_v[:, cols[j]]).astype(BF)
            for k in range(pairs):
                for kk in range(2):
                    at = (2 * k + kk) * r
                    q_g[i * pairs + k, kk, :, cols[j]] = acc[at : at + r]

    def up_tile(i, slot):
        at = pl.ds(pl.multiple_of(i * TILE, TILE), TILE)
        ugrad[at, :] = t_dot(n_v[slot], dpre[...]).astype(BF)

    def down_tile(i, slot):
        at = pl.ds(pl.multiple_of(i * TILE, TILE), TILE)
        g_sum[:, at] = jnp.sum(n_v[slot].astype(F32), axis=0, keepdims=True)
        for f in range(ffl // TILE):
            rows = slice(f * TILE, (f + 1) * TILE)
            dgrad[rows, at] = dot(hid_t[rows, :], n_v[slot]).astype(BF)
        first = pl.multiple_of(core * half * L, L)
        acc = dot(heads_t[...], n_v[slot, pl.ds(first, half * L), :]).astype(BF)
        for k in range(p.m):
            for kk in range(2):
                to = (2 * k + kk) * r
                o_g[k, kk, :, at] = acc[to : to + r]

    def down_owner(j):
        if p.P == 1:
            return j, c
        return 2 * (j // 2) + core, xh * 2 + j % 2

    def down_send():
        for j in range(S):
            own_b, own_c = down_owner(j)
            src = dgrad.at[pl.ds(j * R, R)]
            here = (own_b == b) & (own_c == c)

            @pl.when(jnp.logical_not(here))
            def _():
                remote(src, d_parts.at[b], s_d.at[j], r_d, (a * S + own_b, own_c)).start()

            @pl.when(here)
            def _():
                pltpu.make_async_copy(src, d_parts.at[b], r_d).start()

        remote(o_g.at[:, 1 - core], o_sib, s_o, r_o, sib).start()

    def u_rows(aa, bb):
        return ugrad.at[pl.ds(pl.multiple_of((aa * S + bb) * blk, blk), blk)]

    def up_send():
        def one(k, carry):
            bb = lax.rem(b + k, S)
            for aa in range(A):
                remote(u_rows(aa, bb), u_parts.at[k - 1, aa], s_u, r_u, (a * S + bb, c)).start()
            return carry

        lax.fori_loop(1, S, one, 0)

    def up_along():
        for k in range(1, S):
            drain(u_parts.at[k - 1], r_u)
        for k in range(1, S):

            def add(aa, carry):
                add_rows(u_rows(aa, b), (u_rows(aa, b), u_parts.at[k - 1, aa]), blk)
                return carry

            lax.fori_loop(0, A, add, 0)
        for k in range(1, A):
            aa = lax.rem(a + k, A)
            remote(u_rows(aa, b), u_z.at[k - 1], s_uz, r_uz, (aa * S + b, c)).start()

    def up_home():
        drain(u_z, r_uz)
        for k in range(A):
            source = lax.rem(a - k + A, A)
            for step in range(C):
                cc = lax.rem(c + 1 + step, C)
                row = pl.multiple_of(cc * r, r)
                for j in range(ffl // p.W):
                    at = pl.ds(j * p.W, p.W)
                    if k == 0:
                        src = ugrad.at[
                            pl.ds(pl.multiple_of((a * S + b) * blk + cc * r, r), r), at
                        ]
                    else:
                        src = u_z.at[k - 1, pl.ds(row, r), at]
                    col = pl.multiple_of(unit_run(p, source, c, j), LANES)
                    dst = u_out.at[:, pl.ds(col, p.W)]
                    if step < C - 1:
                        remote(src, dst, s_ua, r_ua, (dp, cc)).start()
                    else:
                        pltpu.make_async_copy(src, dst, r_ua).start()

    def q_rows(aa, bb):
        return q_g.at[pl.ds((aa * S + bb) * X, X), core]

    def q_cross():
        drain(q_sib, r_q)

        def add(i, carry):
            mine = q_g.at[i, core]
            add_rows(mine, (mine, q_sib.at[i]), r)
            return carry

        lax.fori_loop(0, A * S * X, add, 0)

        def one(k, carry):
            bb = lax.rem(b + k, S)
            for aa in range(A):
                remote(q_rows(aa, bb), q_group.at[k - 1, aa], s_qb, r_qb, (a * S + bb, c)).start()
            return carry

        lax.fori_loop(1, S, one, 0)

    def q_along():
        for k in range(1, S):
            drain(q_group.at[k - 1], r_qb)
        for k in range(1, S):

            def add(i, carry):
                aa, xx = lax.div(i, X), lax.rem(i, X)
                mine = q_g.at[(aa * S + b) * X + xx, core]
                add_rows(mine, (mine, q_group.at[k - 1, aa, xx]), r)
                return carry

            lax.fori_loop(0, A * X, add, 0)
        for k in range(1, A):
            aa = lax.rem(a + k, A)
            remote(q_rows(aa, b), q_z.at[k - 1], s_qz, r_qz, (aa * S + b, c)).start()

    def q_home():
        drain(q_z, r_qz)
        for k in range(A):
            source = lax.rem(a - k + A, A)
            for xx in (far, xh):
                for j in range(3):
                    if k == 0:
                        src = q_g.at[(a * S + b) * X + xx, core, :, cols[j]]
                    else:
                        src = q_z.at[k - 1, xx, :, cols[j]]
                    col = pl.multiple_of(j * D + (source * X + xh) * HEAD_DIM, HEAD_DIM)
                    dst = q_out.at[:, pl.ds(col, HEAD_DIM)]
                    if xx is far:
                        remote(src, dst, s_qa, r_qa, xnb).start()
                    else:
                        pltpu.make_async_copy(src, dst, r_qa).start()

    def out_owner(k):
        return lax.div(head * HEAD_DIM, r) + 2 * k + core

    def out_home():
        drain(o_sib, r_o)
        for k in range(p.m):
            mine = o_g.at[k, core]
            add_rows(mine, (mine, o_sib.at[k]), r)
            od, oc = lax.div(out_owner(k), C), lax.rem(out_owner(k), C)

            @pl.when(out_owner(k) != me)
            def _():
                remote(mine, o_parts.at[b], s_oa.at[k], r_oa, (od, oc)).start()

            @pl.when(out_owner(k) == me)
            def _():
                pltpu.make_async_copy(mine, o_parts.at[b], r_oa).start()

    own_v = pltpu.make_async_copy(vec, v_all.at[me], loc.at[7])

    def sums_send():
        up_row = p.hc // LANES

        def sum_rows(i, carry):
            at = pl.ds(pl.multiple_of(i * 64, 64), 64)
            return carry + jnp.sum(dpre[at, :].astype(F32), axis=0, keepdims=True)

        sums = lax.fori_loop(0, p.rows // 64, sum_rows, jnp.zeros((1, ffl), F32))
        for i in range(ffl // LANES):
            vec[up_row + i : up_row + i + 1, :] = sums[:, i * LANES : (i + 1) * LANES]
        share = D // (A * C)
        g_row = up_row + ffl // LANES
        vec[g_row : g_row + 1, :] = g_sum[:, pl.ds(pl.multiple_of(t * share, share), share)]
        own_v.start()

        def one(k, carry):
            other = lax.rem(me + k, p.n)
            dev = (lax.div(other, C), lax.rem(other, C))
            remote(vec, v_all.at[me], s_v, r_v, dev).start()
            return carry

        lax.fori_loop(1, p.n, one, 0)

    def give_back():
        pl.semaphore_signal(free, inc=1, device_id=sib, device_id_type=MESH)

    partial(0, 0)
    partial(0, 1)
    chip_sum(0, order[0])
    partial(0, 2)
    chip_sum(0, order[1])
    partial(0, 3)
    g_forward()
    chip_sum(0, order[2])
    chip_sum(0, order[3])
    give_back()
    unit_grads()
    hop(0, 0, False)
    stream(n2, up_tile, 0, 4)
    hop(0, 1, False)
    stream(n2, up_tile, 4, 8)
    up_send()
    lax.fori_loop(0, half, attend_back, 0)
    partial(1, 0)
    partial(1, 1)
    chip_sum(1, order[0])
    hop(0, 0, True)
    hop(0, 2, False)
    chip_sum(1, order[1])
    partial(1, 2)
    partial(1, 3)
    chip_sum(1, order[2])
    hop(0, 1, True)
    chip_sum(1, order[3])
    up_along()
    stream(n1, q_tile, 0, 4)
    hop(1, 0, False)
    stream(n1, q_tile, 4, 8)
    remote(q_g.at[:, 1 - core], q_sib, s_q, r_q, sib).start()
    q_cross()
    stream(g, down_tile, 0, 4)
    hop(1, 1, False)
    stream(g, down_tile, 4, 8)
    down_send()
    hop(1, 2, False)
    hop(1, 0, True)
    q_along()
    out_home()
    sums_send()
    hop(1, 1, True)
    up_home()
    q_home()
    last(0, o_sum)
    last(1, e_sum)

    drain(u_out, r_ua)
    drain(q_out, r_qa)
    drain(v_all.at[pl.ds(0, p.n - 1)], r_v)
    drain(d_parts, r_d)
    drain(o_parts, r_oa)

    own_v.wait()
    for k in range(2):
        drain(g_rows(c), s_g.at[k])
    drain(v_all.at[pl.ds(0, p.n - 1)], s_v)
    drain(q_sib, s_q)
    drain(o_sib, s_o)
    for k in range(1, S):
        drain(u_parts.at[0], s_u)
        drain(q_group.at[0], s_qb)
    drain(u_z, s_uz)
    drain(q_z, s_qz)
    for _ in range(A):
        drain(ugrad.at[pl.ds(0, (C - 1) * r)], s_ua)
        drain(q_g.at[0, 0], s_qa)
    for k in range(p.m):

        @pl.when(out_owner(k) != me)
        def _():
            drain(o_g.at[k, 0], s_oa.at[k])

    for j in range(S):
        own_b, own_c = down_owner(j)

        @pl.when(jnp.logical_not((own_b == b) & (own_c == c)))
        def _():
            drain(d_parts.at[0], s_d.at[j])

    for k in range(A):
        drain(from_sib.at[0], s_s.at[1, k])
    for j in range(2):
        for k in range(A):
            drain(from_x.at[0, 0], s_x.at[j, k])

            @pl.when(k != a)
            def _():
                drain(from_x.at[0, 0], s_c.at[j, k])


def back(p, *args):
    dma = pltpu.SemaphoreType.DMA
    A, S, C, X, r, R = p.A, p.S, p.C, p.X, p.r, p.R
    L = C * p.tok
    vm = pltpu.VMEM
    hbm = pl.BlockSpec(memory_space=pl.ANY)
    vmem = pl.BlockSpec(memory_space=pltpu.VMEM)
    groups = max(S - 1, 1)
    return pl.pallas_call(
        functools.partial(back_kernel, p),
        out_shape=(
            jax.ShapeDtypeStruct((p.tok, p.d), F32),
            jax.ShapeDtypeStruct((p.tok, p.d), F32),
            jax.ShapeDtypeStruct((r, 3 * p.d), BF),
            jax.ShapeDtypeStruct((r, p.ff), BF),
            jax.ShapeDtypeStruct((S, R, p.d), BF),
            jax.ShapeDtypeStruct((S, r, p.d), BF),
            jax.ShapeDtypeStruct((p.n, 16, LANES), F32),
            jax.ShapeDtypeStruct((A - 1, C * r, p.ffl), BF),
            jax.ShapeDtypeStruct((A - 1, X, r, p.hc), BF),
            jax.ShapeDtypeStruct((p.rows, p.d), BF),
        ),
        input_output_aliases={3: 9},
        in_specs=[hbm] * 10 + [vmem],
        out_specs=[vmem] * 2 + [hbm] * 8,
        scratch_shapes=[
            vm((max(p.rows, p.d), p.ffl), BF),
            vm((p.rows // 2, HEAD_DIM), BF),
            vm((p.rows, p.ffl), BF),
            vm((2, TILE, p.d), BF),
            vm((p.rows // 2, p.hc), BF),
            vm((p.ffl + HEAD_DIM, p.d), BF),
            vm((p.d, p.ffl), BF),
            vm((p.d, p.hc), BF),
            vm((2, p.rows, TILE), BF),
            vm((p.ffl, p.rows), BF),
            vm((HEAD_DIM, p.rows // 2), BF),
            vm((p.rows // 2, HEAD_DIM), BF),
            vm((L, LANES), F32),
            vm((L, LANES), F32),
            vm((2, A, X, p.tok, p.d), BF),
            vm((A, X, p.tok, p.d), BF),
            vm((A, X, p.tok, p.d), BF),
            vm((2, A, p.tok, p.d), BF),
            vm((2, 4, p.tok, p.d), BF),
            vm((p.ffl, p.d), BF),
            vm((A * S * X, 2, r, p.hc), BF),
            vm((A * S * X, r, p.hc), BF),
            vm((groups, A, X, r, p.hc), BF),
            vm((p.m, 2, r, p.d), BF),
            vm((p.m, r, p.d), BF),
            vm((groups, A, C * r, p.ffl), BF),
            vm((1, p.d), F32),
            vm((16, LANES), F32),
            dma((8,)),
            dma((2,)),
            dma((2,)),
            dma,
            dma,
            dma((2, A)),
            dma((2, A)),
            dma((2, A)),
            dma((2, A)),
            dma((2, A)),
            dma((2, 4)),
            dma,
            dma,
            dma,
            dma,
            dma,
            dma,
            dma,
            dma,
            dma,
            dma,
            dma((p.m,)),
            dma,
            dma,
            dma,
            dma,
            dma,
            dma,
            dma,
            dma((S,)),
            dma,
            dma((2,)),
            dma((2,)),
            pltpu.SemaphoreType.REGULAR,
        ],
        compiler_params=pltpu.CompilerParams(
            collective_id=1, has_side_effects=True, vmem_limit_bytes=67043328
        ),
        name="back",
    )(*args)


def finish_kernel(
    p,
    lens,
    x,
    g,
    o_sum,
    e_sum,
    full,
    q_part,
    u_part,
    d_parts,
    o_parts,
    sums,
    qkv_w,
    up_w,
    gain1,
    bias1,
    gain2,
    bias2,
    out,
    grad,
    q_grad,
    u_grad,
    d_grad,
    o_grad,
    q_own,
    u_own,
    g_own,
    g_same,
    gain1_grad,
    bias1_grad,
    gain2_grad,
    bias2_grad,
    q_bias,
    u_bias,
    g_bias,
    row_sums,
):
    A, S, C, X = p.A, p.S, p.C, p.X
    step = pl.program_id(0)

    @pl.when(step == 0)
    def _():
        up_row = p.hc // LANES
        g_row = up_row + p.ffl // LANES
        share = p.d // (A * C)
        for aa in range(A):
            for cc in range(C):
                for row in range(up_row, g_row + 1):
                    total = sums[aa * S * C + cc, row : row + 1, :]
                    for bb in range(1, S):
                        total = total + sums[(aa * S + bb) * C + cc, row : row + 1, :]
                    if row == g_row:
                        at = (aa * C + cc) * share
                        g_bias[:, at : at + share] = total[:, :share]
                        continue
                    unit = (row - up_row) * LANES
                    run = unit // p.W
                    if p.P == 1:
                        first = p.R * ((aa * S + run) * C + cc)
                    else:
                        first = p.R * ((aa * S + 2 * run + cc % 2) * C + cc // 2 * 2)
                    at = first + unit % p.W
                    u_bias[:, at : at + LANES] = total
            for xx in range(X):
                for row in range(up_row):
                    total = jnp.zeros((1, LANES), F32)
                    for bb in range(S):
                        for kk in range(2):
                            total = total + sums[(aa * S + bb) * C + xx * 2 + kk, row : row + 1, :]
                    j, rest = row * LANES // HEAD_DIM, row * LANES % HEAD_DIM
                    at = j * p.d + (aa * X + xx) * HEAD_DIM + rest
                    q_bias[:, at : at + LANES] = total
        me = lax.axis_index("dp") * C + lax.axis_index("ctx")

        def own(vector, size):
            span = max(size * i % LANES + size for i in range(p.n))
            span = (span + LANES - 1) // LANES * LANES
            rest = lax.rem(size * me, LANES)
            at = pl.multiple_of(size * me - rest, LANES)
            piece = pltpu.roll(vector[:, pl.ds(at, span)], lax.rem(span - rest, span), 1)
            return piece[0, :size]

        q_own[...] = own(q_bias, 3 * p.d // p.n)
        u_own[...] = own(u_bias, p.ff // p.n)
        g_own[...] = own(g_bias, p.d // p.n)
        g_same[...] = own(g_bias, p.d // p.n)

    rows = x.shape[0]
    sub = 32
    first = lax.axis_index("ctx") * p.tok + step * rows
    length = lens[0]

    def tokens(at):
        here = pl.ds(at, sub)
        row = lax.broadcasted_iota(jnp.int32, (sub, p.d), 0) + (at + first)
        live = row < length
        xf = x[here, :].astype(F32)
        total = xf + o_sum[here, :] + full[4:5, :]
        out[here, :] = jnp.where(live, total, 0.0).astype(BF)
        mid = xf - jnp.mean(xf, axis=1, keepdims=True)
        inv = lax.rsqrt(jnp.mean(mid * mid, axis=1, keepdims=True) + EPS)
        xhat = mid * inv
        e = e_sum[here, :]
        e_mean = jnp.mean(e, axis=1, keepdims=True)
        dx = inv * (e - e_mean - xhat * jnp.mean(e * xhat, axis=1, keepdims=True))
        go = jnp.where(live, g[here, :].astype(F32), 0.0)
        grad[here, :] = (go + dx).astype(BF)

    tiles(rows, tokens, sub)

    count = q_part.shape[0]
    lane = lax.broadcasted_iota(jnp.int32, (count, LANES), 1)
    kept = jnp.zeros((count, LANES), F32)
    for k, (part, weight, bias, result) in enumerate(
        ((q_part, qkv_w, q_bias, q_grad), (u_part, up_w, u_bias, u_grad))
    ):
        with_grad = jnp.zeros((part.shape[0], LANES), F32)
        with_bias = jnp.zeros((part.shape[0], LANES), F32)
        for n in range(0, part.shape[1], LANES):
            at = slice(n, n + LANES)
            value = part[:, at].astype(F32)
            result[:, at] = value
            w = weight[:, at].astype(F32)
            with_grad = with_grad + w * value
            with_bias = with_bias + w * bias[:, at]
        for o, t in enumerate((with_grad, with_bias)):
            kept = jnp.where(lane == 2 * k + o, jnp.sum(t, axis=1, keepdims=True), kept)
    row_sums[pl.ds(pl.multiple_of(step * count, count), count), :] = kept

    @pl.when(step == pl.num_programs(0) - 1)
    def _():
        turned = row_sums[...].T
        for k, (gain, shift, to_gain, to_shift) in enumerate(
            ((gain1, bias1, gain1_grad, bias1_grad), (gain2, bias2, gain2_grad, bias2_grad))
        ):
            with_grad, with_bias = turned[2 * k, : p.r], turned[2 * k + 1, : p.r]
            to_gain[...] = (with_grad - shift[...].astype(F32) * with_bias) / gain[...].astype(F32)
            to_shift[...] = with_bias

    for parts, result in ((d_parts, d_grad), (o_parts, o_grad)):

        size = min(sub, result.shape[0])

        def add(at):
            here = pl.ds(at, size)
            total = parts[0, here, :].astype(F32)
            for k in range(1, S):
                total = total + parts[k, here, :].astype(F32)
            result[here, :] = total

        tiles(result.shape[0], add, size)


def finish(p, *args):
    steps = max(1, p.r // 32)
    D, r, R = p.d, p.r, p.R

    def rows(count, width):
        return pl.BlockSpec((count // steps, width), lambda i: (i, 0))

    def parts(count):
        return pl.BlockSpec((p.S, count // steps, D), lambda i: (0, i, 0))

    def whole(*shape):
        return pl.BlockSpec(shape, lambda i: (0,) * len(shape))

    tok = rows(p.tok, D)
    return pl.pallas_call(
        functools.partial(finish_kernel, p),
        grid=(steps,),
        out_shape=(
            jax.ShapeDtypeStruct((p.tok, D), BF),
            jax.ShapeDtypeStruct((p.tok, D), BF),
            jax.ShapeDtypeStruct((r, 3 * D), F32),
            jax.ShapeDtypeStruct((r, p.ff), F32),
            jax.ShapeDtypeStruct((R, D), F32),
            jax.ShapeDtypeStruct((r, D), F32),
            jax.ShapeDtypeStruct((3 * D // p.n,), F32),
            jax.ShapeDtypeStruct((p.ff // p.n,), F32),
            *[jax.ShapeDtypeStruct((r,), F32)] * 6,
        ),
        in_specs=[
            pl.BlockSpec(memory_space=pltpu.SMEM),
            tok,
            tok,
            tok,
            tok,
            whole(8, D),
            rows(r, 3 * D),
            rows(r, p.ff),
            parts(R),
            parts(r),
            whole(p.n, 16, LANES),
            rows(r, 3 * D),
            rows(r, p.ff),
            *[whole(r)] * 4,
        ],
        out_specs=[
            tok,
            tok,
            rows(r, 3 * D),
            rows(r, p.ff),
            rows(R, D),
            rows(r, D),
            whole(3 * D // p.n),
            whole(p.ff // p.n),
            *[whole(r)] * 6,
        ],
        scratch_shapes=[
            pltpu.VMEM((1, 3 * D), F32),
            pltpu.VMEM((1, p.ff), F32),
            pltpu.VMEM((1, D), F32),
            pltpu.VMEM((r, LANES), F32),
        ],
        compiler_params=pltpu.CompilerParams(dimension_semantics=("arbitrary",)),
        name="finish",
    )(*args)


def local(
    dp_size,
    ctx_size,
    layer_input,
    lengths,
    cotangent,
    qkv_weight,
    qkv_bias,
    out_weight,
    out_bias,
    up_weight,
    up_bias,
    down_weight,
    down_bias,
    first_gain,
    first_bias,
    second_gain,
    second_bias,
):
    tok, d = layer_input.shape
    ff = up_weight.shape[1]
    p = Plan(dp_size, ctx_size, tok, d, ff)
    A, S, C, X, r, R = p.A, p.S, p.C, p.X, p.r, p.R
    dp, c, a, b, xh, core = place(p)
    me = dp * C + c
    t = a * C + c
    vectors = (
        qkv_bias,
        out_bias,
        up_bias,
        down_bias,
        first_gain,
        first_bias,
        second_gain,
        second_bias,
    )
    (_, g_all, qw, dw, uw, _, n1, n2, hid, slope, heads, joint, full) = front(
        p,
        layer_input,
        cotangent,
        qkv_weight,
        out_weight,
        up_weight,
        down_weight,
        lengths,
        *vectors,
    )
    o_sum, e_sum, q_out, u_out, d_parts, o_parts, v_all, _, _, _ = back(
        p,
        hid,
        heads,
        slope,
        g_all.reshape(p.rows, d),
        joint,
        n1,
        n2,
        dw,
        uw.reshape(d, p.ffl),
        qw.reshape(d, p.hc),
        full,
    )
    (
        output,
        input_grad,
        q_grad,
        u_grad,
        d_grad,
        o_grad,
        q_bias,
        u_bias,
        g_bias,
        g_same,
        gain1_grad,
        bias1_grad,
        gain2_grad,
        bias2_grad,
    ) = finish(
        p,
        lengths,
        layer_input,
        cotangent,
        o_sum,
        e_sum,
        full,
        q_out,
        u_out,
        d_parts,
        o_parts,
        v_all,
        qkv_weight,
        up_weight,
        first_gain,
        first_bias,
        second_gain,
        second_bias,
    )
    return (
        output,
        input_grad,
        q_grad,
        q_bias,
        o_grad,
        g_bias,
        u_grad,
        u_bias,
        d_grad,
        g_same,
        gain1_grad,
        bias1_grad,
        gain2_grad,
        bias2_grad,
    )


def solution(mesh):
    rows = P(("dp", "ctx"), None)
    vector = P(("dp", "ctx"))
    return jax.shard_map(
        functools.partial(local, mesh.shape["dp"], mesh.shape["ctx"]),
        mesh=mesh,
        in_specs=(
            rows,
            P("dp"),
            rows,
            rows,
            vector,
            rows,
            vector,
            rows,
            vector,
            rows,
            vector,
            vector,
            vector,
            vector,
            vector,
        ),
        out_specs=(
            rows,
            rows,
            rows,
            vector,
            rows,
            vector,
            rows,
            vector,
            rows,
            vector,
            vector,
            vector,
            vector,
            vector,
        ),
        check_vma=False,
    )
```

```python
import functools
import math

import jax
import jax.numpy as jnp
from jax import lax
from jax.experimental import pallas as pl
from jax.experimental.pallas import tpu as pltpu
from jax.sharding import PartitionSpec as P

HEADS = 8
HEAD_DIM = 256
ROT = 64
EPS = 1e-05
SCALE = 1.0 / math.sqrt(HEAD_DIM)
MESH = pl.DeviceIdType.MESH
BF = jnp.bfloat16
F32 = jnp.float32
TILE = 256
LANES = 128


class Plan:
    def __init__(self, dp, ctx, tok, d, ff):
        self.C = ctx
        self.X = ctx // 2
        self.A = HEADS // self.X
        self.S = dp // self.A
        self.n = dp * ctx
        self.tok = tok
        self.d = d
        self.ff = ff
        self.r = d // self.n
        self.R = ff // self.n
        self.ffl = self.S * self.R
        self.W = max(self.R, 128)
        self.P = self.W // self.R
        self.hc = 3 * HEAD_DIM
        self.m = HEAD_DIM // self.r // 2
        self.rows = self.A * self.C * tok


def remote(src, dst, send, recv, dev):
    return pltpu.make_async_remote_copy(
        src_ref=src, dst_ref=dst, send_sem=send, recv_sem=recv, device_id=dev, device_id_type=MESH
    )


def drain(ref, sem):
    pltpu.make_async_copy(ref, ref, sem).wait()


def unit_run(p, aa, cc, j):
    if p.P == 1:
        return p.R * ((aa * p.S + j) * p.C + cc)
    return p.R * ((aa * p.S + 2 * j + lax.rem(cc, 2)) * p.C + lax.div(cc, 2) * 2)


def unit_home(p, b, xh, core):
    if p.P == 1:
        return xh * 2 + core, b * p.R
    return xh * 2 + lax.rem(b, 2), (lax.div(b, 2) * 2 + core) * p.R


def place(p):
    dp = lax.axis_index("dp")
    c = lax.axis_index("ctx")
    a = lax.div(dp, p.S)
    b = lax.rem(dp, p.S)
    xh = lax.div(c, 2)
    core = lax.rem(c, 2)
    return dp, c, a, b, xh, core


def greet_all(p, me):
    barrier = pltpu.get_barrier_semaphore()

    def greet(k, carry):
        other = lax.rem(me + k, p.n)
        pl.semaphore_signal(
            barrier,
            inc=1,
            device_id=(lax.div(other, p.C), lax.rem(other, p.C)),
            device_id_type=MESH,
        )
        return carry

    lax.fori_loop(1, p.n, greet, 0)
    pl.semaphore_wait(barrier, p.n - 1)


def dot(x, y):
    return jnp.dot(x, y, preferred_element_type=F32)


def dot_t(x, y):
    return lax.dot_general(x, y, (((1,), (1,)), ((), ())), preferred_element_type=F32)


def t_dot(x, y):
    return lax.dot_general(x, y, (((0,), (0,)), ((), ())), preferred_element_type=F32)


def tiles(count, body, size=TILE):
    def run(i, carry):
        body(pl.multiple_of(i * size, size))
        return carry

    lax.fori_loop(0, count // size, run, 0)


def pick(values, i):
    out = values[0]
    for k in range(1, len(values)):
        out = jnp.where(i == k, values[k], out)
    return out


def far_order(p, a):
    order = []
    lo, hi = 0, p.A - 1
    for _ in range(p.A):
        up_far = hi - a >= a - lo
        order.append(jnp.where(up_far, hi, lo))
        lo = jnp.where(up_far, lo, lo + 1)
        hi = jnp.where(up_far, hi - 1, hi)
    return order


def add_rows(dst, parts, rows):
    step = min(rows, 32)

    def body(k, carry):
        at = pl.ds(pl.multiple_of(k * step, step), step)
        total = parts[0][at, :].astype(F32)
        for part in parts[1:]:
            total = total + part[at, :].astype(F32)
        dst[at, :] = total.astype(dst.dtype)
        return carry

    lax.fori_loop(0, rows // step, body, 0)


def angle_tables(cos_v, sin_v):
    rows = cos_v.shape[0]
    half = ROT // 2

    def body(at):
        shape = (64, LANES)
        lane = lax.broadcasted_iota(jnp.int32, shape, 1)
        pos = (lax.broadcasted_iota(jnp.int32, shape, 0) + at).astype(F32)
        exponent = lax.rem(lane, half).astype(F32) * (-2.0 * math.log(10000.0) / ROT)
        angle = pos * jnp.exp(exponent)
        turned = lane < ROT
        sign = jnp.where(lane < half, -1.0, 1.0)
        cos_v[pl.ds(at, 64), :] = jnp.where(turned, jnp.cos(angle), 1.0)
        sin_v[pl.ds(at, 64), :] = jnp.where(turned, jnp.sin(angle) * sign, 0.0)

    tiles(rows, body, 64)


def turn(v, cos, sin):
    first = v[:, :LANES]
    half = ROT // 2
    lane = lax.broadcasted_iota(jnp.int32, first.shape, 1)
    partner = jnp.where(
        lane < half, pltpu.roll(first, LANES - half, 1), pltpu.roll(first, half, 1)
    )
    return jnp.concatenate([first * cos + partner * sin, v[:, LANES:]], axis=1)


def probabilities(q, k, row0, scale):
    scores = dot_t(q, k) * scale
    row = lax.broadcasted_iota(jnp.int32, scores.shape, 0) + row0
    col = lax.broadcasted_iota(jnp.int32, scores.shape, 1)
    scores = jnp.where(col <= row, scores, -1e30)
    expo = jnp.exp(scores - jnp.max(scores, axis=1, keepdims=True))
    return expo / jnp.sum(expo, axis=1, keepdims=True)


def front_kernel(
    p,
    x,
    g,
    qkv,
    outw,
    up,
    down,
    lens,
    qkv_b,
    out_b,
    up_b,
    down_b,
    gain1,
    bias1,
    gain2,
    bias2,
    xa,
    ga,
    qw,
    dw,
    uw,
    sm,
    n1,
    n2,
    hid,
    slope,
    heads,
    joint,
    rows_out,
    small,
    pads,
    g_v,
    gm,
    sm_v,
    vecs,
    ub,
    qb,
    cos_v,
    sin_v,
    uw_v,
    qw_v,
    xs,
    n1_v,
    n2_v,
    hid_v,
    slope_v,
    heads_v,
    joint_v,
    ux,
    qx,
    loc,
    puts,
    s_ux,
    r_ux,
    s_qx,
    r_qx,
    s_sm,
    r_sm,
    s_up,
    r_up,
    s_upb,
    r_upb,
    s_q,
    r_q,
    s_qb,
    r_qb,
    s_qc,
    r_qc,
    s_o,
    r_o,
    s_ob,
    s_oc,
    r_oc,
    s_d,
    r_d,
    s_r,
    r_r,
    s_l,
    r_l,
    s_x,
    r_x,
    s_s,
    r_s,
):
    A, S, C, r, R = p.A, p.S, p.C, p.r, p.R
    dp, c, a, b, xh, core = place(p)
    me = dp * C + c
    t = a * C + c
    head = a * p.X + xh
    sib = (dp, xh * 2 + 1 - core)
    xnb = (dp, (1 - xh) * 2 + core)
    right = (dp + S, c)
    left = (dp - S, c)
    L = C * p.tok
    half = A // 2

    get_g = pltpu.make_async_copy(g, g_v, loc.at[2])
    get_g.start()
    vectors = (qkv_b, up_b, gain1, bias1, gain2, bias2, out_b)
    greet_all(p, me)

    own_small = pltpu.make_async_copy(small, sm.at[me], loc.at[0])
    own_x = pltpu.make_async_copy(x, xa.at[a, pl.ds(pl.multiple_of(c * p.tok, p.tok), p.tok)], loc.at[1])
    own_x.start()
    own_g = pltpu.make_async_copy(gm, ga.at[a, pl.ds(pl.multiple_of(c * p.tok, p.tok), p.tok)], loc.at[2])

    row_head = lax.div(me * r, HEAD_DIM)
    row_part = lax.div(lax.rem(me * r, HEAD_DIM), 2 * r)
    o_dp, o_ctx = lax.div(row_head, p.X) * S + b, lax.rem(row_head, p.X) * 2 + core
    o_here = (o_dp == dp) & (o_ctx == c)

    def o_rows(k, cc):
        return dw.at[pl.ds(pl.multiple_of(p.ffl + (2 * k + cc) * r, r), r)]

    def o_first(k):
        owner = lax.div(head * HEAD_DIM, r) + 2 * k + core
        return lax.rem(lax.div(owner, C), S) == b

    streams = ((x, xa), (gm, ga))

    def blk(j, k, cc):
        return streams[j][1].at[k, pl.ds(pl.multiple_of(cc * p.tok, p.tok), p.tok)]

    def send_z(j):
        own, slot = streams[j][0], blk(j, a, c)

        @pl.when(a < A - 1)
        def _():
            remote(own, slot, s_r.at[j, 0], r_r.at[j, 0], right).start()

        @pl.when(a > 0)
        def _():
            remote(own, slot, s_l.at[j, 0], r_l.at[j, 0], left).start()

    def send_x(j):
        own, slot = streams[j][0], blk(j, a, c)
        remote(own, slot, s_x.at[j, a], r_x.at[j, a], xnb).start()
        remote(own, slot, s_s.at[j, a], r_s.at[j, a], sib).start()

    last_slot = jnp.where(a < A // 2, A - 1, 0)

    def send_on(j, k, part):
        if j == 0:
            remote(part, part, s_x.at[j, k], r_x.at[j, k], xnb).start()
        else:

            @pl.when(k != last_slot)
            def _():
                remote(part, part, s_x.at[j, k], r_x.at[j, k], xnb).start()

        remote(part, part, s_s.at[j, k], r_s.at[j, k], sib).start()

    def z_step(j, s):
        @pl.when(a - 1 - s >= 0)
        def _():
            k = a - 1 - s
            part = blk(j, k, c)
            drain(part, r_r.at[j, s])

            @pl.when((s + 1 < A - 1) & (a < A - 1))
            def _():
                nxt = jnp.minimum(s + 1, A - 2)
                remote(part, part, s_r.at[j, nxt], r_r.at[j, nxt], right).start()

            send_on(j, k, part)

        @pl.when(a + 1 + s <= A - 1)
        def _():
            k = a + 1 + s
            part = blk(j, k, c)
            drain(part, r_l.at[j, s])

            @pl.when((s + 1 < A - 1) & (a > 0))
            def _():
                nxt = jnp.minimum(s + 1, A - 2)
                remote(part, part, s_l.at[j, nxt], r_l.at[j, nxt], left).start()

            send_on(j, k, part)

    xc = (1 - xh) * 2 + core

    def cross(j, k):
        part = blk(j, k, xc)
        drain(part, r_x.at[j, k])
        remote(part, part, s_s.at[j, k], r_s.at[j, k], sib).start()

    runs = p.ffl // p.W

    def up_cols(aa, cc, j):
        return up.at[:, pl.ds(pl.multiple_of(unit_run(p, aa, cc, j), LANES), p.W)]

    def up_over(i, carry):
        aa, kk = lax.div(i, 2), lax.rem(i, 2)
        for j in range(runs):
            dst = ux.at[aa, kk, :, pl.ds(j * p.W, p.W)]
            remote(up_cols(aa, (1 - xh) * 2 + kk, j), dst, s_ux, r_ux, xnb).start()
        return carry

    def up_along(i, carry):
        aa, kk = lax.rem(a + 1 + lax.div(i, 2), A), lax.rem(i, 2)
        cc = xh * 2 + kk
        here = (aa == a) & (kk == core)
        for j in range(runs):
            dst = uw.at[a, b, c, :, pl.ds(j * p.W, p.W)]

            @pl.when(jnp.logical_not(here))
            def _():
                remote(up_cols(aa, cc, j), dst, s_up, r_up, (aa * S + b, cc)).start()

            @pl.when(here)
            def _():
                pltpu.make_async_copy(up_cols(aa, cc, j), dst, r_up).start()

        return carry

    def up_onward(i, carry):
        aa, kk = lax.rem(a + 1 + lax.div(i, 2), A), lax.rem(i, 2)
        here = (aa == a) & (kk == core)
        src, dst = ux.at[aa, kk], uw.at[a, b, (1 - xh) * 2 + core]

        @pl.when(jnp.logical_not(here))
        def _():
            remote(src, dst, s_up, r_up, (aa * S + b, xh * 2 + kk)).start()

        @pl.when(here)
        def _():
            pltpu.make_async_copy(src, dst, r_up).start()

        return carry

    def q_cols(aa, xx, j):
        col = pl.multiple_of(j * p.d + (aa * p.X + xx) * HEAD_DIM, HEAD_DIM)
        return qkv.at[:, pl.ds(col, HEAD_DIM)]

    def q_over(aa, carry):
        for j in range(3):
            dst = qx.at[aa, :, pl.ds(j * HEAD_DIM, HEAD_DIM)]
            remote(q_cols(aa, 1 - xh, j), dst, s_qx, r_qx, xnb).start()
        return carry

    def q_along(i, carry):
        aa = lax.rem(a + 1 + i, A)
        for j in range(3):
            dst = qw.at[a, b, xh, core, :, pl.ds(j * HEAD_DIM, HEAD_DIM)]

            @pl.when(aa != a)
            def _():
                remote(q_cols(aa, xh, j), dst, s_q, r_q, (aa * S + b, c)).start()

            @pl.when(aa == a)
            def _():
                pltpu.make_async_copy(q_cols(aa, xh, j), dst, r_q).start()

        return carry

    def q_onward(i, carry):
        aa = lax.rem(a + 1 + i, A)
        src, dst = qx.at[aa], qw.at[a, b, 1 - xh, core]

        @pl.when(aa != a)
        def _():
            remote(src, dst, s_q, r_q, (aa * S + b, c)).start()

        @pl.when(aa == a)
        def _():
            pltpu.make_async_copy(src, dst, r_q).start()

        return carry

    def up_cross(k, carry):
        bb = lax.rem(b + k, S)
        remote(uw.at[:, b], uw.at[:, b], s_upb, r_upb, (a * S + bb, c)).start()
        return carry

    def q_cross(k, carry):
        bb = lax.rem(b + k, S)
        part = qw.at[:, b, :, core]
        remote(part, part, s_qb, r_qb, (a * S + bb, c)).start()
        return carry

    def slot_rows(k):
        return pl.ds(pl.multiple_of(k * L, L), L)

    near = far_order(p, a)[::-1]

    def norm_slot(i):
        k = near[i]
        drain(xa.at[k, pl.ds(0, p.X * p.tok)], r_s.at[0, k])
        get = pltpu.make_async_copy(xa.at[k], xs, loc.at[3])
        get.start()
        get.wait()
        mine = lax.div(k, half) == core
        step = 32

        def unit_rows(at):
            rows = xs[pl.ds(at, step), :].astype(F32)
            rows = rows - jnp.mean(rows, axis=1, keepdims=True)
            spread = jnp.mean(rows * rows, axis=1, keepdims=True)
            rows = rows * lax.rsqrt(spread + EPS)
            to = pl.multiple_of(k * L + at, step)
            n2_v[pl.ds(to, step), :] = (rows * vecs[2:3, :] + vecs[3:4, :]).astype(BF)
            return rows

        @pl.when(mine)
        def _():
            def both(at):
                rows = unit_rows(at)
                to = pl.multiple_of(lax.rem(k, half) * L + at, step)
                n1_v[pl.ds(to, step), :] = (rows * vecs[0:1, :] + vecs[1:2, :]).astype(BF)

            tiles(L, both, step)

        @pl.when(jnp.logical_not(mine))
        def _():
            def one(at):
                unit_rows(at)

            tiles(L, one, step)

        pltpu.make_async_copy(n2_v.at[slot_rows(k)], n2.at[slot_rows(k)], puts.at[i]).start()

    def units(i):
        k = near[i]

        def unit_tile(n):
            at = pl.ds(n, TILE)
            w = uw_v[:, :, :, :, at].reshape(p.d, TILE)
            v = dot(n2_v[slot_rows(k), :], w) + ub[:, at]
            phi = 0.5 * (1.0 + lax.erf(v * (1.0 / math.sqrt(2.0))))
            density = jnp.exp(-0.5 * v * v) * (1.0 / math.sqrt(2.0 * math.pi))
            hid_v[slot_rows(k), at] = (v * phi).astype(BF)
            slope_v[slot_rows(k), at] = (phi + v * density).astype(BF)

        tiles(p.ffl, unit_tile)

    d_ctx, d_row = unit_home(p, b, xh, core)
    d_dst = dw.at[pl.ds(pl.multiple_of(d_row, R), R)]
    def small_all():
        def small_send(k, carry):
            other = lax.rem(me + k, p.n)
            dev = (lax.div(other, C), lax.rem(other, C))
            remote(small, sm.at[me], s_sm, r_sm, dev).start()
            return carry

        lax.fori_loop(1, p.n, small_send, 0)

    def down_all():
        for bb in range(S):
            here = (bb == b) & (d_ctx == c)

            @pl.when(jnp.logical_not(here))
            def _():
                remote(down, d_dst, s_d.at[bb], r_d, (a * S + bb, d_ctx)).start()

            @pl.when(here)
            def _():
                pltpu.make_async_copy(down, d_dst, r_d).start()

    def out_send():
        @pl.when(jnp.logical_not(o_here))
        def _():
            remote(outw, o_rows(row_part, core), s_o, r_o.at[row_part], (o_dp, o_ctx)).start()

        @pl.when(o_here)
        def _():
            pltpu.make_async_copy(outw, o_rows(row_part, core), r_o.at[row_part]).start()

    def chunk(which, jj):
        size = vectors[which].shape[0]
        if size % LANES == 0:
            count = 1
        elif LANES % size == 0:
            count = LANES // size
        else:
            count = (LANES - 1) // size + 2
        total = jnp.zeros((1, LANES), F32)
        for o in range(count):
            i = lax.div(LANES * jj, size) + o
            row = jj - lax.div(i * size, LANES)
            good = ((row >= 0) & (row <= 1) & (i < p.n)).astype(F32)
            at = 2 * which + jnp.clip(row, 0, 1)
            total = total + good * sm_v[jnp.minimum(i, p.n - 1), pl.ds(at, 1), :]
        return total

    def vectors_whole():
        own_small.wait()
        drain(sm.at[pl.ds(0, p.n - 1)], r_sm)
        get_small = pltpu.make_async_copy(sm, sm_v, loc.at[0])
        get_small.start()
        get_small.wait()

        def fill(jj, carry):
            for k in range(5):
                vecs[k : k + 1, pl.ds(pl.multiple_of(jj * LANES, LANES), LANES)] = chunk(2 + k, jj)
            return carry

        lax.fori_loop(0, p.d // LANES, fill, 0)
        for j in range(p.ffl // LANES):
            run, rest = j * LANES // p.W, (j * LANES % p.W) // LANES
            first = lax.div(unit_run(p, a, c, run), LANES) + rest
            ub[:, j * LANES : (j + 1) * LANES] = chunk(1, first)
        for j in range(3):
            for k in range(HEAD_DIM // LANES):
                first = (j * p.d + head * HEAD_DIM) // LANES + k
                at = j * HEAD_DIM + k * LANES
                qb[:, at : at + LANES] = chunk(0, first)

    def out_onward(k):
        remote(o_rows(k, core), o_rows(k, core), s_oc.at[k], r_oc.at[k], sib).start()

    def out_first():
        for k in range(p.m):

            @pl.when(o_first(k))
            def _():
                drain(o_rows(k, core), r_o.at[k])

                def o_cross(kk, carry):
                    bb = lax.rem(b + kk, S)
                    rows = o_rows(k, core)
                    remote(rows, rows, s_ob.at[k], r_o.at[k], (a * S + bb, c)).start()
                    return carry

                lax.fori_loop(1, S, o_cross, 0)
                out_onward(k)

    def out_rest():
        for k in range(p.m):

            @pl.when(jnp.logical_not(o_first(k)))
            def _():
                drain(o_rows(k, core), r_o.at[k])
                out_onward(k)

    def load_uw():
        for _ in range(S - 1):
            drain(uw.at[:, b], r_upb)
        get = pltpu.make_async_copy(uw, uw_v, loc.at[3])
        get.start()
        get.wait()

    def send_half_qw():
        for _ in range(S - 1):
            drain(qw.at[:, b, :, core], r_qb)
        part = qw.at[:, :, :, core]
        remote(part, part, s_qc, r_qc, sib).start()

    def load_qw():
        drain(qw.at[:, :, :, 1 - core], r_qc)
        get = pltpu.make_async_copy(qw, qw_v, loc.at[3])
        get.start()
        get.wait()

    def attend(i):
        own = pl.ds(pl.multiple_of(i * L, L), L)
        cols = [pl.ds(j * HEAD_DIM, HEAD_DIM) for j in range(3)]
        for j in range(3):
            w = qw_v[:, :, :, :, :, cols[j]].reshape(p.d, HEAD_DIM)
            v = dot(n1_v[own, :], w) + qb[:, cols[j]]
            if j < 2:
                v = turn(v, cos_v[...], sin_v[...])
            joint_v[own, cols[j]] = v.astype(BF)
        rows = L // 2
        for h in range(2):
            at = pl.ds(pl.multiple_of(i * L + h * rows, rows), rows)
            keys = pl.ds(pl.multiple_of(i * L, L), (h + 1) * rows)
            probs = probabilities(joint_v[at, cols[0]], joint_v[keys, cols[1]], h * rows, SCALE)
            heads_v[at, :] = dot(probs.astype(BF), joint_v[keys, cols[2]]).astype(BF)

    send_z(0)
    send_x(0)

    get_g.wait()
    length = lens[0]

    def mask(at):
        row = lax.broadcasted_iota(jnp.int32, (32, p.d), 0) + (at + c * p.tok)
        rows = g_v[pl.ds(at, 32), :].astype(F32)
        gm[pl.ds(at, 32), :] = jnp.where(row < length, rows, 0.0).astype(BF)

    tiles(p.tok, mask, 32)

    pads[...] = jnp.zeros_like(pads)
    for k, v in enumerate(vectors):
        value = v[...].astype(F32)
        if k == len(vectors) - 1:
            value = value + down_b[...].astype(F32)
        pads[k, 0 : v.shape[0]] = value
    for k, v in enumerate(vectors):
        placed = pltpu.roll(pads[k : k + 1, :], lax.rem(v.shape[0] * me, LANES), 1)
        small[2 * k : 2 * k + 1, :] = placed[:, :LANES]
        small[2 * k + 1 : 2 * k + 2, :] = placed[:, LANES:]
    small[2 * len(vectors) :, :] = jnp.zeros((2, LANES), F32)
    own_small.start()
    own_g.start()
    small_all()
    lax.fori_loop(0, 2 * A, up_over, 0)
    angle_tables(cos_v, sin_v)
    z_step(0, 0)
    cross(0, near[0])
    lax.fori_loop(0, 2 * A, up_along, 0)
    down_all()
    drain(ux, r_ux)
    lax.fori_loop(0, 2 * A, up_onward, 0)
    lax.fori_loop(0, A, q_over, 0)
    z_step(0, 1)
    cross(0, near[1])
    vectors_whole()
    own_x.wait()
    norm_slot(0)
    lax.fori_loop(0, A, q_along, 0)
    send_x(1)
    norm_slot(1)
    drain(qx, r_qx)
    lax.fori_loop(0, A, q_onward, 0)
    out_send()
    cross(0, near[2])
    send_z(1)
    drain(uw.at[:, b], r_up)
    lax.fori_loop(1, S, up_cross, 0)
    drain(qw.at[:, b, :, core], r_q)
    lax.fori_loop(1, S, q_cross, 0)
    norm_slot(2)
    z_step(0, 2)
    cross(1, near[0])
    out_first()
    cross(0, near[3])
    z_step(1, 0)
    norm_slot(3)
    put_n1 = pltpu.make_async_copy(n1_v, n1, loc.at[6])
    put_n1.start()
    put_rows = pltpu.make_async_copy(vecs, rows_out, loc.at[7])
    put_rows.start()
    load_uw()
    send_half_qw()
    units(0)
    z_step(1, 1)
    cross(1, near[1])
    units(1)
    load_qw()
    attend(0)
    units(2)
    z_step(1, 2)
    attend(1)
    cross(1, near[2])
    units(3)
    put_hid = pltpu.make_async_copy(hid_v, hid, loc.at[4])
    put_hid.start()
    put_slope = pltpu.make_async_copy(slope_v, slope, loc.at[5])
    put_slope.start()
    out_rest()

    put_heads = pltpu.make_async_copy(heads_v, heads, loc.at[0])
    put_heads.start()
    put_joint = pltpu.make_async_copy(joint_v, joint, loc.at[1])
    put_joint.start()

    drain(dw.at[pl.ds(0, p.ffl)], r_d)
    for k in range(p.m):
        drain(dw.at[pl.ds(0, r)], r_oc.at[k])
    for k in range(A):

        @pl.when(k != last_slot)
        def _():
            drain(ga.at[k, pl.ds(0, p.X * p.tok)], r_s.at[1, k])

        @pl.when(k == last_slot)
        def _():
            drain(ga.at[k, pl.ds(0, p.tok)], r_s.at[1, k])


    own_g.wait()
    put_hid.wait()
    put_slope.wait()
    put_n1.wait()
    put_rows.wait()
    put_heads.wait()
    put_joint.wait()
    for i in range(A):
        drain(n2_v.at[pl.ds(0, L)], puts.at[i])
    drain(sm.at[pl.ds(0, p.n - 1)], s_sm)
    drain(ux, s_ux)
    drain(qx, s_qx)
    for _ in range(4 * A - 2):
        drain(uw.at[a, b, c], s_up)
    for _ in range(2 * A - 2):
        drain(qw.at[a, b, xh, core], s_q)
    for bb in range(S):

        @pl.when(jnp.logical_not((bb == b) & (d_ctx == c)))
        def _():
            drain(down, s_d.at[bb])

    @pl.when(jnp.logical_not(o_here))
    def _():
        drain(outw, s_o)

    for k in range(p.m):

        @pl.when(o_first(k))
        def _():
            for _ in range(S - 1):
                drain(outw, s_ob.at[k])

    for k in range(p.m):
        drain(dw.at[pl.ds(0, r)], s_oc.at[k])
    for _ in range(S - 1):
        drain(uw.at[:, b], s_upb)
        drain(qw.at[:, b, :, core], s_qb)
    drain(qw.at[:, :, :, core], s_qc)
    for j in range(2):
        for s in range(A - 1):

            @pl.when((a < A - 1) & (a - s >= 0))
            def _():
                drain(x, s_r.at[j, s])

            @pl.when((a > 0) & (a + s <= A - 1))
            def _():
                drain(x, s_l.at[j, s])

        for k in range(A):
            if j == 0:
                drain(x, s_x.at[j, k])
                drain(xa.at[k, pl.ds(0, p.X * p.tok)], s_s.at[j, k])
                continue

            @pl.when(k != last_slot)
            def _():
                drain(x, s_x.at[j, k])
                drain(xa.at[k, pl.ds(0, p.X * p.tok)], s_s.at[j, k])

            @pl.when(k == last_slot)
            def _():
                drain(x, s_s.at[j, k])


def front(p, x, g, qkv, outw, up, down, lens, *vectors):
    dma = pltpu.SemaphoreType.DMA
    A, S, C, r = p.A, p.S, p.C, p.r
    L = C * p.tok
    vm = pltpu.VMEM
    hbm = pl.BlockSpec(memory_space=pl.ANY)
    vmem = pl.BlockSpec(memory_space=pltpu.VMEM)
    half = p.rows // 2
    qw_shape = (A, S, p.X, 2, r, p.hc)
    uw_shape = (A, S, C, r, p.ffl)
    return pl.pallas_call(
        functools.partial(front_kernel, p),
        out_shape=(
            jax.ShapeDtypeStruct((A, L, p.d), BF),
            jax.ShapeDtypeStruct((A, L, p.d), BF),
            jax.ShapeDtypeStruct(qw_shape, BF),
            jax.ShapeDtypeStruct((p.ffl + HEAD_DIM, p.d), BF),
            jax.ShapeDtypeStruct(uw_shape, BF),
            jax.ShapeDtypeStruct((p.n, 16, LANES), F32),
            jax.ShapeDtypeStruct((half, p.d), BF),
            jax.ShapeDtypeStruct((p.rows, p.d), BF),
            jax.ShapeDtypeStruct((p.rows, p.ffl), BF),
            jax.ShapeDtypeStruct((p.rows, p.ffl), BF),
            jax.ShapeDtypeStruct((half, HEAD_DIM), BF),
            jax.ShapeDtypeStruct((half, p.hc), BF),
            jax.ShapeDtypeStruct((8, p.d), F32),
        ),
        in_specs=[hbm] * 6 + [pl.BlockSpec(memory_space=pltpu.SMEM)] + [vmem] * 8,
        out_specs=[hbm] * 13,
        scratch_shapes=[
            vm((16, LANES), F32),
            vm((8, 2 * LANES), F32),
            vm((p.tok, p.d), BF),
            vm((p.tok, p.d), BF),
            vm((p.n, 16, LANES), F32),
            vm((8, p.d), F32),
            vm((1, p.ffl), F32),
            vm((1, p.hc), F32),
            vm((L, LANES), F32),
            vm((L, LANES), F32),
            vm(uw_shape, BF),
            vm(qw_shape, BF),
            vm((L, p.d), BF),
            vm((half, p.d), BF),
            vm((p.rows, p.d), BF),
            vm((p.rows, p.ffl), BF),
            vm((p.rows, p.ffl), BF),
            vm((half, HEAD_DIM), BF),
            vm((half, p.hc), BF),
            vm((A, 2, r, p.ffl), BF),
            vm((A, r, p.hc), BF),
            dma((8,)),
            dma((A,)),
            dma,
            dma,
            dma,
            dma,
            dma,
            dma,
            dma,
            dma,
            dma,
            dma,
            dma,
            dma,
            dma,
            dma,
            dma,
            dma,
            dma,
            dma((p.m,)),
            dma((p.m,)),
            dma((p.m,)),
            dma((p.m,)),
            dma((S,)),
            dma,
            dma((2, A - 1)),
            dma((2, A - 1)),
            dma((2, A - 1)),
            dma((2, A - 1)),
            dma((2, A)),
            dma((2, A)),
            dma((2, A)),
            dma((2, A)),
        ],
        compiler_params=pltpu.CompilerParams(
            collective_id=0, has_side_effects=True, vmem_limit_bytes=60 * 1024 * 1024
        ),
        name="front",
    )(x, g, qkv, outw, up, down, lens, *vectors)


def back_kernel(
    p,
    hid,
    heads,
    slope,
    g_in,
    joint,
    n1,
    n2,
    dw,
    uw,
    qw,
    gains,
    o_sum,
    e_sum,
    q_out,
    u_out,
    d_parts,
    o_parts,
    v_all,
    u_z,
    q_z,
    g,
    hid_v,
    heads_v,
    dpre,
    g_v,
    joint_v,
    dw_v,
    uw_v,
    qw_v,
    n_v,
    hid_t,
    heads_t,
    dh_v,
    cos_v,
    sin_v,
    own,
    to_sib,
    from_sib,
    from_x,
    came,
    dgrad,
    q_g,
    q_sib,
    q_group,
    o_g,
    o_sib,
    u_parts,
    g_sum,
    vec,
    loc,
    n_sem,
    g_sem,
    s_v,
    r_v,
    s_s,
    r_s,
    s_x,
    r_x,
    s_c,
    r_c,
    s_q,
    r_q,
    s_qb,
    r_qb,
    s_qz,
    r_qz,
    s_qa,
    r_qa,
    s_o,
    r_o,
    s_oa,
    r_oa,
    s_u,
    r_u,
    s_uz,
    r_uz,
    s_ua,
    r_ua,
    s_d,
    r_d,
    s_g,
    r_g,
    free,
):
    A, S, C, X, r, R = p.A, p.S, p.C, p.X, p.r, p.R
    dp, c, a, b, xh, core = place(p)
    me = dp * C + c
    t = a * C + c
    head = a * X + xh
    sib = (dp, xh * 2 + 1 - core)
    xnb = (dp, (1 - xh) * 2 + core)
    far = 1 - xh
    L = C * p.tok
    D, ffl = p.d, p.ffl
    half = A // 2
    ugrad = hid_v
    blk = C * r

    loads = [
        pltpu.make_async_copy(src, dst, loc.at[k])
        for k, (src, dst) in enumerate(
            (
                (hid, hid_v.at[pl.ds(0, p.rows)]),
                (dw, dw_v),
                (heads, heads_v),
                (joint, joint_v),
                (slope, dpre),
                (uw, uw_v),
                (qw, qw_v),
            )
        )
    ]
    for load in loads:
        load.start()
    greet_all(p, me)
    last_slot = jnp.where(a < half, A - 1, 0)

    def g_rows(cc):
        return g.at[pl.ds(pl.multiple_of(last_slot * L + cc * p.tok, p.tok), p.tok)]

    remote(g_rows(c), g_rows(c), s_g.at[0], r_g.at[0], xnb).start()
    x_ctx = far * 2 + core
    vec[...] = jnp.zeros_like(vec)
    angle_tables(cos_v, sin_v)

    def g_forward():
        drain(g_rows(x_ctx), r_g.at[0])
        remote(g_rows(x_ctx), g_rows(x_ctx), s_g.at[1], r_g.at[1], sib).start()

    low = a < half
    order = [
        jnp.where(low, A - 1, 0),
        jnp.where(low, A - 2, 1),
        jnp.where(low, 1 - a, A + 1 - a),
        a,
    ]
    inner = (a == 1) | (a == A - 2)

    def slot_rows(k):
        return pl.ds(pl.multiple_of(k * L, L), L)

    def blocks(src, base):
        rows = []
        for cc in (core, 1 - core):
            for side in range(X):
                at = pl.multiple_of(base + (side * 2 + cc) * p.tok, p.tok)
                rows.append(src[pl.ds(at, p.tok), :])
        return jnp.concatenate(rows, axis=0)

    def keep(j, k, n, acc):
        acc = acc.astype(BF)
        for side in range(X):
            own[j, k, side, :, pl.ds(n, TILE)] = acc[side * p.tok : (side + 1) * p.tok]
            to_sib[k, side, :, pl.ds(n, TILE)] = acc[
                (X + side) * p.tok : (X + side + 1) * p.tok
            ]

    def partial(j, i):
        k = order[i]
        mine = lax.div(k, half) == core
        base = pl.multiple_of(lax.rem(k, half) * L, L)
        if j == 0 and i == 0:
            for n in range(3):
                loads[n].wait()
        if j == 1:
            if i == 0:
                loads[5].wait()
                loads[6].wait()
                pl.semaphore_wait(free, 1)
            drain(from_sib.at[k], s_s.at[0, k])
        units = blocks(dpre if j else hid_v, k * L)

        @pl.when(mine)
        def _():
            heads_rows = blocks(joint_v if j else heads_v, base)

            def tile(n):
                at = pl.ds(n, TILE)
                if j == 0:
                    acc = dot(units, dw_v[0:ffl, at]) + dot(heads_rows, dw_v[ffl:, at])
                else:
                    acc = dot_t(units, uw_v[at, :]) * gains[2:3, at]
                    acc += dot_t(heads_rows, qw_v[at, :]) * gains[0:1, at]
                keep(j, k, n, acc)

            tiles(D, tile)

        @pl.when(jnp.logical_not(mine))
        def _():
            def tile(n):
                at = pl.ds(n, TILE)
                if j == 0:
                    acc = dot(units, dw_v[0:ffl, at])
                else:
                    acc = dot_t(units, uw_v[at, :]) * gains[2:3, at]
                keep(j, k, n, acc)

            tiles(D, tile)

        remote(to_sib.at[k], from_sib.at[k], s_s.at[j, k], r_s.at[j, k], sib).start()

    def chip_sum(j, k):
        drain(from_sib.at[k], r_s.at[j, k])
        mine = own.at[j, k, far]
        add_rows(mine, (mine, from_sib.at[k, far]), p.tok)
        remote(mine, from_x.at[j, k], s_x.at[j, k], r_x.at[j, k], xnb).start()
        mine = own.at[j, k, xh]
        add_rows(mine, (mine, from_sib.at[k, xh]), p.tok)

    def hop(j, i, joins):
        k = order[i]
        across = i < 2
        if joins:
            run = inner
        else:
            run = jnp.logical_not(inner) if across else a >= 0

        @pl.when(run)
        def _():
            drain(from_x.at[j, k], r_x.at[j, k])
            mine = own.at[j, k, xh]
            if joins:
                drain(came.at[j, 0], r_c.at[j, lax.rem(k, 2)])
                add_rows(mine, (mine, from_x.at[j, k], came.at[j, lax.rem(k, 2)]), p.tok)
                to, at = k, 2
            else:
                add_rows(mine, (mine, from_x.at[j, k]), p.tok)
                if across:
                    to, at = jnp.where(a == 0, 1, A - 2), lax.rem(k, 2)
                else:
                    to, at = k, 3
            dev = (to * S + b, c)
            remote(mine, came.at[j, at], s_c.at[j, k], r_c.at[j, at], dev).start()

    def last(j, total):
        drain(from_x.at[j, a], r_x.at[j, a])
        drain(came.at[j, 2], r_c.at[j, 2])
        drain(came.at[j, 3], r_c.at[j, 3])
        mine = own.at[j, a, xh]
        add_rows(total, (mine, from_x.at[j, a], came.at[j, 2], came.at[j, 3]), p.tok)

    def unit_grads():
        loads[4].wait()
        for k in range(A):
            rows = slice(k * L, (k + 1) * L)
            for f in range(ffl // TILE):
                at = slice(f * TILE, (f + 1) * TILE)
                hid_t[at, rows] = hid_v[rows, at].astype(F32).T.astype(BF)
        for k in range(half):
            rows = slice(k * L, (k + 1) * L)
            heads_t[:, rows] = heads_v[rows, :].astype(F32).T.astype(BF)

        def g_load(i, slot):
            at = pl.ds(pl.multiple_of(i * TILE, TILE), TILE)
            return pltpu.make_async_copy(g.at[at], g_v.at[slot], g_sem.at[slot])

        drain(g_rows(far * 2 + 1 - core), r_g.at[1])
        g_load(0, 0).start()

        def step(i, carry):
            slot = lax.rem(i, 2)
            g_load(i, slot).wait()

            @pl.when(i + 1 < p.rows // TILE)
            def _():
                g_load(i + 1, 1 - slot).start()

            rows = pl.ds(pl.multiple_of(i * TILE, TILE), TILE)
            for f in range(ffl // TILE):
                at = pl.ds(f * TILE, TILE)
                d_unit = dot_t(g_v[slot], dw_v[f * TILE : (f + 1) * TILE, :])
                dpre[rows, at] = (d_unit * dpre[rows, at].astype(F32)).astype(BF)
            first = core * half * L

            @pl.when((i * TILE >= first) & (i * TILE < first + half * L))
            def _():
                at = pl.ds(pl.multiple_of(i * TILE - first, TILE), TILE)
                dh_v[at, :] = dot_t(g_v[slot], dw_v[ffl:, :]).astype(BF)

            return carry

        lax.fori_loop(0, p.rows // TILE, step, 0)
        loads[3].wait()

    cols = [pl.ds(j * HEAD_DIM, HEAD_DIM) for j in range(3)]
    rows2 = L // 2

    def attend_back(i, carry):
        rows = pl.ds(pl.multiple_of(i * L, L), L)
        dq, dk, dv = [], [], []
        for h in range(2):
            at = pl.ds(pl.multiple_of(i * L + h * rows2, rows2), rows2)
            keys = pl.ds(pl.multiple_of(i * L, L), (h + 1) * rows2)
            q, k, v = joint_v[at, cols[0]], joint_v[keys, cols[1]], joint_v[keys, cols[2]]
            dh = dh_v[at, :]
            probs = probabilities(q, k, h * rows2, SCALE)
            d_probs = dot_t(dh, v)
            delta = jnp.sum(probs * d_probs, axis=1, keepdims=True)
            d_scores = (probs * (d_probs - delta)).astype(BF)
            dq.append(dot(d_scores, k) * SCALE)
            dk.append(t_dot(d_scores, q) * SCALE)
            dv.append(t_dot(probs.astype(BF), dh))
        dq = jnp.concatenate(dq, axis=0)
        dk = jnp.concatenate([dk[0] + dk[1][:rows2], dk[1][rows2:]], axis=0)
        dv = jnp.concatenate([dv[0] + dv[1][:rows2], dv[1][rows2:]], axis=0)
        cos, sin = cos_v[...], sin_v[...]
        for j, d_part in enumerate((turn(dq, cos, -sin), turn(dk, cos, -sin), dv)):
            low = d_part.astype(BF)
            joint_v[rows, cols[j]] = low
            sums = jnp.sum(low.astype(F32), axis=0, keepdims=True)
            for k in range(HEAD_DIM // LANES):
                at = j * (HEAD_DIM // LANES) + k
                vec[at : at + 1, :] += sums[:, k * LANES : (k + 1) * LANES]
        return carry

    def n_load(src, i, slot):
        count = src.shape[0]
        return pltpu.make_async_copy(
            src.at[:, pl.ds(pl.multiple_of(i * TILE, TILE), TILE)],
            n_v.at[slot, pl.ds(0, count)],
            n_sem.at[slot],
        )

    def stream(src, use, low, high):
        n_load(src, low, low % 2).start()

        def step(i, carry):
            slot = lax.rem(i, 2)
            n_load(src, i, slot).wait()

            @pl.when(i + 1 < high)
            def _():
                n_load(src, i + 1, 1 - slot).start()

            use(i, slot)
            return carry

        lax.fori_loop(low, high, step, 0)

    pairs = TILE // (2 * r)

    def q_tile(i, slot):
        for j in range(3):
            acc = t_dot(n_v[slot, 0 : p.rows // 2, :], joint_v[:, cols[j]]).astype(BF)
            for k in range(pairs):
                for kk in range(2):
                    at = (2 * k + kk) * r
                    q_g[i * pairs + k, kk, :, cols[j]] = acc[at : at + r]

    def up_tile(i, slot):
        at = pl.ds(pl.multiple_of(i * TILE, TILE), TILE)
        ugrad[at, :] = t_dot(n_v[slot], dpre[...]).astype(BF)

    def down_tile(i, slot):
        at = pl.ds(pl.multiple_of(i * TILE, TILE), TILE)
        g_sum[:, at] = jnp.sum(n_v[slot].astype(F32), axis=0, keepdims=True)
        for f in range(ffl // TILE):
            rows = slice(f * TILE, (f + 1) * TILE)
            dgrad[rows, at] = dot(hid_t[rows, :], n_v[slot]).astype(BF)
        first = pl.multiple_of(core * half * L, L)
        acc = dot(heads_t[...], n_v[slot, pl.ds(first, half * L), :]).astype(BF)
        for k in range(p.m):
            for kk in range(2):
                to = (2 * k + kk) * r
                o_g[k, kk, :, at] = acc[to : to + r]

    def down_owner(j):
        if p.P == 1:
            return j, c
        return 2 * (j // 2) + core, xh * 2 + j % 2

    def down_send():
        for j in range(S):
            own_b, own_c = down_owner(j)
            src = dgrad.at[pl.ds(j * R, R)]
            here = (own_b == b) & (own_c == c)

            @pl.when(jnp.logical_not(here))
            def _():
                remote(src, d_parts.at[b], s_d.at[j], r_d, (a * S + own_b, own_c)).start()

            @pl.when(here)
            def _():
                pltpu.make_async_copy(src, d_parts.at[b], r_d).start()

        remote(o_g.at[:, 1 - core], o_sib, s_o, r_o, sib).start()

    def u_rows(aa, bb):
        return ugrad.at[pl.ds(pl.multiple_of((aa * S + bb) * blk, blk), blk)]

    def up_send():
        def one(k, carry):
            bb = lax.rem(b + k, S)
            for aa in range(A):
                remote(u_rows(aa, bb), u_parts.at[k - 1, aa], s_u, r_u, (a * S + bb, c)).start()
            return carry

        lax.fori_loop(1, S, one, 0)

    def up_along():
        for k in range(1, S):
            drain(u_parts.at[k - 1], r_u)
        for k in range(1, S):

            def add(aa, carry):
                add_rows(u_rows(aa, b), (u_rows(aa, b), u_parts.at[k - 1, aa]), blk)
                return carry

            lax.fori_loop(0, A, add, 0)
        for k in range(1, A):
            aa = lax.rem(a + k, A)
            remote(u_rows(aa, b), u_z.at[k - 1], s_uz, r_uz, (aa * S + b, c)).start()

    def up_home():
        drain(u_z, r_uz)
        for k in range(A):
            source = lax.rem(a - k + A, A)
            for step in range(C):
                cc = lax.rem(c + 1 + step, C)
                row = pl.multiple_of(cc * r, r)
                for j in range(ffl // p.W):
                    at = pl.ds(j * p.W, p.W)
                    if k == 0:
                        src = ugrad.at[
                            pl.ds(pl.multiple_of((a * S + b) * blk + cc * r, r), r), at
                        ]
                    else:
                        src = u_z.at[k - 1, pl.ds(row, r), at]
                    col = pl.multiple_of(unit_run(p, source, c, j), LANES)
                    dst = u_out.at[:, pl.ds(col, p.W)]
                    if step < C - 1:
                        remote(src, dst, s_ua, r_ua, (dp, cc)).start()
                    else:
                        pltpu.make_async_copy(src, dst, r_ua).start()

    def q_rows(aa, bb):
        return q_g.at[pl.ds((aa * S + bb) * X, X), core]

    def q_cross():
        drain(q_sib, r_q)

        def add(i, carry):
            mine = q_g.at[i, core]
            add_rows(mine, (mine, q_sib.at[i]), r)
            return carry

        lax.fori_loop(0, A * S * X, add, 0)

        def one(k, carry):
            bb = lax.rem(b + k, S)
            for aa in range(A):
                remote(q_rows(aa, bb), q_group.at[k - 1, aa], s_qb, r_qb, (a * S + bb, c)).start()
            return carry

        lax.fori_loop(1, S, one, 0)

    def q_along():
        for k in range(1, S):
            drain(q_group.at[k - 1], r_qb)
        for k in range(1, S):

            def add(i, carry):
                aa, xx = lax.div(i, X), lax.rem(i, X)
                mine = q_g.at[(aa * S + b) * X + xx, core]
                add_rows(mine, (mine, q_group.at[k - 1, aa, xx]), r)
                return carry

            lax.fori_loop(0, A * X, add, 0)
        for k in range(1, A):
            aa = lax.rem(a + k, A)
            remote(q_rows(aa, b), q_z.at[k - 1], s_qz, r_qz, (aa * S + b, c)).start()

    def q_home():
        drain(q_z, r_qz)
        for k in range(A):
            source = lax.rem(a - k + A, A)
            for xx in (far, xh):
                for j in range(3):
                    if k == 0:
                        src = q_g.at[(a * S + b) * X + xx, core, :, cols[j]]
                    else:
                        src = q_z.at[k - 1, xx, :, cols[j]]
                    col = pl.multiple_of(j * D + (source * X + xh) * HEAD_DIM, HEAD_DIM)
                    dst = q_out.at[:, pl.ds(col, HEAD_DIM)]
                    if xx is far:
                        remote(src, dst, s_qa, r_qa, xnb).start()
                    else:
                        pltpu.make_async_copy(src, dst, r_qa).start()

    def out_owner(k):
        return lax.div(head * HEAD_DIM, r) + 2 * k + core

    def out_home():
        drain(o_sib, r_o)
        for k in range(p.m):
            mine = o_g.at[k, core]
            add_rows(mine, (mine, o_sib.at[k]), r)
            od, oc = lax.div(out_owner(k), C), lax.rem(out_owner(k), C)

            @pl.when(out_owner(k) != me)
            def _():
                remote(mine, o_parts.at[b], s_oa.at[k], r_oa, (od, oc)).start()

            @pl.when(out_owner(k) == me)
            def _():
                pltpu.make_async_copy(mine, o_parts.at[b], r_oa).start()

    own_v = pltpu.make_async_copy(vec, v_all.at[me], loc.at[7])

    def sums_send():
        up_row = p.hc // LANES

        def sum_rows(i, carry):
            at = pl.ds(pl.multiple_of(i * 64, 64), 64)
            return carry + jnp.sum(dpre[at, :].astype(F32), axis=0, keepdims=True)

        sums = lax.fori_loop(0, p.rows // 64, sum_rows, jnp.zeros((1, ffl), F32))
        for i in range(ffl // LANES):
            vec[up_row + i : up_row + i + 1, :] = sums[:, i * LANES : (i + 1) * LANES]
        share = D // (A * C)
        g_row = up_row + ffl // LANES
        vec[g_row : g_row + 1, :] = g_sum[:, pl.ds(pl.multiple_of(t * share, share), share)]
        own_v.start()

        def one(k, carry):
            other = lax.rem(me + k, p.n)
            dev = (lax.div(other, C), lax.rem(other, C))
            remote(vec, v_all.at[me], s_v, r_v, dev).start()
            return carry

        lax.fori_loop(1, p.n, one, 0)

    def give_back():
        pl.semaphore_signal(free, inc=1, device_id=sib, device_id_type=MESH)

    partial(0, 0)
    partial(0, 1)
    chip_sum(0, order[0])
    partial(0, 2)
    chip_sum(0, order[1])
    partial(0, 3)
    g_forward()
    chip_sum(0, order[2])
    chip_sum(0, order[3])
    give_back()
    unit_grads()
    hop(0, 0, False)
    stream(n2, up_tile, 0, 4)
    hop(0, 1, False)
    stream(n2, up_tile, 4, 8)
    up_send()
    lax.fori_loop(0, half, attend_back, 0)
    partial(1, 0)
    partial(1, 1)
    chip_sum(1, order[0])
    hop(0, 0, True)
    hop(0, 2, False)
    chip_sum(1, order[1])
    partial(1, 2)
    partial(1, 3)
    chip_sum(1, order[2])
    hop(0, 1, True)
    chip_sum(1, order[3])
    up_along()
    stream(n1, q_tile, 0, 4)
    hop(1, 0, False)
    stream(n1, q_tile, 4, 8)
    remote(q_g.at[:, 1 - core], q_sib, s_q, r_q, sib).start()
    q_cross()
    stream(g, down_tile, 0, 4)
    hop(1, 1, False)
    stream(g, down_tile, 4, 8)
    down_send()
    hop(1, 2, False)
    hop(1, 0, True)
    q_along()
    out_home()
    sums_send()
    hop(1, 1, True)
    up_home()
    q_home()
    last(0, o_sum)
    last(1, e_sum)

    drain(u_out, r_ua)
    drain(q_out, r_qa)
    drain(v_all.at[pl.ds(0, p.n - 1)], r_v)
    drain(d_parts, r_d)
    drain(o_parts, r_oa)

    own_v.wait()
    for k in range(2):
        drain(g_rows(c), s_g.at[k])
    drain(v_all.at[pl.ds(0, p.n - 1)], s_v)
    drain(q_sib, s_q)
    drain(o_sib, s_o)
    for k in range(1, S):
        drain(u_parts.at[0], s_u)
        drain(q_group.at[0], s_qb)
    drain(u_z, s_uz)
    drain(q_z, s_qz)
    for _ in range(A):
        drain(ugrad.at[pl.ds(0, (C - 1) * r)], s_ua)
        drain(q_g.at[0, 0], s_qa)
    for k in range(p.m):

        @pl.when(out_owner(k) != me)
        def _():
            drain(o_g.at[k, 0], s_oa.at[k])

    for j in range(S):
        own_b, own_c = down_owner(j)

        @pl.when(jnp.logical_not((own_b == b) & (own_c == c)))
        def _():
            drain(d_parts.at[0], s_d.at[j])

    for k in range(A):
        drain(from_sib.at[0], s_s.at[1, k])
    for j in range(2):
        for k in range(A):
            drain(from_x.at[0, 0], s_x.at[j, k])

            @pl.when(k != a)
            def _():
                drain(from_x.at[0, 0], s_c.at[j, k])


def back(p, *args):
    dma = pltpu.SemaphoreType.DMA
    A, S, C, X, r, R = p.A, p.S, p.C, p.X, p.r, p.R
    L = C * p.tok
    vm = pltpu.VMEM
    hbm = pl.BlockSpec(memory_space=pl.ANY)
    vmem = pl.BlockSpec(memory_space=pltpu.VMEM)
    groups = max(S - 1, 1)
    return pl.pallas_call(
        functools.partial(back_kernel, p),
        out_shape=(
            jax.ShapeDtypeStruct((p.tok, p.d), F32),
            jax.ShapeDtypeStruct((p.tok, p.d), F32),
            jax.ShapeDtypeStruct((r, 3 * p.d), BF),
            jax.ShapeDtypeStruct((r, p.ff), BF),
            jax.ShapeDtypeStruct((S, R, p.d), BF),
            jax.ShapeDtypeStruct((S, r, p.d), BF),
            jax.ShapeDtypeStruct((p.n, 16, LANES), F32),
            jax.ShapeDtypeStruct((A - 1, C * r, p.ffl), BF),
            jax.ShapeDtypeStruct((A - 1, X, r, p.hc), BF),
            jax.ShapeDtypeStruct((p.rows, p.d), BF),
        ),
        input_output_aliases={3: 9},
        in_specs=[hbm] * 10 + [vmem],
        out_specs=[vmem] * 2 + [hbm] * 8,
        scratch_shapes=[
            vm((max(p.rows, p.d), p.ffl), BF),
            vm((p.rows // 2, HEAD_DIM), BF),
            vm((p.rows, p.ffl), BF),
            vm((2, TILE, p.d), BF),
            vm((p.rows // 2, p.hc), BF),
            vm((p.ffl + HEAD_DIM, p.d), BF),
            vm((p.d, p.ffl), BF),
            vm((p.d, p.hc), BF),
            vm((2, p.rows, TILE), BF),
            vm((p.ffl, p.rows), BF),
            vm((HEAD_DIM, p.rows // 2), BF),
            vm((p.rows // 2, HEAD_DIM), BF),
            vm((L, LANES), F32),
            vm((L, LANES), F32),
            vm((2, A, X, p.tok, p.d), BF),
            vm((A, X, p.tok, p.d), BF),
            vm((A, X, p.tok, p.d), BF),
            vm((2, A, p.tok, p.d), BF),
            vm((2, 4, p.tok, p.d), BF),
            vm((p.ffl, p.d), BF),
            vm((A * S * X, 2, r, p.hc), BF),
            vm((A * S * X, r, p.hc), BF),
            vm((groups, A, X, r, p.hc), BF),
            vm((p.m, 2, r, p.d), BF),
            vm((p.m, r, p.d), BF),
            vm((groups, A, C * r, p.ffl), BF),
            vm((1, p.d), F32),
            vm((16, LANES), F32),
            dma((8,)),
            dma((2,)),
            dma((2,)),
            dma,
            dma,
            dma((2, A)),
            dma((2, A)),
            dma((2, A)),
            dma((2, A)),
            dma((2, A)),
            dma((2, 4)),
            dma,
            dma,
            dma,
            dma,
            dma,
            dma,
            dma,
            dma,
            dma,
            dma,
            dma((p.m,)),
            dma,
            dma,
            dma,
            dma,
            dma,
            dma,
            dma,
            dma((S,)),
            dma,
            dma((2,)),
            dma((2,)),
            pltpu.SemaphoreType.REGULAR,
        ],
        compiler_params=pltpu.CompilerParams(
            collective_id=1, has_side_effects=True, vmem_limit_bytes=67043328
        ),
        name="back",
    )(*args)


def finish_kernel(
    p,
    lens,
    x,
    g,
    o_sum,
    e_sum,
    full,
    q_part,
    u_part,
    d_parts,
    o_parts,
    sums,
    qkv_w,
    up_w,
    gain1,
    bias1,
    gain2,
    bias2,
    out,
    grad,
    q_grad,
    u_grad,
    d_grad,
    o_grad,
    q_own,
    u_own,
    g_own,
    g_same,
    gain1_grad,
    bias1_grad,
    gain2_grad,
    bias2_grad,
    q_bias,
    u_bias,
    g_bias,
    row_sums,
):
    A, S, C, X = p.A, p.S, p.C, p.X
    step = pl.program_id(0)

    @pl.when(step == 0)
    def _():
        up_row = p.hc // LANES
        g_row = up_row + p.ffl // LANES
        share = p.d // (A * C)
        for aa in range(A):
            for cc in range(C):
                for row in range(up_row, g_row + 1):
                    total = sums[aa * S * C + cc, row : row + 1, :]
                    for bb in range(1, S):
                        total = total + sums[(aa * S + bb) * C + cc, row : row + 1, :]
                    if row == g_row:
                        at = (aa * C + cc) * share
                        g_bias[:, at : at + share] = total[:, :share]
                        continue
                    unit = (row - up_row) * LANES
                    run = unit // p.W
                    if p.P == 1:
                        first = p.R * ((aa * S + run) * C + cc)
                    else:
                        first = p.R * ((aa * S + 2 * run + cc % 2) * C + cc // 2 * 2)
                    at = first + unit % p.W
                    u_bias[:, at : at + LANES] = total
            for xx in range(X):
                for row in range(up_row):
                    total = jnp.zeros((1, LANES), F32)
                    for bb in range(S):
                        for kk in range(2):
                            total = total + sums[(aa * S + bb) * C + xx * 2 + kk, row : row + 1, :]
                    j, rest = row * LANES // HEAD_DIM, row * LANES % HEAD_DIM
                    at = j * p.d + (aa * X + xx) * HEAD_DIM + rest
                    q_bias[:, at : at + LANES] = total
        me = lax.axis_index("dp") * C + lax.axis_index("ctx")

        def own(vector, size):
            span = max(size * i % LANES + size for i in range(p.n))
            span = (span + LANES - 1) // LANES * LANES
            rest = lax.rem(size * me, LANES)
            at = pl.multiple_of(size * me - rest, LANES)
            piece = pltpu.roll(vector[:, pl.ds(at, span)], lax.rem(span - rest, span), 1)
            return piece[0, :size]

        q_own[...] = own(q_bias, 3 * p.d // p.n)
        u_own[...] = own(u_bias, p.ff // p.n)
        g_own[...] = own(g_bias, p.d // p.n)
        g_same[...] = own(g_bias, p.d // p.n)

    rows = x.shape[0]
    sub = 32
    first = lax.axis_index("ctx") * p.tok + step * rows
    length = lens[0]

    def tokens(at):
        here = pl.ds(at, sub)
        row = lax.broadcasted_iota(jnp.int32, (sub, p.d), 0) + (at + first)
        live = row < length
        xf = x[here, :].astype(F32)
        total = xf + o_sum[here, :] + full[4:5, :]
        out[here, :] = jnp.where(live, total, 0.0).astype(BF)
        mid = xf - jnp.mean(xf, axis=1, keepdims=True)
        inv = lax.rsqrt(jnp.mean(mid * mid, axis=1, keepdims=True) + EPS)
        xhat = mid * inv
        e = e_sum[here, :]
        e_mean = jnp.mean(e, axis=1, keepdims=True)
        dx = inv * (e - e_mean - xhat * jnp.mean(e * xhat, axis=1, keepdims=True))
        go = jnp.where(live, g[here, :].astype(F32), 0.0)
        grad[here, :] = (go + dx).astype(BF)

    tiles(rows, tokens, sub)

    count = q_part.shape[0]
    lane = lax.broadcasted_iota(jnp.int32, (count, LANES), 1)
    kept = jnp.zeros((count, LANES), F32)
    for k, (part, weight, bias, result) in enumerate(
        ((q_part, qkv_w, q_bias, q_grad), (u_part, up_w, u_bias, u_grad))
    ):
        with_grad = jnp.zeros((part.shape[0], LANES), F32)
        with_bias = jnp.zeros((part.shape[0], LANES), F32)
        for n in range(0, part.shape[1], LANES):
            at = slice(n, n + LANES)
            value = part[:, at].astype(F32)
            result[:, at] = value
            w = weight[:, at].astype(F32)
            with_grad = with_grad + w * value
            with_bias = with_bias + w * bias[:, at]
        for o, t in enumerate((with_grad, with_bias)):
            kept = jnp.where(lane == 2 * k + o, jnp.sum(t, axis=1, keepdims=True), kept)
    row_sums[pl.ds(pl.multiple_of(step * count, count), count), :] = kept

    @pl.when(step == pl.num_programs(0) - 1)
    def _():
        turned = row_sums[...].T
        for k, (gain, shift, to_gain, to_shift) in enumerate(
            ((gain1, bias1, gain1_grad, bias1_grad), (gain2, bias2, gain2_grad, bias2_grad))
        ):
            with_grad, with_bias = turned[2 * k, : p.r], turned[2 * k + 1, : p.r]
            to_gain[...] = (with_grad - shift[...].astype(F32) * with_bias) / gain[...].astype(F32)
            to_shift[...] = with_bias

    for parts, result in ((d_parts, d_grad), (o_parts, o_grad)):

        size = min(sub, result.shape[0])

        def add(at):
            here = pl.ds(at, size)
            total = parts[0, here, :].astype(F32)
            for k in range(1, S):
                total = total + parts[k, here, :].astype(F32)
            result[here, :] = total

        tiles(result.shape[0], add, size)


def finish(p, *args):
    steps = max(1, p.r // 32)
    D, r, R = p.d, p.r, p.R

    def rows(count, width):
        return pl.BlockSpec((count // steps, width), lambda i: (i, 0))

    def parts(count):
        return pl.BlockSpec((p.S, count // steps, D), lambda i: (0, i, 0))

    def whole(*shape):
        return pl.BlockSpec(shape, lambda i: (0,) * len(shape))

    tok = rows(p.tok, D)
    return pl.pallas_call(
        functools.partial(finish_kernel, p),
        grid=(steps,),
        out_shape=(
            jax.ShapeDtypeStruct((p.tok, D), BF),
            jax.ShapeDtypeStruct((p.tok, D), BF),
            jax.ShapeDtypeStruct((r, 3 * D), F32),
            jax.ShapeDtypeStruct((r, p.ff), F32),
            jax.ShapeDtypeStruct((R, D), F32),
            jax.ShapeDtypeStruct((r, D), F32),
            jax.ShapeDtypeStruct((3 * D // p.n,), F32),
            jax.ShapeDtypeStruct((p.ff // p.n,), F32),
            *[jax.ShapeDtypeStruct((r,), F32)] * 6,
        ),
        in_specs=[
            pl.BlockSpec(memory_space=pltpu.SMEM),
            tok,
            tok,
            tok,
            tok,
            whole(8, D),
            rows(r, 3 * D),
            rows(r, p.ff),
            parts(R),
            parts(r),
            whole(p.n, 16, LANES),
            rows(r, 3 * D),
            rows(r, p.ff),
            *[whole(r)] * 4,
        ],
        out_specs=[
            tok,
            tok,
            rows(r, 3 * D),
            rows(r, p.ff),
            rows(R, D),
            rows(r, D),
            whole(3 * D // p.n),
            whole(p.ff // p.n),
            *[whole(r)] * 6,
        ],
        scratch_shapes=[
            pltpu.VMEM((1, 3 * D), F32),
            pltpu.VMEM((1, p.ff), F32),
            pltpu.VMEM((1, D), F32),
            pltpu.VMEM((r, LANES), F32),
        ],
        compiler_params=pltpu.CompilerParams(dimension_semantics=("arbitrary",)),
        name="finish",
    )(*args)


def local(
    dp_size,
    ctx_size,
    layer_input,
    lengths,
    cotangent,
    qkv_weight,
    qkv_bias,
    out_weight,
    out_bias,
    up_weight,
    up_bias,
    down_weight,
    down_bias,
    first_gain,
    first_bias,
    second_gain,
    second_bias,
):
    tok, d = layer_input.shape
    ff = up_weight.shape[1]
    p = Plan(dp_size, ctx_size, tok, d, ff)
    A, S, C, X, r, R = p.A, p.S, p.C, p.X, p.r, p.R
    dp, c, a, b, xh, core = place(p)
    me = dp * C + c
    t = a * C + c
    vectors = (
        qkv_bias,
        out_bias,
        up_bias,
        down_bias,
        first_gain,
        first_bias,
        second_gain,
        second_bias,
    )
    (_, g_all, qw, dw, uw, _, n1, n2, hid, slope, heads, joint, full) = front(
        p,
        layer_input,
        cotangent,
        qkv_weight,
        out_weight,
        up_weight,
        down_weight,
        lengths,
        *vectors,
    )
    o_sum, e_sum, q_out, u_out, d_parts, o_parts, v_all, _, _, _ = back(
        p,
        hid,
        heads,
        slope,
        g_all.reshape(p.rows, d),
        joint,
        n1,
        n2,
        dw,
        uw.reshape(d, p.ffl),
        qw.reshape(d, p.hc),
        full,
    )
    (
        output,
        input_grad,
        q_grad,
        u_grad,
        d_grad,
        o_grad,
        q_bias,
        u_bias,
        g_bias,
        g_same,
        gain1_grad,
        bias1_grad,
        gain2_grad,
        bias2_grad,
    ) = finish(
        p,
        lengths,
        layer_input,
        cotangent,
        o_sum,
        e_sum,
        full,
        q_out,
        u_out,
        d_parts,
        o_parts,
        v_all,
        qkv_weight,
        up_weight,
        first_gain,
        first_bias,
        second_gain,
        second_bias,
    )
    return (
        output,
        input_grad,
        q_grad,
        q_bias,
        o_grad,
        g_bias,
        u_grad,
        u_bias,
        d_grad,
        g_same,
        gain1_grad,
        bias1_grad,
        gain2_grad,
        bias2_grad,
    )


def solution(mesh):
    rows = P(("dp", "ctx"), None)
    vector = P(("dp", "ctx"))
    return jax.shard_map(
        functools.partial(local, mesh.shape["dp"], mesh.shape["ctx"]),
        mesh=mesh,
        in_specs=(
            rows,
            P("dp"),
            rows,
            rows,
            vector,
            rows,
            vector,
            rows,
            vector,
            rows,
            vector,
            vector,
            vector,
            vector,
            vector,
        ),
        out_specs=(
            rows,
            rows,
            rows,
            vector,
            rows,
            vector,
            rows,
            vector,
            rows,
            vector,
            vector,
            vector,
            vector,
            vector,
        ),
        check_vma=False,
    )
```
